32 devices in a mesh: seq: 8 (over y, x, core), head: 4 (over z).
Axes of the slice: x: 2, y: 2, z: 4, core: 2. Of those that a mesh axis runs over, the one named last changes fastest.
Arguments:
- tokens: bfloat16 [3, 2048, 2048], P(None, ('seq', 'head')), may hold values from -6 to 6
- starts: int32 [3, 32], P(None, 'seq'), may hold values from 0 to 1, as said below
- cotangent: bfloat16 [3, 2048, 2048], P(None, ('seq', 'head')), may hold values from -6 to 6
- mix_in: bfloat16 [2048, 6144], P('seq'), may hold values from -0.125 to 0.125
- mix_out: bfloat16 [2048, 2048], P('seq'), may hold values from -0.25 to 0.25
- gate_up: bfloat16 [2048, 2, 5632], P('seq', None, 'head'), may hold values from -0.125 to 0.125
- down_proj: bfloat16 [2048, 5632], P('seq', 'head'), may hold values from -0.15625 to 0.15625
- norm_gain: float32 [2048], replicated, may hold values from 0.5 to 1.5
- ffn_gain: float32 [2048], replicated, may hold values from 0.5 to 1.5
- head_gain: float32 [512], replicated, may hold values from 0.5 to 1.5
- rank_down: bfloat16 [2048, 16], replicated, may hold values from -0.125 to 0.125
- rank_up: float32 [16, 1024], replicated, may hold values from -2.4 to 2.4
- gate_bias: float32 [1024], replicated, may hold values from -0.5 to 7
Outputs:
- output: bfloat16 [3, 2048, 2048], P(None, ('seq', 'head'))
- input_grad: float32 [3, 2048, 2048], P(None, ('seq', 'head'))
- grad_mix_in: float32 [2048, 6144], P(('seq', 'head'))
- grad_mix_out: float32 [2048, 2048], P(('seq', 'head'))
- grad_gate_up: float32 [2048, 2, 5632], P('seq', None, 'head')
- grad_down: float32 [2048, 5632], P('seq', 'head')
- grad_norm_gain: float32 [2048], replicated
- grad_ffn_gain: float32 [2048], replicated
- grad_head_gain: float32 [512], replicated
- grad_rank_down: float32 [2048, 16], replicated
- grad_rank_up: float32 [16, 1024], replicated
- grad_gate_bias: float32 [1024], replicated
The draws below stay inside these ranges and needn't reach their ends.
Inputs may be any that keep to these rules, and one draw needn't show every extreme that they name: starts[b, 0] is 1 for every micro-batch b; two ones of a row lie at least 32 blocks apart, and the last one of a row lies at least 32 blocks before the row's end.
All inputs are finite; a program needn't handle non-finite values.
Results may differ from the reference program's by a relative error of at most 0.015.
The reference program's roundings to bfloat16 on the way count: a program that leaves them out, or rounds other values in their place, can miss the bound.
Values may be sent and summed in bfloat16 or wider, within the bound.
A program may use at most 248 MiB of HBM per device.

```python
import jax
import jax.numpy as jnp
from jax import lax

D = 2048
HEADS = 4
DK = 256
DV = 512
FF = 5632
RANK = 16
BLOCK = 64
MIN_BLOCKS = 32
MB = 3
KEYS = 1024
VALS = 2048
PROJ = 6144
TOKENS_MB = 2048
BLOCKS_MB = 32


def draw_starts(key, part):
    lengths = jax.random.randint(key, (MB, BLOCKS_MB // MIN_BLOCKS + 1), MIN_BLOCKS, 4 * MIN_BLOCKS + 1)
    finish = jnp.cumsum(lengths, axis=1)
    begins = finish - lengths
    places = jnp.arange(BLOCKS_MB, dtype=jnp.int32)
    hits = (begins[:, :, None] == places[None, None, :]) & (places[None, None, :] <= BLOCKS_MB - MIN_BLOCKS)
    return jnp.any(hits, axis=1).astype(jnp.int32)


def level_of(key, dims, cuts, low, top_value):
    def one(axis_at, parts):
        draws = jax.random.uniform(jax.random.fold_in(jax.random.fold_in(key, 6), axis_at), (parts,), jnp.float32, low / len(cuts), top_value / len(cuts))
        return jnp.repeat(jnp.exp(draws), dims[axis_at] // parts).reshape((-1,) + (1,) * (len(dims) - axis_at - 1))

    factor_of = one(*cuts[0])
    for cut in cuts[1:]:
        factor_of = factor_of * one(*cut)
    return factor_of


def normal_values(stream_key, extent, width, bound, cuts=(), held_as=jnp.bfloat16):
    entries = jax.random.normal(stream_key, extent, jnp.float32) * width
    if len(cuts) > 0:
        entries = level_of(stream_key, extent, cuts, -0.22, 0.18) * entries
    return jnp.clip(entries, min=-bound, max=bound).astype(held_as)


def setup_inputs(seed: int = 0) -> dict:
    keys = jax.random.split(jax.random.key(seed), 14)
    return {
        "tokens": normal_values(keys[0], (MB, TOKENS_MB, D), 1.0, 6.0, ((1, 32),)),
        "starts": draw_starts(jax.random.fold_in(keys[13], 71), 0),
        "cotangent": normal_values(keys[2], (MB, TOKENS_MB, D), 1.0, 6.0, ((1, 32),)),
        "mix_in": normal_values(keys[3], (D, PROJ), D ** -0.5, 0.125, ((0, 8),)),
        "mix_out": normal_values(keys[4], (D, VALS), (VALS // 4) ** -0.5, 0.25, ((0, 8),)),
        "gate_up": normal_values(keys[5], (D, 2, FF), D ** -0.5, 0.125, ((0, 8), (2, 4))),
        "down_proj": normal_values(keys[6], (D, FF), (FF // 4) ** -0.5, 0.15625, ((0, 8), (1, 4))),
        "norm_gain": jnp.clip(1.0 + 0.1 * jax.random.normal(keys[7], (D,), jnp.float32), 0.5, 1.5),
        "ffn_gain": jnp.clip(1.0 + 0.1 * jax.random.normal(keys[8], (D,), jnp.float32), 0.5, 1.5),
        "head_gain": jnp.clip(1.0 + 0.1 * jax.random.normal(keys[9], (DV,), jnp.float32), 0.5, 1.5),
        "rank_down": normal_values(keys[10], (D, RANK), D ** -0.5, 0.125),
        "rank_up": normal_values(keys[11], (RANK, KEYS), 0.4, 2.4, (), jnp.float32),
        "gate_bias": jnp.clip(jax.random.uniform(keys[12], (KEYS,), jnp.float32, -0.5, 7.0), -0.5, 7.0),
    }


@jax.custom_vjp
def low(v):
    return lax.optimization_barrier(v.astype(jnp.bfloat16)).astype(jnp.float32)

@jax.custom_vjp
def low_back(v):
    return v

def low_keep(v):
    return (low(v), None)

def low_pass(kept, grad):
    return (grad,)

def back_keep(v):
    return (v, None)

def back_low(kept, grad):
    return (low(grad),)
low.defvjp(low_keep, low_pass)
low_back.defvjp(back_keep, back_low)
highest_precision = lax.Precision.HIGHEST
gate_norm = 16.0

def rms_norm(incoming_values, gain_vec, epsilon):
    return incoming_values * lax.rsqrt(lax.optimization_barrier(jnp.mean(incoming_values * incoming_values, axis=-1, keepdims=True)) + epsilon) * gain_vec

def block_heads(carry_state, inputs):
    queries, keys_in, incoming_values, decays, reset_flag = inputs
    incoming_state = carry_state * (1.0 - reset_flag)
    decay_sum = jnp.cumsum(decays, axis=0)
    decay_total = decay_sum[-1]
    queried_state = queries * jnp.exp(decay_sum) * DK ** (-0.5)
    keyed = keys_in * jnp.exp(-decay_sum)
    scores = jnp.einsum('thk,shk->hts', queried_state, keyed, precision=highest_precision)
    causal = jnp.tril(jnp.ones((BLOCK, BLOCK), dtype=bool))
    scores = jnp.where(causal[None], scores, 0.0)
    output = jnp.einsum('hts,shv->thv', scores, incoming_values, precision=highest_precision)
    output = output + jnp.einsum('syl,ylo->syo', queried_state, incoming_state, precision=highest_precision)
    carried_state_value = keys_in * jnp.exp(decay_total[None] - decay_sum)
    updated_state = jnp.exp(decay_total)[:, :, None] * incoming_state
    updated_state = updated_state + jnp.einsum('uzm,uzn->zmn', carried_state_value, incoming_values, precision=highest_precision)
    return (updated_state, output)

def run_heads(queries, keys_in, incoming_values, decays, flags):
    block_count = queries.shape[0] // BLOCK

    def to_blocks(tensor):
        return tensor.reshape(block_count, BLOCK, tensor.shape[1], tensor.shape[2])
    initial = jnp.zeros((HEADS, DK, DV), jnp.float32)
    final_state, outputs = lax.scan(jax.checkpoint(block_heads), initial, (to_blocks(queries), to_blocks(keys_in), to_blocks(incoming_values), to_blocks(decays), flags.astype(jnp.float32)))
    return outputs.reshape(queries.shape[0], HEADS, DV)

def forward_one(source, flags, params):
    mix_in, mix_out, gate_up, down_proj, norm_gain, ffn_gain, head_gain, rank_down, rank_up, gate_bias = params
    row_count = source.shape[0]
    normed_in = low(rms_norm(source, norm_gain, 1e-06))
    projected = jnp.dot(normed_in, mix_in, precision=highest_precision)
    queries = low(low_back(projected[:, :KEYS]))
    keys_in = low(low_back(projected[:, KEYS:2 * KEYS]))
    incoming_values = low(low_back(projected[:, 2 * KEYS:2 * KEYS + VALS]))
    out_gate = low_back(projected[:, 2 * KEYS + VALS:])
    ranked = jnp.dot(normed_in, rank_down, precision=highest_precision)
    logits = jnp.dot(ranked, rank_up, precision=highest_precision) + gate_bias
    decays = low(low_back(jax.nn.log_sigmoid(logits) / gate_norm))
    mixed_heads = run_heads(queries.reshape(row_count, HEADS, DK), keys_in.reshape(row_count, HEADS, DK), incoming_values.reshape(row_count, HEADS, DV), decays.reshape(row_count, HEADS, DK), flags)
    head_normed = low(low_back(rms_norm(mixed_heads, head_gain, 1e-05))).reshape(row_count, VALS)
    gated = low(head_normed * out_gate * jax.nn.sigmoid(out_gate))
    mixed = low_back(jnp.dot(gated, mix_out.T, precision=highest_precision))
    hidden = source + mixed
    normed_ffn = low(rms_norm(hidden, ffn_gain, 1e-06))
    gate_both = jnp.einsum('td,dsf->tsf', normed_ffn, gate_up, precision=highest_precision)
    gate_lin = low_back(gate_both[:, 0])
    up_lin = low_back(gate_both[:, 1])
    product = low(gate_lin * jax.nn.sigmoid(gate_lin) * up_lin)
    ffn_out = low_back(jnp.dot(product, down_proj.T, precision=highest_precision))
    return hidden + ffn_out

def layer_block(source, starts, params):
    results = []
    for micro_index in range(source.shape[0]):
        results.append(forward_one(source[micro_index], starts[micro_index], params))
    return jnp.stack(results)

def reference(tokens, starts, cotangent, mix_in, mix_out, gate_up, down_proj, norm_gain, ffn_gain, head_gain, rank_down, rank_up, gate_bias):
    params = (mix_in.astype(jnp.float32), mix_out.astype(jnp.float32), gate_up.astype(jnp.float32), down_proj.astype(jnp.float32), norm_gain.astype(jnp.float32), ffn_gain.astype(jnp.float32), head_gain.astype(jnp.float32), rank_down.astype(jnp.float32), rank_up.astype(jnp.float32), gate_bias.astype(jnp.float32))
    source = tokens.astype(jnp.float32)

    def whole(source_in, params_in):
        return layer_block(source_in, starts, params_in)
    primal_values, pullback = jax.vjp(whole, source, params)
    grad_source, grads = pullback(cotangent.astype(jnp.float32))
    return (primal_values.astype(jnp.bfloat16), grad_source, grads[0], grads[1], grads[2], grads[3], grads[4], grads[5], grads[6], grads[7], grads[8], grads[9])
```

```python
import functools

import jax
import jax.numpy as jnp
from jax import lax
from jax.experimental import pallas as pl
from jax.experimental.pallas import tpu as pltpu
from jax.sharding import PartitionSpec as P

HIGHEST = lax.Precision.HIGHEST
GATE_NORM = 16.0
BF16 = jnp.bfloat16
F32 = jnp.float32


def mm(a, b, contract, precision=HIGHEST):
    return lax.dot_general(
        a, b, ((contract[:1], contract[1:]), ((), ())),
        precision=precision, preferred_element_type=F32,
    )


def lower_ones(size):
    rows = lax.broadcasted_iota(jnp.int32, (size, size), 0)
    cols = lax.broadcasted_iota(jnp.int32, (size, size), 1)
    return rows >= cols


def running(decay_low):
    ones = lower_ones(decay_low.shape[0]).astype(F32).astype(BF16)
    return mm(ones, decay_low, (1, 0), None)


def sigmoid(x):
    return 1.0 / (1.0 + jnp.exp(-x))


def state_kernel(flags, qkv, decay, out, state, total_run):
    m, b = pl.program_id(0), pl.program_id(1)
    last = pl.num_programs(1) - 1
    dk = decay.shape[-1]
    keys, values = qkv[0, 0, :, dk : 2 * dk].astype(F32), qkv[0, 0, :, 2 * dk :].astype(F32)
    keep = 1.0 - flags[m, b].astype(F32)

    @pl.when(b == 0)
    def _():
        state[...] = jnp.zeros_like(state)
        total_run[0:1, :] = jnp.zeros((1, dk), F32)
        total_run[1:2, :] = jnp.ones((1, dk), F32)

    run = running(decay[0, 0])
    total = run[-1:, :]
    carried = keys * jnp.exp(total - run)
    state[...] = jnp.exp(total) * (state[...] * keep) + mm(values, carried, (0, 0))
    total_run[0:1, :] += total
    total_run[1:2, :] *= keep

    @pl.when(b == last)
    def _():
        through = jnp.exp(total_run[0:1, :]) * total_run[1:2, :]
        high = through.astype(BF16)
        low = (through - high.astype(F32)).astype(BF16)
        slices, part = out.shape[0], state.shape[0] // out.shape[0]
        tail = out.shape[2] - part
        at = lax.broadcasted_iota(jnp.int32, (tail, dk), 0)
        extra = jnp.where(
            at == 0, high.astype(F32), jnp.where(at == 1, low.astype(F32), 0.0)
        ).astype(BF16)
        for i in range(slices):
            out[i, 0, :part, :] = state[i * part : (i + 1) * part, :].astype(BF16)
            out[i, 0, part:, :] = extra


def prefix_kernel(reverse, own, through, out):
    count = own.shape[0]
    part = out.shape[2]

    def step(k, state):
        j = count - 1 - k if reverse else k
        out[j] = state.astype(BF16)
        decay = through[j, :, 0:1, :].astype(F32) + through[j, :, 1:2, :].astype(F32)
        return decay * state + own[j, :, :part, :].astype(F32)

    lax.fori_loop(0, count, step, jnp.zeros(out.shape[1:], F32))


def mix_kernel(flags, qkv, decay, og, before, gain, o_out, gated, kept, state):
    m, b = pl.program_id(0), pl.program_id(1)
    dk, dv = decay.shape[-1], og.shape[-1]
    q = qkv[0, 0, :, :dk].astype(F32)
    k = qkv[0, 0, :, dk : 2 * dk].astype(F32)
    v = qkv[0, 0, :, 2 * dk :].astype(F32)
    keep = 1.0 - flags[m, b].astype(F32)

    @pl.when(b == 0)
    def _():
        state[...] = before[:, 0].astype(F32).reshape(dv, dk)

    entry = state[...] * keep
    kept[0, 0] = entry
    run = running(decay[0, 0])
    total = run[-1:, :]
    queried = q * jnp.exp(run) * dk ** (-0.5)
    scores = mm(queried, k * jnp.exp(-run), (1, 1))
    scores = jnp.where(lower_ones(scores.shape[0]), scores, 0.0)
    o = mm(scores, v, (1, 0)) + mm(queried, entry, (1, 1))
    state[...] = jnp.exp(total) * entry + mm(v, k * jnp.exp(total - run), (0, 0))
    o_out[0, 0] = o
    scale = lax.rsqrt(jnp.mean(o * o, axis=-1, keepdims=True) + 1e-5)
    normed = (o * scale * gain[...]).astype(BF16).astype(F32)
    gate = og[0, 0]
    gated[0, 0] = (normed * gate * sigmoid(gate)).astype(BF16)


def gate_back_kernel(flags, g_gated, og, o_in, qkv, decay, gain, g_og, g_o, pulled, g_gain,
                     state, total_run):
    m, b = pl.program_id(0), pl.program_id(1)
    last = pl.num_programs(1) - 1
    dk, dv = decay.shape[-1], og.shape[-1]

    @pl.when((m == 0) & (b == 0))
    def _():
        g_gain[...] = jnp.zeros_like(g_gain)

    @pl.when(b == 0)
    def _():
        state[...] = jnp.zeros_like(state)
        total_run[0:1, :] = jnp.zeros((1, dk), F32)
        total_run[1:2, :] = jnp.ones((1, dk), F32)

    gate = og[0, 0]
    grad = g_gated[0, 0].astype(F32)
    sig = sigmoid(gate)
    o = o_in[0, 0]
    scale = lax.rsqrt(jnp.mean(o * o, axis=-1, keepdims=True) + 1e-5)
    plain = o * scale
    normed = (plain * gain[...]).astype(BF16).astype(F32)
    g_on = (grad * gate * sig).astype(BF16).astype(F32)
    g_og[0, 0] = (grad * normed * sig * (1.0 + gate * (1.0 - sig))).astype(BF16)
    scaled = g_on * gain[...]
    inner = jnp.mean(scaled * plain, axis=-1, keepdims=True)
    go = scale * (scaled - plain * inner)
    g_o[0, 0] = go
    g_gain[0:1, :] += jnp.sum(g_on * plain, axis=0, keepdims=True)

    total_run[1:2, :] *= 1.0 - flags[m, b].astype(F32)
    run = running(decay[0, 0])
    reach = (
        qkv[0, 0, :, :dk].astype(F32)
        * jnp.exp(run + total_run[0:1, :])
        * total_run[1:2, :]
        * dk ** (-0.5)
    )
    state[...] += mm(go, reach, (0, 0))
    total_run[0:1, :] += run[-1:, :]

    @pl.when(b == last)
    def _():
        slices, part = pulled.shape[0], dv // pulled.shape[0]
        for i in range(slices):
            pulled[i, 0] = state[i * part : (i + 1) * part, :].astype(BF16)


def mix_back_kernel(flags, qkv, decay, g_o, g_og, kept, after, logits, g_proj, g_logits, g_state):
    m, step = pl.program_id(0), pl.program_id(1)
    b = pl.num_programs(1) - 1 - step
    dk, dv = decay.shape[-1], g_o.shape[-1]
    q = qkv[0, 0, :, :dk].astype(F32)
    k = qkv[0, 0, :, dk : 2 * dk].astype(F32)
    v = qkv[0, 0, :, 2 * dk :].astype(F32)
    keep = 1.0 - flags[m, b].astype(F32)

    @pl.when(step == 0)
    def _():
        g_state[...] = after[:, 0].astype(F32).reshape(dv, dk)

    go, gs, entry = g_o[0, 0], g_state[...], kept[0, 0]
    run = running(decay[0, 0])
    total = run[-1:, :]
    up, down, rest = jnp.exp(run) * dk ** (-0.5), jnp.exp(-run), jnp.exp(total - run)
    decayed = jnp.exp(total)
    queried, keyed, carried = q * up, k * down, k * rest
    causal = lower_ones(q.shape[0])
    scores = jnp.where(causal, mm(queried, keyed, (1, 1)), 0.0)
    g_scores = jnp.where(causal, mm(go, v, (1, 1)), 0.0)
    g_queried = mm(g_scores, keyed, (1, 0)) + mm(go, entry, (1, 0))
    g_keyed = mm(g_scores, queried, (0, 0))
    g_v = mm(scores, go, (0, 0)) + mm(carried, gs, (1, 1))
    g_carried = mm(v, gs, (1, 0))
    g_state[...] = (decayed * gs + mm(go, queried, (0, 0))) * keep
    from_carried = g_carried * carried
    g_total = (
        jnp.sum(decayed * entry * gs, axis=0, keepdims=True)
        + jnp.sum(from_carried, axis=0, keepdims=True)
    )
    g_run = g_queried * queried - g_keyed * keyed - from_carried
    later = mm(causal.astype(F32), g_run, (0, 0)) + g_total
    proj = jnp.concatenate([g_queried * up, g_keyed * down + g_carried * rest, g_v], axis=1)
    width = proj.shape[1]
    g_proj[0, 0, :, :width] = proj.astype(BF16)
    g_proj[0, 0, :, width:] = g_og[0, 0]
    low = later.astype(BF16).astype(F32)
    g_logits[0, 0] = low * sigmoid(-logits[0, 0]) * (1.0 / GATE_NORM)


def params(limit=48):
    return pltpu.CompilerParams(
        dimension_semantics=("arbitrary", "arbitrary"), vmem_limit_bytes=limit << 20
    )


def per_block(rows, width):
    return pl.BlockSpec((1, 1, rows, width), lambda m, b, *_: (b, m, 0, 0))


def backwards(rows, width, count):
    return pl.BlockSpec((1, 1, rows, width), lambda m, b, *_: (count - 1 - b, m, 0, 0))


def per_batch(slices, rows, width):
    return pl.BlockSpec((slices, 1, rows, width), lambda m, b, *_: (0, m, 0, 0))


def states_of(flags, qkv, decays, dv, slices, pad):
    blocks, micro, rows, width = qkv.shape
    dk = decays.shape[-1]
    part = dv // slices
    return pl.pallas_call(
        state_kernel,
        out_shape=jax.ShapeDtypeStruct((slices, micro, part + pad, dk), BF16),
        grid_spec=pltpu.PrefetchScalarGridSpec(
            num_scalar_prefetch=1,
            grid=(micro, blocks),
            in_specs=[per_block(rows, width), per_block(rows, dk)],
            out_specs=per_batch(slices, part + pad, dk),
            scratch_shapes=[pltpu.VMEM((dv, dk), F32), pltpu.VMEM((8, dk), F32)],
        ),
        compiler_params=params(),
        name="states",
    )(flags, qkv, decays)


def prefix_of(own, through, part, reverse):
    return pl.pallas_call(
        functools.partial(prefix_kernel, reverse),
        out_shape=jax.ShapeDtypeStruct(own.shape[:2] + (part, own.shape[3]), BF16),
        in_specs=[pl.BlockSpec(memory_space=pltpu.VMEM)] * 2,
        out_specs=pl.BlockSpec(memory_space=pltpu.VMEM),
        compiler_params=pltpu.CompilerParams(vmem_limit_bytes=48 << 20),
        name="suffix" if reverse else "prefix",
    )(own, through)


def mix_of(flags, qkv, decays, og, before, gain):
    blocks, micro, rows, width = qkv.shape
    dk, dv = decays.shape[-1], og.shape[-1]
    slices, _, part, _ = before.shape
    return pl.pallas_call(
        mix_kernel,
        out_shape=(
            jax.ShapeDtypeStruct((blocks, micro, rows, dv), F32),
            jax.ShapeDtypeStruct((blocks, micro, rows, dv), BF16),
            jax.ShapeDtypeStruct((blocks, micro, dv, dk), F32),
        ),
        grid_spec=pltpu.PrefetchScalarGridSpec(
            num_scalar_prefetch=1,
            grid=(micro, blocks),
            in_specs=[
                per_block(rows, width),
                per_block(rows, dk),
                per_block(rows, dv),
                per_batch(slices, part, dk),
                pl.BlockSpec((1, dv), lambda m, b, *_: (0, 0)),
            ],
            out_specs=(per_block(rows, dv), per_block(rows, dv), per_block(dv, dk)),
            scratch_shapes=[pltpu.VMEM((dv, dk), F32)],
        ),
        compiler_params=params(),
        name="mix",
    )(flags, qkv, decays, og, before, gain)


def gate_back_of(flags, g_gated, og, o, qkv, decays, gain, slices):
    blocks, micro, rows, width = qkv.shape
    dk, dv = decays.shape[-1], og.shape[-1]
    part = dv // slices
    return pl.pallas_call(
        gate_back_kernel,
        out_shape=(
            jax.ShapeDtypeStruct((blocks, micro, rows, dv), BF16),
            jax.ShapeDtypeStruct((blocks, micro, rows, dv), F32),
            jax.ShapeDtypeStruct((slices, micro, part, dk), BF16),
            jax.ShapeDtypeStruct((8, dv), F32),
        ),
        grid_spec=pltpu.PrefetchScalarGridSpec(
            num_scalar_prefetch=1,
            grid=(micro, blocks),
            in_specs=[
                per_block(rows, dv),
                per_block(rows, dv),
                per_block(rows, dv),
                per_block(rows, width),
                per_block(rows, dk),
                pl.BlockSpec((1, dv), lambda m, b, *_: (0, 0)),
            ],
            out_specs=(
                per_block(rows, dv),
                per_block(rows, dv),
                per_batch(slices, part, dk),
                pl.BlockSpec((8, dv), lambda m, b, *_: (0, 0)),
            ),
            scratch_shapes=[pltpu.VMEM((dv, dk), F32), pltpu.VMEM((8, dk), F32)],
        ),
        compiler_params=params(),
        name="gate_back",
    )(flags, g_gated, og, o, qkv, decays, gain)


def mix_back_of(flags, qkv, decays, g_o, g_og, kept, after, logits):
    blocks, micro, rows, width = qkv.shape
    dk, dv = decays.shape[-1], g_o.shape[-1]
    slices, _, part, _ = after.shape
    back = functools.partial(backwards, count=blocks)
    return pl.pallas_call(
        mix_back_kernel,
        out_shape=(
            jax.ShapeDtypeStruct((blocks, micro, rows, width + dv), BF16),
            jax.ShapeDtypeStruct((blocks, micro, rows, dk), F32),
        ),
        grid_spec=pltpu.PrefetchScalarGridSpec(
            num_scalar_prefetch=1,
            grid=(micro, blocks),
            in_specs=[
                back(rows, width),
                back(rows, dk),
                back(rows, dv),
                back(rows, dv),
                back(dv, dk),
                per_batch(slices, part, dk),
                back(rows, dk),
            ],
            out_specs=(back(rows, width + dv), back(rows, dk)),
            scratch_shapes=[pltpu.VMEM((dv, dk), F32)],
        ),
        compiler_params=params(),
        name="mix_back",
    )(flags, qkv, decays, g_o, g_og, kept, after, logits)


def exchange(x, axis):
    return lax.all_to_all(x, axis, split_axis=0, concat_axis=0, tiled=True)


def gather_rows(x, axis):
    return exchange(jnp.broadcast_to(x[None], (lax.axis_size(axis),) + x.shape), axis)


def gather_weight(w):
    return lax.all_gather(w, "seq", axis=0, tiled=True)


def scatter_grad(g):
    return lax.psum_scatter(g.astype(BF16), "seq", scatter_dimension=0, tiled=True)


def dot(a, b, contract, precision=None):
    return lax.dot_general(
        a, b, (((contract[0],), (contract[1],)), ((), ())),
        precision=precision, preferred_element_type=F32,
    )


def rms(x, epsilon):
    return lax.rsqrt(jnp.mean(x * x, axis=-1, keepdims=True) + epsilon)


def norm_back(grad, gain, normed, inv):
    scaled = grad * gain
    inner = jnp.mean(scaled * normed, axis=-1, keepdims=True)
    return inv * (scaled - normed * inner), jnp.sum(grad * normed, axis=0)


def total_of(parts, seq, head):
    flat = jnp.concatenate([p.reshape(-1) for p in parts])
    unit = seq * head * 1024
    length = -(-flat.shape[0] // unit) * unit
    flat = jnp.pad(flat, (0, length - flat.shape[0]))
    piece = exchange(flat.reshape(seq, -1, 128), "seq").sum(0)
    piece = exchange(piece.reshape(head, -1, 128), "head").sum(0)
    piece = lax.all_gather(piece, "head", axis=0, tiled=True)
    whole = lax.all_gather(piece, "seq", axis=0, tiled=True).reshape(-1)
    result, at = [], 0
    for p in parts:
        result.append(whole[at : at + p.size].reshape(p.shape))
        at += p.size
    return result


def on_device(
    tokens, starts, cotangent, mix_in, mix_out, gate_up, down_proj,
    norm_gain, ffn_gain, head_gain, rank_down, rank_up, gate_bias,
):
    micro, rows, width = tokens.shape
    heads, seq = lax.axis_size("head"), lax.axis_size("seq")
    head = lax.axis_index("head")
    keys, dv = rank_up.shape[1], head_gain.shape[0]
    dk, vals = keys // heads, dv * heads
    hidden_units = down_proj.shape[1]
    group = heads * micro * rows
    proj_width = 2 * dk + 2 * dv

    def own_columns(w, start, size):
        return lax.dynamic_slice_in_dim(w, start + head * size, size, 1)

    w_in = gather_weight(
        jnp.concatenate(
            [
                own_columns(mix_in, 0, dk),
                own_columns(mix_in, keys, dk),
                own_columns(mix_in, 2 * keys, dv),
                own_columns(mix_in, 2 * keys + vals, dv),
            ],
            axis=1,
        )
    )
    w_out = gather_weight(mix_out)
    w_gu = gather_weight(gate_up.reshape(gate_up.shape[0], 2 * hidden_units))
    w_down = gather_weight(down_proj)
    up_own = own_columns(rank_up, 0, dk)
    bias_own = lax.dynamic_slice_in_dim(gate_bias, head * dk, dk, 0)

    all_tokens = gather_rows(tokens, "head").reshape(group, width)
    all_cot = gather_rows(cotangent, "head").reshape(group, width)

    source_all = all_tokens.astype(F32)
    xn = (source_all * rms(source_all, 1e-6) * norm_gain).astype(BF16)
    qkv = dot(xn, w_in[:, : 2 * dk + dv], (1, 0)).astype(BF16)
    og = dot(xn, w_in[:, 2 * dk + dv :], (1, 0))
    ranked = dot(xn, rank_down, (1, 0))
    logits = dot(ranked, up_own, (1, 0), HIGHEST) + bias_own
    decays = (jax.nn.log_sigmoid(logits) / GATE_NORM).astype(BF16)

    def blocks(x):
        return x.reshape(heads, micro, rows, x.shape[-1])

    qkv_b, og_b, decays_b = blocks(qkv), blocks(og), blocks(decays)
    gain_row = head_gain.reshape(1, dv)
    part = dv // seq
    own_states = exchange(states_of(starts, qkv_b, decays_b, dv, seq, 16), "seq")
    through = own_states[:, :, part:, :]
    before = exchange(prefix_of(own_states, through, part, False), "seq")
    o_b, gated_b, kept = mix_of(starts, qkv_b, decays_b, og_b, before, gain_row)

    gated = exchange(gated_b, "head")
    gated = gated.transpose(1, 2, 0, 3).reshape(micro * rows, vals)
    source = tokens.astype(F32).reshape(micro * rows, width)
    hidden = source + dot(gated, w_out, (1, 1))
    inv_ffn = rms(hidden, 1e-6)
    plain_ffn = hidden * inv_ffn
    h2 = (plain_ffn * ffn_gain).astype(BF16)

    all_h2 = gather_rows(h2, "head").reshape(group, width)
    gu = dot(all_h2, w_gu, (1, 0))
    gate_lin, up_lin = gu[:, :hidden_units], gu[:, hidden_units:]
    sig = jax.nn.sigmoid(gate_lin)
    act = gate_lin * sig
    product = (act * up_lin).astype(BF16)
    g_product = dot(all_cot, w_down, (1, 0))
    g_gate = (g_product * up_lin * sig * (1.0 + gate_lin * (1.0 - sig))).astype(BF16)
    g_up = (g_product * act).astype(BF16)
    g_gu = jnp.concatenate([g_gate, g_up], axis=1)
    g_h2_part = dot(g_gu, w_gu, (1, 1)).astype(BF16).reshape(heads, micro * rows, width)
    g_h2 = exchange(g_h2_part, "head").astype(F32).sum(0)
    ffn_part = dot(product, w_down, (1, 1)).astype(BF16).reshape(heads, micro * rows, width)
    ffn_out = exchange(ffn_part, "head").astype(F32).sum(0)
    output = (hidden + ffn_out).astype(BF16)
    grad_gu = scatter_grad(dot(all_h2, g_gu, (0, 0))).astype(F32)
    grad_down = scatter_grad(dot(all_cot, product, (0, 0))).astype(F32)

    back_ffn, g_ffn_gain = norm_back(g_h2, ffn_gain, plain_ffn, inv_ffn)
    g_hidden = cotangent.astype(F32).reshape(micro * rows, width) + back_ffn
    g_mixed = g_hidden.astype(BF16)
    g_gated = dot(g_mixed, w_out, (1, 0)).astype(BF16)
    g_gated = g_gated.reshape(micro, rows, heads, dv).transpose(2, 0, 1, 3)
    g_gated_b = exchange(g_gated, "head")
    g_og_b, g_o_b, pulled, g_head_gain = gate_back_of(
        starts, g_gated_b, og_b, o_b, qkv_b, decays_b, gain_row, seq
    )
    own_pulled = exchange(pulled, "seq")
    after = exchange(prefix_of(own_pulled, through, part, True), "seq")
    g_proj_b, g_logits_b = mix_back_of(
        starts, qkv_b, decays_b, g_o_b, g_og_b, kept, after, blocks(logits)
    )
    g_proj, g_logits = g_proj_b.reshape(group, proj_width), g_logits_b.reshape(group, dk)
    g_ranked = dot(g_logits, up_own, (1, 1), HIGHEST)
    g_xn_part = dot(g_proj, w_in, (1, 1)) + dot(
        g_ranked, rank_down.astype(F32), (1, 1), HIGHEST
    )
    g_xn_part = g_xn_part.astype(BF16).reshape(heads, micro * rows, width)
    g_xn = exchange(g_xn_part, "head").astype(F32).sum(0)
    inv_in = rms(source, 1e-6)
    back_in, g_norm_gain = norm_back(g_xn, norm_gain, source * inv_in, inv_in)
    input_grad = g_hidden + back_in

    slab = width // (seq * heads)
    grad_out = scatter_grad(dot(g_mixed, gated, (0, 0)))
    grad_out = exchange(grad_out.reshape(heads, slab, vals), "head").astype(F32).sum(0)
    grad_in = scatter_grad(dot(xn, g_proj, (0, 0)))
    grad_in = exchange(grad_in.reshape(heads, slab, proj_width), "head").astype(F32)
    cuts = ((0, dk), (dk, 2 * dk), (2 * dk, 2 * dk + dv), (2 * dk + dv, proj_width))
    grad_in = jnp.concatenate(
        [grad_in[:, :, a:b].transpose(1, 0, 2).reshape(slab, -1) for a, b in cuts], axis=1
    )
    g_rank_down = dot(xn.astype(F32), g_ranked, (0, 0), HIGHEST)
    g_rank_up = dot(ranked, g_logits, (0, 0), HIGHEST)
    g_rank_up = lax.dynamic_update_slice_in_dim(
        jnp.zeros(rank_up.shape, F32), g_rank_up, head * dk, 1
    )
    g_bias = lax.dynamic_update_slice_in_dim(
        jnp.zeros(gate_bias.shape, F32), g_logits.sum(0), head * dk, 0
    )
    small = total_of(
        [g_norm_gain, g_ffn_gain, g_head_gain[0], g_rank_down, g_rank_up, g_bias], seq, heads
    )
    return (
        output.reshape(tokens.shape),
        input_grad.reshape(tokens.shape),
        grad_in,
        grad_out,
        grad_gu.reshape(grad_gu.shape[0], 2, hidden_units),
        grad_down,
        *small,
    )


def solution(mesh):
    rows = P(None, ("seq", "head"), None)
    return jax.shard_map(
        on_device,
        mesh=mesh,
        in_specs=(
            rows, P(None, "seq"), rows, P("seq", None), P("seq", None),
            P("seq", None, "head"), P("seq", "head"), P(), P(), P(), P(), P(), P(),
        ),
        out_specs=(
            rows, rows, P(("seq", "head"), None), P(("seq", "head"), None),
            P("seq", None, "head"), P("seq", "head"), P(), P(), P(), P(), P(), P(),
        ),
        check_vma=False,
    )
```

```python
import functools

import jax
import jax.numpy as jnp
from jax import lax
from jax.experimental import pallas as pl
from jax.experimental.pallas import tpu as pltpu
from jax.sharding import PartitionSpec as P

HIGHEST = lax.Precision.HIGHEST
GATE_NORM = 16.0
BF16 = jnp.bfloat16
F32 = jnp.float32


def mm(a, b, contract, precision=HIGHEST):
    return lax.dot_general(
        a, b, ((contract[:1], contract[1:]), ((), ())),
        precision=precision, preferred_element_type=F32,
    )


def lower_ones(size):
    rows = lax.broadcasted_iota(jnp.int32, (size, size), 0)
    cols = lax.broadcasted_iota(jnp.int32, (size, size), 1)
    return rows >= cols


def running(decay_low):
    ones = lower_ones(decay_low.shape[0]).astype(F32).astype(BF16)
    return mm(ones, decay_low, (1, 0), None)


def sigmoid(x):
    return 1.0 / (1.0 + jnp.exp(-x))


def state_kernel(flags, qkv, decay, out, state, total_run):
    m, b = pl.program_id(0), pl.program_id(1)
    last = pl.num_programs(1) - 1
    dk = decay.shape[-1]
    keys, values = qkv[0, 0, :, dk : 2 * dk].astype(F32), qkv[0, 0, :, 2 * dk :].astype(F32)
    keep = 1.0 - flags[m, b].astype(F32)

    @pl.when(b == 0)
    def _():
        state[...] = jnp.zeros_like(state)
        total_run[0:1, :] = jnp.zeros((1, dk), F32)
        total_run[1:2, :] = jnp.ones((1, dk), F32)

    run = running(decay[0, 0])
    total = run[-1:, :]
    carried = keys * jnp.exp(total - run)
    state[...] = jnp.exp(total) * (state[...] * keep) + mm(values, carried, (0, 0))
    total_run[0:1, :] += total
    total_run[1:2, :] *= keep

    @pl.when(b == last)
    def _():
        through = jnp.exp(total_run[0:1, :]) * total_run[1:2, :]
        high = through.astype(BF16)
        low = (through - high.astype(F32)).astype(BF16)
        slices, part = out.shape[0], state.shape[0] // out.shape[0]
        tail = out.shape[2] - part
        at = lax.broadcasted_iota(jnp.int32, (tail, dk), 0)
        extra = jnp.where(
            at == 0, high.astype(F32), jnp.where(at == 1, low.astype(F32), 0.0)
        ).astype(BF16)
        for i in range(slices):
            out[i, 0, :part, :] = state[i * part : (i + 1) * part, :].astype(BF16)
            out[i, 0, part:, :] = extra


def prefix_kernel(reverse, own, through, out):
    count = own.shape[0]
    part = out.shape[2]

    def step(k, state):
        j = count - 1 - k if reverse else k
        out[j] = state.astype(BF16)
        decay = through[j, :, 0:1, :].astype(F32) + through[j, :, 1:2, :].astype(F32)
        return decay * state + own[j, :, :part, :].astype(F32)

    lax.fori_loop(0, count, step, jnp.zeros(out.shape[1:], F32))


def mix_kernel(flags, qkv, decay, og, before, gain, o_out, gated, kept, state):
    m, b = pl.program_id(0), pl.program_id(1)
    dk, dv = decay.shape[-1], og.shape[-1]
    q = qkv[0, 0, :, :dk].astype(F32)
    k = qkv[0, 0, :, dk : 2 * dk].astype(F32)
    v = qkv[0, 0, :, 2 * dk :].astype(F32)
    keep = 1.0 - flags[m, b].astype(F32)

    @pl.when(b == 0)
    def _():
        state[...] = before[:, 0].astype(F32).reshape(dv, dk)

    entry = state[...] * keep
    kept[0, 0] = entry
    run = running(decay[0, 0])
    total = run[-1:, :]
    queried = q * jnp.exp(run) * dk ** (-0.5)
    scores = mm(queried, k * jnp.exp(-run), (1, 1))
    scores = jnp.where(lower_ones(scores.shape[0]), scores, 0.0)
    o = mm(scores, v, (1, 0)) + mm(queried, entry, (1, 1))
    state[...] = jnp.exp(total) * entry + mm(v, k * jnp.exp(total - run), (0, 0))
    o_out[0, 0] = o
    scale = lax.rsqrt(jnp.mean(o * o, axis=-1, keepdims=True) + 1e-5)
    normed = (o * scale * gain[...]).astype(BF16).astype(F32)
    gate = og[0, 0]
    gated[0, 0] = (normed * gate * sigmoid(gate)).astype(BF16)


def gate_back_kernel(flags, g_gated, og, o_in, qkv, decay, gain, g_og, g_o, pulled, g_gain,
                     state, total_run):
    m, b = pl.program_id(0), pl.program_id(1)
    last = pl.num_programs(1) - 1
    dk, dv = decay.shape[-1], og.shape[-1]

    @pl.when((m == 0) & (b == 0))
    def _():
        g_gain[...] = jnp.zeros_like(g_gain)

    @pl.when(b == 0)
    def _():
        state[...] = jnp.zeros_like(state)
        total_run[0:1, :] = jnp.zeros((1, dk), F32)
        total_run[1:2, :] = jnp.ones((1, dk), F32)

    gate = og[0, 0]
    grad = g_gated[0, 0].astype(F32)
    sig = sigmoid(gate)
    o = o_in[0, 0]
    scale = lax.rsqrt(jnp.mean(o * o, axis=-1, keepdims=True) + 1e-5)
    plain = o * scale
    normed = (plain * gain[...]).astype(BF16).astype(F32)
    g_on = (grad * gate * sig).astype(BF16).astype(F32)
    g_og[0, 0] = (grad * normed * sig * (1.0 + gate * (1.0 - sig))).astype(BF16)
    scaled = g_on * gain[...]
    inner = jnp.mean(scaled * plain, axis=-1, keepdims=True)
    go = scale * (scaled - plain * inner)
    g_o[0, 0] = go
    g_gain[0:1, :] += jnp.sum(g_on * plain, axis=0, keepdims=True)

    total_run[1:2, :] *= 1.0 - flags[m, b].astype(F32)
    run = running(decay[0, 0])
    reach = (
        qkv[0, 0, :, :dk].astype(F32)
        * jnp.exp(run + total_run[0:1, :])
        * total_run[1:2, :]
        * dk ** (-0.5)
    )
    state[...] += mm(go, reach, (0, 0))
    total_run[0:1, :] += run[-1:, :]

    @pl.when(b == last)
    def _():
        slices, part = pulled.shape[0], dv // pulled.shape[0]
        for i in range(slices):
            pulled[i, 0] = state[i * part : (i + 1) * part, :].astype(BF16)


def mix_back_kernel(flags, qkv, decay, g_o, g_og, kept, after, logits, g_proj, g_logits, g_state):
    m, step = pl.program_id(0), pl.program_id(1)
    b = pl.num_programs(1) - 1 - step
    dk, dv = decay.shape[-1], g_o.shape[-1]
    q = qkv[0, 0, :, :dk].astype(F32)
    k = qkv[0, 0, :, dk : 2 * dk].astype(F32)
    v = qkv[0, 0, :, 2 * dk :].astype(F32)
    keep = 1.0 - flags[m, b].astype(F32)

    @pl.when(step == 0)
    def _():
        g_state[...] = after[:, 0].astype(F32).reshape(dv, dk)

    go, gs, entry = g_o[0, 0], g_state[...], kept[0, 0]
    run = running(decay[0, 0])
    total = run[-1:, :]
    up, down, rest = jnp.exp(run) * dk ** (-0.5), jnp.exp(-run), jnp.exp(total - run)
    decayed = jnp.exp(total)
    queried, keyed, carried = q * up, k * down, k * rest
    causal = lower_ones(q.shape[0])
    scores = jnp.where(causal, mm(queried, keyed, (1, 1)), 0.0)
    g_scores = jnp.where(causal, mm(go, v, (1, 1)), 0.0)
    g_queried = mm(g_scores, keyed, (1, 0)) + mm(go, entry, (1, 0))
    g_keyed = mm(g_scores, queried, (0, 0))
    g_v = mm(scores, go, (0, 0)) + mm(carried, gs, (1, 1))
    g_carried = mm(v, gs, (1, 0))
    g_state[...] = (decayed * gs + mm(go, queried, (0, 0))) * keep
    from_carried = g_carried * carried
    g_total = (
        jnp.sum(decayed * entry * gs, axis=0, keepdims=True)
        + jnp.sum(from_carried, axis=0, keepdims=True)
    )
    g_run = g_queried * queried - g_keyed * keyed - from_carried
    later = mm(causal.astype(F32), g_run, (0, 0)) + g_total
    proj = jnp.concatenate([g_queried * up, g_keyed * down + g_carried * rest, g_v], axis=1)
    width = proj.shape[1]
    g_proj[0, 0, :, :width] = proj.astype(BF16)
    g_proj[0, 0, :, width:] = g_og[0, 0]
    low = later.astype(BF16).astype(F32)
    g_logits[0, 0] = low * sigmoid(-logits[0, 0]) * (1.0 / GATE_NORM)


def params(limit=48):
    return pltpu.CompilerParams(
        dimension_semantics=("arbitrary", "arbitrary"), vmem_limit_bytes=limit << 20
    )


def cost(micros):
    return pl.CostEstimate(flops=0, bytes_accessed=int(micros * 3.0e6), transcendentals=0)


def per_block(rows, width):
    return pl.BlockSpec((1, 1, rows, width), lambda m, b, *_: (b, m, 0, 0))


def backwards(rows, width, count):
    return pl.BlockSpec((1, 1, rows, width), lambda m, b, *_: (count - 1 - b, m, 0, 0))


def per_batch(slices, rows, width):
    return pl.BlockSpec((slices, 1, rows, width), lambda m, b, *_: (0, m, 0, 0))


def states_of(flags, qkv, decays, dv, slices, pad):
    blocks, micro, rows, width = qkv.shape
    dk = decays.shape[-1]
    part = dv // slices
    return pl.pallas_call(
        state_kernel,
        out_shape=jax.ShapeDtypeStruct((slices, micro, part + pad, dk), BF16),
        grid_spec=pltpu.PrefetchScalarGridSpec(
            num_scalar_prefetch=1,
            grid=(micro, blocks),
            in_specs=[per_block(rows, width), per_block(rows, dk)],
            out_specs=per_batch(slices, part + pad, dk),
            scratch_shapes=[pltpu.VMEM((dv, dk), F32), pltpu.VMEM((8, dk), F32)],
        ),
        compiler_params=params(),
        cost_estimate=cost(10),
        name="states",
    )(flags, qkv, decays)


def prefix_of(own, through, part, reverse):
    return pl.pallas_call(
        functools.partial(prefix_kernel, reverse),
        out_shape=jax.ShapeDtypeStruct(own.shape[:2] + (part, own.shape[3]), BF16),
        in_specs=[pl.BlockSpec(memory_space=pltpu.VMEM)] * 2,
        out_specs=pl.BlockSpec(memory_space=pltpu.VMEM),
        compiler_params=pltpu.CompilerParams(vmem_limit_bytes=48 << 20),
        name="suffix" if reverse else "prefix",
    )(own, through)


def mix_of(flags, qkv, decays, og, before, gain):
    blocks, micro, rows, width = qkv.shape
    dk, dv = decays.shape[-1], og.shape[-1]
    slices, _, part, _ = before.shape
    return pl.pallas_call(
        mix_kernel,
        out_shape=(
            jax.ShapeDtypeStruct((blocks, micro, rows, dv), F32),
            jax.ShapeDtypeStruct((blocks, micro, rows, dv), BF16),
            jax.ShapeDtypeStruct((blocks, micro, dv, dk), F32),
        ),
        grid_spec=pltpu.PrefetchScalarGridSpec(
            num_scalar_prefetch=1,
            grid=(micro, blocks),
            in_specs=[
                per_block(rows, width),
                per_block(rows, dk),
                per_block(rows, dv),
                per_batch(slices, part, dk),
                pl.BlockSpec((1, dv), lambda m, b, *_: (0, 0)),
            ],
            out_specs=(per_block(rows, dv), per_block(rows, dv), per_block(dv, dk)),
            scratch_shapes=[pltpu.VMEM((dv, dk), F32)],
        ),
        compiler_params=params(),
        cost_estimate=cost(18),
        name="mix",
    )(flags, qkv, decays, og, before, gain)


def gate_back_of(flags, g_gated, og, o, qkv, decays, gain, slices):
    blocks, micro, rows, width = qkv.shape
    dk, dv = decays.shape[-1], og.shape[-1]
    part = dv // slices
    return pl.pallas_call(
        gate_back_kernel,
        out_shape=(
            jax.ShapeDtypeStruct((blocks, micro, rows, dv), BF16),
            jax.ShapeDtypeStruct((blocks, micro, rows, dv), F32),
            jax.ShapeDtypeStruct((slices, micro, part, dk), BF16),
            jax.ShapeDtypeStruct((8, dv), F32),
        ),
        grid_spec=pltpu.PrefetchScalarGridSpec(
            num_scalar_prefetch=1,
            grid=(micro, blocks),
            in_specs=[
                per_block(rows, dv),
                per_block(rows, dv),
                per_block(rows, dv),
                per_block(rows, width),
                per_block(rows, dk),
                pl.BlockSpec((1, dv), lambda m, b, *_: (0, 0)),
            ],
            out_specs=(
                per_block(rows, dv),
                per_block(rows, dv),
                per_batch(slices, part, dk),
                pl.BlockSpec((8, dv), lambda m, b, *_: (0, 0)),
            ),
            scratch_shapes=[pltpu.VMEM((dv, dk), F32), pltpu.VMEM((8, dk), F32)],
        ),
        compiler_params=params(),
        cost_estimate=cost(12),
        name="gate_back",
    )(flags, g_gated, og, o, qkv, decays, gain)


def mix_back_of(flags, qkv, decays, g_o, g_og, kept, after, logits):
    blocks, micro, rows, width = qkv.shape
    dk, dv = decays.shape[-1], g_o.shape[-1]
    slices, _, part, _ = after.shape
    back = functools.partial(backwards, count=blocks)
    return pl.pallas_call(
        mix_back_kernel,
        out_shape=(
            jax.ShapeDtypeStruct((blocks, micro, rows, width + dv), BF16),
            jax.ShapeDtypeStruct((blocks, micro, rows, dk), F32),
        ),
        grid_spec=pltpu.PrefetchScalarGridSpec(
            num_scalar_prefetch=1,
            grid=(micro, blocks),
            in_specs=[
                back(rows, width),
                back(rows, dk),
                back(rows, dv),
                back(rows, dv),
                back(dv, dk),
                per_batch(slices, part, dk),
                back(rows, dk),
            ],
            out_specs=(back(rows, width + dv), back(rows, dk)),
            scratch_shapes=[pltpu.VMEM((dv, dk), F32)],
        ),
        compiler_params=params(),
        cost_estimate=cost(28),
        name="mix_back",
    )(flags, qkv, decays, g_o, g_og, kept, after, logits)


def weight_grad_kernel(left, right, *rest):
    out, turned = rest[-2:]

    @pl.when(pl.program_id(1) == 0)
    def _():
        turned[...] = left[...].T

    out[...] = jnp.dot(turned[...], right[...], preferred_element_type=F32).astype(BF16)


def weight_grad(left, right, into, columns, start, tile):
    depth, rows = left.shape
    high = min(rows, 512)
    first = start // tile
    given = () if into is None else (into,)
    return pl.pallas_call(
        weight_grad_kernel,
        out_shape=jax.ShapeDtypeStruct((rows, columns), BF16),
        grid=(rows // high, right.shape[1] // tile),
        in_specs=[
            pl.BlockSpec((depth, high), lambda i, j: (0, i)),
            pl.BlockSpec((depth, tile), lambda i, j: (0, j)),
        ]
        + [pl.BlockSpec(memory_space=pl.ANY) for _ in given],
        out_specs=pl.BlockSpec((high, tile), lambda i, j: (i, first + j)),
        scratch_shapes=[pltpu.VMEM((high, depth), BF16)],
        input_output_aliases={2: 0} if given else {},
        compiler_params=params(),
        cost_estimate=pl.CostEstimate(
            flops=2 * depth * rows * right.shape[1],
            bytes_accessed=2 * (depth * rows + (depth + rows) * right.shape[1]),
            transcendentals=0,
        ),
        name="weight_grad",
    )(left, right, *given)


def exchange(x, axis):
    return lax.all_to_all(x, axis, split_axis=0, concat_axis=0, tiled=True)


def gather_rows(x, axis):
    return exchange(jnp.broadcast_to(x[None], (lax.axis_size(axis),) + x.shape), axis)


def gather_weight(w):
    return lax.all_gather(w, "seq", axis=0, tiled=True)


def scatter_grad(g):
    return lax.psum_scatter(g.astype(BF16), "seq", scatter_dimension=0, tiled=True)


def dot(a, b, contract, precision=None):
    return lax.dot_general(
        a, b, (((contract[0],), (contract[1],)), ((), ())),
        precision=precision, preferred_element_type=F32,
    )


def rms(x, epsilon):
    return lax.rsqrt(jnp.mean(x * x, axis=-1, keepdims=True) + epsilon)


def norm_back(grad, gain, normed, inv):
    scaled = grad * gain
    inner = jnp.mean(scaled * normed, axis=-1, keepdims=True)
    return inv * (scaled - normed * inner), jnp.sum(grad * normed, axis=0)


def total_of(parts, seq, head):
    flat = jnp.concatenate([p.reshape(-1) for p in parts])
    unit = seq * head * 1024
    length = -(-flat.shape[0] // unit) * unit
    flat = jnp.pad(flat, (0, length - flat.shape[0]))
    piece = exchange(flat.reshape(seq, -1, 128), "seq").sum(0)
    piece = exchange(piece.reshape(head, -1, 128), "head").sum(0)
    piece = lax.all_gather(piece, "head", axis=0, tiled=True)
    whole = lax.all_gather(piece, "seq", axis=0, tiled=True).reshape(-1)
    result, at = [], 0
    for p in parts:
        result.append(whole[at : at + p.size].reshape(p.shape))
        at += p.size
    return result


def on_device(
    tokens, starts, cotangent, mix_in, mix_out, gate_up, down_proj,
    norm_gain, ffn_gain, head_gain, rank_down, rank_up, gate_bias,
):
    micro, rows, width = tokens.shape
    heads, seq = lax.axis_size("head"), lax.axis_size("seq")
    head = lax.axis_index("head")
    keys, dv = rank_up.shape[1], head_gain.shape[0]
    dk, vals = keys // heads, dv * heads
    hidden_units = down_proj.shape[1]
    group = heads * micro * rows
    proj_width = 2 * dk + 2 * dv

    def own_columns(w, start, size):
        return lax.dynamic_slice_in_dim(w, start + head * size, size, 1)

    mixer = gather_weight(
        jnp.concatenate(
            [
                own_columns(mix_in, 0, dk),
                own_columns(mix_in, keys, dk),
                own_columns(mix_in, 2 * keys, dv),
                own_columns(mix_in, 2 * keys + vals, dv),
                mix_out,
            ],
            axis=1,
        )
    )
    w_in, w_out = mixer[:, :proj_width], mixer[:, proj_width:]
    ffn_weights = gather_weight(
        jnp.concatenate([gate_up.reshape(gate_up.shape[0], 2 * hidden_units), down_proj], axis=1)
    )
    w_gu, w_down = ffn_weights[:, : 2 * hidden_units], ffn_weights[:, 2 * hidden_units :]
    up_own = own_columns(rank_up, 0, dk)
    bias_own = lax.dynamic_slice_in_dim(gate_bias, head * dk, dk, 0)

    all_tokens = gather_rows(tokens, "head").reshape(group, width)
    all_cot = lax.all_gather(cotangent, "head").reshape(group, width)

    source_all = all_tokens.astype(F32)
    xn = (source_all * rms(source_all, 1e-6) * norm_gain).astype(BF16)
    qkv = dot(xn, w_in[:, : 2 * dk + dv], (1, 0)).astype(BF16)
    og = dot(xn, w_in[:, 2 * dk + dv :], (1, 0))
    ranked = dot(xn, rank_down, (1, 0))
    logits = dot(ranked, up_own, (1, 0), HIGHEST) + bias_own
    decays = (jax.nn.log_sigmoid(logits) / GATE_NORM).astype(BF16)

    def blocks(x):
        return x.reshape(heads, micro, rows, x.shape[-1])

    qkv_b, og_b, decays_b = blocks(qkv), blocks(og), blocks(decays)
    gain_row = head_gain.reshape(1, dv)
    part = dv // seq
    own_states = exchange(states_of(starts, qkv_b, decays_b, dv, seq, 16), "seq")
    through = own_states[:, :, part:, :]
    before = exchange(prefix_of(own_states, through, part, False), "seq")
    o_b, gated_b, kept = mix_of(starts, qkv_b, decays_b, og_b, before, gain_row)

    gated = exchange(gated_b, "head")
    gated = gated.transpose(1, 2, 0, 3).reshape(micro * rows, vals)
    source = tokens.astype(F32).reshape(micro * rows, width)
    hidden = source + dot(gated, w_out, (1, 1))
    inv_ffn = rms(hidden, 1e-6)
    plain_ffn = hidden * inv_ffn
    h2 = (plain_ffn * ffn_gain).astype(BF16)

    all_h2 = gather_rows(h2, "head").reshape(group, width)
    gu = dot(all_h2, w_gu, (1, 0))
    gate_lin, up_lin = gu[:, :hidden_units], gu[:, hidden_units:]
    sig = jax.nn.sigmoid(gate_lin)
    act = gate_lin * sig
    product = (act * up_lin).astype(BF16)
    g_product = dot(all_cot, w_down, (1, 0))
    g_gate = (g_product * up_lin * sig * (1.0 + gate_lin * (1.0 - sig))).astype(BF16)
    g_up = (g_product * act).astype(BF16)
    g_gu = jnp.concatenate([g_gate, g_up], axis=1)
    g_h2_part = dot(g_gu, w_gu, (1, 1)).astype(BF16).reshape(heads, micro * rows, width)
    g_h2 = exchange(g_h2_part, "head")
    grad_ffn = weight_grad(all_h2, g_gu, None, 3 * hidden_units, 0, hidden_units)
    grad_ffn = weight_grad(
        all_cot, product, grad_ffn, 3 * hidden_units, 2 * hidden_units, hidden_units
    )
    ffn_part = dot(product, w_down, (1, 1)).astype(BF16).reshape(heads, micro * rows, width)
    g_h2, grad_ffn, ffn_part = lax.optimization_barrier((g_h2, grad_ffn, ffn_part))
    ffn_out = exchange(ffn_part, "head")
    grad_ffn = scatter_grad(grad_ffn)

    g_h2 = g_h2.astype(F32).sum(0)
    back_ffn, g_ffn_gain = norm_back(g_h2, ffn_gain, plain_ffn, inv_ffn)
    g_hidden = cotangent.astype(F32).reshape(micro * rows, width) + back_ffn
    g_mixed = g_hidden.astype(BF16)
    g_gated = dot(g_mixed, w_out, (1, 0)).astype(BF16)
    grad_mix = weight_grad(g_mixed, gated, None, proj_width + vals, proj_width, dv)
    g_gated = g_gated.reshape(micro, rows, heads, dv).transpose(2, 0, 1, 3)
    g_gated_b = exchange(g_gated, "head")
    g_og_b, g_o_b, pulled, g_head_gain = gate_back_of(
        starts, g_gated_b, og_b, o_b, qkv_b, decays_b, gain_row, seq
    )
    own_pulled = exchange(pulled, "seq")
    after = exchange(prefix_of(own_pulled, through, part, True), "seq")
    g_proj_b, g_logits_b = mix_back_of(
        starts, qkv_b, decays_b, g_o_b, g_og_b, kept, after, blocks(logits)
    )
    g_proj_b, g_logits_b, ffn_out = lax.optimization_barrier((g_proj_b, g_logits_b, ffn_out))
    g_proj, g_logits = g_proj_b.reshape(group, proj_width), g_logits_b.reshape(group, dk)
    g_ranked = dot(g_logits, up_own, (1, 1), HIGHEST)
    g_xn_part = dot(g_proj, w_in, (1, 1)) + dot(
        g_ranked, rank_down.astype(F32), (1, 1), HIGHEST
    )
    g_xn_part = g_xn_part.astype(BF16).reshape(heads, micro * rows, width)
    g_xn = exchange(g_xn_part, "head").astype(F32).sum(0)
    output = (hidden + ffn_out.astype(F32).sum(0)).astype(BF16)
    inv_in = rms(source, 1e-6)
    back_in, g_norm_gain = norm_back(g_xn, norm_gain, source * inv_in, inv_in)
    input_grad = g_hidden + back_in

    slab = width // (seq * heads)
    grad_mix = weight_grad(xn, g_proj, grad_mix, proj_width + vals, 0, dv)
    grad_mix, grad_ffn = lax.optimization_barrier((grad_mix, grad_ffn))
    grad_mix = scatter_grad(grad_mix).reshape(heads, slab, proj_width + vals)
    grad_mix = exchange(grad_mix, "head").astype(F32)
    grad_in, grad_out = grad_mix[:, :, :proj_width], grad_mix[:, :, proj_width:].sum(0)
    cuts = ((0, dk), (dk, 2 * dk), (2 * dk, 2 * dk + dv), (2 * dk + dv, proj_width))
    grad_in = jnp.concatenate(
        [grad_in[:, :, a:b].transpose(1, 0, 2).reshape(slab, -1) for a, b in cuts], axis=1
    )
    g_rank_down = dot(xn.astype(F32), g_ranked, (0, 0), HIGHEST)
    g_rank_up = dot(ranked, g_logits, (0, 0), HIGHEST)
    g_rank_up = lax.dynamic_update_slice_in_dim(
        jnp.zeros(rank_up.shape, F32), g_rank_up, head * dk, 1
    )
    g_bias = lax.dynamic_update_slice_in_dim(
        jnp.zeros(gate_bias.shape, F32), g_logits.sum(0), head * dk, 0
    )
    small = total_of(
        [g_norm_gain, g_ffn_gain, g_head_gain[0], g_rank_down, g_rank_up, g_bias], seq, heads
    )
    return (
        output.reshape(tokens.shape),
        input_grad.reshape(tokens.shape),
        grad_in,
        grad_out,
        grad_ffn[:, : 2 * hidden_units].astype(F32).reshape(-1, 2, hidden_units),
        grad_ffn[:, 2 * hidden_units :].astype(F32),
        *small,
    )


def solution(mesh):
    rows = P(None, ("seq", "head"), None)
    return jax.shard_map(
        on_device,
        mesh=mesh,
        in_specs=(
            rows, P(None, "seq"), rows, P("seq", None), P("seq", None),
            P("seq", None, "head"), P("seq", "head"), P(), P(), P(), P(), P(), P(),
        ),
        out_specs=(
            rows, rows, P(("seq", "head"), None), P(("seq", "head"), None),
            P("seq", None, "head"), P("seq", "head"), P(), P(), P(), P(), P(), P(),
        ),
        check_vma=False,
    )
```

```python
import functools

import jax
import jax.numpy as jnp
from jax import lax
from jax.experimental import pallas as pl
from jax.experimental.pallas import tpu as pltpu
from jax.sharding import PartitionSpec as P

HIGHEST = lax.Precision.HIGHEST
GATE_NORM = 16.0
BF16 = jnp.bfloat16
F32 = jnp.float32


def mm(a, b, contract, precision=HIGHEST):
    return lax.dot_general(
        a, b, ((contract[:1], contract[1:]), ((), ())),
        precision=precision, preferred_element_type=F32,
    )


def lower_ones(size):
    rows = lax.broadcasted_iota(jnp.int32, (size, size), 0)
    cols = lax.broadcasted_iota(jnp.int32, (size, size), 1)
    return rows >= cols


def running(decay_low):
    ones = lower_ones(decay_low.shape[0]).astype(F32).astype(BF16)
    return mm(ones, decay_low, (1, 0), None)


def sigmoid(x):
    return 1.0 / (1.0 + jnp.exp(-x))


def state_kernel(flags, qkv, decay, out, state, total_run):
    m, b = pl.program_id(0), pl.program_id(1)
    last = pl.num_programs(1) - 1
    dk = decay.shape[-1]
    keys, values = qkv[0, 0, :, dk : 2 * dk].astype(F32), qkv[0, 0, :, 2 * dk :].astype(F32)
    keep = 1.0 - flags[m, b].astype(F32)

    @pl.when(b == 0)
    def _():
        state[...] = jnp.zeros_like(state)
        total_run[0:1, :] = jnp.zeros((1, dk), F32)
        total_run[1:2, :] = jnp.ones((1, dk), F32)

    run = running(decay[0, 0])
    total = run[-1:, :]
    carried = keys * jnp.exp(total - run)
    state[...] = jnp.exp(total) * (state[...] * keep) + mm(values, carried, (0, 0))
    total_run[0:1, :] += total
    total_run[1:2, :] *= keep

    @pl.when(b == last)
    def _():
        through = jnp.exp(total_run[0:1, :]) * total_run[1:2, :]
        high = through.astype(BF16)
        low = (through - high.astype(F32)).astype(BF16)
        slices, part = out.shape[0], state.shape[0] // out.shape[0]
        tail = out.shape[2] - part
        at = lax.broadcasted_iota(jnp.int32, (tail, dk), 0)
        extra = jnp.where(
            at == 0, high.astype(F32), jnp.where(at == 1, low.astype(F32), 0.0)
        ).astype(BF16)
        for i in range(slices):
            out[i, 0, :part, :] = state[i * part : (i + 1) * part, :].astype(BF16)
            out[i, 0, part:, :] = extra


def mix_kernel(flags, qkv, decay, og, before, gain, o_out, gated, kept, state):
    m, b = pl.program_id(0), pl.program_id(1)
    dk, dv = decay.shape[-1], og.shape[-1]
    q = qkv[0, 0, :, :dk].astype(F32)
    k = qkv[0, 0, :, dk : 2 * dk].astype(F32)
    v = qkv[0, 0, :, 2 * dk :].astype(F32)
    keep = 1.0 - flags[m, b].astype(F32)

    @pl.when(b == 0)
    def _():
        state[...] = before[:, 0].astype(F32).reshape(dv, dk)

    entry = state[...] * keep
    kept[0, 0] = entry
    run = running(decay[0, 0])
    total = run[-1:, :]
    queried = q * jnp.exp(run) * dk ** (-0.5)
    scores = mm(queried, k * jnp.exp(-run), (1, 1))
    scores = jnp.where(lower_ones(scores.shape[0]), scores, 0.0)
    o = mm(scores, v, (1, 0)) + mm(queried, entry, (1, 1))
    state[...] = jnp.exp(total) * entry + mm(v, k * jnp.exp(total - run), (0, 0))
    o_out[0, 0] = o
    scale = lax.rsqrt(jnp.mean(o * o, axis=-1, keepdims=True) + 1e-5)
    normed = (o * scale * gain[...]).astype(BF16).astype(F32)
    gate = og[0, 0]
    gated[0, 0] = (normed * gate * sigmoid(gate)).astype(BF16)


def gate_back_kernel(flags, g_gated, og, o_in, qkv, decay, gain, g_og, g_o, pulled, g_gain,
                     state, total_run):
    m, b = pl.program_id(0), pl.program_id(1)
    last = pl.num_programs(1) - 1
    dk, dv = decay.shape[-1], og.shape[-1]

    @pl.when((m == 0) & (b == 0))
    def _():
        g_gain[...] = jnp.zeros_like(g_gain)

    @pl.when(b == 0)
    def _():
        state[...] = jnp.zeros_like(state)
        total_run[0:1, :] = jnp.zeros((1, dk), F32)
        total_run[1:2, :] = jnp.ones((1, dk), F32)

    gate = og[0, 0]
    grad = g_gated[0, 0].astype(F32)
    sig = sigmoid(gate)
    o = o_in[0, 0]
    scale = lax.rsqrt(jnp.mean(o * o, axis=-1, keepdims=True) + 1e-5)
    plain = o * scale
    normed = (plain * gain[...]).astype(BF16).astype(F32)
    g_on = (grad * gate * sig).astype(BF16).astype(F32)
    g_og[0, 0] = (grad * normed * sig * (1.0 + gate * (1.0 - sig))).astype(BF16)
    scaled = g_on * gain[...]
    inner = jnp.mean(scaled * plain, axis=-1, keepdims=True)
    go = scale * (scaled - plain * inner)
    g_o[0, 0] = go
    g_gain[0:1, :] += jnp.sum(g_on * plain, axis=0, keepdims=True)

    total_run[1:2, :] *= 1.0 - flags[m, b].astype(F32)
    run = running(decay[0, 0])
    reach = (
        qkv[0, 0, :, :dk].astype(F32)
        * jnp.exp(run + total_run[0:1, :])
        * total_run[1:2, :]
        * dk ** (-0.5)
    )
    state[...] += mm(go, reach, (0, 0))
    total_run[0:1, :] += run[-1:, :]

    @pl.when(b == last)
    def _():
        slices, part = pulled.shape[0], dv // pulled.shape[0]
        for i in range(slices):
            pulled[i, 0] = state[i * part : (i + 1) * part, :].astype(BF16)


def mix_back_kernel(flags, qkv, decay, g_o, g_og, kept, after, logits, g_proj, g_logits, g_state):
    m, step = pl.program_id(0), pl.program_id(1)
    b = pl.num_programs(1) - 1 - step
    dk, dv = decay.shape[-1], g_o.shape[-1]
    q = qkv[0, 0, :, :dk].astype(F32)
    k = qkv[0, 0, :, dk : 2 * dk].astype(F32)
    v = qkv[0, 0, :, 2 * dk :].astype(F32)
    keep = 1.0 - flags[m, b].astype(F32)

    @pl.when(step == 0)
    def _():
        g_state[...] = after[:, 0].astype(F32).reshape(dv, dk)

    go, gs, entry = g_o[0, 0], g_state[...], kept[0, 0]
    run = running(decay[0, 0])
    total = run[-1:, :]
    up, down, rest = jnp.exp(run) * dk ** (-0.5), jnp.exp(-run), jnp.exp(total - run)
    decayed = jnp.exp(total)
    queried, keyed, carried = q * up, k * down, k * rest
    causal = lower_ones(q.shape[0])
    scores = jnp.where(causal, mm(queried, keyed, (1, 1)), 0.0)
    g_scores = jnp.where(causal, mm(go, v, (1, 1)), 0.0)
    g_queried = mm(g_scores, keyed, (1, 0)) + mm(go, entry, (1, 0))
    g_keyed = mm(g_scores, queried, (0, 0))
    g_v = mm(scores, go, (0, 0)) + mm(carried, gs, (1, 1))
    g_carried = mm(v, gs, (1, 0))
    g_state[...] = (decayed * gs + mm(go, queried, (0, 0))) * keep
    from_carried = g_carried * carried
    g_total = (
        jnp.sum(decayed * entry * gs, axis=0, keepdims=True)
        + jnp.sum(from_carried, axis=0, keepdims=True)
    )
    g_run = g_queried * queried - g_keyed * keyed - from_carried
    later = mm(causal.astype(F32), g_run, (0, 0)) + g_total
    proj = jnp.concatenate([g_queried * up, g_keyed * down + g_carried * rest, g_v], axis=1)
    width = proj.shape[1]
    g_proj[0, 0, :, :width] = proj.astype(BF16)
    g_proj[0, 0, :, width:] = g_og[0, 0]
    low = later.astype(BF16).astype(F32)
    g_logits[0, 0] = low * sigmoid(-logits[0, 0]) * (1.0 / GATE_NORM)


def params(limit=48):
    return pltpu.CompilerParams(
        dimension_semantics=("arbitrary", "arbitrary"), vmem_limit_bytes=limit << 20
    )


def cost(micros):
    return pl.CostEstimate(flops=0, bytes_accessed=int(micros * 3.0e6), transcendentals=0)


def per_block(rows, width):
    return pl.BlockSpec((1, 1, rows, width), lambda m, b, *_: (b, m, 0, 0))


def backwards(rows, width, count):
    return pl.BlockSpec((1, 1, rows, width), lambda m, b, *_: (count - 1 - b, m, 0, 0))


def per_batch(slices, rows, width):
    return pl.BlockSpec((slices, 1, rows, width), lambda m, b, *_: (0, m, 0, 0))


def states_of(flags, qkv, decays, dv, slices, pad):
    blocks, micro, rows, width = qkv.shape
    dk = decays.shape[-1]
    part = dv // slices
    return pl.pallas_call(
        state_kernel,
        out_shape=jax.ShapeDtypeStruct((slices, micro, part + pad, dk), BF16),
        grid_spec=pltpu.PrefetchScalarGridSpec(
            num_scalar_prefetch=1,
            grid=(micro, blocks),
            in_specs=[per_block(rows, width), per_block(rows, dk)],
            out_specs=per_batch(slices, part + pad, dk),
            scratch_shapes=[pltpu.VMEM((dv, dk), F32), pltpu.VMEM((8, dk), F32)],
        ),
        compiler_params=params(),
        cost_estimate=cost(10),
        name="states",
    )(flags, qkv, decays)


def mix_of(flags, qkv, decays, og, before, gain):
    blocks, micro, rows, width = qkv.shape
    dk, dv = decays.shape[-1], og.shape[-1]
    slices, _, part, _ = before.shape
    return pl.pallas_call(
        mix_kernel,
        out_shape=(
            jax.ShapeDtypeStruct((blocks, micro, rows, dv), F32),
            jax.ShapeDtypeStruct((blocks, micro, rows, dv), BF16),
            jax.ShapeDtypeStruct((blocks, micro, dv, dk), F32),
        ),
        grid_spec=pltpu.PrefetchScalarGridSpec(
            num_scalar_prefetch=1,
            grid=(micro, blocks),
            in_specs=[
                per_block(rows, width),
                per_block(rows, dk),
                per_block(rows, dv),
                per_batch(slices, part, dk),
                pl.BlockSpec((1, dv), lambda m, b, *_: (0, 0)),
            ],
            out_specs=(per_block(rows, dv), per_block(rows, dv), per_block(dv, dk)),
            scratch_shapes=[pltpu.VMEM((dv, dk), F32)],
        ),
        compiler_params=params(),
        cost_estimate=cost(18),
        name="mix",
    )(flags, qkv, decays, og, before, gain)


def gate_back_of(flags, g_gated, og, o, qkv, decays, gain, slices):
    blocks, micro, rows, width = qkv.shape
    dk, dv = decays.shape[-1], og.shape[-1]
    part = dv // slices
    return pl.pallas_call(
        gate_back_kernel,
        out_shape=(
            jax.ShapeDtypeStruct((blocks, micro, rows, dv), BF16),
            jax.ShapeDtypeStruct((blocks, micro, rows, dv), F32),
            jax.ShapeDtypeStruct((slices, micro, part, dk), BF16),
            jax.ShapeDtypeStruct((8, dv), F32),
        ),
        grid_spec=pltpu.PrefetchScalarGridSpec(
            num_scalar_prefetch=1,
            grid=(micro, blocks),
            in_specs=[
                per_block(rows, dv),
                per_block(rows, dv),
                per_block(rows, dv),
                per_block(rows, width),
                per_block(rows, dk),
                pl.BlockSpec((1, dv), lambda m, b, *_: (0, 0)),
            ],
            out_specs=(
                per_block(rows, dv),
                per_block(rows, dv),
                per_batch(slices, part, dk),
                pl.BlockSpec((8, dv), lambda m, b, *_: (0, 0)),
            ),
            scratch_shapes=[pltpu.VMEM((dv, dk), F32), pltpu.VMEM((8, dk), F32)],
        ),
        compiler_params=params(),
        cost_estimate=cost(12),
        name="gate_back",
    )(flags, g_gated, og, o, qkv, decays, gain)


def mix_back_of(flags, qkv, decays, g_o, g_og, kept, after, logits):
    blocks, micro, rows, width = qkv.shape
    dk, dv = decays.shape[-1], g_o.shape[-1]
    slices, _, part, _ = after.shape
    back = functools.partial(backwards, count=blocks)
    return pl.pallas_call(
        mix_back_kernel,
        out_shape=(
            jax.ShapeDtypeStruct((blocks, micro, rows, width + dv), BF16),
            jax.ShapeDtypeStruct((blocks, micro, rows, dk), F32),
        ),
        grid_spec=pltpu.PrefetchScalarGridSpec(
            num_scalar_prefetch=1,
            grid=(micro, blocks),
            in_specs=[
                back(rows, width),
                back(rows, dk),
                back(rows, dv),
                back(rows, dv),
                back(dv, dk),
                per_batch(slices, part, dk),
                back(rows, dk),
            ],
            out_specs=(back(rows, width + dv), back(rows, dk)),
            scratch_shapes=[pltpu.VMEM((dv, dk), F32)],
        ),
        compiler_params=params(),
        cost_estimate=cost(28),
        name="mix_back",
    )(flags, qkv, decays, g_o, g_og, kept, after, logits)


def weight_grad_kernel(left, right, *rest):
    out, turned = rest[-2:]

    @pl.when(pl.program_id(1) == 0)
    def _():
        turned[...] = left[...].T

    out[...] = jnp.dot(turned[...], right[...], preferred_element_type=F32).astype(BF16)


def weight_grad(left, right, into, columns, start, tile):
    depth, rows = left.shape
    high = min(rows, 512)
    first = start // tile
    given = () if into is None else (into,)
    return pl.pallas_call(
        weight_grad_kernel,
        out_shape=jax.ShapeDtypeStruct((rows, columns), BF16),
        grid=(rows // high, right.shape[1] // tile),
        in_specs=[
            pl.BlockSpec((depth, high), lambda i, j: (0, i)),
            pl.BlockSpec((depth, tile), lambda i, j: (0, j)),
        ]
        + [pl.BlockSpec(memory_space=pl.ANY) for _ in given],
        out_specs=pl.BlockSpec((high, tile), lambda i, j: (i, first + j)),
        scratch_shapes=[pltpu.VMEM((high, depth), BF16)],
        input_output_aliases={2: 0} if given else {},
        compiler_params=params(),
        cost_estimate=pl.CostEstimate(
            flops=2 * depth * rows * right.shape[1],
            bytes_accessed=2 * (depth * rows + (depth + rows) * right.shape[1]),
            transcendentals=0,
        ),
        name="weight_grad",
    )(left, right, *given)


def greet(axes):
    barrier = pltpu.get_barrier_semaphore()
    met = 0
    for axis in axes:
        me, count = lax.axis_index(axis), lax.axis_size(axis)
        for hop in range(1, count):
            pl.semaphore_signal(
                barrier, inc=1, device_id={axis: lax.rem(me + hop, count)},
                device_id_type=pl.DeviceIdType.MESH,
            )
        met += count - 1
    pl.semaphore_wait(barrier, met)


def push(src, dst, send, recv, to, axis="head"):
    return pltpu.make_async_remote_copy(
        src_ref=src, dst_ref=dst, send_sem=send, recv_sem=recv,
        device_id={axis: to}, device_id_type=pl.DeviceIdType.MESH,
    )


def near_order(z, count, i):
    both = jnp.minimum(z, count - 1 - z)
    left = z > count - 1 - z
    paired = jnp.where(i % 2 == 1, z - (i + 1) // 2, z + i // 2)
    single = jnp.where(left, z - (i - both), z + (i - both))
    return jnp.where(i <= 2 * both, paired, single)


class Line:
    def __init__(self, own, all_rows, send, recv):
        self.own, self.all, self.send, self.recv = own, all_rows, send, recv
        self.z, self.count, self.rows = lax.axis_index("head"), lax.axis_size("head"), own.shape[0]
        z, count = self.z, self.count
        self.right = push(own, self.at(z), send.at[0], recv.at[z], lax.rem(z + 1, count))
        self.left = push(own, self.at(z), send.at[1], recv.at[z], lax.rem(z + count - 1, count))

    def chunk(self, b):
        return pl.ds(pl.multiple_of(b * self.rows, self.rows), self.rows)

    def at(self, b):
        return self.all.at[self.chunk(b)]

    def start(self):
        pl.when(self.z < self.count - 1)(self.right.start)
        pl.when(self.z > 0)(self.left.start)

    def passing(self, i, b):
        z, count = self.z, self.count
        to = jnp.where(b < z, z + 1, z - 1)
        going = ((b < z) & (z < count - 1)) | ((b > z) & (z > 0))
        copy = push(
            self.at(b), self.at(b), self.send.at[i + 1], self.recv.at[b], lax.rem(to + count, count)
        )
        return copy, going

    def receive(self, i, b):
        copy, going = self.passing(i, b)
        copy.wait_recv()
        pl.when(going)(copy.start)

    def finish(self):
        def sent(i, _):
            copy, going = self.passing(i, near_order(self.z, self.count, i))
            pl.when(going)(copy.wait_send)
            return 0

        lax.fori_loop(1, self.count, sent, 0)
        pl.when(self.z < self.count - 1)(self.right.wait_send)
        pl.when(self.z > 0)(self.left.wait_send)


def gather_norm_kernel(own, gain, normed, rows_all, here_sem, send, recv):
    z, count, rows = lax.axis_index("head"), lax.axis_size("head"), own.shape[0]
    greet(("head",))
    line = Line(own, rows_all, send, recv)
    line.start()
    here = pltpu.make_async_copy(own, line.at(z), here_sem)
    here.start()
    here.wait()
    band = 16

    def step(i, _):
        b = near_order(z, count, i)
        pl.when(i > 0)(lambda: line.receive(i, b))

        def norm(r, _):
            at = pl.ds(pl.multiple_of(b * rows + r * band, band), band)
            x = rows_all[at, :].astype(F32)
            inv = lax.rsqrt(jnp.mean(x * x, axis=-1, keepdims=True) + 1e-6)
            normed[at, :] = (x * inv * gain[...]).astype(BF16)
            return 0

        lax.fori_loop(0, rows // band, norm, 0)
        return 0

    lax.fori_loop(0, count, step, 0)
    line.finish()


def gather_norm(x, gain):
    rows, width = x.shape
    count = lax.axis_size("head")
    vmem = pl.BlockSpec(memory_space=pltpu.VMEM)
    dma = pltpu.SemaphoreType.DMA
    return pl.pallas_call(
        gather_norm_kernel,
        out_shape=jax.ShapeDtypeStruct((count * rows, width), BF16),
        in_specs=[vmem, vmem],
        out_specs=vmem,
        scratch_shapes=[
            pltpu.VMEM((count * rows, width), BF16), dma(()), dma((count + 1,)), dma((count,)),
        ],
        compiler_params=pltpu.CompilerParams(
            collective_id=1, has_side_effects=True, vmem_limit_bytes=32 << 20
        ),
        cost_estimate=cost(50),
        name="gather_norm",
    )(x, gain)


def swap_slices(own, got, send, recv):
    me, count = lax.axis_index("seq"), lax.axis_size("seq")

    def copy(hop, index):
        to = lax.rem(me + hop, count)
        return push(own.at[to], got.at[index], send.at[hop], recv.at[index], to, "seq")

    def start(hop, _):
        copy(hop, me).start()
        return 0

    def wait_recv(hop, _):
        copy(hop, lax.rem(me + hop, count)).wait_recv()
        return 0

    def wait_send(hop, _):
        copy(hop, me).wait_send()
        return 0

    def begin():
        lax.fori_loop(1, count, start, 0)
        got[me] = own[me]

    def end():
        lax.fori_loop(1, count, wait_recv, 0)

    def drain():
        lax.fori_loop(1, count, wait_send, 0)

    return begin, end, drain


def scan_states(reverse, own, through, out):
    count, part = out.shape[0], out.shape[2]

    def step(k, state):
        j = count - 1 - k if reverse else k
        out[j] = state.astype(BF16)
        decay = through[j, :, 0:1, :].astype(F32) + through[j, :, 1:2, :].astype(F32)
        return decay * state + own[j, :, :part, :].astype(F32)

    lax.fori_loop(0, count, step, jnp.zeros(out.shape[1:], F32))


def enter_kernel(own, rows_own, before, through, rows_all,
                 got, scanned, send, recv, send_back, recv_back, here_sem, go, come):
    z, count = lax.axis_index("head"), lax.axis_size("head")
    part = scanned.shape[2]
    greet(("seq", "head"))
    begin, end, drain = swap_slices(own, got, send, recv)
    begin()
    line = Line(rows_own, rows_all, go, come)
    line.start()
    here = pltpu.make_async_copy(rows_own, line.at(z), here_sem)
    here.start()
    end()
    through[...] = got[:, :, part:, :]
    scan_states(False, got, through, scanned)
    begin_back, end_back, drain_back = swap_slices(scanned, before, send_back, recv_back)
    begin_back()

    def step(i, _):
        line.receive(i, near_order(z, count, i))
        return 0

    lax.fori_loop(1, count, step, 0)
    end_back()
    here.wait()
    line.finish()
    drain()
    drain_back()


def enter(own, rows_own, part):
    slices, micro, deep, dk = own.shape
    rows, width = rows_own.shape
    count = lax.axis_size("head")
    vmem, anywhere = pl.BlockSpec(memory_space=pltpu.VMEM), pl.BlockSpec(memory_space=pl.ANY)
    dma = pltpu.SemaphoreType.DMA
    return pl.pallas_call(
        enter_kernel,
        out_shape=(
            jax.ShapeDtypeStruct((slices, micro, part, dk), BF16),
            jax.ShapeDtypeStruct((slices, micro, deep - part, dk), BF16),
            jax.ShapeDtypeStruct((count * rows, width), BF16),
        ),
        in_specs=[vmem, anywhere],
        out_specs=(vmem, vmem, anywhere),
        scratch_shapes=[
            pltpu.VMEM(own.shape, BF16), pltpu.VMEM((slices, micro, part, dk), BF16),
            dma((slices,)), dma((slices,)), dma((slices,)), dma((slices,)),
            dma(()), dma((count + 1,)), dma((count,)),
        ],
        compiler_params=pltpu.CompilerParams(
            collective_id=2, has_side_effects=True, vmem_limit_bytes=32 << 20
        ),
        cost_estimate=cost(50),
        name="enter",
    )(own, rows_own)


def leave_kernel(own, through, after, got, scanned, send, recv, send_back, recv_back):
    greet(("seq",))
    begin, end, drain = swap_slices(own, got, send, recv)
    begin()
    end()
    scan_states(True, got, through, scanned)
    begin_back, end_back, drain_back = swap_slices(scanned, after, send_back, recv_back)
    begin_back()
    end_back()
    drain()
    drain_back()


def leave(own, through):
    vmem = pl.BlockSpec(memory_space=pltpu.VMEM)
    dma = pltpu.SemaphoreType.DMA
    slices = own.shape[0]
    return pl.pallas_call(
        leave_kernel,
        out_shape=jax.ShapeDtypeStruct(own.shape, BF16),
        in_specs=[vmem, vmem],
        out_specs=vmem,
        scratch_shapes=[
            pltpu.VMEM(own.shape, BF16), pltpu.VMEM(own.shape, BF16),
            dma((slices,)), dma((slices,)), dma((slices,)), dma((slices,)),
        ],
        compiler_params=pltpu.CompilerParams(
            collective_id=3, has_side_effects=True, vmem_limit_bytes=32 << 20
        ),
        cost_estimate=cost(25),
        name="leave",
    )(own, through)


def total_kernel(own, out, from_seq, part, from_head, send_a, recv_a, send_b, recv_b,
                 send_c, recv_c, send_d, recv_d):
    seq, head = lax.axis_size("seq"), lax.axis_size("head")
    s, h = lax.axis_index("seq"), lax.axis_index("head")
    greet(("seq", "head"))

    def each(axis, me, count, src, dst, send, recv):
        def copy(hop, index):
            to = lax.rem(me + hop, count)
            return push(src(to), dst(index), send.at[hop], recv.at[index], to, axis)

        for hop in range(1, count):
            copy(hop, me).start()
        for hop in range(1, count):
            copy(hop, lax.rem(me + hop, count)).wait_recv()
        return [copy(hop, me).wait_send for hop in range(1, count)]

    from_seq[s] = own[s]
    sent = each("seq", s, seq, lambda to: own.at[to], lambda i: from_seq.at[i], send_a, recv_a)
    part[...] = jnp.sum(from_seq[...], axis=0)
    from_head[h] = part[h]
    sent += each("head", h, head, lambda to: part.at[to], lambda i: from_head.at[i], send_b, recv_b)
    out[s, h] = jnp.sum(from_head[...], axis=0)
    sent += each("head", h, head, lambda _: out.at[s, h], lambda i: out.at[s, i], send_c, recv_c)
    sent += each("seq", s, seq, lambda _: out.at[s], lambda i: out.at[i], send_d, recv_d)
    for wait in sent:
        wait()


def total_of(parts):
    seq, head = lax.axis_size("seq"), lax.axis_size("head")
    flat = jnp.concatenate([p.reshape(-1) for p in parts])
    deep = -(-flat.shape[0] // (seq * head * 1024)) * 8
    flat = jnp.pad(flat, (0, seq * head * deep * 128 - flat.shape[0]))
    vmem = pl.BlockSpec(memory_space=pltpu.VMEM)
    dma = pltpu.SemaphoreType.DMA
    shape = (seq, head, deep, 128)
    whole = pl.pallas_call(
        total_kernel,
        out_shape=jax.ShapeDtypeStruct(shape, F32),
        in_specs=[vmem],
        out_specs=vmem,
        scratch_shapes=[
            pltpu.VMEM(shape, F32), pltpu.VMEM(shape[1:], F32), pltpu.VMEM(shape[1:], F32),
        ]
        + [dma((n,)) for n in (seq, seq, head, head, head, head, seq, seq)],
        compiler_params=pltpu.CompilerParams(collective_id=4, has_side_effects=True),
        cost_estimate=cost(15),
        name="total",
    )(flat.reshape(shape)).reshape(-1)
    result, at = [], 0
    for p in parts:
        result.append(whole[at : at + p.size].reshape(p.shape))
        at += p.size
    return result


def ffn_kernel(count, x_own, c_all, w, g_x, f_parts, grad,
               wv, xs, cs, act, lin, parts, landed, turned, turned_c, tiles,
               w_sem, own_sem, go_sem, x_sem, p_sem, q_sem, o_sem):
    z = lax.axis_index("head")
    rows, width = x_own.shape
    hidden = act.shape[1] // 3
    chunk = lambda b: pl.ds(pl.multiple_of(b * rows, rows), rows)

    weights = [
        pltpu.make_async_copy(
            w.at[:, pl.ds(k * hidden, hidden)], wv.at[:, pl.ds(k * hidden, hidden)], w_sem.at[k]
        )
        for k in range(3)
    ]
    own = [
        pltpu.make_async_copy(x_own, xs.at[chunk(z)], own_sem.at[0]),
        pltpu.make_async_copy(c_all, cs, own_sem.at[1]),
    ]
    for copy in own + weights:
        copy.start()
    greet(("head",))
    line = Line(x_own, xs, go_sem, x_sem)
    line.start()
    for copy in own + weights:
        copy.wait()

    pieces = p_sem.shape[1]
    piece_rows = rows // pieces

    def piece(b, p):
        start = b * rows + p * piece_rows
        return pl.ds(pl.multiple_of(start, piece_rows), piece_rows)

    def onward(b, p):
        to = jnp.where(b > z, z + 1, z - 1)
        slot = jnp.where((to == b) & (z > b), count, b)
        return push(
            parts.at[piece(b, p)], landed.at[piece(slot, p)],
            p_sem.at[b, p], q_sem.at[slot, p], lax.rem(to + count, count),
        )

    def arrived(slot, p):
        at = piece(slot, p)
        push(landed.at[at], landed.at[at], p_sem.at[0, p], q_sem.at[slot, p], z).wait_recv()
        return landed[at, :].astype(F32)

    inner = (z > 0) & (z < count - 1)

    def relay(b, p):
        at = piece(b, p)
        parts[at, :] = (parts[at, :].astype(F32) + arrived(b, p)).astype(BF16)
        onward(b, p).start()

    def step(i, _):
        b = near_order(z, count, i)

        pl.when(i > 0)(lambda: line.receive(i, b))

        at = chunk(b)
        x = xs[at, :]
        lin[0] = jnp.dot(x, wv[:, :hidden], preferred_element_type=F32)
        lin[1] = jnp.dot(x, wv[:, hidden : 2 * hidden], preferred_element_type=F32)
        lin[2] = jnp.dot(cs[at, :], wv[:, 2 * hidden :], preferred_element_type=F32)
        band = 16

        def act_rows(r, _):
            here = pl.ds(pl.multiple_of(r * band, band), band)
            there = pl.ds(pl.multiple_of(b * rows + r * band, band), band)
            gate, up, g_product = lin[0, here, :], lin[1, here, :], lin[2, here, :]
            sig = sigmoid(gate)
            gated = gate * sig
            act[there, :hidden] = (g_product * up * sig * (1.0 + gate * (1.0 - sig))).astype(BF16)
            act[there, hidden : 2 * hidden] = (g_product * gated).astype(BF16)
            act[there, 2 * hidden :] = (gated * up).astype(BF16)
            return 0

        lax.fori_loop(0, rows // band, act_rows, 0)
        parts[at, :] = mm(act[at, : 2 * hidden], wv[:, : 2 * hidden], (1, 1), None).astype(BF16)

        @pl.when((i > 0) & jnp.logical_not(inner))
        def _():
            for p in range(pieces):
                onward(b, p).start()

        return 0

    lax.fori_loop(0, count, step, 0)

    @pl.when(inner)
    def _():
        for p in range(pieces):
            relay(count - 1 - z, p)

    high = tiles.shape[1]
    steps = width // high

    def store(t, r, k):
        return pltpu.make_async_copy(
            tiles.at[lax.rem(t, 2)],
            grad.at[pl.ds(pl.multiple_of(r * high, high), high), pl.ds(k * hidden, hidden)],
            o_sem.at[lax.rem(t, 2)],
        )

    turned[...] = xs[...].T
    turned_c[...] = cs[...].T
    far_end = jnp.where(z < count - 1 - z, count - 1, 0)

    def slab(r, _):
        for k in range(3):
            t = 3 * r + k

            @pl.when(t >= 2)
            def _():
                store(t, r, k).wait()

            left_rows = (turned_c if k == 2 else turned)[
                pl.ds(pl.multiple_of(r * high, high), high), :
            ]
            tiles[lax.rem(t, 2)] = jnp.dot(
                left_rows, act[:, k * hidden : (k + 1) * hidden], preferred_element_type=F32
            ).astype(BF16)
            store(t, r, k).start()

        @pl.when(inner)
        def _():
            relay(far_end, r)
            relay(count - 1 - far_end, r)

        return 0

    lax.fori_loop(0, steps, slab, 0)

    def part(b, _):
        at = chunk(b)
        f_parts[b] = mm(act[at, 2 * hidden :], wv[:, 2 * hidden :], (1, 1), None).astype(BF16)
        return 0

    lax.fori_loop(0, count, part, 0)

    for p in range(pieces):
        here = pl.ds(p * piece_rows, piece_rows)
        g_x[here, :] = parts[piece(z, p), :].astype(F32)

        @pl.when(z > 0)
        def _():
            g_x[here, :] += arrived(z, p)

        @pl.when(z < count - 1)
        def _():
            g_x[here, :] += arrived(count, p)

    def finish(i, _):
        b = near_order(z, count, i)
        for p in range(pieces):
            onward(b, p).wait_send()
        return 0

    lax.fori_loop(1, count, finish, 0)
    line.finish()
    store(3 * steps - 2, 0, 0).wait()
    store(3 * steps - 1, 0, 0).wait()


def feed_forward(x_own, c_all, w, hidden, count):
    rows, width = x_own.shape
    group = rows * count
    assert count == 4 and width % 4 == 0 and rows % 64 == 0
    anywhere = pl.BlockSpec(memory_space=pl.ANY)
    vmem = pl.BlockSpec(memory_space=pltpu.VMEM)
    dma = pltpu.SemaphoreType.DMA
    return pl.pallas_call(
        functools.partial(ffn_kernel, count),
        out_shape=(
            jax.ShapeDtypeStruct((rows, width), F32),
            jax.ShapeDtypeStruct((count, rows, width), BF16),
            jax.ShapeDtypeStruct((width, 3 * hidden), BF16),
        ),
        in_specs=[anywhere] * 3,
        out_specs=(vmem, vmem, anywhere),
        scratch_shapes=[
            pltpu.VMEM((width, 3 * hidden), BF16),
            pltpu.VMEM((group, width), BF16),
            pltpu.VMEM((group, width), BF16),
            pltpu.VMEM((group, 3 * hidden), BF16),
            pltpu.VMEM((3, rows, hidden), F32),
            pltpu.VMEM((group, width), BF16),
            pltpu.VMEM((group + rows, width), BF16),
            pltpu.VMEM((width, group), BF16),
            pltpu.VMEM((width, group), BF16),
            pltpu.VMEM((2, width // 4, hidden), BF16),
            dma((3,)), dma((2,)), dma((count + 1,)), dma((count,)),
            dma((count, 4)), dma((count + 1, 4)), dma((2,)),
        ],
        compiler_params=pltpu.CompilerParams(
            collective_id=0, has_side_effects=True, vmem_limit_bytes=60 << 20
        ),
        cost_estimate=cost(100),
        name="feed_forward",
    )(x_own, c_all, w)


def exchange(x, axis):
    return lax.all_to_all(x, axis, split_axis=0, concat_axis=0, tiled=True)


def ring(x, axis, hop):
    count = lax.axis_size(axis)
    return lax.ppermute(x, axis, [((i + hop) % count, i) for i in range(count)])


def gather_weight(w):
    return lax.all_gather(w, "seq", axis=0, tiled=True)


def scatter_grad(g):
    return lax.psum_scatter(g.astype(BF16), "seq", scatter_dimension=0, tiled=True)


def dot(a, b, contract, precision=None):
    return lax.dot_general(
        a, b, (((contract[0],), (contract[1],)), ((), ())),
        precision=precision, preferred_element_type=F32,
    )


def rms(x, epsilon):
    return lax.rsqrt(jnp.mean(x * x, axis=-1, keepdims=True) + epsilon)


def norm_back(grad, gain, normed, inv):
    scaled = grad * gain
    inner = jnp.mean(scaled * normed, axis=-1, keepdims=True)
    return inv * (scaled - normed * inner), jnp.sum(grad * normed, axis=0)


def on_device(
    tokens, starts, cotangent, mix_in, mix_out, gate_up, down_proj,
    norm_gain, ffn_gain, head_gain, rank_down, rank_up, gate_bias,
):
    micro, rows, width = tokens.shape
    heads, seq = lax.axis_size("head"), lax.axis_size("seq")
    head = lax.axis_index("head")
    keys, dv = rank_up.shape[1], head_gain.shape[0]
    dk, vals = keys // heads, dv * heads
    hidden_units = down_proj.shape[1]
    group = heads * micro * rows
    proj_width = 2 * dk + 2 * dv

    def own_columns(w, start, size):
        return lax.dynamic_slice_in_dim(w, start + head * size, size, 1)

    w_in = gather_weight(
        jnp.concatenate(
            [
                own_columns(mix_in, 0, dk),
                own_columns(mix_in, keys, dk),
                own_columns(mix_in, 2 * keys, dv),
                own_columns(mix_in, 2 * keys + vals, dv),
            ],
            axis=1,
        )
    )
    later = gather_weight(
        jnp.concatenate(
            [gate_up.reshape(gate_up.shape[0], 2 * hidden_units), down_proj, mix_out], axis=1
        )
    )
    w_out = later[:, 3 * hidden_units :]
    up_own = own_columns(rank_up, 0, dk)
    bias_own = lax.dynamic_slice_in_dim(gate_bias, head * dk, dk, 0)

    xn = gather_norm(tokens.reshape(micro * rows, width), norm_gain.reshape(1, width))
    qkv = dot(xn, w_in[:, : 2 * dk + dv], (1, 0)).astype(BF16)
    og = dot(xn, w_in[:, 2 * dk + dv :], (1, 0))
    ranked = dot(xn, rank_down, (1, 0))
    logits = dot(ranked, up_own, (1, 0), HIGHEST) + bias_own
    decays = (jax.nn.log_sigmoid(logits) / GATE_NORM).astype(BF16)

    def blocks(x):
        return x.reshape(heads, micro, rows, x.shape[-1])

    qkv_b, og_b, decays_b = blocks(qkv), blocks(og), blocks(decays)
    gain_row = head_gain.reshape(1, dv)
    part = dv // seq
    own_states = states_of(starts, qkv_b, decays_b, dv, seq, 16)
    before, through, all_cot = enter(own_states, cotangent.reshape(micro * rows, width), part)
    o_b, gated_b, kept = mix_of(starts, qkv_b, decays_b, og_b, before, gain_row)

    gated = exchange(gated_b, "head")
    gated = gated.transpose(1, 2, 0, 3).reshape(micro * rows, vals)
    source = tokens.astype(F32).reshape(micro * rows, width)
    hidden = source + dot(gated, w_out, (1, 1))
    inv_ffn = rms(hidden, 1e-6)
    plain_ffn = hidden * inv_ffn
    h2 = (plain_ffn * ffn_gain).astype(BF16)

    g_h2, ffn_part, grad_ffn = feed_forward(h2, all_cot, later, hidden_units, heads)
    grad_ffn = scatter_grad(grad_ffn)

    back_ffn, g_ffn_gain = norm_back(g_h2, ffn_gain, plain_ffn, inv_ffn)
    g_hidden = cotangent.astype(F32).reshape(micro * rows, width) + back_ffn
    g_mixed = g_hidden.astype(BF16)
    g_gated = dot(g_mixed, w_out, (1, 0)).astype(BF16)
    grad_mix = weight_grad(g_mixed, gated, None, proj_width + vals, proj_width, dv)
    g_gated = g_gated.reshape(micro, rows, heads, dv).transpose(2, 0, 1, 3)
    g_gated_b = exchange(g_gated, "head")
    g_gated_b, ffn_part = lax.optimization_barrier((g_gated_b, ffn_part))
    ffn_out = ffn_part[head].astype(F32)
    for hop in range(1, heads):
        ffn_out += ring(ffn_part[lax.rem(head + heads - hop, heads)], "head", hop).astype(F32)
    g_og_b, g_o_b, pulled, g_head_gain = gate_back_of(
        starts, g_gated_b, og_b, o_b, qkv_b, decays_b, gain_row, seq
    )
    after = leave(pulled, through)
    g_proj_b, g_logits_b = mix_back_of(
        starts, qkv_b, decays_b, g_o_b, g_og_b, kept, after, blocks(logits)
    )
    g_proj, g_logits = g_proj_b.reshape(group, proj_width), g_logits_b.reshape(group, dk)
    g_ranked = dot(g_logits, up_own, (1, 1), HIGHEST)
    g_xn_part = dot(g_proj, w_in, (1, 1)) + dot(
        g_ranked, rank_down.astype(F32), (1, 1), HIGHEST
    )
    g_xn_part = g_xn_part.astype(BF16).reshape(heads, micro * rows, width)
    g_xn = exchange(g_xn_part, "head").astype(F32).sum(0)
    output = (hidden + ffn_out).astype(BF16)
    inv_in = rms(source, 1e-6)
    back_in, g_norm_gain = norm_back(g_xn, norm_gain, source * inv_in, inv_in)
    input_grad = g_hidden + back_in

    slab = width // (seq * heads)
    grad_mix = weight_grad(xn, g_proj, grad_mix, proj_width + vals, 0, dv)
    grad_mix, grad_ffn = lax.optimization_barrier((grad_mix, grad_ffn))
    grad_mix = scatter_grad(grad_mix).reshape(heads, slab, proj_width + vals)
    grad_mix = exchange(grad_mix, "head").astype(F32)
    grad_in, grad_out = grad_mix[:, :, :proj_width], grad_mix[:, :, proj_width:].sum(0)
    cuts = ((0, dk), (dk, 2 * dk), (2 * dk, 2 * dk + dv), (2 * dk + dv, proj_width))
    grad_in = jnp.concatenate(
        [grad_in[:, :, a:b].transpose(1, 0, 2).reshape(slab, -1) for a, b in cuts], axis=1
    )
    g_rank_down = dot(xn.astype(F32), g_ranked, (0, 0), HIGHEST)
    g_rank_up = dot(ranked, g_logits, (0, 0), HIGHEST)
    g_rank_up = lax.dynamic_update_slice_in_dim(
        jnp.zeros(rank_up.shape, F32), g_rank_up, head * dk, 1
    )
    g_bias = lax.dynamic_update_slice_in_dim(
        jnp.zeros(gate_bias.shape, F32), g_logits.sum(0), head * dk, 0
    )
    small = total_of(
        [g_norm_gain, g_ffn_gain, g_head_gain[0], g_rank_down, g_rank_up, g_bias]
    )
    return (
        output.reshape(tokens.shape),
        input_grad.reshape(tokens.shape),
        grad_in,
        grad_out,
        grad_ffn[:, : 2 * hidden_units].astype(F32).reshape(-1, 2, hidden_units),
        grad_ffn[:, 2 * hidden_units :].astype(F32),
        *small,
    )


def solution(mesh):
    rows = P(None, ("seq", "head"), None)
    return jax.shard_map(
        on_device,
        mesh=mesh,
        in_specs=(
            rows, P(None, "seq"), rows, P("seq", None), P("seq", None),
            P("seq", None, "head"), P("seq", "head"), P(), P(), P(), P(), P(), P(),
        ),
        out_specs=(
            rows, rows, P(("seq", "head"), None), P(("seq", "head"), None),
            P("seq", None, "head"), P("seq", "head"), P(), P(), P(), P(), P(), P(),
        ),
        check_vma=False,
    )
```

```python
import functools

import jax
import jax.numpy as jnp
from jax import lax
from jax.experimental import pallas as pl
from jax.experimental.pallas import tpu as pltpu
from jax.sharding import PartitionSpec as P

HIGHEST = lax.Precision.HIGHEST
GATE_NORM = 16.0
BF16 = jnp.bfloat16
F32 = jnp.float32


def mm(a, b, contract, precision=HIGHEST):
    return lax.dot_general(
        a, b, ((contract[:1], contract[1:]), ((), ())),
        precision=precision, preferred_element_type=F32,
    )


def lower_ones(size):
    rows = lax.broadcasted_iota(jnp.int32, (size, size), 0)
    cols = lax.broadcasted_iota(jnp.int32, (size, size), 1)
    return rows >= cols


def running(decay_low):
    ones = lower_ones(decay_low.shape[0]).astype(F32).astype(BF16)
    return mm(ones, decay_low, (1, 0), None)


def sigmoid(x):
    return 1.0 / (1.0 + jnp.exp(-x))


def state_kernel(flags, qkv, decay, out, state, total_run):
    m, b = pl.program_id(0), pl.program_id(1)
    last = pl.num_programs(1) - 1
    dk = decay.shape[-1]
    keys, values = qkv[0, 0, :, dk : 2 * dk].astype(F32), qkv[0, 0, :, 2 * dk :].astype(F32)
    keep = 1.0 - flags[m, b].astype(F32)

    @pl.when(b == 0)
    def _():
        state[...] = jnp.zeros_like(state)
        total_run[0:1, :] = jnp.zeros((1, dk), F32)
        total_run[1:2, :] = jnp.ones((1, dk), F32)

    run = running(decay[0, 0])
    total = run[-1:, :]
    carried = keys * jnp.exp(total - run)
    state[...] = jnp.exp(total) * (state[...] * keep) + mm(values, carried, (0, 0))
    total_run[0:1, :] += total
    total_run[1:2, :] *= keep

    @pl.when(b == last)
    def _():
        through = jnp.exp(total_run[0:1, :]) * total_run[1:2, :]
        high = through.astype(BF16)
        low = (through - high.astype(F32)).astype(BF16)
        slices, part = out.shape[0], state.shape[0] // out.shape[0]
        tail = out.shape[2] - part
        at = lax.broadcasted_iota(jnp.int32, (tail, dk), 0)
        extra = jnp.where(
            at == 0, high.astype(F32), jnp.where(at == 1, low.astype(F32), 0.0)
        ).astype(BF16)
        for i in range(slices):
            out[i, 0, :part, :] = state[i * part : (i + 1) * part, :].astype(BF16)
            out[i, 0, part:, :] = extra


def mix_kernel(flags, qkv, decay, og, before, gain, o_out, gated, kept, state):
    m, b = pl.program_id(0), pl.program_id(1)
    dk, dv = decay.shape[-1], og.shape[-1]
    q = qkv[0, 0, :, :dk].astype(F32)
    k = qkv[0, 0, :, dk : 2 * dk].astype(F32)
    v = qkv[0, 0, :, 2 * dk :].astype(F32)
    keep = 1.0 - flags[m, b].astype(F32)

    @pl.when(b == 0)
    def _():
        state[...] = before[:, 0].astype(F32).reshape(dv, dk)

    entry = state[...] * keep
    kept[0, 0] = entry
    run = running(decay[0, 0])
    total = run[-1:, :]
    queried = q * jnp.exp(run) * dk ** (-0.5)
    scores = mm(queried, k * jnp.exp(-run), (1, 1))
    scores = jnp.where(lower_ones(scores.shape[0]), scores, 0.0)
    o = mm(scores, v, (1, 0)) + mm(queried, entry, (1, 1))
    state[...] = jnp.exp(total) * entry + mm(v, k * jnp.exp(total - run), (0, 0))
    o_out[0, 0] = o
    scale = lax.rsqrt(jnp.mean(o * o, axis=-1, keepdims=True) + 1e-5)
    normed = (o * scale * gain[...]).astype(BF16).astype(F32)
    gate = og[0, 0]
    gated[0, 0] = (normed * gate * sigmoid(gate)).astype(BF16)


def params(limit=48):
    return pltpu.CompilerParams(
        dimension_semantics=("arbitrary", "arbitrary"), vmem_limit_bytes=limit << 20
    )


def cost(micros):
    return pl.CostEstimate(flops=0, bytes_accessed=int(micros * 3.0e6), transcendentals=0)


def per_block(rows, width):
    return pl.BlockSpec((1, 1, rows, width), lambda m, b, *_: (b, m, 0, 0))


def per_batch(slices, rows, width):
    return pl.BlockSpec((slices, 1, rows, width), lambda m, b, *_: (0, m, 0, 0))


def states_of(flags, qkv, decays, dv, slices, pad):
    blocks, micro, rows, width = qkv.shape
    dk = decays.shape[-1]
    part = dv // slices
    return pl.pallas_call(
        state_kernel,
        out_shape=jax.ShapeDtypeStruct((slices, micro, part + pad, dk), BF16),
        grid_spec=pltpu.PrefetchScalarGridSpec(
            num_scalar_prefetch=1,
            grid=(micro, blocks),
            in_specs=[per_block(rows, width), per_block(rows, dk)],
            out_specs=per_batch(slices, part + pad, dk),
            scratch_shapes=[pltpu.VMEM((dv, dk), F32), pltpu.VMEM((8, dk), F32)],
        ),
        compiler_params=params(),
        cost_estimate=cost(10),
        name="states",
    )(flags, qkv, decays)


def mix_of(flags, qkv, decays, og, before, gain):
    blocks, micro, rows, width = qkv.shape
    dk, dv = decays.shape[-1], og.shape[-1]
    slices, _, part, _ = before.shape
    return pl.pallas_call(
        mix_kernel,
        out_shape=(
            jax.ShapeDtypeStruct((blocks, micro, rows, dv), F32),
            jax.ShapeDtypeStruct((blocks, micro, rows, dv), BF16),
            jax.ShapeDtypeStruct((blocks, micro, dv, dk), F32),
        ),
        grid_spec=pltpu.PrefetchScalarGridSpec(
            num_scalar_prefetch=1,
            grid=(micro, blocks),
            in_specs=[
                per_block(rows, width),
                per_block(rows, dk),
                per_block(rows, dv),
                per_batch(slices, part, dk),
                pl.BlockSpec((1, dv), lambda m, b, *_: (0, 0)),
            ],
            out_specs=(per_block(rows, dv), per_block(rows, dv), per_block(dv, dk)),
            scratch_shapes=[pltpu.VMEM((dv, dk), F32)],
        ),
        compiler_params=params(),
        cost_estimate=cost(18),
        name="mix",
    )(flags, qkv, decays, og, before, gain)


def greet(axes):
    barrier = pltpu.get_barrier_semaphore()
    met = 0
    for axis in axes:
        me, count = lax.axis_index(axis), lax.axis_size(axis)
        for hop in range(1, count):
            pl.semaphore_signal(
                barrier, inc=1, device_id={axis: lax.rem(me + hop, count)},
                device_id_type=pl.DeviceIdType.MESH,
            )
        met += count - 1
    pl.semaphore_wait(barrier, met)


def push(src, dst, send, recv, to, axis="head"):
    return pltpu.make_async_remote_copy(
        src_ref=src, dst_ref=dst, send_sem=send, recv_sem=recv,
        device_id={axis: to}, device_id_type=pl.DeviceIdType.MESH,
    )


def near_order(z, count, i):
    both = jnp.minimum(z, count - 1 - z)
    left = z > count - 1 - z
    paired = jnp.where(i % 2 == 1, z - (i + 1) // 2, z + i // 2)
    single = jnp.where(left, z - (i - both), z + (i - both))
    return jnp.where(i <= 2 * both, paired, single)


class Line:
    def __init__(self, own, all_rows, send, recv):
        self.own, self.all, self.send, self.recv = own, all_rows, send, recv
        self.z, self.count, self.rows = lax.axis_index("head"), lax.axis_size("head"), own.shape[0]
        z, count = self.z, self.count
        self.right = push(own, self.at(z), send.at[0], recv.at[z], lax.rem(z + 1, count))
        self.left = push(own, self.at(z), send.at[1], recv.at[z], lax.rem(z + count - 1, count))

    def chunk(self, b):
        return pl.ds(pl.multiple_of(b * self.rows, self.rows), self.rows)

    def at(self, b):
        return self.all.at[self.chunk(b)]

    def start(self):
        pl.when(self.z < self.count - 1)(self.right.start)
        pl.when(self.z > 0)(self.left.start)

    def passing(self, i, b):
        z, count = self.z, self.count
        to = jnp.where(b < z, z + 1, z - 1)
        going = ((b < z) & (z < count - 1)) | ((b > z) & (z > 0))
        copy = push(
            self.at(b), self.at(b), self.send.at[i + 1], self.recv.at[b], lax.rem(to + count, count)
        )
        return copy, going

    def receive(self, i, b):
        copy, going = self.passing(i, b)
        copy.wait_recv()
        pl.when(going)(copy.start)

    def finish(self):
        def sent(i, _):
            copy, going = self.passing(i, near_order(self.z, self.count, i))
            pl.when(going)(copy.wait_send)
            return 0

        lax.fori_loop(1, self.count, sent, 0)
        pl.when(self.z < self.count - 1)(self.right.wait_send)
        pl.when(self.z > 0)(self.left.wait_send)


class LineSum:
    def __init__(self, parts, landed, send, recv, rows):
        self.parts, self.landed, self.send, self.recv = parts, landed, send, recv
        self.z, self.count = lax.axis_index("head"), lax.axis_size("head")
        self.rows, self.pieces = rows, send.shape[1]
        self.deep = rows // self.pieces
        self.inner = (self.z > 0) & (self.z < self.count - 1)
        self.far_end = jnp.where(self.z < self.count - 1 - self.z, self.count - 1, 0)

    def piece(self, b, p):
        return pl.ds(pl.multiple_of(b * self.rows + p * self.deep, self.deep), self.deep)

    def onward(self, b, p):
        z, count = self.z, self.count
        to = jnp.where(b > z, z + 1, z - 1)
        slot = jnp.where((to == b) & (z > b), count, b)
        return push(
            self.parts.at[self.piece(b, p)], self.landed.at[self.piece(slot, p)],
            self.send.at[b, p], self.recv.at[slot, p], lax.rem(to + count, count),
        )

    def send_all(self):
        @pl.when(jnp.logical_not(self.inner))
        def _():
            for i in range(1, self.count):
                b = jnp.where(self.z == 0, self.count - i, i - 1)
                for p in range(self.pieces):
                    self.onward(b, p).start()

    def arrived(self, slot, p):
        at = self.piece(slot, p)
        push(
            self.landed.at[at], self.landed.at[at], self.send.at[0, p], self.recv.at[slot, p],
            lax.rem(self.z + 1, self.count),
        ).wait_recv()
        return self.landed[at, :].astype(F32)

    def relay(self, b, p):
        at = self.piece(b, p)
        self.parts[at, :] = (self.parts[at, :].astype(F32) + self.arrived(b, p)).astype(BF16)
        self.onward(b, p).start()

    def result(self, out):
        z, count = self.z, self.count
        for p in range(self.pieces):
            here = pl.ds(p * self.deep, self.deep)
            out[here, :] = self.parts[self.piece(z, p), :].astype(F32)

            @pl.when(z > 0)
            def _():
                out[here, :] += self.arrived(z, p)

            @pl.when(z < count - 1)
            def _():
                out[here, :] += self.arrived(count, p)

    def finish(self):
        def sent(i, _):
            b = near_order(self.z, self.count, i)
            for p in range(self.pieces):
                self.onward(b, p).wait_send()
            return 0

        lax.fori_loop(1, self.count, sent, 0)


def gather_norm_kernel(own, gain, normed, rows_all, here_sem, send, recv):
    z, count, rows = lax.axis_index("head"), lax.axis_size("head"), own.shape[0]
    greet(("head",))
    line = Line(own, rows_all, send, recv)
    line.start()
    here = pltpu.make_async_copy(own, line.at(z), here_sem)
    here.start()
    here.wait()
    band = 16

    def step(i, _):
        b = near_order(z, count, i)
        pl.when(i > 0)(lambda: line.receive(i, b))

        def norm(r, _):
            at = pl.ds(pl.multiple_of(b * rows + r * band, band), band)
            x = rows_all[at, :].astype(F32)
            inv = lax.rsqrt(jnp.mean(x * x, axis=-1, keepdims=True) + 1e-6)
            normed[at, :] = (x * inv * gain[...]).astype(BF16)
            return 0

        lax.fori_loop(0, rows // band, norm, 0)
        return 0

    lax.fori_loop(0, count, step, 0)
    line.finish()


def gather_norm(x, gain):
    rows, width = x.shape
    count = lax.axis_size("head")
    vmem = pl.BlockSpec(memory_space=pltpu.VMEM)
    dma = pltpu.SemaphoreType.DMA
    return pl.pallas_call(
        gather_norm_kernel,
        out_shape=jax.ShapeDtypeStruct((count * rows, width), BF16),
        in_specs=[vmem, vmem],
        out_specs=vmem,
        scratch_shapes=[
            pltpu.VMEM((count * rows, width), BF16), dma(()), dma((count + 1,)), dma((count,)),
        ],
        compiler_params=pltpu.CompilerParams(
            collective_id=1, has_side_effects=True, vmem_limit_bytes=32 << 20
        ),
        cost_estimate=cost(50),
        name="gather_norm",
    )(x, gain)


def swap_slices(own, got, send, recv):
    me, count = lax.axis_index("seq"), lax.axis_size("seq")

    def copy(hop, index):
        to = lax.rem(me + hop, count)
        return push(own.at[to], got.at[index], send.at[hop], recv.at[index], to, "seq")

    def start(hop, _):
        copy(hop, me).start()
        return 0

    def wait_recv(hop, _):
        copy(hop, lax.rem(me + hop, count)).wait_recv()
        return 0

    def wait_send(hop, _):
        copy(hop, me).wait_send()
        return 0

    def begin():
        lax.fori_loop(1, count, start, 0)
        got[me] = own[me]

    def end():
        lax.fori_loop(1, count, wait_recv, 0)

    def drain():
        lax.fori_loop(1, count, wait_send, 0)

    return begin, end, drain


def scan_states(reverse, own, through, out):
    count, part = out.shape[0], out.shape[2]

    def step(k, state):
        j = count - 1 - k if reverse else k
        out[j] = state.astype(BF16)
        decay = through[j, :, 0:1, :].astype(F32) + through[j, :, 1:2, :].astype(F32)
        return decay * state + own[j, :, :part, :].astype(F32)

    lax.fori_loop(0, count, step, jnp.zeros(out.shape[1:], F32))


def enter_kernel(own, rows_own, before, through, rows_all,
                 got, scanned, send, recv, send_back, recv_back, here_sem, go, come):
    z, count = lax.axis_index("head"), lax.axis_size("head")
    part = scanned.shape[2]
    greet(("seq", "head"))
    begin, end, drain = swap_slices(own, got, send, recv)
    begin()
    line = Line(rows_own, rows_all, go, come)
    line.start()
    here = pltpu.make_async_copy(rows_own, line.at(z), here_sem)
    here.start()
    end()
    through[...] = got[:, :, part:, :]
    scan_states(False, got, through, scanned)
    begin_back, end_back, drain_back = swap_slices(scanned, before, send_back, recv_back)
    begin_back()

    def step(i, _):
        line.receive(i, near_order(z, count, i))
        return 0

    lax.fori_loop(1, count, step, 0)
    end_back()
    here.wait()
    line.finish()
    drain()
    drain_back()


def enter(own, rows_own, part):
    slices, micro, deep, dk = own.shape
    rows, width = rows_own.shape
    count = lax.axis_size("head")
    vmem, anywhere = pl.BlockSpec(memory_space=pltpu.VMEM), pl.BlockSpec(memory_space=pl.ANY)
    dma = pltpu.SemaphoreType.DMA
    return pl.pallas_call(
        enter_kernel,
        out_shape=(
            jax.ShapeDtypeStruct((slices, micro, part, dk), BF16),
            jax.ShapeDtypeStruct((slices, micro, deep - part, dk), BF16),
            jax.ShapeDtypeStruct((count * rows, width), BF16),
        ),
        in_specs=[vmem, anywhere],
        out_specs=(vmem, vmem, anywhere),
        scratch_shapes=[
            pltpu.VMEM(own.shape, BF16), pltpu.VMEM((slices, micro, part, dk), BF16),
            dma((slices,)), dma((slices,)), dma((slices,)), dma((slices,)),
            dma(()), dma((count + 1,)), dma((count,)),
        ],
        compiler_params=pltpu.CompilerParams(
            collective_id=2, has_side_effects=True, vmem_limit_bytes=32 << 20
        ),
        cost_estimate=cost(50),
        name="enter",
    )(own, rows_own)


def total_kernel(own, out, from_seq, part, from_head, send_a, recv_a, send_b, recv_b,
                 send_c, recv_c, send_d, recv_d):
    seq, head = lax.axis_size("seq"), lax.axis_size("head")
    s, h = lax.axis_index("seq"), lax.axis_index("head")
    greet(("seq", "head"))

    def each(axis, me, count, src, dst, send, recv):
        def copy(hop, index):
            to = lax.rem(me + hop, count)
            return push(src(to), dst(index), send.at[hop], recv.at[index], to, axis)

        for hop in range(1, count):
            copy(hop, me).start()
        for hop in range(1, count):
            copy(hop, lax.rem(me + hop, count)).wait_recv()
        return [copy(hop, me).wait_send for hop in range(1, count)]

    from_seq[s] = own[s]
    sent = each("seq", s, seq, lambda to: own.at[to], lambda i: from_seq.at[i], send_a, recv_a)
    part[...] = jnp.sum(from_seq[...], axis=0)
    from_head[h] = part[h]
    sent += each("head", h, head, lambda to: part.at[to], lambda i: from_head.at[i], send_b, recv_b)
    out[s, h] = jnp.sum(from_head[...], axis=0)
    sent += each("head", h, head, lambda _: out.at[s, h], lambda i: out.at[s, i], send_c, recv_c)
    sent += each("seq", s, seq, lambda _: out.at[s], lambda i: out.at[i], send_d, recv_d)
    for wait in sent:
        wait()


def total_of(parts):
    seq, head = lax.axis_size("seq"), lax.axis_size("head")
    flat = jnp.concatenate([p.reshape(-1) for p in parts])
    deep = -(-flat.shape[0] // (seq * head * 1024)) * 8
    flat = jnp.pad(flat, (0, seq * head * deep * 128 - flat.shape[0]))
    vmem = pl.BlockSpec(memory_space=pltpu.VMEM)
    dma = pltpu.SemaphoreType.DMA
    shape = (seq, head, deep, 128)
    whole = pl.pallas_call(
        total_kernel,
        out_shape=jax.ShapeDtypeStruct(shape, F32),
        in_specs=[vmem],
        out_specs=vmem,
        scratch_shapes=[
            pltpu.VMEM(shape, F32), pltpu.VMEM(shape[1:], F32), pltpu.VMEM(shape[1:], F32),
        ]
        + [dma((n,)) for n in (seq, seq, head, head, head, head, seq, seq)],
        compiler_params=pltpu.CompilerParams(collective_id=4, has_side_effects=True),
        cost_estimate=cost(15),
        name="total",
    )(flat.reshape(shape)).reshape(-1)
    result, at = [], 0
    for p in parts:
        result.append(whole[at : at + p.size].reshape(p.shape))
        at += p.size
    return result


def ffn_kernel(count, x_own, c_all, w, g_x, f_parts, grad,
               wv, xs, cs, act, lin, parts, landed, turned, turned_c, tiles,
               w_sem, own_sem, go_sem, x_sem, p_sem, q_sem, o_sem):
    z = lax.axis_index("head")
    rows, width = x_own.shape
    hidden = act.shape[1] // 3
    chunk = lambda b: pl.ds(pl.multiple_of(b * rows, rows), rows)

    weights = [
        pltpu.make_async_copy(
            w.at[:, pl.ds(k * hidden, hidden)], wv.at[:, pl.ds(k * hidden, hidden)], w_sem.at[k]
        )
        for k in range(3)
    ]
    own = [
        pltpu.make_async_copy(x_own, xs.at[chunk(z)], own_sem.at[0]),
        pltpu.make_async_copy(c_all, cs, own_sem.at[1]),
    ]
    for copy in own + weights:
        copy.start()
    greet(("head",))
    line = Line(x_own, xs, go_sem, x_sem)
    line.start()
    for copy in own + weights:
        copy.wait()

    total = LineSum(parts, landed, p_sem, q_sem, rows)

    def step(i, _):
        b = near_order(z, count, i)

        pl.when(i > 0)(lambda: line.receive(i, b))

        at = chunk(b)
        x = xs[at, :]
        lin[0] = jnp.dot(x, wv[:, :hidden], preferred_element_type=F32)
        lin[1] = jnp.dot(x, wv[:, hidden : 2 * hidden], preferred_element_type=F32)
        lin[2] = jnp.dot(cs[at, :], wv[:, 2 * hidden :], preferred_element_type=F32)
        band = 16

        def act_rows(r, _):
            here = pl.ds(pl.multiple_of(r * band, band), band)
            there = pl.ds(pl.multiple_of(b * rows + r * band, band), band)
            gate, up, g_product = lin[0, here, :], lin[1, here, :], lin[2, here, :]
            sig = sigmoid(gate)
            gated = gate * sig
            act[there, :hidden] = (g_product * up * sig * (1.0 + gate * (1.0 - sig))).astype(BF16)
            act[there, hidden : 2 * hidden] = (g_product * gated).astype(BF16)
            act[there, 2 * hidden :] = (gated * up).astype(BF16)
            return 0

        lax.fori_loop(0, rows // band, act_rows, 0)
        parts[at, :] = mm(act[at, : 2 * hidden], wv[:, : 2 * hidden], (1, 1), None).astype(BF16)

        @pl.when((i > 0) & jnp.logical_not(total.inner))
        def _():
            for p in range(total.pieces):
                total.onward(b, p).start()

        return 0

    lax.fori_loop(0, count, step, 0)

    @pl.when(total.inner)
    def _():
        for p in range(total.pieces):
            total.relay(count - 1 - z, p)

    high = tiles.shape[1]
    steps = width // high
    first = grad.shape[1] - 3 * hidden

    def store(t, r, k):
        return pltpu.make_async_copy(
            tiles.at[lax.rem(t, 2)],
            grad.at[
                pl.ds(pl.multiple_of(r * high, high), high), pl.ds(first + k * hidden, hidden)
            ],
            o_sem.at[lax.rem(t, 2)],
        )

    turned[...] = xs[...].T
    turned_c[...] = cs[...].T

    def slab(r, _):
        for k in range(3):
            t = 3 * r + k

            @pl.when(t >= 2)
            def _():
                store(t, r, k).wait()

            left_rows = (turned_c if k == 2 else turned)[
                pl.ds(pl.multiple_of(r * high, high), high), :
            ]
            tiles[lax.rem(t, 2)] = jnp.dot(
                left_rows, act[:, k * hidden : (k + 1) * hidden], preferred_element_type=F32
            ).astype(BF16)
            store(t, r, k).start()

        @pl.when(total.inner)
        def _():
            total.relay(total.far_end, r)
            total.relay(count - 1 - total.far_end, r)

        return 0

    lax.fori_loop(0, steps, slab, 0)

    def part(b, _):
        at = chunk(b)
        f_parts[b] = mm(act[at, 2 * hidden :], wv[:, 2 * hidden :], (1, 1), None).astype(BF16)
        return 0

    lax.fori_loop(0, count, part, 0)

    total.result(g_x)
    total.finish()
    line.finish()
    store(3 * steps - 2, 0, 0).wait()
    store(3 * steps - 1, 0, 0).wait()


def feed_forward(x_own, c_all, w, hidden, count):
    rows, width = x_own.shape
    group = rows * count
    assert count == 4 and width % 4 == 0 and rows % 64 == 0
    anywhere = pl.BlockSpec(memory_space=pl.ANY)
    vmem = pl.BlockSpec(memory_space=pltpu.VMEM)
    dma = pltpu.SemaphoreType.DMA
    return pl.pallas_call(
        functools.partial(ffn_kernel, count),
        out_shape=(
            jax.ShapeDtypeStruct((rows, width), F32),
            jax.ShapeDtypeStruct((count, rows, width), BF16),
            jax.ShapeDtypeStruct((width, 3 * hidden), BF16),
        ),
        in_specs=[anywhere] * 3,
        out_specs=(vmem, vmem, anywhere),
        scratch_shapes=[
            pltpu.VMEM((width, 3 * hidden), BF16),
            pltpu.VMEM((group, width), BF16),
            pltpu.VMEM((group, width), BF16),
            pltpu.VMEM((group, 3 * hidden), BF16),
            pltpu.VMEM((3, rows, hidden), F32),
            pltpu.VMEM((group, width), BF16),
            pltpu.VMEM((group + rows, width), BF16),
            pltpu.VMEM((width, group), BF16),
            pltpu.VMEM((width, group), BF16),
            pltpu.VMEM((2, width // 4, hidden), BF16),
            dma((3,)), dma((2,)), dma((count + 1,)), dma((count,)),
            dma((count, 4)), dma((count + 1, 4)), dma((2,)),
        ],
        compiler_params=pltpu.CompilerParams(
            collective_id=0, has_side_effects=True, vmem_limit_bytes=60 << 20
        ),
        cost_estimate=cost(100),
        name="feed_forward",
    )(x_own, c_all, w)


def split(x):
    high = x.astype(BF16)
    return high, (x - high.astype(F32)).astype(BF16)


def mms(left, right, contract):
    total = mm(left[0], right[0], contract, None)
    if len(right) > 1:
        total += mm(left[0], right[1], contract, None)
    if len(left) > 1:
        total += mm(left[1], right[0], contract, None)
    return total


def back_kernel(keep, gated_own, og, o_in, qkv, decay, logits, through, gain, left, right,
                kept_in, parts_in, g_proj, g_logits, g_gain, f_out, g_out,
                gated_all, go, runs, g_queried, g_keyed, g_values, pulls, weights, kept,
                parts, landed, state, sending, got, scanned, after, turned, tiles, in_sem, t_sem,
                z_send, z_recv, s_send, s_recv, b_send, b_recv, p_sem, q_sem):
    h, head = lax.axis_index("head"), lax.axis_size("head")
    count, micro, rows, dk = decay.shape
    dv = og.shape[-1]
    width = qkv.shape[-1]
    slices, part = sending.shape[0], sending.shape[2]
    scale = dk ** (-0.5)
    loads = [
        pltpu.make_async_copy(parts_in, parts, in_sem.at[0]),
        pltpu.make_async_copy(kept_in, kept, in_sem.at[1]),
    ]
    for load in loads:
        load.start()
    greet(("seq", "head"))

    def to_head(hop, slot):
        to = lax.rem(h + hop, head)
        return push(gated_own.at[to], gated_all.at[slot], z_send.at[hop], z_recv.at[slot], to)

    for hop in range(1, head):
        to_head(hop, h).start()
    gated_all[h] = gated_own[h]

    causal = lower_ones(rows)
    before = [jnp.zeros((1, dk), F32)] * micro
    alive = [jnp.ones((1, dk), F32)] * micro
    for b in range(count):
        for m in range(micro):
            run = running(decay[b, m])
            runs[b, m] = run
            alive[m] = alive[m] * keep[b, m]
            weights[b, m] = jnp.exp(before[m]) * alive[m]
            before[m] = before[m] + run[rows - 1 : rows, :]
    g_gain[...] = jnp.zeros_like(g_gain)
    state[...] = jnp.zeros_like(state)

    turned[...] = left[...].T
    high, wide = tiles.shape[1:]
    across_tiles = g_out.shape[1] // wide

    def store(t):
        at = pl.ds(pl.multiple_of((t // across_tiles) * high, high), high)
        columns = pl.ds(pl.multiple_of(lax.rem(t, across_tiles) * wide, wide), wide)
        return pltpu.make_async_copy(
            tiles.at[lax.rem(t, 2)], g_out.at[at, columns], t_sem.at[lax.rem(t, 2)]
        )

    def tile(t, _):
        @pl.when(t >= 2)
        def _():
            store(t - 2).wait()

        at = pl.ds(pl.multiple_of((t // across_tiles) * high, high), high)
        columns = pl.ds(pl.multiple_of(lax.rem(t, across_tiles) * wide, wide), wide)
        tiles[lax.rem(t, 2)] = jnp.dot(
            turned[at, :], right[:, columns], preferred_element_type=F32
        ).astype(BF16)
        store(t).start()
        return 0

    tile_count = (g_out.shape[0] // high) * across_tiles
    lax.fori_loop(0, tile_count, tile, 0)

    def gates(i, _):
        b = near_order(h, head, i)
        pl.when(i > 0)(lambda: to_head(lax.rem(b - h + head, head), b).wait_recv())
        for m in range(micro):
            gate, o = og[b, m], o_in[b, m]
            grad = gated_all[b, m].astype(F32)
            sig = sigmoid(gate)
            inv = lax.rsqrt(jnp.mean(o * o, axis=-1, keepdims=True) + 1e-5)
            plain = o * inv
            normed = (plain * gain[...]).astype(BF16).astype(F32)
            g_on = (grad * gate * sig).astype(BF16).astype(F32)
            g_proj[b, m, :, width:] = (
                grad * normed * sig * (1.0 + gate * (1.0 - sig))
            ).astype(BF16)
            scaled = g_on * gain[...]
            g_o = inv * (scaled - plain * jnp.mean(scaled * plain, axis=-1, keepdims=True))
            go[b, m] = g_o
            g_gain[0:1, :] += jnp.sum(g_on * plain, axis=0, keepdims=True)
            queried = qkv[b, m, :, :dk].astype(F32) * (jnp.exp(runs[b, m]) * scale)
            pull = mms(split(g_o), split(queried), (0, 0))
            pulls[b, m] = pull
            state[m] += pull * weights[b, m]
        return 0

    lax.fori_loop(0, head, gates, 0)
    for i in range(slices):
        sending[i] = state[:, i * part : (i + 1) * part, :].astype(BF16)
    begin, end, drain = swap_slices(sending, got, s_send, s_recv)
    begin()
    for load in loads:
        load.wait()
    total = LineSum(parts, landed, p_sem, q_sem, f_out.shape[0])
    total.send_all()

    def inside(b, _):
        for m in range(micro):
            q = qkv[b, m, :, :dk].astype(F32)
            k = qkv[b, m, :, dk : 2 * dk].astype(F32)
            v = (qkv[b, m, :, 2 * dk :],)
            run = runs[b, m]
            queried, keyed = split(q * (jnp.exp(run) * scale)), split(k * jnp.exp(-run))
            g_o, entry = split(go[b, m]), split(kept[b, m])
            scores = split(jnp.where(causal, mms(queried, keyed, (1, 1)), 0.0))
            g_scores = split(jnp.where(causal, mms(g_o, v, (1, 1)), 0.0))
            g_queried[b, m] = mms(g_scores, keyed, (1, 0)) + mms(g_o, entry, (1, 0))
            g_keyed[b, m] = mms(g_scores, queried, (0, 0))
            g_values[b, m] = mms(scores, g_o, (0, 0))
        pl.when(total.inner)(lambda: total.relay(total.far_end, b))
        return 0

    lax.fori_loop(0, count, inside, 0)
    end()
    scan_states(True, got, through, scanned)
    begin_back, end_back, drain_back = swap_slices(scanned, after, b_send, b_recv)
    begin_back()

    @pl.when(total.inner)
    def _():
        for p in range(total.pieces):
            total.relay(head - 1 - total.far_end, p)
        for p in range(total.pieces):
            total.relay(head - 1 - h, p)

    end_back()
    for i in range(slices):
        state[:, i * part : (i + 1) * part, :] = after[i].astype(F32)

    def across(step, _):
        b = count - 1 - step
        for m in range(micro):
            q = qkv[b, m, :, :dk].astype(F32)
            k = qkv[b, m, :, dk : 2 * dk].astype(F32)
            v = (qkv[b, m, :, 2 * dk :],)
            run = runs[b, m]
            last = run[rows - 1 : rows, :]
            up, down, rest = jnp.exp(run) * scale, jnp.exp(-run), jnp.exp(last - run)
            decayed = jnp.exp(last)
            gs = state[m]
            gs_parts = split(gs)
            carried = k * rest
            g_v = g_values[b, m] + mms(split(carried), gs_parts, (1, 1))
            g_carried = mms(v, gs_parts, (1, 0))
            from_carried = g_carried * carried
            g_total = jnp.sum(decayed * kept[b, m] * gs, axis=0, keepdims=True) + jnp.sum(
                from_carried, axis=0, keepdims=True
            )
            state[m] = (decayed * gs + pulls[b, m]) * keep[b, m]
            gq, gk = g_queried[b, m], g_keyed[b, m]
            g_run = gq * (q * up) - gk * (k * down) - from_carried
            later = mms((causal.astype(F32).astype(BF16),), split(g_run), (0, 0)) + g_total
            g_proj[b, m, :, :dk] = (gq * up).astype(BF16)
            g_proj[b, m, :, dk : 2 * dk] = (gk * down + g_carried * rest).astype(BF16)
            g_proj[b, m, :, 2 * dk : width] = g_v.astype(BF16)
            g_logits[b, m] = (
                later.astype(BF16).astype(F32) * sigmoid(-logits[b, m]) * (1.0 / GATE_NORM)
            )
        return 0

    lax.fori_loop(0, count, across, 0)
    total.result(f_out)
    total.finish()
    store(tile_count - 2).wait()
    store(tile_count - 1).wait()
    drain()
    drain_back()
    for hop in range(1, head):
        to_head(hop, h).wait_send()


def attention_back(
    keep, gated_own, og, o, qkv, decays, logits, through, gain, left, right, kept, parts
):
    blocks, micro, rows, width = qkv.shape
    dk, dv = decays.shape[-1], og.shape[-1]
    head, seq = lax.axis_size("head"), lax.axis_size("seq")
    own_rows = parts.shape[0] // head
    vmem, anywhere = pl.BlockSpec(memory_space=pltpu.VMEM), pl.BlockSpec(memory_space=pl.ANY)
    dma = pltpu.SemaphoreType.DMA
    blocked = lambda w, kind: pltpu.VMEM((blocks, micro, rows, w), kind)
    states = (seq, micro, dv // seq, dk)
    return pl.pallas_call(
        back_kernel,
        out_shape=(
            jax.ShapeDtypeStruct((blocks, micro, rows, width + dv), BF16),
            jax.ShapeDtypeStruct((blocks, micro, rows, dk), F32),
            jax.ShapeDtypeStruct((8, dv), F32),
            jax.ShapeDtypeStruct((own_rows, parts.shape[1]), F32),
            jax.ShapeDtypeStruct((left.shape[1], right.shape[1]), BF16),
        ),
        in_specs=[vmem] * 11 + [anywhere] * 2,
        out_specs=(vmem,) * 4 + (anywhere,),
        scratch_shapes=[
            blocked(dv, BF16), blocked(dv, F32), blocked(dk, F32),
            blocked(dk, F32), blocked(dk, F32), blocked(dv, F32),
            pltpu.VMEM((blocks, micro, dv, dk), F32), pltpu.VMEM((blocks, micro, 1, dk), F32),
            pltpu.VMEM((blocks, micro, dv, dk), F32),
            pltpu.VMEM(parts.shape, BF16),
            pltpu.VMEM((parts.shape[0] + own_rows, parts.shape[1]), BF16),
            pltpu.VMEM((micro, dv, dk), F32),
            pltpu.VMEM(states, BF16), pltpu.VMEM(states, BF16), pltpu.VMEM(states, BF16),
            pltpu.VMEM(states, BF16),
            pltpu.VMEM(left.shape[::-1], BF16),
            pltpu.VMEM((2, left.shape[1] // 4, right.shape[1] // 2), BF16),
            dma((2,)), dma((2,)), dma((head,)), dma((head,)), dma((seq,)), dma((seq,)), dma((seq,)),
            dma((seq,)), dma((head, 4)), dma((head + 1, 4)),
        ],
        compiler_params=pltpu.CompilerParams(
            collective_id=3, has_side_effects=True, vmem_limit_bytes=60 << 20
        ),
        cost_estimate=cost(80),
        name="attention_back",
    )(keep, gated_own, og, o, qkv, decays, logits, through, gain, left, right, kept, parts)


def finish_kernel(xn_in, proj_in, w_in, g_logits, ranked, up_own, rank_down,
                  g_x, grad, g_down, g_up, g_bias,
                  turned, proj, w, outgoing, mine, paired, peers, slab, heads_in, parts, landed, slim_high,
                  slim_low, in_sem, pair_send, pair_recv, peer_send, peer_recv, x_send, x_recv,
                  p_sem, q_sem):
    s, seq = lax.axis_index("seq"), lax.axis_size("seq")
    h, head = lax.axis_index("head"), lax.axis_size("head")
    rows, width = g_x.shape
    deep = grad.shape[0] * head
    side = lax.rem(s, 2)
    pairs = seq // 2
    own_pair = s // 2

    loads = [
        pltpu.make_async_copy(proj_in, proj, in_sem.at[0]),
        pltpu.make_async_copy(w_in, w, in_sem.at[1]),
        pltpu.make_async_copy(xn_in, landed.at[pl.ds(0, xn_in.shape[0])], in_sem.at[2]),
    ]
    for load in loads:
        load.start()
    for load in loads:
        load.wait()
    turned[...] = landed[: xn_in.shape[0], :].T
    greet(("seq", "head"))
    total = LineSum(parts, landed, p_sem, q_sem, rows)
    logit_parts = split(g_logits[...])
    g_ranked = mms(logit_parts, split(up_own[...]), (1, 1))
    slim = split(g_ranked)
    slim_high[...], slim_low[...] = slim

    def chunk(i, _):
        b = near_order(h, head, head - 1 - i)
        at = pl.ds(pl.multiple_of(b * rows, rows), rows)
        rank_part = mms((slim_high[at, :], slim_low[at, :]), (rank_down[...],), (1, 1))
        parts[at, :] = (mm(proj[at, :], w[...], (1, 1), None) + rank_part).astype(BF16)

        @pl.when((b != h) & jnp.logical_not(total.inner))
        def _():
            for p in range(total.pieces):
                total.onward(b, p).start()

        return 0

    lax.fori_loop(0, head, chunk, 0)

    def block(i):
        return pl.ds(pl.multiple_of(i * deep, deep), deep)

    def to_partner(k):
        return push(
            outgoing.at[k], paired.at[k], pair_send.at[k], pair_recv.at[k], s + 1 - 2 * side, "seq"
        )

    def to_peer(k):
        return push(
            mine.at[k], peers.at[own_pair], peer_send.at[k], peer_recv.at[own_pair],
            2 * k + side, "seq",
        )

    def gone(k, _):
        outgoing[k] = jnp.dot(
            turned[block(2 * k + 1 - side), :], proj[...], preferred_element_type=F32
        ).astype(BF16)
        to_partner(k).start()
        return 0

    lax.fori_loop(0, pairs, gone, 0)

    def kept(k, _):
        here = jnp.dot(turned[block(2 * k + side), :], proj[...], preferred_element_type=F32)
        to_partner(k).wait_recv()
        mine[k] = (here + paired[k].astype(F32)).astype(BF16)
        pl.when(own_pair != k)(to_peer(k).start)

        @pl.when(total.inner & (k < total.pieces))
        def _():
            total.relay(total.far_end, k)
            total.relay(head - 1 - total.far_end, k)

        return 0

    lax.fori_loop(0, pairs, kept, 0)

    @pl.when(total.inner)
    def _():
        for p in range(pairs, total.pieces):
            total.relay(total.far_end, p)
            total.relay(head - 1 - total.far_end, p)
        for p in range(total.pieces):
            total.relay(head - 1 - h, p)

    g_down[...] = mms((turned[...],), slim, (1, 0))
    g_up[...] = mms(split(ranked[...]), logit_parts, (0, 0))
    g_bias[...] = jnp.broadcast_to(jnp.sum(g_logits[...], axis=0, keepdims=True), g_bias.shape)

    def arrived(k):
        return push(
            mine.at[k], peers.at[k], peer_send.at[k], peer_recv.at[k],
            lax.rem(s + 1, seq), "seq",
        )

    peers[own_pair] = mine[own_pair]
    for k in range(pairs):
        pl.when(own_pair != k)(arrived(k).wait_recv)
    band = 16

    def add_rows(r, _):
        at = pl.ds(pl.multiple_of(r * band, band), band)
        slab[at, :] = jnp.sum(peers[:, at, :].astype(F32), axis=0).astype(BF16)
        return 0

    lax.fori_loop(0, deep // band, add_rows, 0)
    thin = grad.shape[0]

    def to_head(hop, slot):
        to = lax.rem(h + hop, head)
        return push(
            slab.at[pl.ds(pl.multiple_of(to * thin, thin), thin)], heads_in.at[slot],
            x_send.at[hop], x_recv.at[slot], to,
        )

    for hop in range(1, head):
        to_head(hop, h).start()
    heads_in[h] = slab[pl.ds(pl.multiple_of(h * thin, thin), thin), :]
    total.result(g_x)
    for hop in range(1, head):
        to_head(hop, lax.rem(h + hop, head)).wait_recv()
    dk = g_up.shape[1]
    dv = slab.shape[1] // 2 - dk
    for j in range(head):
        at, start = 0, 0
        for size in (dk, dk, dv, dv):
            grad[:, start + j * size : start + (j + 1) * size] = heads_in[
                j, :, at : at + size
            ].astype(F32)
            at, start = at + size, start + head * size
    for k in range(pairs):
        to_partner(k).wait_send()
        pl.when(own_pair != k)(to_peer(k).wait_send)
    for hop in range(1, head):
        to_head(hop, h).wait_send()
    total.finish()


def finish(xn, g_proj, w_in, g_logits, ranked, up_own, rank_down):
    seq, head = lax.axis_size("seq"), lax.axis_size("head")
    group, width = xn.shape
    columns, rank = w_in.shape[1], ranked.shape[1]
    deep, rows, pairs = width // seq, group // head, seq // 2
    dk = up_own.shape[1]
    vmem, anywhere = pl.BlockSpec(memory_space=pltpu.VMEM), pl.BlockSpec(memory_space=pl.ANY)
    dma = pltpu.SemaphoreType.DMA
    blocks = pltpu.VMEM((pairs, deep, columns), BF16)
    return pl.pallas_call(
        finish_kernel,
        out_shape=(
            jax.ShapeDtypeStruct((rows, width), F32),
            jax.ShapeDtypeStruct((deep // head, columns * head), F32),
            jax.ShapeDtypeStruct((width, rank), F32),
            jax.ShapeDtypeStruct((rank, dk), F32),
            jax.ShapeDtypeStruct((8, dk), F32),
        ),
        in_specs=[anywhere] * 3 + [vmem] * 4,
        out_specs=(vmem,) * 5,
        scratch_shapes=[
            pltpu.VMEM((width, group), BF16), pltpu.VMEM(g_proj.shape, BF16),
            pltpu.VMEM(w_in.shape, BF16), blocks, blocks, blocks, blocks,
            pltpu.VMEM((deep, columns), BF16), pltpu.VMEM((head, deep // head, columns), BF16),
            pltpu.VMEM((group, width), BF16), pltpu.VMEM((group + rows, width), BF16),
            pltpu.VMEM(ranked.shape, BF16), pltpu.VMEM(ranked.shape, BF16),
            dma((3,)), dma((pairs,)), dma((pairs,)), dma((pairs,)), dma((pairs,)),
            dma((head,)), dma((head,)), dma((head, 4)), dma((head + 1, 4)),
        ],
        compiler_params=pltpu.CompilerParams(
            collective_id=5, has_side_effects=True, vmem_limit_bytes=56 << 20
        ),
        cost_estimate=cost(60),
        name="finish",
    )(xn, g_proj, w_in, g_logits, ranked, up_own, rank_down)


def exchange(x, axis):
    return lax.all_to_all(x, axis, split_axis=0, concat_axis=0, tiled=True)


def gather_weight(w):
    return lax.all_gather(w, "seq", axis=0, tiled=True)


def scatter_grad(g):
    return lax.psum_scatter(g.astype(BF16), "seq", scatter_dimension=0, tiled=True)


def dot(a, b, contract, precision=None):
    return lax.dot_general(
        a, b, (((contract[0],), (contract[1],)), ((), ())),
        precision=precision, preferred_element_type=F32,
    )


def rms(x, epsilon):
    return lax.rsqrt(jnp.mean(x * x, axis=-1, keepdims=True) + epsilon)


def norm_back(grad, gain, normed, inv):
    scaled = grad * gain
    inner = jnp.mean(scaled * normed, axis=-1, keepdims=True)
    return inv * (scaled - normed * inner), jnp.sum(grad * normed, axis=0)


def on_device(
    tokens, starts, cotangent, mix_in, mix_out, gate_up, down_proj,
    norm_gain, ffn_gain, head_gain, rank_down, rank_up, gate_bias,
):
    micro, rows, width = tokens.shape
    heads, seq = lax.axis_size("head"), lax.axis_size("seq")
    head = lax.axis_index("head")
    keys, dv = rank_up.shape[1], head_gain.shape[0]
    dk, vals = keys // heads, dv * heads
    hidden_units = down_proj.shape[1]
    group = heads * micro * rows
    proj_width = 2 * dk + 2 * dv

    def own_columns(w, start, size):
        return lax.dynamic_slice_in_dim(w, start + head * size, size, 1)

    w_in = gather_weight(
        jnp.concatenate(
            [
                own_columns(mix_in, 0, dk),
                own_columns(mix_in, keys, dk),
                own_columns(mix_in, 2 * keys, dv),
                own_columns(mix_in, 2 * keys + vals, dv),
            ],
            axis=1,
        )
    )
    later = gather_weight(
        jnp.concatenate(
            [gate_up.reshape(gate_up.shape[0], 2 * hidden_units), down_proj, mix_out], axis=1
        )
    )
    w_out = later[:, 3 * hidden_units :]
    up_own = own_columns(rank_up, 0, dk)
    bias_own = lax.dynamic_slice_in_dim(gate_bias, head * dk, dk, 0)

    xn = gather_norm(tokens.reshape(micro * rows, width), norm_gain.reshape(1, width))
    qkv = dot(xn, w_in[:, : 2 * dk + dv], (1, 0)).astype(BF16)
    og = dot(xn, w_in[:, 2 * dk + dv :], (1, 0))
    ranked = dot(xn, rank_down, (1, 0))
    logits = dot(ranked, up_own, (1, 0), HIGHEST) + bias_own
    decays = (jax.nn.log_sigmoid(logits) / GATE_NORM).astype(BF16)

    def blocks(x):
        return x.reshape(heads, micro, rows, x.shape[-1])

    qkv_b, og_b, decays_b = blocks(qkv), blocks(og), blocks(decays)
    gain_row = head_gain.reshape(1, dv)
    part = dv // seq
    own_states = states_of(starts, qkv_b, decays_b, dv, seq, 16)
    before, through, all_cot = enter(own_states, cotangent.reshape(micro * rows, width), part)
    o_b, gated_b, kept = mix_of(starts, qkv_b, decays_b, og_b, before, gain_row)

    gated = exchange(gated_b, "head")
    gated = gated.transpose(1, 2, 0, 3).reshape(micro * rows, vals)
    source = tokens.astype(F32).reshape(micro * rows, width)
    hidden = source + dot(gated, w_out, (1, 1))
    inv_ffn = rms(hidden, 1e-6)
    plain_ffn = hidden * inv_ffn
    h2 = (plain_ffn * ffn_gain).astype(BF16)

    g_h2, ffn_part, grad_ffn = feed_forward(h2, all_cot, later, hidden_units, heads)
    grad_ffn = scatter_grad(grad_ffn)

    back_ffn, g_ffn_gain = norm_back(g_h2, ffn_gain, plain_ffn, inv_ffn)
    g_hidden = cotangent.astype(F32).reshape(micro * rows, width) + back_ffn
    g_mixed = g_hidden.astype(BF16)
    g_gated = dot(g_mixed, w_out, (1, 0)).astype(BF16)
    g_gated = g_gated.reshape(micro, rows, heads, dv).transpose(2, 0, 1, 3)
    keep = 1.0 - jnp.broadcast_to(starts.T[:, :, None, None], (heads, micro, 1, dk)).astype(F32)
    g_proj_b, g_logits_b, g_head_gain, ffn_out, grad_out = attention_back(
        keep, g_gated, og_b, o_b, qkv_b, decays_b, blocks(logits), through, gain_row,
        g_mixed, gated, kept, ffn_part.reshape(group, width),
    )
    grad_out = scatter_grad(grad_out)
    output = (hidden + ffn_out).astype(BF16)
    g_proj, g_logits = g_proj_b.reshape(group, proj_width), g_logits_b.reshape(group, dk)
    g_xn, grad_in, g_rank_down, g_rank_up, g_bias = finish(
        xn, g_proj, w_in, g_logits, ranked, up_own, rank_down
    )
    g_xn, grad_ffn = lax.optimization_barrier((g_xn, grad_ffn))
    inv_in = rms(source, 1e-6)
    back_in, g_norm_gain = norm_back(g_xn, norm_gain, source * inv_in, inv_in)
    input_grad = g_hidden + back_in

    g_rank_up = lax.dynamic_update_slice_in_dim(
        jnp.zeros(rank_up.shape, F32), g_rank_up, head * dk, 1
    )
    g_bias = lax.dynamic_update_slice_in_dim(
        jnp.zeros(gate_bias.shape, F32), g_bias[0], head * dk, 0
    )
    small = total_of(
        [g_norm_gain, g_ffn_gain, g_head_gain[0], g_rank_down, g_rank_up, g_bias]
    )
    slab = width // (seq * heads)
    small, grad_out = lax.optimization_barrier((small, grad_out))
    grad_out = exchange(grad_out.reshape(heads, slab, vals), "head").astype(F32).sum(0)
    return (
        output.reshape(tokens.shape),
        input_grad.reshape(tokens.shape),
        grad_in,
        grad_out,
        grad_ffn[:, : 2 * hidden_units].astype(F32).reshape(-1, 2, hidden_units),
        grad_ffn[:, 2 * hidden_units :].astype(F32),
        *small,
    )


def solution(mesh):
    rows = P(None, ("seq", "head"), None)
    return jax.shard_map(
        on_device,
        mesh=mesh,
        in_specs=(
            rows, P(None, "seq"), rows, P("seq", None), P("seq", None),
            P("seq", None, "head"), P("seq", "head"), P(), P(), P(), P(), P(), P(),
        ),
        out_specs=(
            rows, rows, P(("seq", "head"), None), P(("seq", "head"), None),
            P("seq", None, "head"), P("seq", "head"), P(), P(), P(), P(), P(), P(),
        ),
        check_vma=False,
    )
```

```python
import functools

import jax
import jax.numpy as jnp
from jax import lax
from jax.experimental import pallas as pl
from jax.experimental.pallas import tpu as pltpu
from jax.sharding import PartitionSpec as P

HIGHEST = lax.Precision.HIGHEST
GATE_NORM = 16.0
BF16 = jnp.bfloat16
F32 = jnp.float32


def mm(a, b, contract, precision=HIGHEST):
    return lax.dot_general(
        a, b, ((contract[:1], contract[1:]), ((), ())),
        precision=precision, preferred_element_type=F32,
    )


def lower_ones(size):
    rows = lax.broadcasted_iota(jnp.int32, (size, size), 0)
    cols = lax.broadcasted_iota(jnp.int32, (size, size), 1)
    return rows >= cols


def running(decay_low):
    ones = lower_ones(decay_low.shape[0]).astype(F32).astype(BF16)
    return mm(ones, decay_low, (1, 0), None)


def sigmoid(x):
    return 1.0 / (1.0 + jnp.exp(-x))


def state_kernel(flags, qkv, decay, out, state, total_run):
    m, b = pl.program_id(0), pl.program_id(1)
    last = pl.num_programs(1) - 1
    dk = decay.shape[-1]
    keys, values = qkv[0, 0, :, dk : 2 * dk].astype(F32), qkv[0, 0, :, 2 * dk :].astype(F32)
    keep = 1.0 - flags[m, b].astype(F32)

    @pl.when(b == 0)
    def _():
        state[...] = jnp.zeros_like(state)
        total_run[0:1, :] = jnp.zeros((1, dk), F32)
        total_run[1:2, :] = jnp.ones((1, dk), F32)

    run = running(decay[0, 0])
    total = run[-1:, :]
    carried = keys * jnp.exp(total - run)
    state[...] = jnp.exp(total) * (state[...] * keep) + mm(values, carried, (0, 0))
    total_run[0:1, :] += total
    total_run[1:2, :] *= keep

    @pl.when(b == last)
    def _():
        through = jnp.exp(total_run[0:1, :]) * total_run[1:2, :]
        high = through.astype(BF16)
        low = (through - high.astype(F32)).astype(BF16)
        slices, part = out.shape[0], state.shape[0] // out.shape[0]
        tail = out.shape[2] - part
        at = lax.broadcasted_iota(jnp.int32, (tail, dk), 0)
        extra = jnp.where(
            at == 0, high.astype(F32), jnp.where(at == 1, low.astype(F32), 0.0)
        ).astype(BF16)
        for i in range(slices):
            out[i, 0, :part, :] = state[i * part : (i + 1) * part, :].astype(BF16)
            out[i, 0, part:, :] = extra


def mix_kernel(flags, qkv, decay, og, before, gain, o_out, gated, kept, state):
    m, b = pl.program_id(0), pl.program_id(1)
    dk, dv = decay.shape[-1], og.shape[-1]
    q = qkv[0, 0, :, :dk].astype(F32)
    k = qkv[0, 0, :, dk : 2 * dk].astype(F32)
    v = qkv[0, 0, :, 2 * dk :].astype(F32)
    keep = 1.0 - flags[m, b].astype(F32)

    @pl.when(b == 0)
    def _():
        state[...] = before[:, 0].astype(F32).reshape(dv, dk)

    entry = state[...] * keep
    kept[0, 0] = entry
    run = running(decay[0, 0])
    total = run[-1:, :]
    queried = q * jnp.exp(run) * dk ** (-0.5)
    scores = mm(queried, k * jnp.exp(-run), (1, 1))
    scores = jnp.where(lower_ones(scores.shape[0]), scores, 0.0)
    o = mm(scores, v, (1, 0)) + mm(queried, entry, (1, 1))
    state[...] = jnp.exp(total) * entry + mm(v, k * jnp.exp(total - run), (0, 0))
    o_out[0, 0] = o
    scale = lax.rsqrt(jnp.mean(o * o, axis=-1, keepdims=True) + 1e-5)
    normed = (o * scale * gain[...]).astype(BF16).astype(F32)
    gate = og[0, 0]
    gated[0, 0] = (normed * gate * sigmoid(gate)).astype(BF16)


def params(limit=48):
    return pltpu.CompilerParams(
        dimension_semantics=("arbitrary", "arbitrary"), vmem_limit_bytes=limit << 20
    )


def cost(micros):
    return pl.CostEstimate(flops=0, bytes_accessed=int(micros * 3.0e6), transcendentals=0)


def per_block(rows, width):
    return pl.BlockSpec((1, 1, rows, width), lambda m, b, *_: (b, m, 0, 0))


def per_batch(slices, rows, width):
    return pl.BlockSpec((slices, 1, rows, width), lambda m, b, *_: (0, m, 0, 0))


def states_of(flags, qkv, decays, dv, slices, pad):
    blocks, micro, rows, width = qkv.shape
    dk = decays.shape[-1]
    part = dv // slices
    return pl.pallas_call(
        state_kernel,
        out_shape=jax.ShapeDtypeStruct((slices, micro, part + pad, dk), BF16),
        grid_spec=pltpu.PrefetchScalarGridSpec(
            num_scalar_prefetch=1,
            grid=(micro, blocks),
            in_specs=[per_block(rows, width), per_block(rows, dk)],
            out_specs=per_batch(slices, part + pad, dk),
            scratch_shapes=[pltpu.VMEM((dv, dk), F32), pltpu.VMEM((8, dk), F32)],
        ),
        compiler_params=params(),
        cost_estimate=cost(10),
        name="states",
    )(flags, qkv, decays)


def mix_of(flags, qkv, decays, og, before, gain):
    blocks, micro, rows, width = qkv.shape
    dk, dv = decays.shape[-1], og.shape[-1]
    slices, _, part, _ = before.shape
    return pl.pallas_call(
        mix_kernel,
        out_shape=(
            jax.ShapeDtypeStruct((blocks, micro, rows, dv), F32),
            jax.ShapeDtypeStruct((blocks, micro, rows, dv), BF16),
            jax.ShapeDtypeStruct((blocks, micro, dv, dk), F32),
        ),
        grid_spec=pltpu.PrefetchScalarGridSpec(
            num_scalar_prefetch=1,
            grid=(micro, blocks),
            in_specs=[
                per_block(rows, width),
                per_block(rows, dk),
                per_block(rows, dv),
                per_batch(slices, part, dk),
                pl.BlockSpec((1, dv), lambda m, b, *_: (0, 0)),
            ],
            out_specs=(per_block(rows, dv), per_block(rows, dv), per_block(dv, dk)),
            scratch_shapes=[pltpu.VMEM((dv, dk), F32)],
        ),
        compiler_params=params(),
        cost_estimate=cost(18),
        name="mix",
    )(flags, qkv, decays, og, before, gain)


def greet(axes):
    barrier = pltpu.get_barrier_semaphore()
    met = 0
    for axis in axes:
        me, count = lax.axis_index(axis), lax.axis_size(axis)
        for hop in range(1, count):
            pl.semaphore_signal(
                barrier, inc=1, device_id={axis: lax.rem(me + hop, count)},
                device_id_type=pl.DeviceIdType.MESH,
            )
        met += count - 1
    pl.semaphore_wait(barrier, met)


def push(src, dst, send, recv, to, axis="head"):
    return pltpu.make_async_remote_copy(
        src_ref=src, dst_ref=dst, send_sem=send, recv_sem=recv,
        device_id={axis: to}, device_id_type=pl.DeviceIdType.MESH,
    )


def near_order(z, count, i):
    both = jnp.minimum(z, count - 1 - z)
    left = z > count - 1 - z
    paired = jnp.where(i % 2 == 1, z - (i + 1) // 2, z + i // 2)
    single = jnp.where(left, z - (i - both), z + (i - both))
    return jnp.where(i <= 2 * both, paired, single)


class Line:
    def __init__(self, own, all_rows, send, recv):
        self.own, self.all, self.send, self.recv = own, all_rows, send, recv
        self.z, self.count, self.rows = lax.axis_index("head"), lax.axis_size("head"), own.shape[0]
        z, count = self.z, self.count
        self.right = push(own, self.at(z), send.at[0], recv.at[z], lax.rem(z + 1, count))
        self.left = push(own, self.at(z), send.at[1], recv.at[z], lax.rem(z + count - 1, count))

    def chunk(self, b):
        return pl.ds(pl.multiple_of(b * self.rows, self.rows), self.rows)

    def at(self, b):
        return self.all.at[self.chunk(b)]

    def start(self):
        pl.when(self.z < self.count - 1)(self.right.start)
        pl.when(self.z > 0)(self.left.start)

    def passing(self, i, b):
        z, count = self.z, self.count
        to = jnp.where(b < z, z + 1, z - 1)
        going = ((b < z) & (z < count - 1)) | ((b > z) & (z > 0))
        copy = push(
            self.at(b), self.at(b), self.send.at[i + 1], self.recv.at[b], lax.rem(to + count, count)
        )
        return copy, going

    def receive(self, i, b):
        copy, going = self.passing(i, b)
        copy.wait_recv()
        pl.when(going)(copy.start)

    def finish(self):
        def sent(i, _):
            copy, going = self.passing(i, near_order(self.z, self.count, i))
            pl.when(going)(copy.wait_send)
            return 0

        lax.fori_loop(1, self.count, sent, 0)
        pl.when(self.z < self.count - 1)(self.right.wait_send)
        pl.when(self.z > 0)(self.left.wait_send)


class LineSum:
    def __init__(self, parts, landed, send, recv, rows):
        self.parts, self.landed, self.send, self.recv = parts, landed, send, recv
        self.z, self.count = lax.axis_index("head"), lax.axis_size("head")
        self.rows, self.pieces = rows, send.shape[1]
        self.deep = rows // self.pieces
        self.inner = (self.z > 0) & (self.z < self.count - 1)
        self.far_end = jnp.where(self.z < self.count - 1 - self.z, self.count - 1, 0)

    def piece(self, b, p):
        return pl.ds(pl.multiple_of(b * self.rows + p * self.deep, self.deep), self.deep)

    def onward(self, b, p):
        z, count = self.z, self.count
        to = jnp.where(b > z, z + 1, z - 1)
        slot = jnp.where((to == b) & (z > b), count, b)
        return push(
            self.parts.at[self.piece(b, p)], self.landed.at[self.piece(slot, p)],
            self.send.at[b, p], self.recv.at[slot, p], lax.rem(to + count, count),
        )

    def send_all(self):
        @pl.when(jnp.logical_not(self.inner))
        def _():
            for i in range(1, self.count):
                b = jnp.where(self.z == 0, self.count - i, i - 1)
                for p in range(self.pieces):
                    self.onward(b, p).start()

    def arrived(self, slot, p):
        at = self.piece(slot, p)
        push(
            self.landed.at[at], self.landed.at[at], self.send.at[0, p], self.recv.at[slot, p],
            lax.rem(self.z + 1, self.count),
        ).wait_recv()
        return self.landed[at, :].astype(F32)

    def relay(self, b, p):
        at = self.piece(b, p)
        self.parts[at, :] = (self.parts[at, :].astype(F32) + self.arrived(b, p)).astype(BF16)
        self.onward(b, p).start()

    def relay_in_turn(self, j):
        pieces = self.pieces

        @pl.when(self.inner & (j < pieces))
        def _():
            self.relay(self.count - 1 - self.z, j)

        @pl.when(self.inner & (j >= pieces))
        def _():
            self.relay(self.far_end, j - pieces)

        @pl.when(self.inner & (j > pieces))
        def _():
            self.relay(self.count - 1 - self.far_end, j - pieces - 1)

    def relay_last(self):
        @pl.when(self.inner)
        def _():
            self.relay(self.count - 1 - self.far_end, self.pieces - 1)

    def result(self, out):
        z, count = self.z, self.count
        for p in range(self.pieces):
            here = pl.ds(p * self.deep, self.deep)
            out[here, :] = self.parts[self.piece(z, p), :].astype(F32)

            @pl.when(z > 0)
            def _():
                out[here, :] += self.arrived(z, p)

            @pl.when(z < count - 1)
            def _():
                out[here, :] += self.arrived(count, p)

    def finish(self):
        def sent(i, _):
            b = near_order(self.z, self.count, i)
            for p in range(self.pieces):
                self.onward(b, p).wait_send()
            return 0

        lax.fori_loop(1, self.count, sent, 0)


class PairSum:
    def __init__(self, mine, paired, peers, pair_send, pair_recv, peer_send, peer_recv):
        self.mine, self.paired, self.peers = mine, paired, peers
        self.sems = pair_send, pair_recv, peer_send, peer_recv
        self.s, self.seq = lax.axis_index("seq"), lax.axis_size("seq")
        self.side, self.pairs, self.own = lax.rem(self.s, 2), self.seq // 2, self.s // 2
        self.deep = mine.shape[1]

    def block(self, k, other=False):
        i = 2 * k + (1 - self.side if other else self.side)
        return pl.ds(pl.multiple_of(i * self.deep, self.deep), self.deep)

    def to_partner(self, src, k):
        return push(
            src, self.paired.at[k], self.sems[0].at[k], self.sems[1].at[k],
            self.s + 1 - 2 * self.side, "seq",
        )

    def to_peer(self, k):
        return push(
            self.mine.at[k], self.peers.at[self.own], self.sems[2].at[k], self.sems[3].at[self.own],
            2 * k + self.side, "seq",
        )

    def pass_on(self, k):
        pl.when(self.own != k)(self.to_peer(k).start)

    def collect(self, out):
        self.peers[self.own] = self.mine[self.own]
        for k in range(self.pairs):
            copy = push(
                self.mine.at[k], self.peers.at[k], self.sems[2].at[k], self.sems[3].at[k],
                lax.rem(self.s + 1, self.seq), "seq",
            )
            pl.when(self.own != k)(copy.wait_recv)
        band = 16

        def add_rows(r, _):
            at = pl.ds(pl.multiple_of(r * band, band), band)
            out[at, :] = jnp.sum(self.peers[:, at, :].astype(F32), axis=0).astype(out.dtype)
            return 0

        lax.fori_loop(0, self.deep // band, add_rows, 0)

    def finish(self, src):
        for k in range(self.pairs):
            self.to_partner(src(k), k).wait_send()
            pl.when(self.own != k)(self.to_peer(k).wait_send)


def gather_norm_kernel(own, gain, normed, rows_all, here_sem, send, recv):
    z, count, rows = lax.axis_index("head"), lax.axis_size("head"), own.shape[0]
    greet(("head",))
    line = Line(own, rows_all, send, recv)
    line.start()
    here = pltpu.make_async_copy(own, line.at(z), here_sem)
    here.start()
    here.wait()
    band = 16

    def step(i, _):
        b = near_order(z, count, i)
        pl.when(i > 0)(lambda: line.receive(i, b))

        def norm(r, _):
            at = pl.ds(pl.multiple_of(b * rows + r * band, band), band)
            x = rows_all[at, :].astype(F32)
            inv = lax.rsqrt(jnp.mean(x * x, axis=-1, keepdims=True) + 1e-6)
            normed[at, :] = (x * inv * gain[...]).astype(BF16)
            return 0

        lax.fori_loop(0, rows // band, norm, 0)
        return 0

    lax.fori_loop(0, count, step, 0)
    line.finish()


def gather_norm(x, gain):
    rows, width = x.shape
    count = lax.axis_size("head")
    vmem = pl.BlockSpec(memory_space=pltpu.VMEM)
    dma = pltpu.SemaphoreType.DMA
    return pl.pallas_call(
        gather_norm_kernel,
        out_shape=jax.ShapeDtypeStruct((count * rows, width), BF16),
        in_specs=[vmem, vmem],
        out_specs=vmem,
        scratch_shapes=[
            pltpu.VMEM((count * rows, width), BF16), dma(()), dma((count + 1,)), dma((count,)),
        ],
        compiler_params=pltpu.CompilerParams(
            collective_id=1, has_side_effects=True, vmem_limit_bytes=32 << 20
        ),
        cost_estimate=cost(50),
        name="gather_norm",
    )(x, gain)


def swap_slices(own, got, send, recv):
    me, count = lax.axis_index("seq"), lax.axis_size("seq")

    def copy(hop, index):
        to = lax.rem(me + hop, count)
        return push(own.at[to], got.at[index], send.at[hop], recv.at[index], to, "seq")

    def start(hop, _):
        copy(hop, me).start()
        return 0

    def wait_recv(hop, _):
        copy(hop, lax.rem(me + hop, count)).wait_recv()
        return 0

    def wait_send(hop, _):
        copy(hop, me).wait_send()
        return 0

    def begin():
        lax.fori_loop(1, count, start, 0)
        got[me] = own[me]

    def end():
        lax.fori_loop(1, count, wait_recv, 0)

    def drain():
        lax.fori_loop(1, count, wait_send, 0)

    return begin, end, drain


def scan_states(reverse, own, through, out):
    count, part = out.shape[0], out.shape[2]

    def step(k, state):
        j = count - 1 - k if reverse else k
        out[j] = state.astype(BF16)
        decay = through[j, :, 0:1, :].astype(F32) + through[j, :, 1:2, :].astype(F32)
        return decay * state + own[j, :, :part, :].astype(F32)

    lax.fori_loop(0, count, step, jnp.zeros(out.shape[1:], F32))


def enter_kernel(own, rows_own, before, through, rows_all,
                 got, scanned, send, recv, send_back, recv_back, here_sem, go, come):
    z, count = lax.axis_index("head"), lax.axis_size("head")
    part = scanned.shape[2]
    greet(("seq", "head"))
    begin, end, drain = swap_slices(own, got, send, recv)
    begin()
    line = Line(rows_own, rows_all, go, come)
    line.start()
    here = pltpu.make_async_copy(rows_own, line.at(z), here_sem)
    here.start()
    end()
    through[...] = got[:, :, part:, :]
    scan_states(False, got, through, scanned)
    begin_back, end_back, drain_back = swap_slices(scanned, before, send_back, recv_back)
    begin_back()

    def step(i, _):
        line.receive(i, near_order(z, count, i))
        return 0

    lax.fori_loop(1, count, step, 0)
    end_back()
    here.wait()
    line.finish()
    drain()
    drain_back()


def enter(own, rows_own, part):
    slices, micro, deep, dk = own.shape
    rows, width = rows_own.shape
    count = lax.axis_size("head")
    vmem, anywhere = pl.BlockSpec(memory_space=pltpu.VMEM), pl.BlockSpec(memory_space=pl.ANY)
    dma = pltpu.SemaphoreType.DMA
    return pl.pallas_call(
        enter_kernel,
        out_shape=(
            jax.ShapeDtypeStruct((slices, micro, part, dk), BF16),
            jax.ShapeDtypeStruct((slices, micro, deep - part, dk), BF16),
            jax.ShapeDtypeStruct((count * rows, width), BF16),
        ),
        in_specs=[vmem, anywhere],
        out_specs=(vmem, vmem, anywhere),
        scratch_shapes=[
            pltpu.VMEM(own.shape, BF16), pltpu.VMEM((slices, micro, part, dk), BF16),
            dma((slices,)), dma((slices,)), dma((slices,)), dma((slices,)),
            dma(()), dma((count + 1,)), dma((count,)),
        ],
        compiler_params=pltpu.CompilerParams(
            collective_id=2, has_side_effects=True, vmem_limit_bytes=32 << 20
        ),
        cost_estimate=cost(50),
        name="enter",
    )(own, rows_own)


def total_kernel(own, out, from_seq, part, from_head, send_a, recv_a, send_b, recv_b,
                 send_c, recv_c, send_d, recv_d):
    seq, head = lax.axis_size("seq"), lax.axis_size("head")
    s, h = lax.axis_index("seq"), lax.axis_index("head")
    greet(("seq", "head"))

    def each(axis, me, count, src, dst, send, recv):
        def copy(hop, index):
            to = lax.rem(me + hop, count)
            return push(src(to), dst(index), send.at[hop], recv.at[index], to, axis)

        for hop in range(1, count):
            copy(hop, me).start()
        for hop in range(1, count):
            copy(hop, lax.rem(me + hop, count)).wait_recv()
        return [copy(hop, me).wait_send for hop in range(1, count)]

    from_seq[s] = own[s]
    sent = each("seq", s, seq, lambda to: own.at[to], lambda i: from_seq.at[i], send_a, recv_a)
    part[...] = jnp.sum(from_seq[...], axis=0)
    from_head[h] = part[h]
    sent += each("head", h, head, lambda to: part.at[to], lambda i: from_head.at[i], send_b, recv_b)
    out[s, h] = jnp.sum(from_head[...], axis=0)
    sent += each("head", h, head, lambda _: out.at[s, h], lambda i: out.at[s, i], send_c, recv_c)
    sent += each("seq", s, seq, lambda _: out.at[s], lambda i: out.at[i], send_d, recv_d)
    for wait in sent:
        wait()


def total_of(parts):
    seq, head = lax.axis_size("seq"), lax.axis_size("head")
    flat = jnp.concatenate([p.reshape(-1) for p in parts])
    deep = -(-flat.shape[0] // (seq * head * 1024)) * 8
    flat = jnp.pad(flat, (0, seq * head * deep * 128 - flat.shape[0]))
    vmem = pl.BlockSpec(memory_space=pltpu.VMEM)
    dma = pltpu.SemaphoreType.DMA
    shape = (seq, head, deep, 128)
    whole = pl.pallas_call(
        total_kernel,
        out_shape=jax.ShapeDtypeStruct(shape, F32),
        in_specs=[vmem],
        out_specs=vmem,
        scratch_shapes=[
            pltpu.VMEM(shape, F32), pltpu.VMEM(shape[1:], F32), pltpu.VMEM(shape[1:], F32),
        ]
        + [dma((n,)) for n in (seq, seq, head, head, head, head, seq, seq)],
        compiler_params=pltpu.CompilerParams(collective_id=4, has_side_effects=True),
        cost_estimate=cost(15),
        name="total",
    )(flat.reshape(shape)).reshape(-1)
    result, at = [], 0
    for p in parts:
        result.append(whole[at : at + p.size].reshape(p.shape))
        at += p.size
    return result


def ffn_kernel(count, x_own, c_all, w, g_x, f_parts, grad,
               wv, xs, cs, act, lin, parts, landed, turned, turned_c, tiles,
               w_sem, own_sem, go_sem, x_sem, p_sem, q_sem, o_sem):
    z = lax.axis_index("head")
    rows, width = x_own.shape
    hidden = act.shape[1] // 3
    chunk = lambda b: pl.ds(pl.multiple_of(b * rows, rows), rows)

    weights = [
        pltpu.make_async_copy(
            w.at[:, pl.ds(k * hidden, hidden)], wv.at[:, pl.ds(k * hidden, hidden)], w_sem.at[k]
        )
        for k in range(3)
    ]
    own = [
        pltpu.make_async_copy(x_own, xs.at[chunk(z)], own_sem.at[0]),
        pltpu.make_async_copy(c_all, cs, own_sem.at[1]),
    ]
    for copy in own + weights:
        copy.start()
    greet(("head",))
    line = Line(x_own, xs, go_sem, x_sem)
    line.start()
    for copy in own + weights:
        copy.wait()

    total = LineSum(parts, landed, p_sem, q_sem, rows)

    def step(i, _):
        b = near_order(z, count, i)

        pl.when(i > 0)(lambda: line.receive(i, b))

        at = chunk(b)
        x = xs[at, :]
        lin[0] = jnp.dot(x, wv[:, :hidden], preferred_element_type=F32)
        lin[1] = jnp.dot(x, wv[:, hidden : 2 * hidden], preferred_element_type=F32)
        lin[2] = jnp.dot(cs[at, :], wv[:, 2 * hidden :], preferred_element_type=F32)
        band = 16

        def act_rows(r, _):
            here = pl.ds(pl.multiple_of(r * band, band), band)
            there = pl.ds(pl.multiple_of(b * rows + r * band, band), band)
            gate, up, g_product = lin[0, here, :], lin[1, here, :], lin[2, here, :]
            sig = sigmoid(gate)
            gated = gate * sig
            act[there, :hidden] = (g_product * up * sig * (1.0 + gate * (1.0 - sig))).astype(BF16)
            act[there, hidden : 2 * hidden] = (g_product * gated).astype(BF16)
            act[there, 2 * hidden :] = (gated * up).astype(BF16)
            return 0

        lax.fori_loop(0, rows // band, act_rows, 0)
        parts[at, :] = mm(act[at, : 2 * hidden], wv[:, : 2 * hidden], (1, 1), None).astype(BF16)

        @pl.when((i > 0) & jnp.logical_not(total.inner))
        def _():
            for p in range(total.pieces):
                total.onward(b, p).start()

        return 0

    lax.fori_loop(0, count, step, 0)

    high = tiles.shape[1]
    steps = width // high

    def store(t, r, k):
        down = pl.ds(pl.multiple_of(r * high, high), high)
        into = grad.at[down, pl.ds(k * hidden, hidden)]
        return pltpu.make_async_copy(tiles.at[lax.rem(t, 2)], into, o_sem.at[lax.rem(t, 2)])

    turned[...] = xs[...].T
    turned_c[...] = cs[...].T

    def tile(r, k):
        t = 3 * r + k

        @pl.when(t >= 2)
        def _():
            store(t, r, k).wait()

        left_rows = (turned_c if k == 2 else turned)[
            pl.ds(pl.multiple_of(r * high, high), high), :
        ]
        tiles[lax.rem(t, 2)] = jnp.dot(
            left_rows, act[:, k * hidden : (k + 1) * hidden], preferred_element_type=F32
        ).astype(BF16)
        store(t, r, k).start()

    def slab(r, _):
        tile(r, 0)
        tile(r, 1)
        total.relay_in_turn(2 * r)
        tile(r, 2)
        at = chunk(r)
        f_parts[r] = mm(act[at, 2 * hidden :], wv[:, 2 * hidden :], (1, 1), None).astype(BF16)
        total.relay_in_turn(2 * r + 1)
        return 0

    lax.fori_loop(0, steps, slab, 0)
    total.relay_last()
    total.result(g_x)
    total.finish()
    line.finish()
    store(3 * steps - 2, 0, 0).wait()
    store(3 * steps - 1, 0, 0).wait()


def feed_forward(x_own, c_all, w, hidden, count):
    rows, width = x_own.shape
    group = rows * count
    assert count == 4 and width % 4 == 0 and rows % 64 == 0
    anywhere = pl.BlockSpec(memory_space=pl.ANY)
    vmem = pl.BlockSpec(memory_space=pltpu.VMEM)
    dma = pltpu.SemaphoreType.DMA
    return pl.pallas_call(
        functools.partial(ffn_kernel, count),
        out_shape=(
            jax.ShapeDtypeStruct((rows, width), F32),
            jax.ShapeDtypeStruct((count, rows, width), BF16),
            jax.ShapeDtypeStruct((width, 3 * hidden), BF16),
        ),
        in_specs=[anywhere] * 3,
        out_specs=(vmem, vmem, anywhere),
        scratch_shapes=[
            pltpu.VMEM((width, 3 * hidden), BF16),
            pltpu.VMEM((group, width), BF16),
            pltpu.VMEM((group, width), BF16),
            pltpu.VMEM((group, 3 * hidden), BF16),
            pltpu.VMEM((3, rows, hidden), F32),
            pltpu.VMEM((group, width), BF16),
            pltpu.VMEM((group + rows, width), BF16),
            pltpu.VMEM((width, group), BF16),
            pltpu.VMEM((width, group), BF16),
            pltpu.VMEM((2, width // 4, hidden), BF16),
            dma((3,)), dma((2,)), dma((count + 1,)), dma((count,)),
            dma((count, 4)), dma((count + 1, 4)), dma((2,)),
        ],
        compiler_params=pltpu.CompilerParams(
            collective_id=0, has_side_effects=True, vmem_limit_bytes=60 << 20
        ),
        cost_estimate=cost(100),
        name="feed_forward",
    )(x_own, c_all, w)


def split(x):
    high = x.astype(BF16)
    return high, (x - high.astype(F32)).astype(BF16)


def mms(left, right, contract):
    total = mm(left[0], right[0], contract, None)
    if len(right) > 1:
        total += mm(left[0], right[1], contract, None)
    if len(left) > 1:
        total += mm(left[1], right[0], contract, None)
    return total


def back_kernel(keep, gated_own, og, o_in, qkv, decay, logits, through, gain, left, right,
                kept_in, parts_in, g_proj, g_logits, g_gain, f_out, g_out,
                gated_all, go, runs, g_queried, g_keyed, g_values, pulls, weights, kept,
                parts, landed, state, sending, got, scanned, after, turned, tiles, in_sem, t_sem,
                z_send, z_recv, s_send, s_recv, b_send, b_recv, p_sem, q_sem):
    h, head = lax.axis_index("head"), lax.axis_size("head")
    count, micro, rows, dk = decay.shape
    dv = og.shape[-1]
    width = qkv.shape[-1]
    slices, part = sending.shape[0], sending.shape[2]
    scale = dk ** (-0.5)
    loads = [
        pltpu.make_async_copy(parts_in, parts, in_sem.at[0]),
        pltpu.make_async_copy(kept_in, kept, in_sem.at[1]),
    ]
    for load in loads:
        load.start()
    greet(("seq", "head"))

    def to_head(hop, slot):
        to = lax.rem(h + hop, head)
        columns = gated_own.at[:, pl.ds(pl.multiple_of(to * dv, dv), dv)]
        return push(columns, gated_all.at[slot], z_send.at[hop], z_recv.at[slot], to)

    for hop in range(1, head):
        to_head(hop, h).start()
    gated_all[h] = gated_own[:, pl.ds(pl.multiple_of(h * dv, dv), dv)]

    causal = lower_ones(rows)
    before = [jnp.zeros((1, dk), F32)] * micro
    alive = [jnp.ones((1, dk), F32)] * micro
    for b in range(count):
        for m in range(micro):
            run = running(decay[b, m])
            runs[b, m] = run
            alive[m] = alive[m] * keep[b, m]
            weights[b, m] = jnp.exp(before[m]) * alive[m]
            before[m] = before[m] + run[rows - 1 : rows, :]
    g_gain[...] = jnp.zeros_like(g_gain)
    state[...] = jnp.zeros_like(state)

    turned[...] = left[...].T
    high, wide = tiles.shape[1:]
    across_tiles = g_out.shape[1] // wide

    def store(t):
        at = pl.ds(pl.multiple_of((t // across_tiles) * high, high), high)
        columns = pl.ds(pl.multiple_of(lax.rem(t, across_tiles) * wide, wide), wide)
        return pltpu.make_async_copy(
            tiles.at[lax.rem(t, 2)], g_out.at[at, columns], t_sem.at[lax.rem(t, 2)]
        )

    def tile(t, _):
        @pl.when(t >= 2)
        def _():
            store(t - 2).wait()

        at = pl.ds(pl.multiple_of((t // across_tiles) * high, high), high)
        columns = pl.ds(pl.multiple_of(lax.rem(t, across_tiles) * wide, wide), wide)
        tiles[lax.rem(t, 2)] = jnp.dot(
            turned[at, :], right[:, columns], preferred_element_type=F32
        ).astype(BF16)
        store(t).start()
        return 0

    tile_count = (g_out.shape[0] // high) * across_tiles
    lax.fori_loop(0, tile_count, tile, 0)

    def gates(i, _):
        b = near_order(h, head, i)
        pl.when(i > 0)(lambda: to_head(lax.rem(b - h + head, head), b).wait_recv())
        for m in range(micro):
            gate, o = og[b, m], o_in[b, m]
            grad = gated_all[b, m * rows : (m + 1) * rows, :].astype(F32)
            sig = sigmoid(gate)
            inv = lax.rsqrt(jnp.mean(o * o, axis=-1, keepdims=True) + 1e-5)
            plain = o * inv
            normed = (plain * gain[...]).astype(BF16).astype(F32)
            g_on = (grad * gate * sig).astype(BF16).astype(F32)
            g_proj[b, m, :, width:] = (
                grad * normed * sig * (1.0 + gate * (1.0 - sig))
            ).astype(BF16)
            scaled = g_on * gain[...]
            g_o = inv * (scaled - plain * jnp.mean(scaled * plain, axis=-1, keepdims=True))
            go[b, m] = g_o
            g_gain[0:1, :] += jnp.sum(g_on * plain, axis=0, keepdims=True)
            queried = qkv[b, m, :, :dk].astype(F32) * (jnp.exp(runs[b, m]) * scale)
            pull = mms(split(g_o), split(queried), (0, 0))
            pulls[b, m] = pull
            state[m] += pull * weights[b, m]
        return 0

    lax.fori_loop(0, head, gates, 0)
    for i in range(slices):
        sending[i] = state[:, i * part : (i + 1) * part, :].astype(BF16)
    begin, end, drain = swap_slices(sending, got, s_send, s_recv)
    begin()
    for load in loads:
        load.wait()
    total = LineSum(parts, landed, p_sem, q_sem, f_out.shape[0])
    total.send_all()

    def inside(b, _):
        for m in range(micro):
            q = qkv[b, m, :, :dk].astype(F32)
            k = qkv[b, m, :, dk : 2 * dk].astype(F32)
            v = (qkv[b, m, :, 2 * dk :],)
            run = runs[b, m]
            queried, keyed = split(q * (jnp.exp(run) * scale)), split(k * jnp.exp(-run))
            g_o, entry = split(go[b, m]), split(kept[b, m])
            scores = split(jnp.where(causal, mms(queried, keyed, (1, 1)), 0.0))
            g_scores = split(jnp.where(causal, mms(g_o, v, (1, 1)), 0.0))
            g_queried[b, m] = mms(g_scores, keyed, (1, 0)) + mms(g_o, entry, (1, 0))
            g_keyed[b, m] = mms(g_scores, queried, (0, 0))
            g_values[b, m] = mms(scores, g_o, (0, 0))
        pl.when(total.inner)(lambda: total.relay(total.far_end, b))
        return 0

    lax.fori_loop(0, count, inside, 0)
    end()
    scan_states(True, got, through, scanned)
    begin_back, end_back, drain_back = swap_slices(scanned, after, b_send, b_recv)
    begin_back()

    @pl.when(total.inner)
    def _():
        for p in range(total.pieces):
            total.relay(head - 1 - total.far_end, p)
        for p in range(total.pieces):
            total.relay(head - 1 - h, p)

    end_back()
    for i in range(slices):
        state[:, i * part : (i + 1) * part, :] = after[i].astype(F32)

    def across(step, _):
        b = count - 1 - step
        for m in range(micro):
            q = qkv[b, m, :, :dk].astype(F32)
            k = qkv[b, m, :, dk : 2 * dk].astype(F32)
            v = (qkv[b, m, :, 2 * dk :],)
            run = runs[b, m]
            last = run[rows - 1 : rows, :]
            up, down, rest = jnp.exp(run) * scale, jnp.exp(-run), jnp.exp(last - run)
            decayed = jnp.exp(last)
            gs = state[m]
            gs_parts = split(gs)
            carried = k * rest
            g_v = g_values[b, m] + mms(split(carried), gs_parts, (1, 1))
            g_carried = mms(v, gs_parts, (1, 0))
            from_carried = g_carried * carried
            g_total = jnp.sum(decayed * kept[b, m] * gs, axis=0, keepdims=True) + jnp.sum(
                from_carried, axis=0, keepdims=True
            )
            state[m] = (decayed * gs + pulls[b, m]) * keep[b, m]
            gq, gk = g_queried[b, m], g_keyed[b, m]
            g_run = gq * (q * up) - gk * (k * down) - from_carried
            later = mms((causal.astype(F32).astype(BF16),), split(g_run), (0, 0)) + g_total
            g_proj[b, m, :, :dk] = (gq * up).astype(BF16)
            g_proj[b, m, :, dk : 2 * dk] = (gk * down + g_carried * rest).astype(BF16)
            g_proj[b, m, :, 2 * dk : width] = g_v.astype(BF16)
            g_logits[b, m] = (
                later.astype(BF16).astype(F32) * sigmoid(-logits[b, m]) * (1.0 / GATE_NORM)
            )
        return 0

    lax.fori_loop(0, count, across, 0)
    total.result(f_out)
    total.finish()
    store(tile_count - 2).wait()
    store(tile_count - 1).wait()
    drain()
    drain_back()
    for hop in range(1, head):
        to_head(hop, h).wait_send()


def attention_back(
    keep, gated_own, og, o, qkv, decays, logits, through, gain, left, right, kept, parts
):
    blocks, micro, rows, width = qkv.shape
    dk, dv = decays.shape[-1], og.shape[-1]
    head, seq = lax.axis_size("head"), lax.axis_size("seq")
    own_rows = parts.shape[0] // head
    vmem, anywhere = pl.BlockSpec(memory_space=pltpu.VMEM), pl.BlockSpec(memory_space=pl.ANY)
    dma = pltpu.SemaphoreType.DMA
    blocked = lambda w, kind: pltpu.VMEM((blocks, micro, rows, w), kind)
    states = (seq, micro, dv // seq, dk)
    return pl.pallas_call(
        back_kernel,
        out_shape=(
            jax.ShapeDtypeStruct((blocks, micro, rows, width + dv), BF16),
            jax.ShapeDtypeStruct((blocks, micro, rows, dk), F32),
            jax.ShapeDtypeStruct((8, dv), F32),
            jax.ShapeDtypeStruct((own_rows, parts.shape[1]), F32),
            jax.ShapeDtypeStruct((left.shape[1], right.shape[1]), BF16),
        ),
        in_specs=[vmem] * 11 + [anywhere] * 2,
        out_specs=(vmem,) * 4 + (anywhere,),
        scratch_shapes=[
            pltpu.VMEM((blocks, micro * rows, dv), BF16), blocked(dv, F32), blocked(dk, F32),
            blocked(dk, F32), blocked(dk, F32), blocked(dv, F32),
            pltpu.VMEM((blocks, micro, dv, dk), F32), pltpu.VMEM((blocks, micro, 1, dk), F32),
            pltpu.VMEM((blocks, micro, dv, dk), F32),
            pltpu.VMEM(parts.shape, BF16),
            pltpu.VMEM((parts.shape[0] + own_rows, parts.shape[1]), BF16),
            pltpu.VMEM((micro, dv, dk), F32),
            pltpu.VMEM(states, BF16), pltpu.VMEM(states, BF16), pltpu.VMEM(states, BF16),
            pltpu.VMEM(states, BF16),
            pltpu.VMEM(left.shape[::-1], BF16),
            pltpu.VMEM((2, left.shape[1] // 4, right.shape[1] // 2), BF16),
            dma((2,)), dma((2,)), dma((head,)), dma((head,)), dma((seq,)), dma((seq,)), dma((seq,)),
            dma((seq,)), dma((head, 4)), dma((head + 1, 4)),
        ],
        compiler_params=pltpu.CompilerParams(
            collective_id=3, has_side_effects=True, vmem_limit_bytes=60 << 20
        ),
        cost_estimate=cost(80),
        name="attention_back",
    )(keep, gated_own, og, o, qkv, decays, logits, through, gain, left, right, kept, parts)


def finish_kernel(xn_in, proj_in, w_in, g_logits, ranked, up_own, rank_down,
                  g_x, grad, g_down, g_up, g_bias,
                  turned, proj, w, outgoing, mine, paired, peers, slab, heads_in, parts, landed, slim_high,
                  slim_low, in_sem, pair_send, pair_recv, peer_send, peer_recv, x_send, x_recv,
                  p_sem, q_sem):
    h, head = lax.axis_index("head"), lax.axis_size("head")
    rows, width = g_x.shape
    deep = grad.shape[0] * head
    pairs = lax.axis_size("seq") // 2

    loads = [
        pltpu.make_async_copy(proj_in, proj, in_sem.at[0]),
        pltpu.make_async_copy(w_in, w, in_sem.at[1]),
        pltpu.make_async_copy(xn_in, landed.at[pl.ds(0, xn_in.shape[0])], in_sem.at[2]),
    ]
    for load in loads:
        load.start()
    for load in loads:
        load.wait()
    turned[...] = landed[: xn_in.shape[0], :].T
    greet(("seq", "head"))
    total = LineSum(parts, landed, p_sem, q_sem, rows)
    logit_parts = split(g_logits[...])
    g_ranked = mms(logit_parts, split(up_own[...]), (1, 1))
    slim = split(g_ranked)
    slim_high[...], slim_low[...] = slim

    def chunk(i, _):
        b = near_order(h, head, head - 1 - i)
        at = pl.ds(pl.multiple_of(b * rows, rows), rows)
        rank_part = mms((slim_high[at, :], slim_low[at, :]), (rank_down[...],), (1, 1))
        parts[at, :] = (mm(proj[at, :], w[...], (1, 1), None) + rank_part).astype(BF16)

        @pl.when((b != h) & jnp.logical_not(total.inner))
        def _():
            for p in range(total.pieces):
                total.onward(b, p).start()

        return 0

    lax.fori_loop(0, head, chunk, 0)

    sums = PairSum(mine, paired, peers, pair_send, pair_recv, peer_send, peer_recv)

    def gone(k, _):
        outgoing[k] = jnp.dot(
            turned[sums.block(k, True), :], proj[...], preferred_element_type=F32
        ).astype(BF16)
        sums.to_partner(outgoing.at[k], k).start()
        return 0

    lax.fori_loop(0, pairs, gone, 0)

    def kept(k, _):
        here = jnp.dot(turned[sums.block(k), :], proj[...], preferred_element_type=F32)
        sums.to_partner(outgoing.at[k], k).wait_recv()
        mine[k] = (here + paired[k].astype(F32)).astype(BF16)
        sums.pass_on(k)

        @pl.when(total.inner & (k < total.pieces))
        def _():
            total.relay(total.far_end, k)

        @pl.when(total.inner & (k > 0) & (k <= total.pieces))
        def _():
            total.relay(head - 1 - total.far_end, k - 1)

        return 0

    lax.fori_loop(0, pairs, kept, 0)

    @pl.when(total.inner)
    def _():
        for p in range(pairs, total.pieces + 1):
            if p < total.pieces:
                total.relay(total.far_end, p)
            total.relay(head - 1 - total.far_end, p - 1)
        for p in range(total.pieces):
            total.relay(head - 1 - h, p)

    g_down[...] = mms((turned[...],), slim, (1, 0))
    g_up[...] = mms(split(ranked[...]), logit_parts, (0, 0))
    g_bias[...] = jnp.broadcast_to(jnp.sum(g_logits[...], axis=0, keepdims=True), g_bias.shape)

    sums.collect(slab)
    thin = grad.shape[0]

    def to_head(hop, slot):
        to = lax.rem(h + hop, head)
        return push(
            slab.at[pl.ds(pl.multiple_of(to * thin, thin), thin)], heads_in.at[slot],
            x_send.at[hop], x_recv.at[slot], to,
        )

    for hop in range(1, head):
        to_head(hop, h).start()
    heads_in[h] = slab[pl.ds(pl.multiple_of(h * thin, thin), thin), :]
    total.result(g_x)
    for hop in range(1, head):
        to_head(hop, lax.rem(h + hop, head)).wait_recv()
    dk = g_up.shape[1]
    dv = slab.shape[1] // 2 - dk
    for j in range(head):
        at, start = 0, 0
        for size in (dk, dk, dv, dv):
            grad[:, start + j * size : start + (j + 1) * size] = heads_in[
                j, :, at : at + size
            ].astype(F32)
            at, start = at + size, start + head * size
    sums.finish(lambda k: outgoing.at[k])
    for hop in range(1, head):
        to_head(hop, h).wait_send()
    total.finish()


def finish(xn, g_proj, w_in, g_logits, ranked, up_own, rank_down):
    seq, head = lax.axis_size("seq"), lax.axis_size("head")
    group, width = xn.shape
    columns, rank = w_in.shape[1], ranked.shape[1]
    deep, rows, pairs = width // seq, group // head, seq // 2
    dk = up_own.shape[1]
    vmem, anywhere = pl.BlockSpec(memory_space=pltpu.VMEM), pl.BlockSpec(memory_space=pl.ANY)
    dma = pltpu.SemaphoreType.DMA
    blocks = pltpu.VMEM((pairs, deep, columns), BF16)
    return pl.pallas_call(
        finish_kernel,
        out_shape=(
            jax.ShapeDtypeStruct((rows, width), F32),
            jax.ShapeDtypeStruct((deep // head, columns * head), F32),
            jax.ShapeDtypeStruct((width, rank), F32),
            jax.ShapeDtypeStruct((rank, dk), F32),
            jax.ShapeDtypeStruct((8, dk), F32),
        ),
        in_specs=[anywhere] * 3 + [vmem] * 4,
        out_specs=(vmem,) * 5,
        scratch_shapes=[
            pltpu.VMEM((width, group), BF16), pltpu.VMEM(g_proj.shape, BF16),
            pltpu.VMEM(w_in.shape, BF16), blocks, blocks, blocks, blocks,
            pltpu.VMEM((deep, columns), BF16), pltpu.VMEM((head, deep // head, columns), BF16),
            pltpu.VMEM((group, width), BF16), pltpu.VMEM((group + rows, width), BF16),
            pltpu.VMEM(ranked.shape, BF16), pltpu.VMEM(ranked.shape, BF16),
            dma((3,)), dma((pairs,)), dma((pairs,)), dma((pairs,)), dma((pairs,)),
            dma((head,)), dma((head,)), dma((head, 4)), dma((head + 1, 4)),
        ],
        compiler_params=pltpu.CompilerParams(
            collective_id=5, has_side_effects=True, vmem_limit_bytes=56 << 20
        ),
        cost_estimate=cost(60),
        name="finish",
    )(xn, g_proj, w_in, g_logits, ranked, up_own, rank_down)


def exchange(x, axis):
    return lax.all_to_all(x, axis, split_axis=0, concat_axis=0, tiled=True)


def gather_weight(w):
    return lax.all_gather(w, "seq", axis=0, tiled=True)


def scatter_grad(g):
    return lax.psum_scatter(g.astype(BF16), "seq", scatter_dimension=0, tiled=True)


def dot(a, b, contract, precision=None):
    return lax.dot_general(
        a, b, (((contract[0],), (contract[1],)), ((), ())),
        precision=precision, preferred_element_type=F32,
    )


def rms(x, epsilon):
    return lax.rsqrt(jnp.mean(x * x, axis=-1, keepdims=True) + epsilon)


def norm_back(grad, gain, normed, inv):
    scaled = grad * gain
    inner = jnp.mean(scaled * normed, axis=-1, keepdims=True)
    return inv * (scaled - normed * inner), jnp.sum(grad * normed, axis=0)


def on_device(
    tokens, starts, cotangent, mix_in, mix_out, gate_up, down_proj,
    norm_gain, ffn_gain, head_gain, rank_down, rank_up, gate_bias,
):
    micro, rows, width = tokens.shape
    heads, seq = lax.axis_size("head"), lax.axis_size("seq")
    head = lax.axis_index("head")
    keys, dv = rank_up.shape[1], head_gain.shape[0]
    dk, vals = keys // heads, dv * heads
    hidden_units = down_proj.shape[1]
    group = heads * micro * rows
    proj_width = 2 * dk + 2 * dv

    def own_columns(w, start, size):
        return lax.dynamic_slice_in_dim(w, start + head * size, size, 1)

    w_in = gather_weight(
        jnp.concatenate(
            [
                own_columns(mix_in, 0, dk),
                own_columns(mix_in, keys, dk),
                own_columns(mix_in, 2 * keys, dv),
                own_columns(mix_in, 2 * keys + vals, dv),
            ],
            axis=1,
        )
    )
    later = gather_weight(
        jnp.concatenate(
            [gate_up.reshape(gate_up.shape[0], 2 * hidden_units), down_proj, mix_out], axis=1
        )
    )
    w_out = later[:, 3 * hidden_units :]
    up_own = own_columns(rank_up, 0, dk)
    bias_own = lax.dynamic_slice_in_dim(gate_bias, head * dk, dk, 0)

    xn = gather_norm(tokens.reshape(micro * rows, width), norm_gain.reshape(1, width))
    qkv = dot(xn, w_in[:, : 2 * dk + dv], (1, 0)).astype(BF16)
    og = dot(xn, w_in[:, 2 * dk + dv :], (1, 0))
    ranked = dot(xn, rank_down, (1, 0))
    logits = dot(ranked, up_own, (1, 0), HIGHEST) + bias_own
    decays = (jax.nn.log_sigmoid(logits) / GATE_NORM).astype(BF16)

    def blocks(x):
        return x.reshape(heads, micro, rows, x.shape[-1])

    qkv_b, og_b, decays_b = blocks(qkv), blocks(og), blocks(decays)
    gain_row = head_gain.reshape(1, dv)
    part = dv // seq
    own_states = states_of(starts, qkv_b, decays_b, dv, seq, 16)
    before, through, all_cot = enter(own_states, cotangent.reshape(micro * rows, width), part)
    o_b, gated_b, kept = mix_of(starts, qkv_b, decays_b, og_b, before, gain_row)

    gated = exchange(gated_b, "head")
    gated = gated.transpose(1, 2, 0, 3).reshape(micro * rows, vals)
    source = tokens.astype(F32).reshape(micro * rows, width)
    hidden = source + dot(gated, w_out, (1, 1))
    inv_ffn = rms(hidden, 1e-6)
    plain_ffn = hidden * inv_ffn
    h2 = (plain_ffn * ffn_gain).astype(BF16)

    g_h2, ffn_part, grad_ffn = feed_forward(h2, all_cot, later, hidden_units, heads)
    grad_ffn = scatter_grad(grad_ffn)

    back_ffn, g_ffn_gain = norm_back(g_h2, ffn_gain, plain_ffn, inv_ffn)
    g_hidden = cotangent.astype(F32).reshape(micro * rows, width) + back_ffn
    g_mixed = g_hidden.astype(BF16)
    g_gated = dot(g_mixed, w_out, (1, 0)).astype(BF16)
    keep = 1.0 - jnp.broadcast_to(starts.T[:, :, None, None], (heads, micro, 1, dk)).astype(F32)
    g_proj_b, g_logits_b, g_head_gain, ffn_out, grad_out = attention_back(
        keep, g_gated, og_b, o_b, qkv_b, decays_b, blocks(logits), through, gain_row,
        g_mixed, gated, kept, ffn_part.reshape(group, width),
    )
    grad_out = scatter_grad(grad_out)
    output = (hidden + ffn_out).astype(BF16)
    g_proj, g_logits = g_proj_b.reshape(group, proj_width), g_logits_b.reshape(group, dk)
    g_xn, grad_in, g_rank_down, g_rank_up, g_bias = finish(
        xn, g_proj, w_in, g_logits, ranked, up_own, rank_down
    )
    g_xn, grad_ffn = lax.optimization_barrier((g_xn, grad_ffn))
    inv_in = rms(source, 1e-6)
    back_in, g_norm_gain = norm_back(g_xn, norm_gain, source * inv_in, inv_in)
    input_grad = g_hidden + back_in

    g_rank_up = lax.dynamic_update_slice_in_dim(
        jnp.zeros(rank_up.shape, F32), g_rank_up, head * dk, 1
    )
    g_bias = lax.dynamic_update_slice_in_dim(
        jnp.zeros(gate_bias.shape, F32), g_bias[0], head * dk, 0
    )
    small = total_of(
        [g_norm_gain, g_ffn_gain, g_head_gain[0], g_rank_down, g_rank_up, g_bias]
    )
    slab = width // (seq * heads)
    small, grad_out = lax.optimization_barrier((small, grad_out))
    grad_out = exchange(grad_out.reshape(heads, slab, vals), "head").astype(F32).sum(0)
    return (
        output.reshape(tokens.shape),
        input_grad.reshape(tokens.shape),
        grad_in,
        grad_out,
        grad_ffn[:, : 2 * hidden_units].astype(F32).reshape(-1, 2, hidden_units),
        grad_ffn[:, 2 * hidden_units :].astype(F32),
        *small,
    )


def solution(mesh):
    rows = P(None, ("seq", "head"), None)
    return jax.shard_map(
        on_device,
        mesh=mesh,
        in_specs=(
            rows, P(None, "seq"), rows, P("seq", None), P("seq", None),
            P("seq", None, "head"), P("seq", "head"), P(), P(), P(), P(), P(), P(),
        ),
        out_specs=(
            rows, rows, P(("seq", "head"), None), P(("seq", "head"), None),
            P("seq", None, "head"), P("seq", "head"), P(), P(), P(), P(), P(), P(),
        ),
        check_vma=False,
    )
```

```python
import functools

import jax
import jax.numpy as jnp
from jax import lax
from jax.experimental import pallas as pl
from jax.experimental.pallas import tpu as pltpu
from jax.sharding import PartitionSpec as P

HIGHEST = lax.Precision.HIGHEST
GATE_NORM = 16.0
BF16 = jnp.bfloat16
F32 = jnp.float32


def mm(a, b, contract, precision=HIGHEST):
    return lax.dot_general(
        a, b, ((contract[:1], contract[1:]), ((), ())),
        precision=precision, preferred_element_type=F32,
    )


def lower_ones(size):
    rows = lax.broadcasted_iota(jnp.int32, (size, size), 0)
    cols = lax.broadcasted_iota(jnp.int32, (size, size), 1)
    return rows >= cols


def running(decay_low):
    ones = lower_ones(decay_low.shape[0]).astype(F32).astype(BF16)
    return mm(ones, decay_low, (1, 0), None)


def sigmoid(x):
    return 1.0 / (1.0 + jnp.exp(-x))


def state_kernel(flags, qkv, decay, out, state, total_run):
    m, b = pl.program_id(0), pl.program_id(1)
    last = pl.num_programs(1) - 1
    dk = decay.shape[-1]
    keys, values = qkv[0, 0, :, dk : 2 * dk].astype(F32), qkv[0, 0, :, 2 * dk :].astype(F32)
    keep = 1.0 - flags[m, b].astype(F32)

    @pl.when(b == 0)
    def _():
        state[...] = jnp.zeros_like(state)
        total_run[0:1, :] = jnp.zeros((1, dk), F32)
        total_run[1:2, :] = jnp.ones((1, dk), F32)

    run = running(decay[0, 0])
    total = run[-1:, :]
    carried = keys * jnp.exp(total - run)
    state[...] = jnp.exp(total) * (state[...] * keep) + mm(values, carried, (0, 0))
    total_run[0:1, :] += total
    total_run[1:2, :] *= keep

    @pl.when(b == last)
    def _():
        through = jnp.exp(total_run[0:1, :]) * total_run[1:2, :]
        high = through.astype(BF16)
        low = (through - high.astype(F32)).astype(BF16)
        slices, part = out.shape[0], state.shape[0] // out.shape[0]
        tail = out.shape[2] - part
        at = lax.broadcasted_iota(jnp.int32, (tail, dk), 0)
        extra = jnp.where(
            at == 0, high.astype(F32), jnp.where(at == 1, low.astype(F32), 0.0)
        ).astype(BF16)
        for i in range(slices):
            out[i, 0, :part, :] = state[i * part : (i + 1) * part, :].astype(BF16)
            out[i, 0, part:, :] = extra


def mix_kernel(flags, qkv, decay, og, before, gain, o_out, gated, kept, state):
    m, b = pl.program_id(0), pl.program_id(1)
    dk, dv = decay.shape[-1], og.shape[-1]
    q = qkv[0, 0, :, :dk].astype(F32)
    k = qkv[0, 0, :, dk : 2 * dk].astype(F32)
    v = qkv[0, 0, :, 2 * dk :].astype(F32)
    keep = 1.0 - flags[m, b].astype(F32)

    @pl.when(b == 0)
    def _():
        state[...] = before[:, 0].astype(F32).reshape(dv, dk)

    entry = state[...] * keep
    kept[0, 0] = entry
    run = running(decay[0, 0])
    total = run[-1:, :]
    queried = q * jnp.exp(run) * dk ** (-0.5)
    scores = mm(queried, k * jnp.exp(-run), (1, 1))
    scores = jnp.where(lower_ones(scores.shape[0]), scores, 0.0)
    o = mm(scores, v, (1, 0)) + mm(queried, entry, (1, 1))
    state[...] = jnp.exp(total) * entry + mm(v, k * jnp.exp(total - run), (0, 0))
    o_out[0, 0] = o
    scale = lax.rsqrt(jnp.mean(o * o, axis=-1, keepdims=True) + 1e-5)
    normed = (o * scale * gain[...]).astype(BF16).astype(F32)
    gate = og[0, 0]
    gated[0, 0] = (normed * gate * sigmoid(gate)).astype(BF16)


def params(limit=48):
    return pltpu.CompilerParams(
        dimension_semantics=("arbitrary", "arbitrary"), vmem_limit_bytes=limit << 20
    )


def cost(micros):
    return pl.CostEstimate(flops=0, bytes_accessed=int(micros * 3.0e6), transcendentals=0)


def per_block(rows, width):
    return pl.BlockSpec((1, 1, rows, width), lambda m, b, *_: (b, m, 0, 0))


def per_batch(slices, rows, width):
    return pl.BlockSpec((slices, 1, rows, width), lambda m, b, *_: (0, m, 0, 0))


def states_of(flags, qkv, decays, dv, slices, pad):
    blocks, micro, rows, width = qkv.shape
    dk = decays.shape[-1]
    part = dv // slices
    return pl.pallas_call(
        state_kernel,
        out_shape=jax.ShapeDtypeStruct((slices, micro, part + pad, dk), BF16),
        grid_spec=pltpu.PrefetchScalarGridSpec(
            num_scalar_prefetch=1,
            grid=(micro, blocks),
            in_specs=[per_block(rows, width), per_block(rows, dk)],
            out_specs=per_batch(slices, part + pad, dk),
            scratch_shapes=[pltpu.VMEM((dv, dk), F32), pltpu.VMEM((8, dk), F32)],
        ),
        compiler_params=params(),
        cost_estimate=cost(10),
        name="states",
    )(flags, qkv, decays)


def mix_of(flags, qkv, decays, og, before, gain):
    blocks, micro, rows, width = qkv.shape
    dk, dv = decays.shape[-1], og.shape[-1]
    slices, _, part, _ = before.shape
    return pl.pallas_call(
        mix_kernel,
        out_shape=(
            jax.ShapeDtypeStruct((blocks, micro, rows, dv), F32),
            jax.ShapeDtypeStruct((blocks, micro, rows, dv), BF16),
            jax.ShapeDtypeStruct((blocks, micro, dv, dk), F32),
        ),
        grid_spec=pltpu.PrefetchScalarGridSpec(
            num_scalar_prefetch=1,
            grid=(micro, blocks),
            in_specs=[
                per_block(rows, width),
                per_block(rows, dk),
                per_block(rows, dv),
                per_batch(slices, part, dk),
                pl.BlockSpec((1, dv), lambda m, b, *_: (0, 0)),
            ],
            out_specs=(per_block(rows, dv), per_block(rows, dv), per_block(dv, dk)),
            scratch_shapes=[pltpu.VMEM((dv, dk), F32)],
        ),
        compiler_params=params(),
        cost_estimate=cost(18),
        name="mix",
    )(flags, qkv, decays, og, before, gain)


def greet(axes):
    barrier = pltpu.get_barrier_semaphore()
    met = 0
    for axis in axes:
        me, count = lax.axis_index(axis), lax.axis_size(axis)
        for hop in range(1, count):
            pl.semaphore_signal(
                barrier, inc=1, device_id={axis: lax.rem(me + hop, count)},
                device_id_type=pl.DeviceIdType.MESH,
            )
        met += count - 1
    pl.semaphore_wait(barrier, met)


def push(src, dst, send, recv, to, axis="head"):
    return pltpu.make_async_remote_copy(
        src_ref=src, dst_ref=dst, send_sem=send, recv_sem=recv,
        device_id={axis: to}, device_id_type=pl.DeviceIdType.MESH,
    )


def near_order(z, count, i):
    both = jnp.minimum(z, count - 1 - z)
    left = z > count - 1 - z
    paired = jnp.where(i % 2 == 1, z - (i + 1) // 2, z + i // 2)
    single = jnp.where(left, z - (i - both), z + (i - both))
    return jnp.where(i <= 2 * both, paired, single)


class Line:
    def __init__(self, own, all_rows, send, recv):
        self.own, self.all, self.send, self.recv = own, all_rows, send, recv
        self.z, self.count, self.rows = lax.axis_index("head"), lax.axis_size("head"), own.shape[0]
        z, count = self.z, self.count
        self.right = push(own, self.at(z), send.at[0], recv.at[z], lax.rem(z + 1, count))
        self.left = push(own, self.at(z), send.at[1], recv.at[z], lax.rem(z + count - 1, count))

    def chunk(self, b):
        return pl.ds(pl.multiple_of(b * self.rows, self.rows), self.rows)

    def at(self, b):
        return self.all.at[self.chunk(b)]

    def start(self):
        pl.when(self.z < self.count - 1)(self.right.start)
        pl.when(self.z > 0)(self.left.start)

    def passing(self, i, b):
        z, count = self.z, self.count
        to = jnp.where(b < z, z + 1, z - 1)
        going = ((b < z) & (z < count - 1)) | ((b > z) & (z > 0))
        copy = push(
            self.at(b), self.at(b), self.send.at[i + 1], self.recv.at[b], lax.rem(to + count, count)
        )
        return copy, going

    def receive(self, i, b):
        copy, going = self.passing(i, b)
        copy.wait_recv()
        pl.when(going)(copy.start)

    def finish(self):
        def sent(i, _):
            copy, going = self.passing(i, near_order(self.z, self.count, i))
            pl.when(going)(copy.wait_send)
            return 0

        lax.fori_loop(1, self.count, sent, 0)
        pl.when(self.z < self.count - 1)(self.right.wait_send)
        pl.when(self.z > 0)(self.left.wait_send)


class LineSum:
    def __init__(self, parts, landed, send, recv, rows):
        self.parts, self.landed, self.send, self.recv = parts, landed, send, recv
        self.z, self.count = lax.axis_index("head"), lax.axis_size("head")
        self.rows, self.pieces = rows, send.shape[1]
        self.deep = rows // self.pieces
        self.inner = (self.z > 0) & (self.z < self.count - 1)
        self.far_end = jnp.where(self.z < self.count - 1 - self.z, self.count - 1, 0)

    def piece(self, b, p):
        return pl.ds(pl.multiple_of(b * self.rows + p * self.deep, self.deep), self.deep)

    def onward(self, b, p):
        z, count = self.z, self.count
        to = jnp.where(b > z, z + 1, z - 1)
        slot = jnp.where((to == b) & (z > b), count, b)
        return push(
            self.parts.at[self.piece(b, p)], self.landed.at[self.piece(slot, p)],
            self.send.at[b, p], self.recv.at[slot, p], lax.rem(to + count, count),
        )

    def send_all(self):
        @pl.when(jnp.logical_not(self.inner))
        def _():
            for i in range(1, self.count):
                b = jnp.where(self.z == 0, self.count - i, i - 1)
                for p in range(self.pieces):
                    self.onward(b, p).start()

    def arrived(self, slot, p):
        at = self.piece(slot, p)
        push(
            self.landed.at[at], self.landed.at[at], self.send.at[0, p], self.recv.at[slot, p],
            lax.rem(self.z + 1, self.count),
        ).wait_recv()
        return self.landed[at, :].astype(F32)

    def relay(self, b, p):
        at = self.piece(b, p)
        self.parts[at, :] = (self.parts[at, :].astype(F32) + self.arrived(b, p)).astype(BF16)
        self.onward(b, p).start()

    def relay_in_turn(self, j):
        pieces = self.pieces

        @pl.when(self.inner & (j < pieces))
        def _():
            self.relay(self.count - 1 - self.z, j)

        @pl.when(self.inner & (j >= pieces))
        def _():
            self.relay(self.far_end, j - pieces)

        @pl.when(self.inner & (j > pieces))
        def _():
            self.relay(self.count - 1 - self.far_end, j - pieces - 1)

    def relay_last(self):
        @pl.when(self.inner)
        def _():
            self.relay(self.count - 1 - self.far_end, self.pieces - 1)

    def result(self, out):
        z, count = self.z, self.count
        for p in range(self.pieces):
            here = pl.ds(p * self.deep, self.deep)
            out[here, :] = self.parts[self.piece(z, p), :].astype(F32)

            @pl.when(z > 0)
            def _():
                out[here, :] += self.arrived(z, p)

            @pl.when(z < count - 1)
            def _():
                out[here, :] += self.arrived(count, p)

    def finish(self):
        def sent(i, _):
            b = near_order(self.z, self.count, i)
            for p in range(self.pieces):
                self.onward(b, p).wait_send()
            return 0

        lax.fori_loop(1, self.count, sent, 0)


class PairSum:
    def __init__(self, mine, paired, peers, pair_send, pair_recv, peer_send, peer_recv):
        self.mine, self.paired, self.peers = mine, paired, peers
        self.sems = pair_send, pair_recv, peer_send, peer_recv
        self.s, self.seq = lax.axis_index("seq"), lax.axis_size("seq")
        self.side, self.pairs, self.own = lax.rem(self.s, 2), self.seq // 2, self.s // 2
        self.deep = mine.shape[1]

    def block(self, k, other=False):
        i = 2 * k + (1 - self.side if other else self.side)
        return pl.ds(pl.multiple_of(i * self.deep, self.deep), self.deep)

    def to_partner(self, src, k):
        return push(
            src, self.paired.at[k], self.sems[0].at[k], self.sems[1].at[k],
            self.s + 1 - 2 * self.side, "seq",
        )

    def to_peer(self, k):
        return push(
            self.mine.at[k], self.peers.at[self.own], self.sems[2].at[k], self.sems[3].at[self.own],
            2 * k + self.side, "seq",
        )

    def pass_on(self, k):
        pl.when(self.own != k)(self.to_peer(k).start)

    def collect(self, out):
        self.peers[self.own] = self.mine[self.own]
        for k in range(self.pairs):
            copy = push(
                self.mine.at[k], self.peers.at[k], self.sems[2].at[k], self.sems[3].at[k],
                lax.rem(self.s + 1, self.seq), "seq",
            )
            pl.when(self.own != k)(copy.wait_recv)
        band = 16

        def add_rows(r, _):
            at = pl.ds(pl.multiple_of(r * band, band), band)
            out[at, :] = jnp.sum(self.peers[:, at, :].astype(F32), axis=0).astype(out.dtype)
            return 0

        lax.fori_loop(0, self.deep // band, add_rows, 0)

    def finish(self, src):
        for k in range(self.pairs):
            self.to_partner(src(k), k).wait_send()
            pl.when(self.own != k)(self.to_peer(k).wait_send)


def gather_norm_kernel(own, gain, normed, rows_all, here_sem, send, recv):
    z, count, rows = lax.axis_index("head"), lax.axis_size("head"), own.shape[0]
    greet(("head",))
    line = Line(own, rows_all, send, recv)
    line.start()
    here = pltpu.make_async_copy(own, line.at(z), here_sem)
    here.start()
    here.wait()
    band = 16

    def step(i, _):
        b = near_order(z, count, i)
        pl.when(i > 0)(lambda: line.receive(i, b))

        def norm(r, _):
            at = pl.ds(pl.multiple_of(b * rows + r * band, band), band)
            x = rows_all[at, :].astype(F32)
            inv = lax.rsqrt(jnp.mean(x * x, axis=-1, keepdims=True) + 1e-6)
            normed[at, :] = (x * inv * gain[...]).astype(BF16)
            return 0

        lax.fori_loop(0, rows // band, norm, 0)
        return 0

    lax.fori_loop(0, count, step, 0)
    line.finish()


def gather_norm(x, gain):
    rows, width = x.shape
    count = lax.axis_size("head")
    vmem = pl.BlockSpec(memory_space=pltpu.VMEM)
    dma = pltpu.SemaphoreType.DMA
    return pl.pallas_call(
        gather_norm_kernel,
        out_shape=jax.ShapeDtypeStruct((count * rows, width), BF16),
        in_specs=[vmem, vmem],
        out_specs=vmem,
        scratch_shapes=[
            pltpu.VMEM((count * rows, width), BF16), dma(()), dma((count + 1,)), dma((count,)),
        ],
        compiler_params=pltpu.CompilerParams(
            collective_id=1, has_side_effects=True, vmem_limit_bytes=32 << 20
        ),
        cost_estimate=cost(50),
        name="gather_norm",
    )(x, gain)


def swap_slices(own, got, send, recv):
    me, count = lax.axis_index("seq"), lax.axis_size("seq")

    def copy(hop, index):
        to = lax.rem(me + hop, count)
        return push(own.at[to], got.at[index], send.at[hop], recv.at[index], to, "seq")

    def start(hop, _):
        copy(hop, me).start()
        return 0

    def wait_recv(hop, _):
        copy(hop, lax.rem(me + hop, count)).wait_recv()
        return 0

    def wait_send(hop, _):
        copy(hop, me).wait_send()
        return 0

    def begin():
        lax.fori_loop(1, count, start, 0)
        got[me] = own[me]

    def end():
        lax.fori_loop(1, count, wait_recv, 0)

    def drain():
        lax.fori_loop(1, count, wait_send, 0)

    return begin, end, drain


def scan_states(reverse, own, through, out):
    count, part = out.shape[0], out.shape[2]

    def step(k, state):
        j = count - 1 - k if reverse else k
        out[j] = state.astype(BF16)
        decay = through[j, :, 0:1, :].astype(F32) + through[j, :, 1:2, :].astype(F32)
        return decay * state + own[j, :, :part, :].astype(F32)

    lax.fori_loop(0, count, step, jnp.zeros(out.shape[1:], F32))


def enter_kernel(own, rows_own, before, through, rows_all,
                 got, scanned, send, recv, send_back, recv_back, here_sem, go, come):
    z, count = lax.axis_index("head"), lax.axis_size("head")
    part = scanned.shape[2]
    greet(("seq", "head"))
    begin, end, drain = swap_slices(own, got, send, recv)
    begin()
    line = Line(rows_own, rows_all, go, come)
    line.start()
    here = pltpu.make_async_copy(rows_own, line.at(z), here_sem)
    here.start()
    end()
    through[...] = got[:, :, part:, :]
    scan_states(False, got, through, scanned)
    begin_back, end_back, drain_back = swap_slices(scanned, before, send_back, recv_back)
    begin_back()

    def step(i, _):
        line.receive(i, near_order(z, count, i))
        return 0

    lax.fori_loop(1, count, step, 0)
    end_back()
    here.wait()
    line.finish()
    drain()
    drain_back()


def enter(own, rows_own, part):
    slices, micro, deep, dk = own.shape
    rows, width = rows_own.shape
    count = lax.axis_size("head")
    vmem, anywhere = pl.BlockSpec(memory_space=pltpu.VMEM), pl.BlockSpec(memory_space=pl.ANY)
    dma = pltpu.SemaphoreType.DMA
    return pl.pallas_call(
        enter_kernel,
        out_shape=(
            jax.ShapeDtypeStruct((slices, micro, part, dk), BF16),
            jax.ShapeDtypeStruct((slices, micro, deep - part, dk), BF16),
            jax.ShapeDtypeStruct((count * rows, width), BF16),
        ),
        in_specs=[vmem, anywhere],
        out_specs=(vmem, vmem, anywhere),
        scratch_shapes=[
            pltpu.VMEM(own.shape, BF16), pltpu.VMEM((slices, micro, part, dk), BF16),
            dma((slices,)), dma((slices,)), dma((slices,)), dma((slices,)),
            dma(()), dma((count + 1,)), dma((count,)),
        ],
        compiler_params=pltpu.CompilerParams(
            collective_id=2, has_side_effects=True, vmem_limit_bytes=32 << 20
        ),
        cost_estimate=cost(50),
        name="enter",
    )(own, rows_own)


def total_kernel(own, out, from_seq, part, from_head, send_a, recv_a, send_b, recv_b,
                 send_c, recv_c, send_d, recv_d):
    seq, head = lax.axis_size("seq"), lax.axis_size("head")
    s, h = lax.axis_index("seq"), lax.axis_index("head")
    greet(("seq", "head"))

    def each(axis, me, count, src, dst, send, recv):
        def copy(hop, index):
            to = lax.rem(me + hop, count)
            return push(src(to), dst(index), send.at[hop], recv.at[index], to, axis)

        for hop in range(1, count):
            copy(hop, me).start()
        for hop in range(1, count):
            copy(hop, lax.rem(me + hop, count)).wait_recv()
        return [copy(hop, me).wait_send for hop in range(1, count)]

    from_seq[s] = own[s]
    sent = each("seq", s, seq, lambda to: own.at[to], lambda i: from_seq.at[i], send_a, recv_a)
    part[...] = jnp.sum(from_seq[...], axis=0)
    from_head[h] = part[h]
    sent += each("head", h, head, lambda to: part.at[to], lambda i: from_head.at[i], send_b, recv_b)
    out[s, h] = jnp.sum(from_head[...], axis=0)
    sent += each("head", h, head, lambda _: out.at[s, h], lambda i: out.at[s, i], send_c, recv_c)
    sent += each("seq", s, seq, lambda _: out.at[s], lambda i: out.at[i], send_d, recv_d)
    for wait in sent:
        wait()


def total_of(parts):
    seq, head = lax.axis_size("seq"), lax.axis_size("head")
    flat = jnp.concatenate([p.reshape(-1) for p in parts])
    deep = -(-flat.shape[0] // (seq * head * 1024)) * 8
    flat = jnp.pad(flat, (0, seq * head * deep * 128 - flat.shape[0]))
    vmem = pl.BlockSpec(memory_space=pltpu.VMEM)
    dma = pltpu.SemaphoreType.DMA
    shape = (seq, head, deep, 128)
    whole = pl.pallas_call(
        total_kernel,
        out_shape=jax.ShapeDtypeStruct(shape, F32),
        in_specs=[vmem],
        out_specs=vmem,
        scratch_shapes=[
            pltpu.VMEM(shape, F32), pltpu.VMEM(shape[1:], F32), pltpu.VMEM(shape[1:], F32),
        ]
        + [dma((n,)) for n in (seq, seq, head, head, head, head, seq, seq)],
        compiler_params=pltpu.CompilerParams(collective_id=4, has_side_effects=True),
        cost_estimate=cost(15),
        name="total",
    )(flat.reshape(shape)).reshape(-1)
    result, at = [], 0
    for p in parts:
        result.append(whole[at : at + p.size].reshape(p.shape))
        at += p.size
    return result


def ffn_kernel(count, x_own, c_all, w, g_x, f_parts, grad, grad_down,
               wv, xs, cs, act, lin, parts, landed, turned, turned_c, tiles,
               w_sem, own_sem, go_sem, x_sem, p_sem, q_sem, o_sem):
    z = lax.axis_index("head")
    rows, width = x_own.shape
    hidden = act.shape[1] // 3
    chunk = lambda b: pl.ds(pl.multiple_of(b * rows, rows), rows)

    weights = [
        pltpu.make_async_copy(
            w.at[:, pl.ds(k * hidden, hidden)], wv.at[:, pl.ds(k * hidden, hidden)], w_sem.at[k]
        )
        for k in range(3)
    ]
    own = [
        pltpu.make_async_copy(x_own, xs.at[chunk(z)], own_sem.at[0]),
        pltpu.make_async_copy(c_all, cs, own_sem.at[1]),
    ]
    for copy in own + weights:
        copy.start()
    greet(("head",))
    line = Line(x_own, xs, go_sem, x_sem)
    line.start()
    for copy in own + weights:
        copy.wait()

    total = LineSum(parts, landed, p_sem, q_sem, rows)

    def step(i, _):
        b = near_order(z, count, i)

        pl.when(i > 0)(lambda: line.receive(i, b))

        at = chunk(b)
        x = xs[at, :]
        lin[0] = jnp.dot(x, wv[:, :hidden], preferred_element_type=F32)
        lin[1] = jnp.dot(x, wv[:, hidden : 2 * hidden], preferred_element_type=F32)
        lin[2] = jnp.dot(cs[at, :], wv[:, 2 * hidden :], preferred_element_type=F32)
        band = 16

        def act_rows(r, _):
            here = pl.ds(pl.multiple_of(r * band, band), band)
            there = pl.ds(pl.multiple_of(b * rows + r * band, band), band)
            gate, up, g_product = lin[0, here, :], lin[1, here, :], lin[2, here, :]
            sig = sigmoid(gate)
            gated = gate * sig
            act[there, :hidden] = (g_product * up * sig * (1.0 + gate * (1.0 - sig))).astype(BF16)
            act[there, hidden : 2 * hidden] = (g_product * gated).astype(BF16)
            act[there, 2 * hidden :] = (gated * up).astype(BF16)
            return 0

        lax.fori_loop(0, rows // band, act_rows, 0)
        parts[at, :] = mm(act[at, : 2 * hidden], wv[:, : 2 * hidden], (1, 1), None).astype(BF16)

        @pl.when((i > 0) & jnp.logical_not(total.inner))
        def _():
            for p in range(total.pieces):
                total.onward(b, p).start()

        return 0

    lax.fori_loop(0, count, step, 0)

    high = tiles.shape[1]
    steps = width // high

    def store(t, r, k):
        down = pl.ds(pl.multiple_of(r * high, high), high)
        into = grad_down.at[down] if k == 2 else grad.at[down, pl.ds(k * hidden, hidden)]
        return pltpu.make_async_copy(tiles.at[lax.rem(t, 2)], into, o_sem.at[lax.rem(t, 2)])

    turned[...] = xs[...].T
    turned_c[...] = cs[...].T

    def tile(r, k):
        t = 3 * r + k

        @pl.when(t >= 2)
        def _():
            store(t, r, k).wait()

        left_rows = (turned_c if k == 2 else turned)[
            pl.ds(pl.multiple_of(r * high, high), high), :
        ]
        tiles[lax.rem(t, 2)] = jnp.dot(
            left_rows, act[:, k * hidden : (k + 1) * hidden], preferred_element_type=F32
        ).astype(BF16)
        store(t, r, k).start()

    def slab(r, _):
        tile(r, 0)
        tile(r, 1)
        total.relay_in_turn(2 * r)
        tile(r, 2)
        at = chunk(r)
        f_parts[r] = mm(act[at, 2 * hidden :], wv[:, 2 * hidden :], (1, 1), None).astype(BF16)
        total.relay_in_turn(2 * r + 1)
        return 0

    lax.fori_loop(0, steps, slab, 0)
    total.relay_last()
    total.result(g_x)
    total.finish()
    line.finish()
    store(3 * steps - 2, 0, 0).wait()
    store(3 * steps - 1, 0, 0).wait()


def feed_forward(x_own, c_all, w, hidden, count):
    rows, width = x_own.shape
    group = rows * count
    assert count == 4 and width % 4 == 0 and rows % 64 == 0
    anywhere = pl.BlockSpec(memory_space=pl.ANY)
    vmem = pl.BlockSpec(memory_space=pltpu.VMEM)
    dma = pltpu.SemaphoreType.DMA
    return pl.pallas_call(
        functools.partial(ffn_kernel, count),
        out_shape=(
            jax.ShapeDtypeStruct((rows, width), F32),
            jax.ShapeDtypeStruct((count, rows, width), BF16),
            jax.ShapeDtypeStruct((width, 2 * hidden), BF16),
            jax.ShapeDtypeStruct((width, hidden), BF16),
        ),
        in_specs=[anywhere] * 3,
        out_specs=(vmem, vmem, anywhere, anywhere),
        scratch_shapes=[
            pltpu.VMEM((width, 3 * hidden), BF16),
            pltpu.VMEM((group, width), BF16),
            pltpu.VMEM((group, width), BF16),
            pltpu.VMEM((group, 3 * hidden), BF16),
            pltpu.VMEM((3, rows, hidden), F32),
            pltpu.VMEM((group, width), BF16),
            pltpu.VMEM((group + rows, width), BF16),
            pltpu.VMEM((width, group), BF16),
            pltpu.VMEM((width, group), BF16),
            pltpu.VMEM((2, width // 4, hidden), BF16),
            dma((3,)), dma((2,)), dma((count + 1,)), dma((count,)),
            dma((count, 4)), dma((count + 1, 4)), dma((2,)),
        ],
        compiler_params=pltpu.CompilerParams(
            collective_id=0, has_side_effects=True, vmem_limit_bytes=60 << 20
        ),
        cost_estimate=cost(100),
        name="feed_forward",
    )(x_own, c_all, w)


def split(x):
    high = x.astype(BF16)
    return high, (x - high.astype(F32)).astype(BF16)


def mms(left, right, contract):
    total = mm(left[0], right[0], contract, None)
    if len(right) > 1:
        total += mm(left[0], right[1], contract, None)
    if len(left) > 1:
        total += mm(left[1], right[0], contract, None)
    return total


def back_kernel(keep, gated_own, og, o_in, qkv, decay, logits, through, gain, left, right,
                kept_in, parts_in, g_proj, g_logits, g_gain, f_out, g_out,
                gated_all, go, runs, g_queried, g_keyed, g_values, pulls, weights, kept,
                parts, landed, state, sending, got, scanned, after, turned, tiles, in_sem, t_sem,
                z_send, z_recv, s_send, s_recv, b_send, b_recv, p_sem, q_sem):
    h, head = lax.axis_index("head"), lax.axis_size("head")
    count, micro, rows, dk = decay.shape
    dv = og.shape[-1]
    width = qkv.shape[-1]
    slices, part = sending.shape[0], sending.shape[2]
    scale = dk ** (-0.5)
    loads = [
        pltpu.make_async_copy(parts_in, parts, in_sem.at[0]),
        pltpu.make_async_copy(kept_in, kept, in_sem.at[1]),
    ]
    for load in loads:
        load.start()
    greet(("seq", "head"))

    def to_head(hop, slot):
        to = lax.rem(h + hop, head)
        columns = gated_own.at[:, pl.ds(pl.multiple_of(to * dv, dv), dv)]
        return push(columns, gated_all.at[slot], z_send.at[hop], z_recv.at[slot], to)

    for hop in range(1, head):
        to_head(hop, h).start()
    gated_all[h] = gated_own[:, pl.ds(pl.multiple_of(h * dv, dv), dv)]

    causal = lower_ones(rows)
    before = [jnp.zeros((1, dk), F32)] * micro
    alive = [jnp.ones((1, dk), F32)] * micro
    for b in range(count):
        for m in range(micro):
            run = running(decay[b, m])
            runs[b, m] = run
            alive[m] = alive[m] * keep[b, m]
            weights[b, m] = jnp.exp(before[m]) * alive[m]
            before[m] = before[m] + run[rows - 1 : rows, :]
    g_gain[...] = jnp.zeros_like(g_gain)
    state[...] = jnp.zeros_like(state)

    turned[...] = left[...].T
    high, wide = tiles.shape[1:]
    across_tiles = g_out.shape[1] // wide

    def store(t):
        at = pl.ds(pl.multiple_of((t // across_tiles) * high, high), high)
        columns = pl.ds(pl.multiple_of(lax.rem(t, across_tiles) * wide, wide), wide)
        return pltpu.make_async_copy(
            tiles.at[lax.rem(t, 2)], g_out.at[at, columns], t_sem.at[lax.rem(t, 2)]
        )

    def tile(t, _):
        @pl.when(t >= 2)
        def _():
            store(t - 2).wait()

        at = pl.ds(pl.multiple_of((t // across_tiles) * high, high), high)
        columns = pl.ds(pl.multiple_of(lax.rem(t, across_tiles) * wide, wide), wide)
        tiles[lax.rem(t, 2)] = jnp.dot(
            turned[at, :], right[:, columns], preferred_element_type=F32
        ).astype(BF16)
        store(t).start()
        return 0

    tile_count = (g_out.shape[0] // high) * across_tiles
    lax.fori_loop(0, tile_count, tile, 0)

    def gates(i, _):
        b = near_order(h, head, i)
        pl.when(i > 0)(lambda: to_head(lax.rem(b - h + head, head), b).wait_recv())
        for m in range(micro):
            gate, o = og[b, m], o_in[b, m]
            grad = gated_all[b, m * rows : (m + 1) * rows, :].astype(F32)
            sig = sigmoid(gate)
            inv = lax.rsqrt(jnp.mean(o * o, axis=-1, keepdims=True) + 1e-5)
            plain = o * inv
            normed = (plain * gain[...]).astype(BF16).astype(F32)
            g_on = (grad * gate * sig).astype(BF16).astype(F32)
            g_proj[b, m, :, width:] = (
                grad * normed * sig * (1.0 + gate * (1.0 - sig))
            ).astype(BF16)
            scaled = g_on * gain[...]
            g_o = inv * (scaled - plain * jnp.mean(scaled * plain, axis=-1, keepdims=True))
            go[b, m] = g_o
            g_gain[0:1, :] += jnp.sum(g_on * plain, axis=0, keepdims=True)
            queried = qkv[b, m, :, :dk].astype(F32) * (jnp.exp(runs[b, m]) * scale)
            pull = mms(split(g_o), split(queried), (0, 0))
            pulls[b, m] = pull
            state[m] += pull * weights[b, m]
        return 0

    lax.fori_loop(0, head, gates, 0)
    for i in range(slices):
        sending[i] = state[:, i * part : (i + 1) * part, :].astype(BF16)
    begin, end, drain = swap_slices(sending, got, s_send, s_recv)
    begin()
    for load in loads:
        load.wait()
    total = LineSum(parts, landed, p_sem, q_sem, f_out.shape[0])
    total.send_all()

    def inside(b, _):
        for m in range(micro):
            q = qkv[b, m, :, :dk].astype(F32)
            k = qkv[b, m, :, dk : 2 * dk].astype(F32)
            v = (qkv[b, m, :, 2 * dk :],)
            run = runs[b, m]
            queried, keyed = split(q * (jnp.exp(run) * scale)), split(k * jnp.exp(-run))
            g_o, entry = split(go[b, m]), split(kept[b, m])
            scores = split(jnp.where(causal, mms(queried, keyed, (1, 1)), 0.0))
            g_scores = split(jnp.where(causal, mms(g_o, v, (1, 1)), 0.0))
            g_queried[b, m] = mms(g_scores, keyed, (1, 0)) + mms(g_o, entry, (1, 0))
            g_keyed[b, m] = mms(g_scores, queried, (0, 0))
            g_values[b, m] = mms(scores, g_o, (0, 0))
        pl.when(total.inner)(lambda: total.relay(total.far_end, b))
        return 0

    lax.fori_loop(0, count, inside, 0)
    end()
    scan_states(True, got, through, scanned)
    begin_back, end_back, drain_back = swap_slices(scanned, after, b_send, b_recv)
    begin_back()

    @pl.when(total.inner)
    def _():
        for p in range(total.pieces):
            total.relay(head - 1 - total.far_end, p)
        for p in range(total.pieces):
            total.relay(head - 1 - h, p)

    end_back()
    for i in range(slices):
        state[:, i * part : (i + 1) * part, :] = after[i].astype(F32)

    def across(step, _):
        b = count - 1 - step
        for m in range(micro):
            q = qkv[b, m, :, :dk].astype(F32)
            k = qkv[b, m, :, dk : 2 * dk].astype(F32)
            v = (qkv[b, m, :, 2 * dk :],)
            run = runs[b, m]
            last = run[rows - 1 : rows, :]
            up, down, rest = jnp.exp(run) * scale, jnp.exp(-run), jnp.exp(last - run)
            decayed = jnp.exp(last)
            gs = state[m]
            gs_parts = split(gs)
            carried = k * rest
            g_v = g_values[b, m] + mms(split(carried), gs_parts, (1, 1))
            g_carried = mms(v, gs_parts, (1, 0))
            from_carried = g_carried * carried
            g_total = jnp.sum(decayed * kept[b, m] * gs, axis=0, keepdims=True) + jnp.sum(
                from_carried, axis=0, keepdims=True
            )
            state[m] = (decayed * gs + pulls[b, m]) * keep[b, m]
            gq, gk = g_queried[b, m], g_keyed[b, m]
            g_run = gq * (q * up) - gk * (k * down) - from_carried
            later = mms((causal.astype(F32).astype(BF16),), split(g_run), (0, 0)) + g_total
            g_proj[b, m, :, :dk] = (gq * up).astype(BF16)
            g_proj[b, m, :, dk : 2 * dk] = (gk * down + g_carried * rest).astype(BF16)
            g_proj[b, m, :, 2 * dk : width] = g_v.astype(BF16)
            g_logits[b, m] = (
                later.astype(BF16).astype(F32) * sigmoid(-logits[b, m]) * (1.0 / GATE_NORM)
            )
        return 0

    lax.fori_loop(0, count, across, 0)
    total.result(f_out)
    total.finish()
    store(tile_count - 2).wait()
    store(tile_count - 1).wait()
    drain()
    drain_back()
    for hop in range(1, head):
        to_head(hop, h).wait_send()


def attention_back(
    keep, gated_own, og, o, qkv, decays, logits, through, gain, left, right, kept, parts
):
    blocks, micro, rows, width = qkv.shape
    dk, dv = decays.shape[-1], og.shape[-1]
    head, seq = lax.axis_size("head"), lax.axis_size("seq")
    own_rows = parts.shape[0] // head
    vmem, anywhere = pl.BlockSpec(memory_space=pltpu.VMEM), pl.BlockSpec(memory_space=pl.ANY)
    dma = pltpu.SemaphoreType.DMA
    blocked = lambda w, kind: pltpu.VMEM((blocks, micro, rows, w), kind)
    states = (seq, micro, dv // seq, dk)
    return pl.pallas_call(
        back_kernel,
        out_shape=(
            jax.ShapeDtypeStruct((blocks, micro, rows, width + dv), BF16),
            jax.ShapeDtypeStruct((blocks, micro, rows, dk), F32),
            jax.ShapeDtypeStruct((8, dv), F32),
            jax.ShapeDtypeStruct((own_rows, parts.shape[1]), F32),
            jax.ShapeDtypeStruct((left.shape[1], right.shape[1]), BF16),
        ),
        in_specs=[vmem] * 11 + [anywhere] * 2,
        out_specs=(vmem,) * 4 + (anywhere,),
        scratch_shapes=[
            pltpu.VMEM((blocks, micro * rows, dv), BF16), blocked(dv, F32), blocked(dk, F32),
            blocked(dk, F32), blocked(dk, F32), blocked(dv, F32),
            pltpu.VMEM((blocks, micro, dv, dk), F32), pltpu.VMEM((blocks, micro, 1, dk), F32),
            pltpu.VMEM((blocks, micro, dv, dk), F32),
            pltpu.VMEM(parts.shape, BF16),
            pltpu.VMEM((parts.shape[0] + own_rows, parts.shape[1]), BF16),
            pltpu.VMEM((micro, dv, dk), F32),
            pltpu.VMEM(states, BF16), pltpu.VMEM(states, BF16), pltpu.VMEM(states, BF16),
            pltpu.VMEM(states, BF16),
            pltpu.VMEM(left.shape[::-1], BF16),
            pltpu.VMEM((2, left.shape[1] // 4, right.shape[1] // 2), BF16),
            dma((2,)), dma((2,)), dma((head,)), dma((head,)), dma((seq,)), dma((seq,)), dma((seq,)),
            dma((seq,)), dma((head, 4)), dma((head + 1, 4)),
        ],
        compiler_params=pltpu.CompilerParams(
            collective_id=3, has_side_effects=True, vmem_limit_bytes=60 << 20
        ),
        cost_estimate=cost(80),
        name="attention_back",
    )(keep, gated_own, og, o, qkv, decays, logits, through, gain, left, right, kept, parts)


def finish_kernel(xn_in, proj_in, w_in, g_logits, ranked, up_own, rank_down,
                  g_x, grad, g_down, g_up, g_bias,
                  turned, proj, w, outgoing, mine, paired, peers, slab, heads_in, parts, landed, slim_high,
                  slim_low, in_sem, pair_send, pair_recv, peer_send, peer_recv, x_send, x_recv,
                  p_sem, q_sem):
    h, head = lax.axis_index("head"), lax.axis_size("head")
    rows, width = g_x.shape
    deep = grad.shape[0] * head
    pairs = lax.axis_size("seq") // 2

    loads = [
        pltpu.make_async_copy(proj_in, proj, in_sem.at[0]),
        pltpu.make_async_copy(w_in, w, in_sem.at[1]),
        pltpu.make_async_copy(xn_in, landed.at[pl.ds(0, xn_in.shape[0])], in_sem.at[2]),
    ]
    for load in loads:
        load.start()
    for load in loads:
        load.wait()
    turned[...] = landed[: xn_in.shape[0], :].T
    greet(("seq", "head"))
    total = LineSum(parts, landed, p_sem, q_sem, rows)
    logit_parts = split(g_logits[...])
    g_ranked = mms(logit_parts, split(up_own[...]), (1, 1))
    slim = split(g_ranked)
    slim_high[...], slim_low[...] = slim

    def chunk(i, _):
        b = near_order(h, head, head - 1 - i)
        at = pl.ds(pl.multiple_of(b * rows, rows), rows)
        rank_part = mms((slim_high[at, :], slim_low[at, :]), (rank_down[...],), (1, 1))
        parts[at, :] = (mm(proj[at, :], w[...], (1, 1), None) + rank_part).astype(BF16)

        @pl.when((b != h) & jnp.logical_not(total.inner))
        def _():
            for p in range(total.pieces):
                total.onward(b, p).start()

        return 0

    lax.fori_loop(0, head, chunk, 0)

    sums = PairSum(mine, paired, peers, pair_send, pair_recv, peer_send, peer_recv)

    def gone(k, _):
        outgoing[k] = jnp.dot(
            turned[sums.block(k, True), :], proj[...], preferred_element_type=F32
        ).astype(BF16)
        sums.to_partner(outgoing.at[k], k).start()
        return 0

    lax.fori_loop(0, pairs, gone, 0)

    def kept(k, _):
        here = jnp.dot(turned[sums.block(k), :], proj[...], preferred_element_type=F32)
        sums.to_partner(outgoing.at[k], k).wait_recv()
        mine[k] = (here + paired[k].astype(F32)).astype(BF16)
        sums.pass_on(k)

        @pl.when(total.inner & (k < total.pieces))
        def _():
            total.relay(total.far_end, k)

        @pl.when(total.inner & (k > 0) & (k <= total.pieces))
        def _():
            total.relay(head - 1 - total.far_end, k - 1)

        return 0

    lax.fori_loop(0, pairs, kept, 0)

    @pl.when(total.inner)
    def _():
        for p in range(pairs, total.pieces + 1):
            if p < total.pieces:
                total.relay(total.far_end, p)
            total.relay(head - 1 - total.far_end, p - 1)
        for p in range(total.pieces):
            total.relay(head - 1 - h, p)

    g_down[...] = mms((turned[...],), slim, (1, 0))
    g_up[...] = mms(split(ranked[...]), logit_parts, (0, 0))
    g_bias[...] = jnp.broadcast_to(jnp.sum(g_logits[...], axis=0, keepdims=True), g_bias.shape)

    sums.collect(slab)
    thin = grad.shape[0]

    def to_head(hop, slot):
        to = lax.rem(h + hop, head)
        return push(
            slab.at[pl.ds(pl.multiple_of(to * thin, thin), thin)], heads_in.at[slot],
            x_send.at[hop], x_recv.at[slot], to,
        )

    for hop in range(1, head):
        to_head(hop, h).start()
    heads_in[h] = slab[pl.ds(pl.multiple_of(h * thin, thin), thin), :]
    total.result(g_x)
    for hop in range(1, head):
        to_head(hop, lax.rem(h + hop, head)).wait_recv()
    dk = g_up.shape[1]
    dv = slab.shape[1] // 2 - dk
    for j in range(head):
        at, start = 0, 0
        for size in (dk, dk, dv, dv):
            grad[:, start + j * size : start + (j + 1) * size] = heads_in[
                j, :, at : at + size
            ].astype(F32)
            at, start = at + size, start + head * size
    sums.finish(lambda k: outgoing.at[k])
    for hop in range(1, head):
        to_head(hop, h).wait_send()
    total.finish()


def finish(xn, g_proj, w_in, g_logits, ranked, up_own, rank_down):
    seq, head = lax.axis_size("seq"), lax.axis_size("head")
    group, width = xn.shape
    columns, rank = w_in.shape[1], ranked.shape[1]
    deep, rows, pairs = width // seq, group // head, seq // 2
    dk = up_own.shape[1]
    vmem, anywhere = pl.BlockSpec(memory_space=pltpu.VMEM), pl.BlockSpec(memory_space=pl.ANY)
    dma = pltpu.SemaphoreType.DMA
    blocks = pltpu.VMEM((pairs, deep, columns), BF16)
    return pl.pallas_call(
        finish_kernel,
        out_shape=(
            jax.ShapeDtypeStruct((rows, width), F32),
            jax.ShapeDtypeStruct((deep // head, columns * head), F32),
            jax.ShapeDtypeStruct((width, rank), F32),
            jax.ShapeDtypeStruct((rank, dk), F32),
            jax.ShapeDtypeStruct((8, dk), F32),
        ),
        in_specs=[anywhere] * 3 + [vmem] * 4,
        out_specs=(vmem,) * 5,
        scratch_shapes=[
            pltpu.VMEM((width, group), BF16), pltpu.VMEM(g_proj.shape, BF16),
            pltpu.VMEM(w_in.shape, BF16), blocks, blocks, blocks, blocks,
            pltpu.VMEM((deep, columns), BF16), pltpu.VMEM((head, deep // head, columns), BF16),
            pltpu.VMEM((group, width), BF16), pltpu.VMEM((group + rows, width), BF16),
            pltpu.VMEM(ranked.shape, BF16), pltpu.VMEM(ranked.shape, BF16),
            dma((3,)), dma((pairs,)), dma((pairs,)), dma((pairs,)), dma((pairs,)),
            dma((head,)), dma((head,)), dma((head, 4)), dma((head + 1, 4)),
        ],
        compiler_params=pltpu.CompilerParams(
            collective_id=5, has_side_effects=True, vmem_limit_bytes=56 << 20
        ),
        cost_estimate=cost(60),
        name="finish",
    )(xn, g_proj, w_in, g_logits, ranked, up_own, rank_down)


def exchange(x, axis):
    return lax.all_to_all(x, axis, split_axis=0, concat_axis=0, tiled=True)


def gather_weight(w):
    return lax.all_gather(w, "seq", axis=0, tiled=True)


def scatter_grad(g):
    return lax.psum_scatter(g.astype(BF16), "seq", scatter_dimension=0, tiled=True)


def dot(a, b, contract, precision=None):
    return lax.dot_general(
        a, b, (((contract[0],), (contract[1],)), ((), ())),
        precision=precision, preferred_element_type=F32,
    )


def rms(x, epsilon):
    return lax.rsqrt(jnp.mean(x * x, axis=-1, keepdims=True) + epsilon)


def norm_back(grad, gain, normed, inv):
    scaled = grad * gain
    inner = jnp.mean(scaled * normed, axis=-1, keepdims=True)
    return inv * (scaled - normed * inner), jnp.sum(grad * normed, axis=0)


def on_device(
    tokens, starts, cotangent, mix_in, mix_out, gate_up, down_proj,
    norm_gain, ffn_gain, head_gain, rank_down, rank_up, gate_bias,
):
    micro, rows, width = tokens.shape
    heads, seq = lax.axis_size("head"), lax.axis_size("seq")
    head = lax.axis_index("head")
    keys, dv = rank_up.shape[1], head_gain.shape[0]
    dk, vals = keys // heads, dv * heads
    hidden_units = down_proj.shape[1]
    group = heads * micro * rows
    proj_width = 2 * dk + 2 * dv

    def own_columns(w, start, size):
        return lax.dynamic_slice_in_dim(w, start + head * size, size, 1)

    w_in = gather_weight(
        jnp.concatenate(
            [
                own_columns(mix_in, 0, dk),
                own_columns(mix_in, keys, dk),
                own_columns(mix_in, 2 * keys, dv),
                own_columns(mix_in, 2 * keys + vals, dv),
            ],
            axis=1,
        )
    )
    later = gather_weight(
        jnp.concatenate(
            [gate_up.reshape(gate_up.shape[0], 2 * hidden_units), down_proj, mix_out], axis=1
        )
    )
    w_out = later[:, 3 * hidden_units :]
    up_own = own_columns(rank_up, 0, dk)
    bias_own = lax.dynamic_slice_in_dim(gate_bias, head * dk, dk, 0)

    xn = gather_norm(tokens.reshape(micro * rows, width), norm_gain.reshape(1, width))
    qkv = dot(xn, w_in[:, : 2 * dk + dv], (1, 0)).astype(BF16)
    og = dot(xn, w_in[:, 2 * dk + dv :], (1, 0))
    ranked = dot(xn, rank_down, (1, 0))
    logits = dot(ranked, up_own, (1, 0), HIGHEST) + bias_own
    decays = (jax.nn.log_sigmoid(logits) / GATE_NORM).astype(BF16)

    def blocks(x):
        return x.reshape(heads, micro, rows, x.shape[-1])

    qkv_b, og_b, decays_b = blocks(qkv), blocks(og), blocks(decays)
    gain_row = head_gain.reshape(1, dv)
    part = dv // seq
    own_states = states_of(starts, qkv_b, decays_b, dv, seq, 16)
    before, through, all_cot = enter(own_states, cotangent.reshape(micro * rows, width), part)
    o_b, gated_b, kept = mix_of(starts, qkv_b, decays_b, og_b, before, gain_row)

    gated = exchange(gated_b, "head")
    gated = gated.transpose(1, 2, 0, 3).reshape(micro * rows, vals)
    source = tokens.astype(F32).reshape(micro * rows, width)
    hidden = source + dot(gated, w_out, (1, 1))
    inv_ffn = rms(hidden, 1e-6)
    plain_ffn = hidden * inv_ffn
    h2 = (plain_ffn * ffn_gain).astype(BF16)

    g_h2, ffn_part, grad_gu, grad_down = feed_forward(h2, all_cot, later, hidden_units, heads)
    grad_gu, grad_down = scatter_grad(grad_gu), scatter_grad(grad_down)

    back_ffn, g_ffn_gain = norm_back(g_h2, ffn_gain, plain_ffn, inv_ffn)
    g_hidden = cotangent.astype(F32).reshape(micro * rows, width) + back_ffn
    g_mixed = g_hidden.astype(BF16)
    g_gated = dot(g_mixed, w_out, (1, 0)).astype(BF16)
    keep = 1.0 - jnp.broadcast_to(starts.T[:, :, None, None], (heads, micro, 1, dk)).astype(F32)
    g_proj_b, g_logits_b, g_head_gain, ffn_out, grad_out = attention_back(
        keep, g_gated, og_b, o_b, qkv_b, decays_b, blocks(logits), through, gain_row,
        g_mixed, gated, kept, ffn_part.reshape(group, width),
    )
    grad_out = scatter_grad(grad_out)
    output = (hidden + ffn_out).astype(BF16)
    g_proj, g_logits = g_proj_b.reshape(group, proj_width), g_logits_b.reshape(group, dk)
    g_xn, grad_in, g_rank_down, g_rank_up, g_bias = finish(
        xn, g_proj, w_in, g_logits, ranked, up_own, rank_down
    )
    g_xn, grad_gu = lax.optimization_barrier((g_xn, grad_gu))
    inv_in = rms(source, 1e-6)
    back_in, g_norm_gain = norm_back(g_xn, norm_gain, source * inv_in, inv_in)
    input_grad = g_hidden + back_in
    slab = width // (seq * heads)
    g_norm_gain, grad_out = lax.optimization_barrier((g_norm_gain, grad_out))
    grad_out = exchange(grad_out.reshape(heads, slab, vals), "head").astype(F32).sum(0)

    g_rank_up = lax.dynamic_update_slice_in_dim(
        jnp.zeros(rank_up.shape, F32), g_rank_up, head * dk, 1
    )
    g_bias = lax.dynamic_update_slice_in_dim(
        jnp.zeros(gate_bias.shape, F32), g_bias[0], head * dk, 0
    )
    small = total_of(
        [g_norm_gain, g_ffn_gain, g_head_gain[0], g_rank_down, g_rank_up, g_bias]
    )
    small, grad_down = lax.optimization_barrier((small, grad_down))
    return (
        output.reshape(tokens.shape),
        input_grad.reshape(tokens.shape),
        grad_in,
        grad_out,
        grad_gu.astype(F32).reshape(-1, 2, hidden_units),
        grad_down.astype(F32),
        *small,
    )


def solution(mesh):
    rows = P(None, ("seq", "head"), None)
    return jax.shard_map(
        on_device,
        mesh=mesh,
        in_specs=(
            rows, P(None, "seq"), rows, P("seq", None), P("seq", None),
            P("seq", None, "head"), P("seq", "head"), P(), P(), P(), P(), P(), P(),
        ),
        out_specs=(
            rows, rows, P(("seq", "head"), None), P(("seq", "head"), None),
            P("seq", None, "head"), P("seq", "head"), P(), P(), P(), P(), P(), P(),
        ),
        check_vma=False,
    )
```

```python
import functools

import jax
import jax.numpy as jnp
from jax import lax
from jax.experimental import pallas as pl
from jax.experimental.pallas import tpu as pltpu
from jax.sharding import PartitionSpec as P

HIGHEST = lax.Precision.HIGHEST
GATE_NORM = 16.0
BF16 = jnp.bfloat16
F32 = jnp.float32


def mm(a, b, contract, precision=HIGHEST):
    return lax.dot_general(
        a, b, ((contract[:1], contract[1:]), ((), ())),
        precision=precision, preferred_element_type=F32,
    )


def split(x):
    high = x.astype(BF16)
    return high, (x - high.astype(F32)).astype(BF16)


def mms(left, right, contract):
    total = mm(left[0], right[0], contract, None)
    if len(right) > 1:
        total += mm(left[0], right[1], contract, None)
    if len(left) > 1:
        total += mm(left[1], right[0], contract, None)
    return total


def lower_ones(size):
    rows = lax.broadcasted_iota(jnp.int32, (size, size), 0)
    cols = lax.broadcasted_iota(jnp.int32, (size, size), 1)
    return rows >= cols


def running(decay_low):
    ones = lower_ones(decay_low.shape[0]).astype(F32).astype(BF16)
    return mm(ones, decay_low, (1, 0), None)


def sigmoid(x):
    return 1.0 / (1.0 + jnp.exp(-x))


def cost(micros):
    return pl.CostEstimate(flops=0, bytes_accessed=int(micros * 3.0e6), transcendentals=0)


def greet(axes):
    barrier = pltpu.get_barrier_semaphore()
    met = 0
    for axis in axes:
        me, count = lax.axis_index(axis), lax.axis_size(axis)
        for hop in range(1, count):
            pl.semaphore_signal(
                barrier, inc=1, device_id={axis: lax.rem(me + hop, count)},
                device_id_type=pl.DeviceIdType.MESH,
            )
        met += count - 1
    pl.semaphore_wait(barrier, met)


def push(src, dst, send, recv, to, axis="head"):
    return pltpu.make_async_remote_copy(
        src_ref=src, dst_ref=dst, send_sem=send, recv_sem=recv,
        device_id={axis: to}, device_id_type=pl.DeviceIdType.MESH,
    )


def near_order(z, count, i):
    both = jnp.minimum(z, count - 1 - z)
    left = z > count - 1 - z
    paired = jnp.where(i % 2 == 1, z - (i + 1) // 2, z + i // 2)
    single = jnp.where(left, z - (i - both), z + (i - both))
    return jnp.where(i <= 2 * both, paired, single)


class Line:
    def __init__(self, own, all_rows, send, recv):
        self.own, self.all, self.send, self.recv = own, all_rows, send, recv
        self.z, self.count, self.rows = lax.axis_index("head"), lax.axis_size("head"), own.shape[0]
        z, count = self.z, self.count
        self.right = push(own, self.at(z), send.at[0], recv.at[z], lax.rem(z + 1, count))
        self.left = push(own, self.at(z), send.at[1], recv.at[z], lax.rem(z + count - 1, count))

    def chunk(self, b):
        return pl.ds(pl.multiple_of(b * self.rows, self.rows), self.rows)

    def at(self, b):
        return self.all.at[self.chunk(b)]

    def start(self):
        pl.when(self.z < self.count - 1)(self.right.start)
        pl.when(self.z > 0)(self.left.start)

    def passing(self, i, b):
        z, count = self.z, self.count
        to = jnp.where(b < z, z + 1, z - 1)
        going = ((b < z) & (z < count - 1)) | ((b > z) & (z > 0))
        copy = push(
            self.at(b), self.at(b), self.send.at[i + 1], self.recv.at[b], lax.rem(to + count, count)
        )
        return copy, going

    def receive(self, i, b):
        copy, going = self.passing(i, b)
        copy.wait_recv()
        pl.when(going)(copy.start)

    def finish(self):
        def sent(i, _):
            copy, going = self.passing(i, near_order(self.z, self.count, i))
            pl.when(going)(copy.wait_send)
            return 0

        lax.fori_loop(1, self.count, sent, 0)
        pl.when(self.z < self.count - 1)(self.right.wait_send)
        pl.when(self.z > 0)(self.left.wait_send)


class LineSum:
    def __init__(self, parts, landed, send, recv, rows):
        self.parts, self.landed, self.send, self.recv = parts, landed, send, recv
        self.z, self.count = lax.axis_index("head"), lax.axis_size("head")
        self.rows, self.pieces = rows, send.shape[1]
        self.deep = rows // self.pieces
        self.inner = (self.z > 0) & (self.z < self.count - 1)
        self.far_end = jnp.where(self.z < self.count - 1 - self.z, self.count - 1, 0)

    def piece(self, b, p):
        return pl.ds(pl.multiple_of(b * self.rows + p * self.deep, self.deep), self.deep)

    def onward(self, b, p):
        z, count = self.z, self.count
        to = jnp.where(b > z, z + 1, z - 1)
        slot = jnp.where((to == b) & (z > b), count, b)
        return push(
            self.parts.at[self.piece(b, p)], self.landed.at[self.piece(slot, p)],
            self.send.at[b, p], self.recv.at[slot, p], lax.rem(to + count, count),
        )

    def send_all(self):
        @pl.when(jnp.logical_not(self.inner))
        def _():
            for i in range(1, self.count):
                b = jnp.where(self.z == 0, self.count - i, i - 1)
                for p in range(self.pieces):
                    self.onward(b, p).start()

    def arrived(self, slot, p):
        at = self.piece(slot, p)
        push(
            self.landed.at[at], self.landed.at[at], self.send.at[0, p], self.recv.at[slot, p],
            lax.rem(self.z + 1, self.count),
        ).wait_recv()
        return self.landed[at, :].astype(F32)

    def relay(self, b, p):
        at = self.piece(b, p)
        self.parts[at, :] = (self.parts[at, :].astype(F32) + self.arrived(b, p)).astype(BF16)
        self.onward(b, p).start()

    def relay_in_turn(self, j):
        pieces = self.pieces

        @pl.when(self.inner & (j < pieces))
        def _():
            self.relay(self.count - 1 - self.z, j)

        @pl.when(self.inner & (j >= pieces))
        def _():
            self.relay(self.far_end, j - pieces)

        @pl.when(self.inner & (j > pieces))
        def _():
            self.relay(self.count - 1 - self.far_end, j - pieces - 1)

    def relay_last(self):
        @pl.when(self.inner)
        def _():
            self.relay(self.count - 1 - self.far_end, self.pieces - 1)

    def result(self, out):
        z, count = self.z, self.count
        for p in range(self.pieces):
            here = pl.ds(p * self.deep, self.deep)
            out[here, :] = self.parts[self.piece(z, p), :].astype(F32)

            @pl.when(z > 0)
            def _():
                out[here, :] += self.arrived(z, p)

            @pl.when(z < count - 1)
            def _():
                out[here, :] += self.arrived(count, p)

    def finish(self):
        def sent(i, _):
            b = near_order(self.z, self.count, i)
            for p in range(self.pieces):
                self.onward(b, p).wait_send()
            return 0

        lax.fori_loop(1, self.count, sent, 0)


class PairSum:
    def __init__(self, mine, paired, inbox, pair_send, pair_recv, send, recv):
        self.mine, self.paired, self.inbox = mine, paired, inbox
        self.pair_send, self.pair_recv, self.send, self.recv = pair_send, pair_recv, send, recv
        self.s, self.pairs = lax.axis_index("seq"), lax.axis_size("seq") // 2
        self.side, self.own = lax.rem(self.s, 2), self.s // 2
        self.deep, self.half = mine.shape[1], mine.shape[2] // 2
        self.levels = self.pairs.bit_length() - 1
        assert self.pairs == 1 << self.levels

    def block(self, k, other=False):
        i = 2 * k + (1 - self.side if other else self.side)
        return pl.ds(pl.multiple_of(i * self.deep, self.deep), self.deep)

    def to_partner(self, src, k):
        return push(
            src, self.paired.at[k], self.pair_send.at[k], self.pair_recv.at[k],
            self.s + 1 - 2 * self.side, "seq",
        )

    def bit(self, i, level):
        return lax.rem(i // (1 << level), 2)

    def move(self, side, slot, k, level):
        columns = pl.ds(side * self.half, self.half)
        to = self.s + (1 - 2 * self.bit(self.own, level)) * (2 << level)
        return push(
            self.mine.at[k, :, columns], self.inbox.at[slot, :, columns],
            self.send.at[side, slot], self.recv.at[side, slot], to, "seq",
        )

    def moves(self, side, step):
        order = list(range(self.levels))
        if side:
            order.reverse()
        level, free = order[step], sorted(order[step + 1 :])
        fixed = sum((self.bit(self.own, d) * (1 << d) for d in order[:step]), 0)
        offset = self.pairs - (1 << (self.levels - step))
        here = self.bit(self.own, level) * (1 << level)
        for c in range(1 << len(free)):
            rest = fixed + sum(((c >> j) & 1) << d for j, d in enumerate(free))
            yield offset + c, rest + here, rest + (1 << level) - here, level

    def pass_on(self, k):
        top = 1 << (self.levels - 1)
        pl.when(self.bit(k, 0) != self.bit(self.own, 0))(self.move(0, k // 2, k, 0).start)
        pl.when(k // top != self.own // top)(
            self.move(1, lax.rem(k, top), k, self.levels - 1).start
        )

    def advance(self, step):
        for side in range(2):
            columns = slice(side * self.half, (side + 1) * self.half)
            for slot, keep, gone, level in self.moves(side, step):
                self.move(side, slot, gone, level).wait_recv()
                self.mine[keep, :, columns] = (
                    self.mine[keep, :, columns].astype(F32)
                    + self.inbox[slot, :, columns].astype(F32)
                ).astype(BF16)
            if step + 1 < self.levels:
                for slot, keep, gone, level in self.moves(side, step + 1):
                    self.move(side, slot, gone, level).start()

    def finish(self, src):
        for k in range(self.pairs):
            self.to_partner(src(k), k).wait_send()
        for side in range(2):
            for step in range(self.levels):
                for slot, keep, gone, level in self.moves(side, step):
                    self.move(side, slot, gone, level).wait_send()


def gather_norm_kernel(own, gain, shard, normed, rows_of_all, rows_all, here_sem, send, recv,
                       w_sem, w_peer, w_pair, w_recv):
    z, count, rows = lax.axis_index("head"), lax.axis_size("head"), own.shape[0]
    greet(("seq", "head"))
    line = Line(own, rows_all, send, recv)
    line.start()
    here = pltpu.make_async_copy(own, line.at(z), here_sem)
    here.start()

    s, deep = lax.axis_index("seq"), shard.shape[0]
    side, pairs, own_pair = lax.rem(s, 2), lax.axis_size("seq") // 2, s // 2
    partner = s + 1 - 2 * side

    def shard_at(i):
        return rows_of_all.at[pl.ds(pl.multiple_of(i * deep, deep), deep)]

    def to_peer(k):
        return push(shard, shard_at(s), w_peer.at[k], w_recv.at[s], 2 * k + side, "seq")

    def from_peer(k):
        i = 2 * k + side
        return push(shard, shard_at(i), w_peer.at[k], w_recv.at[i], partner, "seq")

    def to_partner(k):
        i = 2 * k + side
        return push(shard_at(i), shard_at(i), w_pair.at[k], w_recv.at[i], partner, "seq")

    def from_partner(k):
        i = 2 * k + 1 - side
        return push(shard_at(i), shard_at(i), w_pair.at[k], w_recv.at[i], partner, "seq")

    mine = pltpu.make_async_copy(shard, shard_at(s), w_sem)
    mine.start()
    for k in range(pairs):
        pl.when(own_pair != k)(to_peer(k).start)
    mine.wait()
    to_partner(own_pair).start()
    here.wait()
    band = 16

    def step(i, _):
        b = near_order(z, count, i)
        pl.when(i > 0)(lambda: line.receive(i, b))

        def norm(r, _):
            at = pl.ds(pl.multiple_of(b * rows + r * band, band), band)
            x = rows_all[at, :].astype(F32)
            inv = lax.rsqrt(jnp.mean(x * x, axis=-1, keepdims=True) + 1e-6)
            normed[at, :] = (x * inv * gain[...]).astype(BF16)
            return 0

        lax.fori_loop(0, rows // band, norm, 0)
        return 0

    lax.fori_loop(0, count, step, 0)
    for k in range(pairs):

        @pl.when(own_pair != k)
        def _():
            from_peer(k).wait_recv()
            to_partner(k).start()

    for k in range(pairs):
        from_partner(k).wait_recv()
    for k in range(pairs):
        to_partner(k).wait_send()
        pl.when(own_pair != k)(to_peer(k).wait_send)
    line.finish()


def gather_norm(x, gain, shard):
    rows, width = x.shape
    seq = lax.axis_size("seq")
    anywhere = pl.BlockSpec(memory_space=pl.ANY)
    count = lax.axis_size("head")
    vmem = pl.BlockSpec(memory_space=pltpu.VMEM)
    dma = pltpu.SemaphoreType.DMA
    return pl.pallas_call(
        gather_norm_kernel,
        out_shape=(
            jax.ShapeDtypeStruct((count * rows, width), BF16),
            jax.ShapeDtypeStruct((seq * shard.shape[0], shard.shape[1]), BF16),
        ),
        in_specs=[vmem, vmem, anywhere],
        out_specs=(vmem, anywhere),
        scratch_shapes=[
            pltpu.VMEM((count * rows, width), BF16), dma(()), dma((count + 1,)), dma((count,)),
            dma(()), dma((seq // 2,)), dma((seq // 2,)), dma((seq,)),
        ],
        compiler_params=pltpu.CompilerParams(
            collective_id=1, has_side_effects=True, vmem_limit_bytes=32 << 20
        ),
        cost_estimate=cost(50),
        name="gather_norm",
    )(x, gain, shard)


def swap_slices(own, got, send, recv):
    me, count = lax.axis_index("seq"), lax.axis_size("seq")

    def copy(hop, index):
        to = lax.rem(me + hop, count)
        return push(own.at[to], got.at[index], send.at[hop], recv.at[index], to, "seq")

    def start(hop, _):
        copy(hop, me).start()
        return 0

    def wait_recv(hop, _):
        copy(hop, lax.rem(me + hop, count)).wait_recv()
        return 0

    def wait_send(hop, _):
        copy(hop, me).wait_send()
        return 0

    def begin():
        lax.fori_loop(1, count, start, 0)
        got[me] = own[me]

    def end():
        lax.fori_loop(1, count, wait_recv, 0)

    def drain():
        lax.fori_loop(1, count, wait_send, 0)

    return begin, end, drain


def scan_states(reverse, own, through, out):
    count, part = out.shape[0], out.shape[2]

    def step(k, state):
        j = count - 1 - k if reverse else k
        out[j] = state.astype(BF16)
        decay = through[j, :, 0:1, :].astype(F32) + through[j, :, 1:2, :].astype(F32)
        return decay * state + own[j, :, :part, :].astype(F32)

    lax.fori_loop(0, count, step, jnp.zeros(out.shape[1:], F32))


def total_kernel(own, out, from_seq, part, from_head, send_a, recv_a, send_b, recv_b,
                 send_c, recv_c, send_d, recv_d):
    seq, head = lax.axis_size("seq"), lax.axis_size("head")
    s, h = lax.axis_index("seq"), lax.axis_index("head")
    greet(("seq", "head"))

    def each(axis, me, count, src, dst, send, recv):
        def copy(hop, index):
            to = lax.rem(me + hop, count)
            return push(src(to), dst(index), send.at[hop], recv.at[index], to, axis)

        for hop in range(1, count):
            copy(hop, me).start()
        for hop in range(1, count):
            copy(hop, lax.rem(me + hop, count)).wait_recv()
        return [copy(hop, me).wait_send for hop in range(1, count)]

    from_seq[s] = own[s]
    sent = each("seq", s, seq, lambda to: own.at[to], lambda i: from_seq.at[i], send_a, recv_a)
    part[...] = jnp.sum(from_seq[...], axis=0)
    from_head[h] = part[h]
    sent += each("head", h, head, lambda to: part.at[to], lambda i: from_head.at[i], send_b, recv_b)
    out[s, h] = jnp.sum(from_head[...], axis=0)
    sent += each("head", h, head, lambda _: out.at[s, h], lambda i: out.at[s, i], send_c, recv_c)
    sent += each("seq", s, seq, lambda _: out.at[s], lambda i: out.at[i], send_d, recv_d)
    for wait in sent:
        wait()


def total_of(parts):
    seq, head = lax.axis_size("seq"), lax.axis_size("head")
    flat = jnp.concatenate([p.reshape(-1) for p in parts])
    deep = -(-flat.shape[0] // (seq * head * 1024)) * 8
    flat = jnp.pad(flat, (0, seq * head * deep * 128 - flat.shape[0]))
    vmem = pl.BlockSpec(memory_space=pltpu.VMEM)
    dma = pltpu.SemaphoreType.DMA
    shape = (seq, head, deep, 128)
    whole = pl.pallas_call(
        total_kernel,
        out_shape=jax.ShapeDtypeStruct(shape, F32),
        in_specs=[vmem],
        out_specs=vmem,
        scratch_shapes=[
            pltpu.VMEM(shape, F32), pltpu.VMEM(shape[1:], F32), pltpu.VMEM(shape[1:], F32),
        ]
        + [dma((n,)) for n in (seq, seq, head, head, head, head, seq, seq)],
        compiler_params=pltpu.CompilerParams(collective_id=4, has_side_effects=True),
        cost_estimate=cost(15),
        name="total",
    )(flat.reshape(shape)).reshape(-1)
    result, at = [], 0
    for p in parts:
        result.append(whole[at : at + p.size].reshape(p.shape))
        at += p.size
    return result


def front_kernel(keep, qkv, decay, og, gain, rows_own, o_out, gated, through, kept_out, rows_all,
                 kept, runs, state, sending, got, scanned, before, leaving,
                 here_sem, go, come, s_send, s_recv, b_send, b_recv, z_send, z_recv, k_sem):
    h, head = lax.axis_index("head"), lax.axis_size("head")
    count, micro, rows, dk = decay.shape
    dv = og.shape[-1]
    slices, part = scanned.shape[0], scanned.shape[2]
    scale = dk ** (-0.5)
    greet(("seq", "head"))
    line = Line(rows_own, rows_all, go, come)
    line.start()
    here = pltpu.make_async_copy(rows_own, line.at(h), here_sem)
    here.start()

    state[...] = jnp.zeros_like(state)
    passed = [jnp.zeros((1, dk), F32)] * micro
    alive = [jnp.ones((1, dk), F32)] * micro
    for b in range(count):
        for m in range(micro):
            run = running(decay[b, m])
            runs[b, m] = run
            last = run[rows - 1 : rows, :]
            carried = qkv[b, m, :, dk : 2 * dk].astype(F32) * jnp.exp(last - run)
            fresh = mms((qkv[b, m, :, 2 * dk :],), split(carried), (0, 0))
            kept[b, m] = fresh
            state[m] = jnp.exp(last) * (state[m] * keep[b, m]) + fresh
            passed[m] = passed[m] + last
            alive[m] = alive[m] * keep[b, m]
    tail = sending.shape[2] - part
    at = lax.broadcasted_iota(jnp.int32, (tail, dk), 0)
    for m in range(micro):
        high, low = split(jnp.exp(passed[m]) * alive[m])
        extra = jnp.where(
            at == 0, high.astype(F32), jnp.where(at == 1, low.astype(F32), 0.0)
        ).astype(BF16)
        for i in range(slices):
            sending[i, m, :part, :] = state[m, i * part : (i + 1) * part, :].astype(BF16)
            sending[i, m, part:, :] = extra
    begin, end, drain = swap_slices(sending, got, s_send, s_recv)
    begin()
    causal = lower_ones(rows)

    def inside(b, _):
        for m in range(micro):
            run = runs[b, m]
            queried = split(qkv[b, m, :, :dk].astype(F32) * (jnp.exp(run) * scale))
            keyed = split(qkv[b, m, :, dk : 2 * dk].astype(F32) * jnp.exp(-run))
            scores = jnp.where(causal, mms(queried, keyed, (1, 1)), 0.0)
            o_out[b, m] = mms(split(scores), (qkv[b, m, :, 2 * dk :],), (1, 0))
        return 0

    lax.fori_loop(0, count, inside, 0)
    line.receive(1, near_order(h, head, 1))
    end()
    through[...] = got[:, :, part:, :]
    scan_states(False, got, through, scanned)
    begin_back, end_back, drain_back = swap_slices(scanned, before, b_send, b_recv)
    begin_back()
    line.receive(2, near_order(h, head, 2))
    end_back()
    for i in range(slices):
        state[:, i * part : (i + 1) * part, :] = before[i].astype(F32)

    def to_owner(b):
        columns = gated.at[:, pl.ds(pl.multiple_of(h * dv, dv), dv)]
        return push(leaving.at[b], columns, z_send.at[b], z_recv.at[h], b)

    def save(b):
        return pltpu.make_async_copy(kept.at[b], kept_out.at[b], k_sem.at[b])

    def across(b, _):
        for m in range(micro):
            run = runs[b, m]
            queried = split(qkv[b, m, :, :dk].astype(F32) * (jnp.exp(run) * scale))
            entry = state[m] * keep[b, m]
            state[m] = jnp.exp(run[rows - 1 : rows, :]) * entry + kept[b, m]
            kept[b, m] = entry
            o = o_out[b, m] + mms(queried, split(entry), (1, 1))
            o_out[b, m] = o
            inv = lax.rsqrt(jnp.mean(o * o, axis=-1, keepdims=True) + 1e-5)
            normed = (o * inv * gain[...]).astype(BF16).astype(F32)
            gate = og[b, m]
            leaving[b, m * rows : (m + 1) * rows, :] = (normed * gate * sigmoid(gate)).astype(BF16)
        save(b).start()
        pl.when(b != h)(to_owner(b).start)

        @pl.when(b == 1)
        def _():
            line.receive(3, near_order(h, head, 3))

        return 0

    lax.fori_loop(0, count, across, 0)
    gated[:, pl.ds(pl.multiple_of(h * dv, dv), dv)] = leaving[h]
    for hop in range(1, head):
        other = lax.rem(h + hop, head)
        columns = gated.at[:, pl.ds(pl.multiple_of(other * dv, dv), dv)]
        push(leaving.at[other], columns, z_send.at[other], z_recv.at[other], other).wait_recv()
        to_owner(other).wait_send()
    for b in range(count):
        save(b).wait()
    here.wait()
    line.finish()
    drain()
    drain_back()


def attention_forward(keep, qkv, decays, og, gain, rows_own):
    blocks, micro, rows, width = qkv.shape
    dk, dv = decays.shape[-1], og.shape[-1]
    head, seq = lax.axis_size("head"), lax.axis_size("seq")
    assert blocks == head and head == 4
    part, tail = dv // seq, 16
    own_rows = micro * rows
    vmem, anywhere = pl.BlockSpec(memory_space=pltpu.VMEM), pl.BlockSpec(memory_space=pl.ANY)
    dma = pltpu.SemaphoreType.DMA
    states, wider = (seq, micro, part, dk), (seq, micro, part + tail, dk)
    return pl.pallas_call(
        front_kernel,
        out_shape=(
            jax.ShapeDtypeStruct((blocks, micro, rows, dv), F32),
            jax.ShapeDtypeStruct((own_rows, head * dv), BF16),
            jax.ShapeDtypeStruct((seq, micro, tail, dk), BF16),
            jax.ShapeDtypeStruct((blocks, micro, dv, dk), F32),
            jax.ShapeDtypeStruct((head * rows_own.shape[0], rows_own.shape[1]), BF16),
        ),
        in_specs=[vmem] * 5 + [anywhere],
        out_specs=(vmem,) * 3 + (anywhere,) * 2,
        scratch_shapes=[
            pltpu.VMEM((blocks, micro, dv, dk), F32), pltpu.VMEM((blocks, micro, rows, dk), F32),
            pltpu.VMEM((micro, dv, dk), F32), pltpu.VMEM(wider, BF16), pltpu.VMEM(wider, BF16),
            pltpu.VMEM(states, BF16), pltpu.VMEM(states, BF16),
            pltpu.VMEM((blocks, own_rows, dv), BF16),
            dma(()), dma((head + 1,)), dma((head,)), dma((seq,)), dma((seq,)), dma((seq,)),
            dma((seq,)), dma((head,)), dma((head,)), dma((blocks,)),
        ],
        compiler_params=pltpu.CompilerParams(
            collective_id=2, has_side_effects=True, vmem_limit_bytes=40 << 20
        ),
        cost_estimate=cost(60),
        name="attention_forward",
    )(keep, qkv, decays, og, gain, rows_own)


def ffn_kernel(count, x_own, c_all, w, g_x, f_parts, grad,
               wv, xs, cs, act, lin, parts, landed, turned, turned_c, tiles,
               w_sem, own_sem, go_sem, x_sem, p_sem, q_sem, o_sem):
    z = lax.axis_index("head")
    rows, width = x_own.shape
    hidden = act.shape[1] // 3
    chunk = lambda b: pl.ds(pl.multiple_of(b * rows, rows), rows)

    weights = [
        pltpu.make_async_copy(
            w.at[:, pl.ds(k * hidden, hidden)], wv.at[:, pl.ds(k * hidden, hidden)], w_sem.at[k]
        )
        for k in range(3)
    ]
    own = [
        pltpu.make_async_copy(x_own, xs.at[chunk(z)], own_sem.at[0]),
        pltpu.make_async_copy(c_all, cs, own_sem.at[1]),
    ]
    for copy in own + weights:
        copy.start()
    greet(("head",))
    line = Line(x_own, xs, go_sem, x_sem)
    line.start()
    for copy in own + weights:
        copy.wait()

    total = LineSum(parts, landed, p_sem, q_sem, rows)

    def step(i, _):
        b = near_order(z, count, i)

        pl.when(i > 0)(lambda: line.receive(i, b))

        at = chunk(b)
        x = xs[at, :]
        lin[0] = jnp.dot(x, wv[:, :hidden], preferred_element_type=F32)
        lin[1] = jnp.dot(x, wv[:, hidden : 2 * hidden], preferred_element_type=F32)
        lin[2] = jnp.dot(cs[at, :], wv[:, 2 * hidden :], preferred_element_type=F32)
        band = 16

        def act_rows(r, _):
            here = pl.ds(pl.multiple_of(r * band, band), band)
            there = pl.ds(pl.multiple_of(b * rows + r * band, band), band)
            gate, up, g_product = lin[0, here, :], lin[1, here, :], lin[2, here, :]
            sig = sigmoid(gate)
            gated = gate * sig
            act[there, :hidden] = (g_product * up * sig * (1.0 + gate * (1.0 - sig))).astype(BF16)
            act[there, hidden : 2 * hidden] = (g_product * gated).astype(BF16)
            act[there, 2 * hidden :] = (gated * up).astype(BF16)
            return 0

        lax.fori_loop(0, rows // band, act_rows, 0)
        parts[at, :] = mm(act[at, : 2 * hidden], wv[:, : 2 * hidden], (1, 1), None).astype(BF16)

        @pl.when((i > 0) & jnp.logical_not(total.inner))
        def _():
            for p in range(total.pieces):
                total.onward(b, p).start()

        return 0

    lax.fori_loop(0, count, step, 0)

    high = tiles.shape[1]
    steps = width // high
    first = grad.shape[1] - 3 * hidden

    def store(t, r, k):
        down = pl.ds(pl.multiple_of(r * high, high), high)
        into = grad.at[down, pl.ds(first + k * hidden, hidden)]
        return pltpu.make_async_copy(tiles.at[lax.rem(t, 2)], into, o_sem.at[lax.rem(t, 2)])

    turned[...] = xs[...].T
    turned_c[...] = cs[...].T

    def tile(r, k):
        t = 3 * r + k

        @pl.when(t >= 2)
        def _():
            store(t, r, k).wait()

        left_rows = (turned_c if k == 2 else turned)[
            pl.ds(pl.multiple_of(r * high, high), high), :
        ]
        tiles[lax.rem(t, 2)] = jnp.dot(
            left_rows, act[:, k * hidden : (k + 1) * hidden], preferred_element_type=F32
        ).astype(BF16)
        store(t, r, k).start()

    def slab(r, _):
        tile(r, 0)
        tile(r, 1)
        total.relay_in_turn(2 * r)
        tile(r, 2)
        at = chunk(r)
        f_parts[r] = mm(act[at, 2 * hidden :], wv[:, 2 * hidden :], (1, 1), None).astype(BF16)
        total.relay_in_turn(2 * r + 1)
        return 0

    lax.fori_loop(0, steps, slab, 0)
    total.relay_last()
    total.result(g_x)
    total.finish()
    line.finish()
    store(3 * steps - 2, 0, 0).wait()
    store(3 * steps - 1, 0, 0).wait()


def feed_forward(x_own, c_all, w, hidden, count):
    rows, width = x_own.shape
    group = rows * count
    assert count == 4 and width % 4 == 0 and rows % 64 == 0
    anywhere = pl.BlockSpec(memory_space=pl.ANY)
    vmem = pl.BlockSpec(memory_space=pltpu.VMEM)
    dma = pltpu.SemaphoreType.DMA
    return pl.pallas_call(
        functools.partial(ffn_kernel, count),
        out_shape=(
            jax.ShapeDtypeStruct((rows, width), F32),
            jax.ShapeDtypeStruct((count, rows, width), BF16),
            jax.ShapeDtypeStruct(w.shape, BF16),
        ),
        in_specs=[anywhere] * 3,
        out_specs=(vmem, vmem, anywhere),
        scratch_shapes=[
            pltpu.VMEM((width, 3 * hidden), BF16),
            pltpu.VMEM((group, width), BF16),
            pltpu.VMEM((group, width), BF16),
            pltpu.VMEM((group, 3 * hidden), BF16),
            pltpu.VMEM((3, rows, hidden), F32),
            pltpu.VMEM((group, width), BF16),
            pltpu.VMEM((group + rows, width), BF16),
            pltpu.VMEM((width, group), BF16),
            pltpu.VMEM((width, group), BF16),
            pltpu.VMEM((2, width // 4, hidden), BF16),
            dma((3,)), dma((2,)), dma((count + 1,)), dma((count,)),
            dma((count, 4)), dma((count + 1, 4)), dma((2,)),
        ],
        compiler_params=pltpu.CompilerParams(
            collective_id=0, has_side_effects=True, vmem_limit_bytes=60 << 20
        ),
        cost_estimate=cost(100),
        name="feed_forward",
    )(x_own, c_all, w)


def back_kernel(keep, gated_own, og, o_in, qkv, decay, logits, through, gain, kept_in, parts_in,
                g_proj, g_logits, g_gain, f_out,
                gated_all, go, runs, g_queried, g_keyed, g_values, pulls, weights, kept,
                parts, landed, state, sending, got, scanned, after, in_sem, z_send, z_recv, s_send, s_recv, b_send, b_recv, p_sem, q_sem):
    h, head = lax.axis_index("head"), lax.axis_size("head")
    count, micro, rows, dk = decay.shape
    dv = og.shape[-1]
    width = qkv.shape[-1]
    slices, part = sending.shape[0], sending.shape[2]
    scale = dk ** (-0.5)
    loads = [
        pltpu.make_async_copy(parts_in, parts, in_sem.at[0]),
        pltpu.make_async_copy(kept_in, kept, in_sem.at[1]),
    ]
    for load in loads:
        load.start()
    greet(("seq", "head"))

    def to_head(hop, slot):
        to = lax.rem(h + hop, head)
        columns = gated_own.at[:, pl.ds(pl.multiple_of(to * dv, dv), dv)]
        return push(columns, gated_all.at[slot], z_send.at[hop], z_recv.at[slot], to)

    for hop in range(1, head):
        to_head(hop, h).start()
    gated_all[h] = gated_own[:, pl.ds(pl.multiple_of(h * dv, dv), dv)]

    causal = lower_ones(rows)
    before = [jnp.zeros((1, dk), F32)] * micro
    alive = [jnp.ones((1, dk), F32)] * micro
    for b in range(count):
        for m in range(micro):
            run = running(decay[b, m])
            runs[b, m] = run
            alive[m] = alive[m] * keep[b, m]
            weights[b, m] = jnp.exp(before[m]) * alive[m]
            before[m] = before[m] + run[rows - 1 : rows, :]
    g_gain[...] = jnp.zeros_like(g_gain)
    state[...] = jnp.zeros_like(state)

    def gates(i, _):
        b = near_order(h, head, i)
        pl.when(i > 0)(lambda: to_head(lax.rem(b - h + head, head), b).wait_recv())
        for m in range(micro):
            gate, o = og[b, m], o_in[b, m]
            grad = gated_all[b, m * rows : (m + 1) * rows, :].astype(F32)
            sig = sigmoid(gate)
            inv = lax.rsqrt(jnp.mean(o * o, axis=-1, keepdims=True) + 1e-5)
            plain = o * inv
            normed = (plain * gain[...]).astype(BF16).astype(F32)
            g_on = (grad * gate * sig).astype(BF16).astype(F32)
            g_proj[b, m, :, width:] = (
                grad * normed * sig * (1.0 + gate * (1.0 - sig))
            ).astype(BF16)
            scaled = g_on * gain[...]
            g_o = inv * (scaled - plain * jnp.mean(scaled * plain, axis=-1, keepdims=True))
            go[b, m] = g_o
            g_gain[0:1, :] += jnp.sum(g_on * plain, axis=0, keepdims=True)
            queried = qkv[b, m, :, :dk].astype(F32) * (jnp.exp(runs[b, m]) * scale)
            pull = mms(split(g_o), split(queried), (0, 0))
            pulls[b, m] = pull
            state[m] += pull * weights[b, m]
        return 0

    lax.fori_loop(0, head, gates, 0)
    for i in range(slices):
        sending[i] = state[:, i * part : (i + 1) * part, :].astype(BF16)
    begin, end, drain = swap_slices(sending, got, s_send, s_recv)
    begin()
    for load in loads:
        load.wait()
    total = LineSum(parts, landed, p_sem, q_sem, f_out.shape[0])
    total.send_all()

    def inside(b, _):
        for m in range(micro):
            q = qkv[b, m, :, :dk].astype(F32)
            k = qkv[b, m, :, dk : 2 * dk].astype(F32)
            v = (qkv[b, m, :, 2 * dk :],)
            run = runs[b, m]
            queried, keyed = split(q * (jnp.exp(run) * scale)), split(k * jnp.exp(-run))
            g_o, entry = split(go[b, m]), split(kept[b, m])
            scores = split(jnp.where(causal, mms(queried, keyed, (1, 1)), 0.0))
            g_scores = split(jnp.where(causal, mms(g_o, v, (1, 1)), 0.0))
            g_queried[b, m] = mms(g_scores, keyed, (1, 0)) + mms(g_o, entry, (1, 0))
            g_keyed[b, m] = mms(g_scores, queried, (0, 0))
            g_values[b, m] = mms(scores, g_o, (0, 0))
        pl.when(total.inner)(lambda: total.relay(total.far_end, b))
        return 0

    lax.fori_loop(0, count, inside, 0)
    end()
    scan_states(True, got, through, scanned)
    begin_back, end_back, drain_back = swap_slices(scanned, after, b_send, b_recv)
    begin_back()

    @pl.when(total.inner)
    def _():
        for p in range(total.pieces):
            total.relay(head - 1 - total.far_end, p)
        for p in range(total.pieces):
            total.relay(head - 1 - h, p)

    end_back()
    for i in range(slices):
        state[:, i * part : (i + 1) * part, :] = after[i].astype(F32)

    def across(step, _):
        b = count - 1 - step
        for m in range(micro):
            q = qkv[b, m, :, :dk].astype(F32)
            k = qkv[b, m, :, dk : 2 * dk].astype(F32)
            v = (qkv[b, m, :, 2 * dk :],)
            run = runs[b, m]
            last = run[rows - 1 : rows, :]
            up, down, rest = jnp.exp(run) * scale, jnp.exp(-run), jnp.exp(last - run)
            decayed = jnp.exp(last)
            gs = state[m]
            gs_parts = split(gs)
            carried = k * rest
            g_v = g_values[b, m] + mms(split(carried), gs_parts, (1, 1))
            g_carried = mms(v, gs_parts, (1, 0))
            from_carried = g_carried * carried
            g_total = jnp.sum(decayed * kept[b, m] * gs, axis=0, keepdims=True) + jnp.sum(
                from_carried, axis=0, keepdims=True
            )
            state[m] = (decayed * gs + pulls[b, m]) * keep[b, m]
            gq, gk = g_queried[b, m], g_keyed[b, m]
            g_run = gq * (q * up) - gk * (k * down) - from_carried
            later = mms((causal.astype(F32).astype(BF16),), split(g_run), (0, 0)) + g_total
            g_proj[b, m, :, :dk] = (gq * up).astype(BF16)
            g_proj[b, m, :, dk : 2 * dk] = (gk * down + g_carried * rest).astype(BF16)
            g_proj[b, m, :, 2 * dk : width] = g_v.astype(BF16)
            g_logits[b, m] = (
                later.astype(BF16).astype(F32) * sigmoid(-logits[b, m]) * (1.0 / GATE_NORM)
            )
        return 0

    lax.fori_loop(0, count, across, 0)
    total.result(f_out)
    total.finish()
    drain()
    drain_back()
    for hop in range(1, head):
        to_head(hop, h).wait_send()


def attention_back(
    keep, gated_own, og, o, qkv, decays, logits, through, gain, kept, parts
):
    blocks, micro, rows, width = qkv.shape
    dk, dv = decays.shape[-1], og.shape[-1]
    head, seq = lax.axis_size("head"), lax.axis_size("seq")
    own_rows = parts.shape[0] // head
    vmem, anywhere = pl.BlockSpec(memory_space=pltpu.VMEM), pl.BlockSpec(memory_space=pl.ANY)
    dma = pltpu.SemaphoreType.DMA
    blocked = lambda w, kind: pltpu.VMEM((blocks, micro, rows, w), kind)
    states = (seq, micro, dv // seq, dk)
    return pl.pallas_call(
        back_kernel,
        out_shape=(
            jax.ShapeDtypeStruct((blocks, micro, rows, width + dv), BF16),
            jax.ShapeDtypeStruct((blocks, micro, rows, dk), F32),
            jax.ShapeDtypeStruct((8, dv), F32),
            jax.ShapeDtypeStruct((own_rows, parts.shape[1]), F32),
        ),
        in_specs=[vmem] * 9 + [anywhere] * 2,
        out_specs=(vmem,) * 4,
        scratch_shapes=[
            pltpu.VMEM((blocks, micro * rows, dv), BF16), blocked(dv, F32), blocked(dk, F32),
            blocked(dk, F32), blocked(dk, F32), blocked(dv, F32),
            pltpu.VMEM((blocks, micro, dv, dk), F32), pltpu.VMEM((blocks, micro, 1, dk), F32),
            pltpu.VMEM((blocks, micro, dv, dk), F32),
            pltpu.VMEM(parts.shape, BF16),
            pltpu.VMEM((parts.shape[0] + own_rows, parts.shape[1]), BF16),
            pltpu.VMEM((micro, dv, dk), F32),
            pltpu.VMEM(states, BF16), pltpu.VMEM(states, BF16), pltpu.VMEM(states, BF16),
            pltpu.VMEM(states, BF16),
            dma((2,)), dma((head,)), dma((head,)), dma((seq,)), dma((seq,)), dma((seq,)),
            dma((seq,)), dma((head, 4)), dma((head + 1, 4)),
        ],
        compiler_params=pltpu.CompilerParams(
            collective_id=3, has_side_effects=True, vmem_limit_bytes=60 << 20
        ),
        cost_estimate=cost(80),
        name="attention_back",
    )(keep, gated_own, og, o, qkv, decays, logits, through, gain, kept, parts)


def finish_kernel(xn_in, proj_in, w_in, g_logits, ranked, up_own, rank_down,
                  g_x, grad, g_down, g_up, g_bias,
                  turned, proj, w, outgoing, mine, paired, inbox, heads_in, parts, landed,
                  slim_high, slim_low, in_sem, pair_send, pair_recv, send, recv, x_send, x_recv,
                  p_sem, q_sem):
    h, head = lax.axis_index("head"), lax.axis_size("head")
    rows, width = g_x.shape
    deep = grad.shape[0] * head
    pairs = lax.axis_size("seq") // 2

    loads = [
        pltpu.make_async_copy(proj_in, proj, in_sem.at[0]),
        pltpu.make_async_copy(w_in, w, in_sem.at[1]),
        pltpu.make_async_copy(xn_in, landed.at[pl.ds(0, xn_in.shape[0])], in_sem.at[2]),
    ]
    for load in loads:
        load.start()
    sums = PairSum(mine, paired, inbox, pair_send, pair_recv, send, recv)
    for load in loads:
        load.wait()
    turned[...] = landed[: xn_in.shape[0], :].T
    greet(("seq", "head"))
    total = LineSum(parts, landed, p_sem, q_sem, rows)
    logit_parts = split(g_logits[...])
    g_ranked = mms(logit_parts, split(up_own[...]), (1, 1))
    slim = split(g_ranked)
    slim_high[...], slim_low[...] = slim

    def chunk(i, _):
        b = near_order(h, head, head - 1 - i)
        at = pl.ds(pl.multiple_of(b * rows, rows), rows)
        rank_part = mms((slim_high[at, :], slim_low[at, :]), (rank_down[...],), (1, 1))
        parts[at, :] = (mm(proj[at, :], w[...], (1, 1), None) + rank_part).astype(BF16)

        @pl.when((b != h) & jnp.logical_not(total.inner))
        def _():
            for p in range(total.pieces):
                total.onward(b, p).start()

        return 0

    lax.fori_loop(0, head, chunk, 0)

    def gone(k, _):
        outgoing[k] = jnp.dot(
            turned[sums.block(k, True), :], proj[...], preferred_element_type=F32
        ).astype(BF16)
        sums.to_partner(outgoing.at[k], k).start()
        return 0

    lax.fori_loop(0, pairs, gone, 0)

    def kept(k, _):
        here = jnp.dot(turned[sums.block(k), :], proj[...], preferred_element_type=F32)
        sums.to_partner(outgoing.at[k], k).wait_recv()
        mine[k] = (here + paired[k].astype(F32)).astype(BF16)
        sums.pass_on(k)

        @pl.when(total.inner & (k < total.pieces))
        def _():
            total.relay(total.far_end, k)

        @pl.when(total.inner & (k > 0) & (k <= total.pieces))
        def _():
            total.relay(head - 1 - total.far_end, k - 1)

        return 0

    lax.fori_loop(0, pairs, kept, 0)

    @pl.when(total.inner)
    def _():
        for p in range(pairs, total.pieces + 1):
            if p < total.pieces:
                total.relay(total.far_end, p)
            total.relay(head - 1 - total.far_end, p - 1)
        for p in range(total.pieces):
            total.relay(head - 1 - h, p)

    g_down[...] = mms((turned[...],), slim, (1, 0))
    g_up[...] = mms(split(ranked[...]), logit_parts, (0, 0))
    g_bias[...] = jnp.broadcast_to(jnp.sum(g_logits[...], axis=0, keepdims=True), g_bias.shape)

    thin = grad.shape[0]

    def to_head(hop, slot):
        to = lax.rem(h + hop, head)
        at = pl.ds(pl.multiple_of(to * thin, thin), thin)
        return push(mine.at[sums.own, at, :], heads_in.at[slot], x_send.at[hop], x_recv.at[slot], to)

    for step in range(sums.levels):
        sums.advance(step)
    for hop in range(1, head):
        to_head(hop, h).start()
    own_rows = pl.ds(pl.multiple_of(h * thin, thin), thin)
    heads_in[h] = mine[sums.own, own_rows, :]
    total.result(g_x)
    for hop in range(1, head):
        to_head(hop, lax.rem(h + hop, head)).wait_recv()
    dk = g_up.shape[1]
    dv = mine.shape[2] // 2 - dk
    for j in range(head):
        at, start = 0, 0
        for size in (dk, dk, dv, dv):
            grad[:, start + j * size : start + (j + 1) * size] = heads_in[
                j, :, at : at + size
            ].astype(F32)
            at, start = at + size, start + head * size
    sums.finish(lambda k: outgoing.at[k])
    for hop in range(1, head):
        to_head(hop, h).wait_send()
    total.finish()


def finish(xn, g_proj, w_in, g_logits, ranked, up_own, rank_down):
    seq, head = lax.axis_size("seq"), lax.axis_size("head")
    group, width = xn.shape
    columns, rank = w_in.shape[1], ranked.shape[1]
    deep, rows, pairs = width // seq, group // head, seq // 2
    dk = up_own.shape[1]
    vmem, anywhere = pl.BlockSpec(memory_space=pltpu.VMEM), pl.BlockSpec(memory_space=pl.ANY)
    dma = pltpu.SemaphoreType.DMA
    blocks = lambda count, w: pltpu.VMEM((count, deep, w), BF16)
    ends = lambda w: pltpu.VMEM((head, deep // head, w), BF16)
    moves = dma((2, pairs - 1))
    return pl.pallas_call(
        finish_kernel,
        out_shape=(
            jax.ShapeDtypeStruct((rows, width), F32),
            jax.ShapeDtypeStruct((deep // head, columns * head), F32),
            jax.ShapeDtypeStruct((width, rank), F32),
            jax.ShapeDtypeStruct((rank, dk), F32),
            jax.ShapeDtypeStruct((8, dk), F32),
        ),
        in_specs=[anywhere] * 3 + [vmem] * 4,
        out_specs=(vmem,) * 5,
        scratch_shapes=[
            pltpu.VMEM((width, group), BF16), pltpu.VMEM(g_proj.shape, BF16),
            pltpu.VMEM(w_in.shape, BF16), blocks(pairs, columns), blocks(pairs, columns),
            blocks(pairs, columns), blocks(pairs - 1, columns), ends(columns),
            pltpu.VMEM((group, width), BF16), pltpu.VMEM((group + rows, width), BF16),
            pltpu.VMEM(ranked.shape, BF16), pltpu.VMEM(ranked.shape, BF16),
            dma((3,)), dma((pairs,)), dma((pairs,)), moves, moves, dma((head,)), dma((head,)),
            dma((head, 4)), dma((head + 1, 4)),
        ],
        compiler_params=pltpu.CompilerParams(
            collective_id=5, has_side_effects=True, vmem_limit_bytes=60 << 20
        ),
        cost_estimate=cost(60),
        name="finish",
    )(xn, g_proj, w_in, g_logits, ranked, up_own, rank_down)


def weight_grad_kernel(left, right, *rest):
    out, turned = rest[-2:]

    @pl.when(pl.program_id(1) == 0)
    def _():
        turned[...] = left[...].T

    out[...] = jnp.dot(turned[...], right[...], preferred_element_type=F32).astype(BF16)


def weight_grad(left, right, into, columns, start, tile):
    depth, rows = left.shape
    high = min(rows, 512)
    first = start // tile
    given = () if into is None else (into,)
    return pl.pallas_call(
        weight_grad_kernel,
        out_shape=jax.ShapeDtypeStruct((rows, columns), BF16),
        grid=(rows // high, right.shape[1] // tile),
        in_specs=[
            pl.BlockSpec((depth, high), lambda i, j: (0, i)),
            pl.BlockSpec((depth, tile), lambda i, j: (0, j)),
        ]
        + [pl.BlockSpec(memory_space=pl.ANY) for _ in given],
        out_specs=pl.BlockSpec((high, tile), lambda i, j: (i, first + j)),
        scratch_shapes=[pltpu.VMEM((high, depth), BF16)],
        input_output_aliases={2: 0} if given else {},
        compiler_params=pltpu.CompilerParams(
            dimension_semantics=("arbitrary", "arbitrary"), vmem_limit_bytes=48 << 20
        ),
        cost_estimate=pl.CostEstimate(
            flops=2 * depth * rows * right.shape[1],
            bytes_accessed=2 * (depth * rows + (depth + rows) * right.shape[1]),
            transcendentals=0,
        ),
        name="weight_grad",
    )(left, right, *given)


def gather_weight(w):
    return lax.all_gather(w, "seq", axis=0, tiled=True)


def scatter_grad(g):
    return lax.psum_scatter(g.astype(BF16), "seq", scatter_dimension=0, tiled=True)


def dot(a, b, contract, precision=None):
    return lax.dot_general(
        a, b, (((contract[0],), (contract[1],)), ((), ())),
        precision=precision, preferred_element_type=F32,
    )


def rms(x, epsilon):
    return lax.rsqrt(jnp.mean(x * x, axis=-1, keepdims=True) + epsilon)


def norm_back(grad, gain, normed, inv):
    scaled = grad * gain
    inner = jnp.mean(scaled * normed, axis=-1, keepdims=True)
    return inv * (scaled - normed * inner), jnp.sum(grad * normed, axis=0)


def on_device(
    tokens, starts, cotangent, mix_in, mix_out, gate_up, down_proj,
    norm_gain, ffn_gain, head_gain, rank_down, rank_up, gate_bias,
):
    micro, rows, width = tokens.shape
    heads, seq = lax.axis_size("head"), lax.axis_size("seq")
    head = lax.axis_index("head")
    keys, dv = rank_up.shape[1], head_gain.shape[0]
    dk, vals = keys // heads, dv * heads
    hidden_units = down_proj.shape[1]
    group = heads * micro * rows
    proj_width = 2 * dk + 2 * dv

    def own_columns(w, start, size):
        return lax.dynamic_slice_in_dim(w, start + head * size, size, 1)

    w_in_own = jnp.concatenate(
        [
            own_columns(mix_in, 0, dk),
            own_columns(mix_in, keys, dk),
            own_columns(mix_in, 2 * keys, dv),
            own_columns(mix_in, 2 * keys + vals, dv),
        ],
        axis=1,
    )
    later = gather_weight(
        jnp.concatenate(
            [gate_up.reshape(gate_up.shape[0], 2 * hidden_units), down_proj, mix_out], axis=1
        )
    )
    w_out = later[:, 3 * hidden_units :]
    up_own = own_columns(rank_up, 0, dk)
    bias_own = lax.dynamic_slice_in_dim(gate_bias, head * dk, dk, 0)

    xn, w_in = gather_norm(
        tokens.reshape(micro * rows, width), norm_gain.reshape(1, width), w_in_own
    )
    qkv = dot(xn, w_in[:, : 2 * dk + dv], (1, 0)).astype(BF16)
    og = dot(xn, w_in[:, 2 * dk + dv :], (1, 0))
    ranked = dot(xn, rank_down, (1, 0))
    logits = dot(ranked, up_own, (1, 0), HIGHEST) + bias_own
    decays = (jax.nn.log_sigmoid(logits) / GATE_NORM).astype(BF16)

    def blocks(x):
        return x.reshape(heads, micro, rows, x.shape[-1])

    qkv_b, og_b, decays_b = blocks(qkv), blocks(og), blocks(decays)
    gain_row = head_gain.reshape(1, dv)
    keep = 1.0 - jnp.broadcast_to(starts.T[:, :, None, None], (heads, micro, 1, dk)).astype(F32)
    o_b, gated, through, kept, all_cot = attention_forward(
        keep, qkv_b, decays_b, og_b, gain_row, cotangent.reshape(micro * rows, width)
    )

    source = tokens.astype(F32).reshape(micro * rows, width)
    hidden = source + dot(gated, w_out, (1, 1))
    inv_ffn = rms(hidden, 1e-6)
    plain_ffn = hidden * inv_ffn
    h2 = (plain_ffn * ffn_gain).astype(BF16)

    g_h2, ffn_part, grads = feed_forward(h2, all_cot, later, hidden_units, heads)

    back_ffn, g_ffn_gain = norm_back(g_h2, ffn_gain, plain_ffn, inv_ffn)
    g_hidden = cotangent.astype(F32).reshape(micro * rows, width) + back_ffn
    g_mixed = g_hidden.astype(BF16)
    grads = scatter_grad(weight_grad(g_mixed, gated, grads, later.shape[1], 0, dv))
    g_gated = dot(g_mixed, w_out, (1, 0)).astype(BF16)
    g_proj_b, g_logits_b, g_head_gain, ffn_out = attention_back(
        keep, g_gated, og_b, o_b, qkv_b, decays_b, blocks(logits), through, gain_row, kept, ffn_part.reshape(group, width),
    )
    output = (hidden + ffn_out).astype(BF16)
    g_proj, g_logits = g_proj_b.reshape(group, proj_width), g_logits_b.reshape(group, dk)
    g_xn, grad_in, g_rank_down, g_rank_up, g_bias = finish(
        xn, g_proj, w_in, g_logits, ranked, up_own, rank_down
    )
    inv_in = rms(source, 1e-6)
    back_in, g_norm_gain = norm_back(g_xn, norm_gain, source * inv_in, inv_in)
    input_grad = g_hidden + back_in

    g_rank_up = lax.dynamic_update_slice_in_dim(
        jnp.zeros(rank_up.shape, F32), g_rank_up, head * dk, 1
    )
    g_bias = lax.dynamic_update_slice_in_dim(
        jnp.zeros(gate_bias.shape, F32), g_bias[0], head * dk, 0
    )
    small = total_of(
        [g_norm_gain, g_ffn_gain, g_head_gain[0], g_rank_down, g_rank_up, g_bias]
    )
    slab = width // (seq * heads)
    grad_ffn = grads[:, vals:]
    grad_out = lax.all_to_all(
        grads[:, :vals].reshape(heads, slab, vals), "head", split_axis=0, concat_axis=0, tiled=True
    )
    grad_out = grad_out.astype(F32).sum(0)
    return (
        output.reshape(tokens.shape),
        input_grad.reshape(tokens.shape),
        grad_in,
        grad_out,
        grad_ffn[:, : 2 * hidden_units].astype(F32).reshape(-1, 2, hidden_units),
        grad_ffn[:, 2 * hidden_units :].astype(F32),
        *small,
    )


def solution(mesh):
    rows = P(None, ("seq", "head"), None)
    return jax.shard_map(
        on_device,
        mesh=mesh,
        in_specs=(
            rows, P(None, "seq"), rows, P("seq", None), P("seq", None),
            P("seq", None, "head"), P("seq", "head"), P(), P(), P(), P(), P(), P(),
        ),
        out_specs=(
            rows, rows, P(("seq", "head"), None), P(("seq", "head"), None),
            P("seq", None, "head"), P("seq", "head"), P(), P(), P(), P(), P(), P(),
        ),
        check_vma=False,
    )
```

```python
import functools

import jax
import jax.numpy as jnp
from jax import lax
from jax.experimental import pallas as pl
from jax.experimental.pallas import tpu as pltpu
from jax.sharding import PartitionSpec as P

HIGHEST = lax.Precision.HIGHEST
GATE_NORM = 16.0
BF16 = jnp.bfloat16
F32 = jnp.float32


def mm(a, b, contract, precision=HIGHEST):
    return lax.dot_general(
        a, b, ((contract[:1], contract[1:]), ((), ())),
        precision=precision, preferred_element_type=F32,
    )


def split(x):
    high = x.astype(BF16)
    return high, (x - high.astype(F32)).astype(BF16)


def mms(left, right, contract):
    total = mm(left[0], right[0], contract, None)
    if len(right) > 1:
        total += mm(left[0], right[1], contract, None)
    if len(left) > 1:
        total += mm(left[1], right[0], contract, None)
    return total


def lower_ones(size):
    rows = lax.broadcasted_iota(jnp.int32, (size, size), 0)
    cols = lax.broadcasted_iota(jnp.int32, (size, size), 1)
    return rows >= cols


def running(decay_low):
    ones = lower_ones(decay_low.shape[0]).astype(F32).astype(BF16)
    return mm(ones, decay_low, (1, 0), None)


def sigmoid(x):
    return 1.0 / (1.0 + jnp.exp(-x))


def cost(micros):
    return pl.CostEstimate(flops=0, bytes_accessed=int(micros * 3.0e6), transcendentals=0)


def greet(axes):
    barrier = pltpu.get_barrier_semaphore()
    met = 0
    for axis in axes:
        me, count = lax.axis_index(axis), lax.axis_size(axis)
        for hop in range(1, count):
            pl.semaphore_signal(
                barrier, inc=1, device_id={axis: lax.rem(me + hop, count)},
                device_id_type=pl.DeviceIdType.MESH,
            )
        met += count - 1
    pl.semaphore_wait(barrier, met)


def push(src, dst, send, recv, to, axis="head"):
    return pltpu.make_async_remote_copy(
        src_ref=src, dst_ref=dst, send_sem=send, recv_sem=recv,
        device_id={axis: to}, device_id_type=pl.DeviceIdType.MESH,
    )


def near_order(z, count, i):
    both = jnp.minimum(z, count - 1 - z)
    left = z > count - 1 - z
    paired = jnp.where(i % 2 == 1, z - (i + 1) // 2, z + i // 2)
    single = jnp.where(left, z - (i - both), z + (i - both))
    return jnp.where(i <= 2 * both, paired, single)


class Line:
    def __init__(self, own, all_rows, send, recv):
        self.own, self.all, self.send, self.recv = own, all_rows, send, recv
        self.z, self.count, self.rows = lax.axis_index("head"), lax.axis_size("head"), own.shape[0]
        z, count = self.z, self.count
        self.right = push(own, self.at(z), send.at[0], recv.at[z], lax.rem(z + 1, count))
        self.left = push(own, self.at(z), send.at[1], recv.at[z], lax.rem(z + count - 1, count))

    def chunk(self, b):
        return pl.ds(pl.multiple_of(b * self.rows, self.rows), self.rows)

    def at(self, b):
        return self.all.at[self.chunk(b)]

    def start(self):
        pl.when(self.z < self.count - 1)(self.right.start)
        pl.when(self.z > 0)(self.left.start)

    def passing(self, i, b):
        z, count = self.z, self.count
        to = jnp.where(b < z, z + 1, z - 1)
        going = ((b < z) & (z < count - 1)) | ((b > z) & (z > 0))
        copy = push(
            self.at(b), self.at(b), self.send.at[i + 1], self.recv.at[b], lax.rem(to + count, count)
        )
        return copy, going

    def receive(self, i, b):
        copy, going = self.passing(i, b)
        copy.wait_recv()
        pl.when(going)(copy.start)

    def finish(self):
        def sent(i, _):
            copy, going = self.passing(i, near_order(self.z, self.count, i))
            pl.when(going)(copy.wait_send)
            return 0

        lax.fori_loop(1, self.count, sent, 0)
        pl.when(self.z < self.count - 1)(self.right.wait_send)
        pl.when(self.z > 0)(self.left.wait_send)


class LineSum:
    def __init__(self, parts, landed, send, recv, rows):
        self.parts, self.landed, self.send, self.recv = parts, landed, send, recv
        self.z, self.count = lax.axis_index("head"), lax.axis_size("head")
        self.rows, self.pieces = rows, send.shape[1]
        self.deep = rows // self.pieces
        self.inner = (self.z > 0) & (self.z < self.count - 1)
        self.far_end = jnp.where(self.z < self.count - 1 - self.z, self.count - 1, 0)

    def piece(self, b, p):
        return pl.ds(pl.multiple_of(b * self.rows + p * self.deep, self.deep), self.deep)

    def onward(self, b, p):
        z, count = self.z, self.count
        to = jnp.where(b > z, z + 1, z - 1)
        slot = jnp.where((to == b) & (z > b), count, b)
        return push(
            self.parts.at[self.piece(b, p)], self.landed.at[self.piece(slot, p)],
            self.send.at[b, p], self.recv.at[slot, p], lax.rem(to + count, count),
        )

    def send_all(self):
        @pl.when(jnp.logical_not(self.inner))
        def _():
            for i in range(1, self.count):
                b = jnp.where(self.z == 0, self.count - i, i - 1)
                for p in range(self.pieces):
                    self.onward(b, p).start()

    def arrived(self, slot, p):
        at = self.piece(slot, p)
        push(
            self.landed.at[at], self.landed.at[at], self.send.at[0, p], self.recv.at[slot, p],
            lax.rem(self.z + 1, self.count),
        ).wait_recv()
        return self.landed[at, :].astype(F32)

    def relay(self, b, p):
        at = self.piece(b, p)
        self.parts[at, :] = (self.parts[at, :].astype(F32) + self.arrived(b, p)).astype(BF16)
        self.onward(b, p).start()

    def relay_in_turn(self, j):
        pieces = self.pieces

        @pl.when(self.inner & (j < pieces))
        def _():
            self.relay(self.count - 1 - self.z, j)

        @pl.when(self.inner & (j >= pieces))
        def _():
            self.relay(self.far_end, j - pieces)

        @pl.when(self.inner & (j > pieces))
        def _():
            self.relay(self.count - 1 - self.far_end, j - pieces - 1)

    def relay_last(self):
        @pl.when(self.inner)
        def _():
            self.relay(self.count - 1 - self.far_end, self.pieces - 1)

    def result(self, out):
        z, count = self.z, self.count
        for p in range(self.pieces):
            here = pl.ds(p * self.deep, self.deep)
            out[here, :] = self.parts[self.piece(z, p), :].astype(F32)

            @pl.when(z > 0)
            def _():
                out[here, :] += self.arrived(z, p)

            @pl.when(z < count - 1)
            def _():
                out[here, :] += self.arrived(count, p)

    def finish(self):
        def sent(i, _):
            b = near_order(self.z, self.count, i)
            for p in range(self.pieces):
                self.onward(b, p).wait_send()
            return 0

        lax.fori_loop(1, self.count, sent, 0)


class PairSum:
    def __init__(self, mine, paired, inbox, pair_send, pair_recv, send, recv):
        self.mine, self.paired, self.inbox = mine, paired, inbox
        self.pair_send, self.pair_recv, self.send, self.recv = pair_send, pair_recv, send, recv
        self.s, self.pairs = lax.axis_index("seq"), lax.axis_size("seq") // 2
        self.side, self.own = lax.rem(self.s, 2), self.s // 2
        self.deep, self.half = mine.shape[1], mine.shape[2] // 2
        self.levels = self.pairs.bit_length() - 1
        assert self.pairs == 1 << self.levels

    def block(self, k, other=False):
        i = 2 * k + (1 - self.side if other else self.side)
        return pl.ds(pl.multiple_of(i * self.deep, self.deep), self.deep)

    def to_partner(self, src, k):
        return push(
            src, self.paired.at[k], self.pair_send.at[k], self.pair_recv.at[k],
            self.s + 1 - 2 * self.side, "seq",
        )

    def bit(self, i, level):
        return lax.rem(i // (1 << level), 2)

    def move(self, side, slot, k, level):
        columns = pl.ds(side * self.half, self.half)
        to = self.s + (1 - 2 * self.bit(self.own, level)) * (2 << level)
        return push(
            self.mine.at[k, :, columns], self.inbox.at[slot, :, columns],
            self.send.at[side, slot], self.recv.at[side, slot], to, "seq",
        )

    def moves(self, side, step):
        order = list(range(self.levels))
        if side:
            order.reverse()
        level, free = order[step], sorted(order[step + 1 :])
        fixed = sum((self.bit(self.own, d) * (1 << d) for d in order[:step]), 0)
        offset = self.pairs - (1 << (self.levels - step))
        here = self.bit(self.own, level) * (1 << level)
        for c in range(1 << len(free)):
            rest = fixed + sum(((c >> j) & 1) << d for j, d in enumerate(free))
            yield offset + c, rest + here, rest + (1 << level) - here, level

    def pass_on(self, k):
        top = 1 << (self.levels - 1)
        pl.when(self.bit(k, 0) != self.bit(self.own, 0))(self.move(0, k // 2, k, 0).start)
        pl.when(k // top != self.own // top)(
            self.move(1, lax.rem(k, top), k, self.levels - 1).start
        )

    def advance(self, step):
        for side in range(2):
            columns = slice(side * self.half, (side + 1) * self.half)
            for slot, keep, gone, level in self.moves(side, step):
                self.move(side, slot, gone, level).wait_recv()
                self.mine[keep, :, columns] = (
                    self.mine[keep, :, columns].astype(F32)
                    + self.inbox[slot, :, columns].astype(F32)
                ).astype(BF16)
            if step + 1 < self.levels:
                for slot, keep, gone, level in self.moves(side, step + 1):
                    self.move(side, slot, gone, level).start()

    def finish(self, src):
        for k in range(self.pairs):
            self.to_partner(src(k), k).wait_send()
        for side in range(2):
            for step in range(self.levels):
                for slot, keep, gone, level in self.moves(side, step):
                    self.move(side, slot, gone, level).wait_send()


def gather_norm_kernel(own, gain, shard, normed, rows_of_all, rows_all, here_sem, send, recv,
                       w_sem, w_peer, w_pair, w_recv):
    z, count, rows = lax.axis_index("head"), lax.axis_size("head"), own.shape[0]
    greet(("seq", "head"))
    line = Line(own, rows_all, send, recv)
    line.start()
    here = pltpu.make_async_copy(own, line.at(z), here_sem)
    here.start()

    s, deep = lax.axis_index("seq"), shard.shape[0]
    side, pairs, own_pair = lax.rem(s, 2), lax.axis_size("seq") // 2, s // 2
    partner = s + 1 - 2 * side

    def shard_at(i):
        return rows_of_all.at[pl.ds(pl.multiple_of(i * deep, deep), deep)]

    def to_peer(k):
        return push(shard, shard_at(s), w_peer.at[k], w_recv.at[s], 2 * k + side, "seq")

    def from_peer(k):
        i = 2 * k + side
        return push(shard, shard_at(i), w_peer.at[k], w_recv.at[i], partner, "seq")

    def to_partner(k):
        i = 2 * k + side
        return push(shard_at(i), shard_at(i), w_pair.at[k], w_recv.at[i], partner, "seq")

    def from_partner(k):
        i = 2 * k + 1 - side
        return push(shard_at(i), shard_at(i), w_pair.at[k], w_recv.at[i], partner, "seq")

    mine = pltpu.make_async_copy(shard, shard_at(s), w_sem)
    mine.start()
    for k in range(pairs):
        pl.when(own_pair != k)(to_peer(k).start)
    mine.wait()
    to_partner(own_pair).start()
    here.wait()
    band = 16

    def step(i, _):
        b = near_order(z, count, i)
        pl.when(i > 0)(lambda: line.receive(i, b))

        def norm(r, _):
            at = pl.ds(pl.multiple_of(b * rows + r * band, band), band)
            x = rows_all[at, :].astype(F32)
            inv = lax.rsqrt(jnp.mean(x * x, axis=-1, keepdims=True) + 1e-6)
            normed[at, :] = (x * inv * gain[...]).astype(BF16)
            return 0

        lax.fori_loop(0, rows // band, norm, 0)
        return 0

    lax.fori_loop(0, count, step, 0)
    for k in range(pairs):

        @pl.when(own_pair != k)
        def _():
            from_peer(k).wait_recv()
            to_partner(k).start()

    for k in range(pairs):
        from_partner(k).wait_recv()
    for k in range(pairs):
        to_partner(k).wait_send()
        pl.when(own_pair != k)(to_peer(k).wait_send)
    line.finish()


def gather_norm(x, gain, shard):
    rows, width = x.shape
    seq = lax.axis_size("seq")
    anywhere = pl.BlockSpec(memory_space=pl.ANY)
    count = lax.axis_size("head")
    vmem = pl.BlockSpec(memory_space=pltpu.VMEM)
    dma = pltpu.SemaphoreType.DMA
    return pl.pallas_call(
        gather_norm_kernel,
        out_shape=(
            jax.ShapeDtypeStruct((count * rows, width), BF16),
            jax.ShapeDtypeStruct((seq * shard.shape[0], shard.shape[1]), BF16),
        ),
        in_specs=[vmem, vmem, anywhere],
        out_specs=(vmem, anywhere),
        scratch_shapes=[
            pltpu.VMEM((count * rows, width), BF16), dma(()), dma((count + 1,)), dma((count,)),
            dma(()), dma((seq // 2,)), dma((seq // 2,)), dma((seq,)),
        ],
        compiler_params=pltpu.CompilerParams(
            collective_id=1, has_side_effects=True, vmem_limit_bytes=32 << 20
        ),
        cost_estimate=cost(50),
        name="gather_norm",
    )(x, gain, shard)


def swap_slices(own, got, send, recv):
    me, count = lax.axis_index("seq"), lax.axis_size("seq")

    def copy(hop, index):
        to = lax.rem(me + hop, count)
        return push(own.at[to], got.at[index], send.at[hop], recv.at[index], to, "seq")

    def start(hop, _):
        copy(hop, me).start()
        return 0

    def wait_recv(hop, _):
        copy(hop, lax.rem(me + hop, count)).wait_recv()
        return 0

    def wait_send(hop, _):
        copy(hop, me).wait_send()
        return 0

    def begin():
        lax.fori_loop(1, count, start, 0)
        got[me] = own[me]

    def end():
        lax.fori_loop(1, count, wait_recv, 0)

    def drain():
        lax.fori_loop(1, count, wait_send, 0)

    return begin, end, drain


def scan_states(reverse, own, through, out):
    count, part = out.shape[0], out.shape[2]

    def step(k, state):
        j = count - 1 - k if reverse else k
        out[j] = state.astype(BF16)
        decay = through[j, :, 0:1, :].astype(F32) + through[j, :, 1:2, :].astype(F32)
        return decay * state + own[j, :, :part, :].astype(F32)

    lax.fori_loop(0, count, step, jnp.zeros(out.shape[1:], F32))


def front_kernel(keep, qkv, decay, og, gain, rows_own, o_out, gated, through, kept_out, rows_all,
                 kept, runs, state, sending, got, scanned, before, leaving,
                 here_sem, go, come, s_send, s_recv, b_send, b_recv, z_send, z_recv, k_sem):
    h, head = lax.axis_index("head"), lax.axis_size("head")
    count, micro, rows, dk = decay.shape
    dv = og.shape[-1]
    slices, part = scanned.shape[0], scanned.shape[2]
    scale = dk ** (-0.5)
    greet(("seq", "head"))
    line = Line(rows_own, rows_all, go, come)
    line.start()
    here = pltpu.make_async_copy(rows_own, line.at(h), here_sem)
    here.start()

    state[...] = jnp.zeros_like(state)
    passed = [jnp.zeros((1, dk), F32)] * micro
    alive = [jnp.ones((1, dk), F32)] * micro
    for b in range(count):
        for m in range(micro):
            run = running(decay[b, m])
            runs[b, m] = run
            last = run[rows - 1 : rows, :]
            carried = qkv[b, m, :, dk : 2 * dk].astype(F32) * jnp.exp(last - run)
            fresh = mms((qkv[b, m, :, 2 * dk :],), split(carried), (0, 0))
            kept[b, m] = fresh
            state[m] = jnp.exp(last) * (state[m] * keep[b, m]) + fresh
            passed[m] = passed[m] + last
            alive[m] = alive[m] * keep[b, m]
    tail = sending.shape[2] - part
    at = lax.broadcasted_iota(jnp.int32, (tail, dk), 0)
    for m in range(micro):
        high, low = split(jnp.exp(passed[m]) * alive[m])
        extra = jnp.where(
            at == 0, high.astype(F32), jnp.where(at == 1, low.astype(F32), 0.0)
        ).astype(BF16)
        for i in range(slices):
            sending[i, m, :part, :] = state[m, i * part : (i + 1) * part, :].astype(BF16)
            sending[i, m, part:, :] = extra
    begin, end, drain = swap_slices(sending, got, s_send, s_recv)
    begin()
    causal = lower_ones(rows)

    def inside(b, _):
        for m in range(micro):
            run = runs[b, m]
            queried = split(qkv[b, m, :, :dk].astype(F32) * (jnp.exp(run) * scale))
            keyed = split(qkv[b, m, :, dk : 2 * dk].astype(F32) * jnp.exp(-run))
            scores = jnp.where(causal, mms(queried, keyed, (1, 1)), 0.0)
            o_out[b, m] = mms(split(scores), (qkv[b, m, :, 2 * dk :],), (1, 0))
        return 0

    lax.fori_loop(0, count, inside, 0)
    line.receive(1, near_order(h, head, 1))
    end()
    through[...] = got[:, :, part:, :]
    scan_states(False, got, through, scanned)
    begin_back, end_back, drain_back = swap_slices(scanned, before, b_send, b_recv)
    begin_back()
    line.receive(2, near_order(h, head, 2))
    end_back()
    for i in range(slices):
        state[:, i * part : (i + 1) * part, :] = before[i].astype(F32)

    def to_owner(b):
        columns = gated.at[:, pl.ds(pl.multiple_of(h * dv, dv), dv)]
        return push(leaving.at[b], columns, z_send.at[b], z_recv.at[h], b)

    def save(b):
        return pltpu.make_async_copy(kept.at[b], kept_out.at[b], k_sem.at[b])

    def across(b, _):
        for m in range(micro):
            run = runs[b, m]
            queried = split(qkv[b, m, :, :dk].astype(F32) * (jnp.exp(run) * scale))
            entry = state[m] * keep[b, m]
            state[m] = jnp.exp(run[rows - 1 : rows, :]) * entry + kept[b, m]
            kept[b, m] = entry
            o = o_out[b, m] + mms(queried, split(entry), (1, 1))
            o_out[b, m] = o
            inv = lax.rsqrt(jnp.mean(o * o, axis=-1, keepdims=True) + 1e-5)
            normed = (o * inv * gain[...]).astype(BF16).astype(F32)
            gate = og[b, m]
            leaving[b, m * rows : (m + 1) * rows, :] = (normed * gate * sigmoid(gate)).astype(BF16)
        save(b).start()
        pl.when(b != h)(to_owner(b).start)

        @pl.when(b == 1)
        def _():
            line.receive(3, near_order(h, head, 3))

        return 0

    lax.fori_loop(0, count, across, 0)
    gated[:, pl.ds(pl.multiple_of(h * dv, dv), dv)] = leaving[h]
    for hop in range(1, head):
        other = lax.rem(h + hop, head)
        columns = gated.at[:, pl.ds(pl.multiple_of(other * dv, dv), dv)]
        push(leaving.at[other], columns, z_send.at[other], z_recv.at[other], other).wait_recv()
        to_owner(other).wait_send()
    for b in range(count):
        save(b).wait()
    here.wait()
    line.finish()
    drain()
    drain_back()


def attention_forward(keep, qkv, decays, og, gain, rows_own):
    blocks, micro, rows, width = qkv.shape
    dk, dv = decays.shape[-1], og.shape[-1]
    head, seq = lax.axis_size("head"), lax.axis_size("seq")
    assert blocks == head and head == 4
    part, tail = dv // seq, 16
    own_rows = micro * rows
    vmem, anywhere = pl.BlockSpec(memory_space=pltpu.VMEM), pl.BlockSpec(memory_space=pl.ANY)
    dma = pltpu.SemaphoreType.DMA
    states, wider = (seq, micro, part, dk), (seq, micro, part + tail, dk)
    return pl.pallas_call(
        front_kernel,
        out_shape=(
            jax.ShapeDtypeStruct((blocks, micro, rows, dv), F32),
            jax.ShapeDtypeStruct((own_rows, head * dv), BF16),
            jax.ShapeDtypeStruct((seq, micro, tail, dk), BF16),
            jax.ShapeDtypeStruct((blocks, micro, dv, dk), F32),
            jax.ShapeDtypeStruct((head * rows_own.shape[0], rows_own.shape[1]), BF16),
        ),
        in_specs=[vmem] * 5 + [anywhere],
        out_specs=(vmem,) * 3 + (anywhere,) * 2,
        scratch_shapes=[
            pltpu.VMEM((blocks, micro, dv, dk), F32), pltpu.VMEM((blocks, micro, rows, dk), F32),
            pltpu.VMEM((micro, dv, dk), F32), pltpu.VMEM(wider, BF16), pltpu.VMEM(wider, BF16),
            pltpu.VMEM(states, BF16), pltpu.VMEM(states, BF16),
            pltpu.VMEM((blocks, own_rows, dv), BF16),
            dma(()), dma((head + 1,)), dma((head,)), dma((seq,)), dma((seq,)), dma((seq,)),
            dma((seq,)), dma((head,)), dma((head,)), dma((blocks,)),
        ],
        compiler_params=pltpu.CompilerParams(
            collective_id=2, has_side_effects=True, vmem_limit_bytes=40 << 20
        ),
        cost_estimate=cost(90),
        name="attention_forward",
    )(keep, qkv, decays, og, gain, rows_own)


def ffn_kernel(count, x_own, c_all, w, g_x, f_parts, grad,
               wv, xs, cs, act, lin, parts, landed, turned, turned_c, tiles,
               w_sem, own_sem, go_sem, x_sem, p_sem, q_sem, o_sem):
    z = lax.axis_index("head")
    rows, width = x_own.shape
    hidden = act.shape[1] // 3
    chunk = lambda b: pl.ds(pl.multiple_of(b * rows, rows), rows)

    weights = [
        pltpu.make_async_copy(
            w.at[:, pl.ds(k * hidden, hidden)], wv.at[:, pl.ds(k * hidden, hidden)], w_sem.at[k]
        )
        for k in range(3)
    ]
    own = [
        pltpu.make_async_copy(x_own, xs.at[chunk(z)], own_sem.at[0]),
        pltpu.make_async_copy(c_all, cs, own_sem.at[1]),
    ]
    for copy in own + weights:
        copy.start()
    greet(("head",))
    line = Line(x_own, xs, go_sem, x_sem)
    line.start()
    for copy in own + weights:
        copy.wait()

    total = LineSum(parts, landed, p_sem, q_sem, rows)

    def step(i, _):
        b = near_order(z, count, i)

        pl.when(i > 0)(lambda: line.receive(i, b))

        at = chunk(b)
        x = xs[at, :]
        lin[0] = jnp.dot(x, wv[:, :hidden], preferred_element_type=F32)
        lin[1] = jnp.dot(x, wv[:, hidden : 2 * hidden], preferred_element_type=F32)
        lin[2] = jnp.dot(cs[at, :], wv[:, 2 * hidden :], preferred_element_type=F32)
        band = 16

        def act_rows(r, _):
            here = pl.ds(pl.multiple_of(r * band, band), band)
            there = pl.ds(pl.multiple_of(b * rows + r * band, band), band)
            gate, up, g_product = lin[0, here, :], lin[1, here, :], lin[2, here, :]
            sig = sigmoid(gate)
            gated = gate * sig
            act[there, :hidden] = (g_product * up * sig * (1.0 + gate * (1.0 - sig))).astype(BF16)
            act[there, hidden : 2 * hidden] = (g_product * gated).astype(BF16)
            act[there, 2 * hidden :] = (gated * up).astype(BF16)
            return 0

        lax.fori_loop(0, rows // band, act_rows, 0)
        parts[at, :] = mm(act[at, : 2 * hidden], wv[:, : 2 * hidden], (1, 1), None).astype(BF16)

        @pl.when((i > 0) & jnp.logical_not(total.inner))
        def _():
            for p in range(total.pieces):
                total.onward(b, p).start()

        return 0

    lax.fori_loop(0, count, step, 0)

    high = tiles.shape[1]
    steps = width // high
    first = grad.shape[1] - 3 * hidden

    def store(t, r, k):
        down = pl.ds(pl.multiple_of(r * high, high), high)
        into = grad.at[down, pl.ds(first + k * hidden, hidden)]
        return pltpu.make_async_copy(tiles.at[lax.rem(t, 2)], into, o_sem.at[lax.rem(t, 2)])

    turned[...] = xs[...].T
    turned_c[...] = cs[...].T

    def tile(r, k):
        t = 3 * r + k

        @pl.when(t >= 2)
        def _():
            store(t, r, k).wait()

        left_rows = (turned_c if k == 2 else turned)[
            pl.ds(pl.multiple_of(r * high, high), high), :
        ]
        tiles[lax.rem(t, 2)] = jnp.dot(
            left_rows, act[:, k * hidden : (k + 1) * hidden], preferred_element_type=F32
        ).astype(BF16)
        store(t, r, k).start()

    def slab(r, _):
        tile(r, 0)
        tile(r, 1)
        total.relay_in_turn(2 * r)
        tile(r, 2)
        at = chunk(r)
        f_parts[r] = mm(act[at, 2 * hidden :], wv[:, 2 * hidden :], (1, 1), None).astype(BF16)
        total.relay_in_turn(2 * r + 1)
        return 0

    lax.fori_loop(0, steps, slab, 0)
    total.relay_last()
    total.result(g_x)
    total.finish()
    line.finish()
    store(3 * steps - 2, 0, 0).wait()
    store(3 * steps - 1, 0, 0).wait()


def feed_forward(x_own, c_all, w, hidden, count):
    rows, width = x_own.shape
    group = rows * count
    assert count == 4 and width % 4 == 0 and rows % 64 == 0
    anywhere = pl.BlockSpec(memory_space=pl.ANY)
    vmem = pl.BlockSpec(memory_space=pltpu.VMEM)
    dma = pltpu.SemaphoreType.DMA
    return pl.pallas_call(
        functools.partial(ffn_kernel, count),
        out_shape=(
            jax.ShapeDtypeStruct((rows, width), F32),
            jax.ShapeDtypeStruct((count, rows, width), BF16),
            jax.ShapeDtypeStruct(w.shape, BF16),
        ),
        in_specs=[anywhere] * 3,
        out_specs=(vmem, vmem, anywhere),
        scratch_shapes=[
            pltpu.VMEM((width, 3 * hidden), BF16),
            pltpu.VMEM((group, width), BF16),
            pltpu.VMEM((group, width), BF16),
            pltpu.VMEM((group, 3 * hidden), BF16),
            pltpu.VMEM((3, rows, hidden), F32),
            pltpu.VMEM((group, width), BF16),
            pltpu.VMEM((group + rows, width), BF16),
            pltpu.VMEM((width, group), BF16),
            pltpu.VMEM((width, group), BF16),
            pltpu.VMEM((2, width // 4, hidden), BF16),
            dma((3,)), dma((2,)), dma((count + 1,)), dma((count,)),
            dma((count, 4)), dma((count + 1, 4)), dma((2,)),
        ],
        compiler_params=pltpu.CompilerParams(
            collective_id=0, has_side_effects=True, vmem_limit_bytes=60 << 20
        ),
        cost_estimate=cost(100),
        name="feed_forward",
    )(x_own, c_all, w)


def back_kernel(keep, gated_own, og, o_in, qkv, decay, logits, through, gain, kept_in, parts_in,
                g_proj, g_logits, g_gain, f_out,
                gated_all, go, runs, g_queried, g_keyed, g_values, pulls, weights, kept,
                parts, landed, state, sending, got, scanned, after, in_sem, z_send, z_recv, s_send, s_recv, b_send, b_recv, p_sem, q_sem):
    h, head = lax.axis_index("head"), lax.axis_size("head")
    count, micro, rows, dk = decay.shape
    dv = og.shape[-1]
    width = qkv.shape[-1]
    slices, part = sending.shape[0], sending.shape[2]
    scale = dk ** (-0.5)
    loads = [
        pltpu.make_async_copy(parts_in, parts, in_sem.at[0]),
        pltpu.make_async_copy(kept_in, kept, in_sem.at[1]),
    ]
    for load in loads:
        load.start()
    greet(("seq", "head"))

    def to_head(hop, slot):
        to = lax.rem(h + hop, head)
        columns = gated_own.at[:, pl.ds(pl.multiple_of(to * dv, dv), dv)]
        return push(columns, gated_all.at[slot], z_send.at[hop], z_recv.at[slot], to)

    for hop in range(1, head):
        to_head(hop, h).start()
    gated_all[h] = gated_own[:, pl.ds(pl.multiple_of(h * dv, dv), dv)]

    causal = lower_ones(rows)
    before = [jnp.zeros((1, dk), F32)] * micro
    alive = [jnp.ones((1, dk), F32)] * micro
    for b in range(count):
        for m in range(micro):
            run = running(decay[b, m])
            runs[b, m] = run
            alive[m] = alive[m] * keep[b, m]
            weights[b, m] = jnp.exp(before[m]) * alive[m]
            before[m] = before[m] + run[rows - 1 : rows, :]
    g_gain[...] = jnp.zeros_like(g_gain)
    state[...] = jnp.zeros_like(state)

    def gates(i, _):
        b = near_order(h, head, i)
        pl.when(i > 0)(lambda: to_head(lax.rem(b - h + head, head), b).wait_recv())
        for m in range(micro):
            gate, o = og[b, m], o_in[b, m]
            grad = gated_all[b, m * rows : (m + 1) * rows, :].astype(F32)
            sig = sigmoid(gate)
            inv = lax.rsqrt(jnp.mean(o * o, axis=-1, keepdims=True) + 1e-5)
            plain = o * inv
            normed = (plain * gain[...]).astype(BF16).astype(F32)
            g_on = (grad * gate * sig).astype(BF16).astype(F32)
            g_proj[b, m, :, width:] = (
                grad * normed * sig * (1.0 + gate * (1.0 - sig))
            ).astype(BF16)
            scaled = g_on * gain[...]
            g_o = inv * (scaled - plain * jnp.mean(scaled * plain, axis=-1, keepdims=True))
            go[b, m] = g_o
            g_gain[0:1, :] += jnp.sum(g_on * plain, axis=0, keepdims=True)
            queried = qkv[b, m, :, :dk].astype(F32) * (jnp.exp(runs[b, m]) * scale)
            pull = mms(split(g_o), split(queried), (0, 0))
            pulls[b, m] = pull
            state[m] += pull * weights[b, m]
        return 0

    lax.fori_loop(0, head, gates, 0)
    for i in range(slices):
        sending[i] = state[:, i * part : (i + 1) * part, :].astype(BF16)
    begin, end, drain = swap_slices(sending, got, s_send, s_recv)
    begin()
    for load in loads:
        load.wait()
    total = LineSum(parts, landed, p_sem, q_sem, f_out.shape[0])
    total.send_all()

    def inside(b, _):
        for m in range(micro):
            q = qkv[b, m, :, :dk].astype(F32)
            k = qkv[b, m, :, dk : 2 * dk].astype(F32)
            v = (qkv[b, m, :, 2 * dk :],)
            run = runs[b, m]
            queried, keyed = split(q * (jnp.exp(run) * scale)), split(k * jnp.exp(-run))
            g_o, entry = split(go[b, m]), split(kept[b, m])
            scores = split(jnp.where(causal, mms(queried, keyed, (1, 1)), 0.0))
            g_scores = split(jnp.where(causal, mms(g_o, v, (1, 1)), 0.0))
            g_queried[b, m] = mms(g_scores, keyed, (1, 0)) + mms(g_o, entry, (1, 0))
            g_keyed[b, m] = mms(g_scores, queried, (0, 0))
            g_values[b, m] = mms(scores, g_o, (0, 0))
        pl.when(total.inner)(lambda: total.relay(total.far_end, b))
        return 0

    lax.fori_loop(0, count, inside, 0)
    end()
    scan_states(True, got, through, scanned)
    begin_back, end_back, drain_back = swap_slices(scanned, after, b_send, b_recv)
    begin_back()

    @pl.when(total.inner)
    def _():
        for p in range(total.pieces):
            total.relay(head - 1 - total.far_end, p)
        for p in range(total.pieces):
            total.relay(head - 1 - h, p)

    end_back()
    for i in range(slices):
        state[:, i * part : (i + 1) * part, :] = after[i].astype(F32)

    def across(step, _):
        b = count - 1 - step
        for m in range(micro):
            q = qkv[b, m, :, :dk].astype(F32)
            k = qkv[b, m, :, dk : 2 * dk].astype(F32)
            v = (qkv[b, m, :, 2 * dk :],)
            run = runs[b, m]
            last = run[rows - 1 : rows, :]
            up, down, rest = jnp.exp(run) * scale, jnp.exp(-run), jnp.exp(last - run)
            decayed = jnp.exp(last)
            gs = state[m]
            gs_parts = split(gs)
            carried = k * rest
            g_v = g_values[b, m] + mms(split(carried), gs_parts, (1, 1))
            g_carried = mms(v, gs_parts, (1, 0))
            from_carried = g_carried * carried
            g_total = jnp.sum(decayed * kept[b, m] * gs, axis=0, keepdims=True) + jnp.sum(
                from_carried, axis=0, keepdims=True
            )
            state[m] = (decayed * gs + pulls[b, m]) * keep[b, m]
            gq, gk = g_queried[b, m], g_keyed[b, m]
            g_run = gq * (q * up) - gk * (k * down) - from_carried
            later = mms((causal.astype(F32).astype(BF16),), split(g_run), (0, 0)) + g_total
            g_proj[b, m, :, :dk] = (gq * up).astype(BF16)
            g_proj[b, m, :, dk : 2 * dk] = (gk * down + g_carried * rest).astype(BF16)
            g_proj[b, m, :, 2 * dk : width] = g_v.astype(BF16)
            g_logits[b, m] = (
                later.astype(BF16).astype(F32) * sigmoid(-logits[b, m]) * (1.0 / GATE_NORM)
            )
        return 0

    lax.fori_loop(0, count, across, 0)
    total.result(f_out)
    total.finish()
    drain()
    drain_back()
    for hop in range(1, head):
        to_head(hop, h).wait_send()


def attention_back(
    keep, gated_own, og, o, qkv, decays, logits, through, gain, kept, parts
):
    blocks, micro, rows, width = qkv.shape
    dk, dv = decays.shape[-1], og.shape[-1]
    head, seq = lax.axis_size("head"), lax.axis_size("seq")
    own_rows = parts.shape[0] // head
    vmem, anywhere = pl.BlockSpec(memory_space=pltpu.VMEM), pl.BlockSpec(memory_space=pl.ANY)
    dma = pltpu.SemaphoreType.DMA
    blocked = lambda w, kind: pltpu.VMEM((blocks, micro, rows, w), kind)
    states = (seq, micro, dv // seq, dk)
    return pl.pallas_call(
        back_kernel,
        out_shape=(
            jax.ShapeDtypeStruct((blocks, micro, rows, width + dv), BF16),
            jax.ShapeDtypeStruct((blocks, micro, rows, dk), F32),
            jax.ShapeDtypeStruct((8, dv), F32),
            jax.ShapeDtypeStruct((own_rows, parts.shape[1]), F32),
        ),
        in_specs=[vmem] * 9 + [anywhere] * 2,
        out_specs=(vmem,) * 4,
        scratch_shapes=[
            pltpu.VMEM((blocks, micro * rows, dv), BF16), blocked(dv, F32), blocked(dk, F32),
            blocked(dk, F32), blocked(dk, F32), blocked(dv, F32),
            pltpu.VMEM((blocks, micro, dv, dk), F32), pltpu.VMEM((blocks, micro, 1, dk), F32),
            pltpu.VMEM((blocks, micro, dv, dk), F32),
            pltpu.VMEM(parts.shape, BF16),
            pltpu.VMEM((parts.shape[0] + own_rows, parts.shape[1]), BF16),
            pltpu.VMEM((micro, dv, dk), F32),
            pltpu.VMEM(states, BF16), pltpu.VMEM(states, BF16), pltpu.VMEM(states, BF16),
            pltpu.VMEM(states, BF16),
            dma((2,)), dma((head,)), dma((head,)), dma((seq,)), dma((seq,)), dma((seq,)),
            dma((seq,)), dma((head, 4)), dma((head + 1, 4)),
        ],
        compiler_params=pltpu.CompilerParams(
            collective_id=3, has_side_effects=True, vmem_limit_bytes=60 << 20
        ),
        cost_estimate=cost(80),
        name="attention_back",
    )(keep, gated_own, og, o, qkv, decays, logits, through, gain, kept, parts)


def finish_kernel(xn_in, proj_in, w_in, g_logits, ranked, up_own, rank_down, source, g_hidden,
                  gain, g_ffn, g_head,
                  g_x, grad, norm_sum, ffn_sum, head_sum, bias_sum, up_sum, down_sum,
                  turned, proj, w, outgoing, mine, paired, inbox, heads_in, parts, landed,
                  slim_high, slim_low, small, small_in, small_part,
                  small_heads, small_all, rows_sum, in_sem, pair_send, pair_recv, send, recv, x_send, x_recv,
                  p_sem, q_sem, a_send, a_recv, b_send, b_recv, c_send, c_recv):
    h, head = lax.axis_index("head"), lax.axis_size("head")
    rows, width = g_x.shape
    deep = grad.shape[0] * head
    pairs = lax.axis_size("seq") // 2

    loads = [
        pltpu.make_async_copy(proj_in, proj, in_sem.at[0]),
        pltpu.make_async_copy(w_in, w, in_sem.at[1]),
        pltpu.make_async_copy(xn_in, landed.at[pl.ds(0, xn_in.shape[0])], in_sem.at[2]),
    ]
    for load in loads:
        load.start()
    sums = PairSum(mine, paired, inbox, pair_send, pair_recv, send, recv)
    for load in loads:
        load.wait()
    turned[...] = landed[: xn_in.shape[0], :].T
    greet(("seq", "head"))
    total = LineSum(parts, landed, p_sem, q_sem, rows)
    logit_parts = split(g_logits[...])
    g_ranked = mms(logit_parts, split(up_own[...]), (1, 1))
    slim = split(g_ranked)
    slim_high[...], slim_low[...] = slim

    def chunk(i, _):
        b = near_order(h, head, head - 1 - i)
        at = pl.ds(pl.multiple_of(b * rows, rows), rows)
        rank_part = mms((slim_high[at, :], slim_low[at, :]), (rank_down[...],), (1, 1))
        parts[at, :] = (mm(proj[at, :], w[...], (1, 1), None) + rank_part).astype(BF16)

        @pl.when((b != h) & jnp.logical_not(total.inner))
        def _():
            for p in range(total.pieces):
                total.onward(b, p).start()

        return 0

    lax.fori_loop(0, head, chunk, 0)

    def gone(k, _):
        outgoing[k] = jnp.dot(
            turned[sums.block(k, True), :], proj[...], preferred_element_type=F32
        ).astype(BF16)
        sums.to_partner(outgoing.at[k], k).start()
        return 0

    lax.fori_loop(0, pairs, gone, 0)

    def kept(k, _):
        here = jnp.dot(turned[sums.block(k), :], proj[...], preferred_element_type=F32)
        sums.to_partner(outgoing.at[k], k).wait_recv()
        mine[k] = (here + paired[k].astype(F32)).astype(BF16)
        sums.pass_on(k)

        @pl.when(total.inner & (k < total.pieces))
        def _():
            total.relay(total.far_end, k)

        @pl.when(total.inner & (k > 0) & (k <= total.pieces))
        def _():
            total.relay(head - 1 - total.far_end, k - 1)

        return 0

    lax.fori_loop(0, pairs, kept, 0)

    @pl.when(total.inner)
    def _():
        for p in range(pairs, total.pieces + 1):
            if p < total.pieces:
                total.relay(total.far_end, p)
            total.relay(head - 1 - total.far_end, p - 1)
        for p in range(total.pieces):
            total.relay(head - 1 - h, p)

    thin = grad.shape[0]

    def to_head(hop, slot):
        to = lax.rem(h + hop, head)
        at = pl.ds(pl.multiple_of(to * thin, thin), thin)
        return push(mine.at[sums.own, at, :], heads_in.at[slot], x_send.at[hop], x_recv.at[slot], to)

    sums.advance(0)

    total.result(g_x)
    rows_sum[...] = jnp.zeros_like(rows_sum)
    band = rows_sum.shape[0]

    def norm_rows(r, _):
        at = pl.ds(pl.multiple_of(r * band, band), band)
        x = source[at, :].astype(F32)
        inv = lax.rsqrt(jnp.mean(x * x, axis=-1, keepdims=True) + 1e-6)
        plain, g = x * inv, g_x[at, :]
        scaled = g * gain[...]
        inner = jnp.mean(scaled * plain, axis=-1, keepdims=True)
        rows_sum[...] += g * plain
        g_x[at, :] = g_hidden[at, :] + inv * (scaled - plain * inner)
        return 0

    lax.fori_loop(0, rows // band, norm_rows, 0)
    rank, dk = up_own.shape
    low, keys = rank // 2, up_sum.shape[1]
    g_down = mms(slim, (turned[...],), (0, 1))
    g_up = mms(split(ranked[...]), logit_parts, (0, 0))
    small[...] = jnp.zeros_like(small)
    small[:low, :width] = g_down[:low]
    small[:low, width:] = g_down[low:]
    own_keys = pl.multiple_of(h * dk, dk)
    small[low:, pl.ds(own_keys, dk)] = g_up[:low]
    small[low:, pl.ds(keys + own_keys, dk)] = g_up[low:]
    small[low : low + 1, width:] = jnp.sum(rows_sum[...], axis=0, keepdims=True)
    small[low + 1 : low + 2, width:] = g_ffn[...]
    small[low + 2 : low + 3, width : width + g_head.shape[1]] = g_head[0:1, :]
    small[low + 3 : low + 4, pl.ds(width + own_keys, dk)] = jnp.sum(
        g_logits[...], axis=0, keepdims=True
    )
    s, seq = lax.axis_index("seq"), lax.axis_size("seq")
    wide = small.shape[1] // seq

    def piece(ref, i):
        return ref.at[:, pl.ds(pl.multiple_of(i * wide, wide), wide)]

    def begin_small(axis, me, count, copy):
        for hop in range(1, count):
            copy(hop, me, lax.rem(me + hop, count)).start()

    def end_small(axis, me, count, copy):
        for hop in range(1, count):
            other = lax.rem(me + hop, count)
            copy(hop, other, other).wait_recv()

    def scatter(hop, slot, to):
        return push(
            piece(small, to), small_in.at[slot], a_send.at[hop], a_recv.at[slot], to, "seq"
        )

    def between(hop, slot, to):
        return push(small_part, small_heads.at[slot], b_send.at[hop], b_recv.at[slot], to)

    def spread(hop, slot, to):
        return push(
            small_part, piece(small_all, slot), c_send.at[hop], c_recv.at[slot], to, "seq"
        )

    begin_small("seq", s, seq, scatter)
    small_in[s] = small[:, pl.ds(pl.multiple_of(s * wide, wide), wide)]
    for step in range(1, sums.levels):
        sums.advance(step)
    for hop in range(1, head):
        to_head(hop, h).start()
    own_rows = pl.ds(pl.multiple_of(h * thin, thin), thin)
    heads_in[h] = mine[sums.own, own_rows, :]
    end_small("seq", s, seq, scatter)
    small_part[...] = jnp.sum(small_in[...], axis=0)
    begin_small("head", h, head, between)
    small_heads[h] = small_part[...]
    end_small("head", h, head, between)
    for hop in range(1, head):
        between(hop, h, lax.rem(h + hop, head)).wait_send()
    small_part[...] = jnp.sum(small_heads[...], axis=0)
    begin_small("seq", s, seq, spread)
    small_all[:, pl.ds(pl.multiple_of(s * wide, wide), wide)] = small_part[...]
    for hop in range(1, head):
        to_head(hop, lax.rem(h + hop, head)).wait_recv()
    dv = mine.shape[2] // 2 - dk
    for j in range(head):
        at, start = 0, 0
        for size in (dk, dk, dv, dv):
            grad[:, start + j * size : start + (j + 1) * size] = heads_in[
                j, :, at : at + size
            ].astype(F32)
            at, start = at + size, start + head * size
    end_small("seq", s, seq, spread)
    down_sum[:low, :] = small_all[:low, :width]
    down_sum[low:, :] = small_all[:low, width:]
    up_sum[:low, :] = small_all[low:, :keys]
    up_sum[low:, :] = small_all[low:, keys : 2 * keys]
    norm_sum[...] = small_all[low : low + 1, width:]
    ffn_sum[...] = small_all[low + 1 : low + 2, width:]
    head_sum[...] = small_all[low + 2 : low + 3, width : width + head_sum.shape[1]]
    bias_sum[...] = small_all[low + 3 : low + 4, width : width + keys]
    for hop in range(1, seq):
        scatter(hop, s, lax.rem(s + hop, seq)).wait_send()
        spread(hop, s, lax.rem(s + hop, seq)).wait_send()
    sums.finish(lambda k: outgoing.at[k])
    for hop in range(1, head):
        to_head(hop, h).wait_send()
    total.finish()


def finish(
    xn, g_proj, w_in, g_logits, ranked, up_own, rank_down, source, g_hidden, gain, g_ffn, g_head
):
    seq, head = lax.axis_size("seq"), lax.axis_size("head")
    group, width = xn.shape
    columns, rank = w_in.shape[1], ranked.shape[1]
    deep, rows, pairs = width // seq, group // head, seq // 2
    dk = up_own.shape[1]
    vmem, anywhere = pl.BlockSpec(memory_space=pltpu.VMEM), pl.BlockSpec(memory_space=pl.ANY)
    dma = pltpu.SemaphoreType.DMA
    blocks = lambda count, w: pltpu.VMEM((count, deep, w), BF16)
    ends = lambda w: pltpu.VMEM((head, deep // head, w), BF16)
    moves = dma((2, pairs - 1))
    return pl.pallas_call(
        finish_kernel,
        out_shape=(
            jax.ShapeDtypeStruct((rows, width), F32),
            jax.ShapeDtypeStruct((deep // head, columns * head), F32),
            jax.ShapeDtypeStruct((1, width), F32),
            jax.ShapeDtypeStruct((1, width), F32),
            jax.ShapeDtypeStruct((1, g_head.shape[1]), F32),
            jax.ShapeDtypeStruct((1, dk * head), F32),
            jax.ShapeDtypeStruct((rank, dk * head), F32),
            jax.ShapeDtypeStruct((rank, width), F32),
        ),
        in_specs=[anywhere] * 3 + [vmem] * 9,
        out_specs=(vmem,) * 8,
        scratch_shapes=[
            pltpu.VMEM((width, group), BF16), pltpu.VMEM(g_proj.shape, BF16),
            pltpu.VMEM(w_in.shape, BF16), blocks(pairs, columns), blocks(pairs, columns),
            blocks(pairs, columns), blocks(pairs - 1, columns), ends(columns),
            pltpu.VMEM((group, width), BF16), pltpu.VMEM((group + rows, width), BF16),
            pltpu.VMEM(ranked.shape, BF16), pltpu.VMEM(ranked.shape, BF16),
            pltpu.VMEM((rank, 2 * width), F32), pltpu.VMEM((seq, rank, 2 * width // seq), F32),
            pltpu.VMEM((rank, 2 * width // seq), F32),
            pltpu.VMEM((head, rank, 2 * width // seq), F32),
            pltpu.VMEM((rank, 2 * width), F32), pltpu.VMEM((16, width), F32),
            dma((3,)), dma((pairs,)), dma((pairs,)), moves, moves, dma((head,)), dma((head,)),
            dma((head, 4)), dma((head + 1, 4)),
            dma((seq,)), dma((seq,)), dma((head,)), dma((head,)), dma((seq,)), dma((seq,)),
        ],
        compiler_params=pltpu.CompilerParams(
            collective_id=5, has_side_effects=True, vmem_limit_bytes=60 << 20
        ),
        cost_estimate=cost(95),
        name="finish",
    )(xn, g_proj, w_in, g_logits, ranked, up_own, rank_down, source, g_hidden, gain, g_ffn, g_head)


def weight_grad_kernel(left, right, *rest):
    out, turned = rest[-2:]

    @pl.when(pl.program_id(1) == 0)
    def _():
        turned[...] = left[...].T

    out[...] = jnp.dot(turned[...], right[...], preferred_element_type=F32).astype(BF16)


def weight_grad(left, right, into, columns, start, tile):
    depth, rows = left.shape
    high = min(rows, 512)
    first = start // tile
    given = () if into is None else (into,)
    return pl.pallas_call(
        weight_grad_kernel,
        out_shape=jax.ShapeDtypeStruct((rows, columns), BF16),
        grid=(rows // high, right.shape[1] // tile),
        in_specs=[
            pl.BlockSpec((depth, high), lambda i, j: (0, i)),
            pl.BlockSpec((depth, tile), lambda i, j: (0, j)),
        ]
        + [pl.BlockSpec(memory_space=pl.ANY) for _ in given],
        out_specs=pl.BlockSpec((high, tile), lambda i, j: (i, first + j)),
        scratch_shapes=[pltpu.VMEM((high, depth), BF16)],
        input_output_aliases={2: 0} if given else {},
        compiler_params=pltpu.CompilerParams(
            dimension_semantics=("arbitrary", "arbitrary"), vmem_limit_bytes=48 << 20
        ),
        cost_estimate=pl.CostEstimate(
            flops=2 * depth * rows * right.shape[1],
            bytes_accessed=2 * (depth * rows + (depth + rows) * right.shape[1]),
            transcendentals=0,
        ),
        name="weight_grad",
    )(left, right, *given)


def gather_weight(w):
    return lax.all_gather(w, "seq", axis=0, tiled=True)


def scatter_grad(g):
    return lax.psum_scatter(g.astype(BF16), "seq", scatter_dimension=0, tiled=True)


def dot(a, b, contract, precision=None):
    return lax.dot_general(
        a, b, (((contract[0],), (contract[1],)), ((), ())),
        precision=precision, preferred_element_type=F32,
    )


def rms(x, epsilon):
    return lax.rsqrt(jnp.mean(x * x, axis=-1, keepdims=True) + epsilon)


def norm_back(grad, gain, normed, inv):
    scaled = grad * gain
    inner = jnp.mean(scaled * normed, axis=-1, keepdims=True)
    return inv * (scaled - normed * inner), jnp.sum(grad * normed, axis=0)


def on_device(
    tokens, starts, cotangent, mix_in, mix_out, gate_up, down_proj,
    norm_gain, ffn_gain, head_gain, rank_down, rank_up, gate_bias,
):
    micro, rows, width = tokens.shape
    heads, seq = lax.axis_size("head"), lax.axis_size("seq")
    head = lax.axis_index("head")
    keys, dv = rank_up.shape[1], head_gain.shape[0]
    dk, vals = keys // heads, dv * heads
    hidden_units = down_proj.shape[1]
    group = heads * micro * rows
    proj_width = 2 * dk + 2 * dv

    def own_columns(w, start, size):
        return lax.dynamic_slice_in_dim(w, start + head * size, size, 1)

    w_in_own = jnp.concatenate(
        [
            own_columns(mix_in, 0, dk),
            own_columns(mix_in, keys, dk),
            own_columns(mix_in, 2 * keys, dv),
            own_columns(mix_in, 2 * keys + vals, dv),
        ],
        axis=1,
    )
    later = gather_weight(
        jnp.concatenate(
            [gate_up.reshape(gate_up.shape[0], 2 * hidden_units), down_proj, mix_out], axis=1
        )
    )
    w_out = later[:, 3 * hidden_units :]
    up_own = own_columns(rank_up, 0, dk)
    bias_own = lax.dynamic_slice_in_dim(gate_bias, head * dk, dk, 0)

    xn, w_in = gather_norm(
        tokens.reshape(micro * rows, width), norm_gain.reshape(1, width), w_in_own
    )
    qkv = dot(xn, w_in[:, : 2 * dk + dv], (1, 0)).astype(BF16)
    og = dot(xn, w_in[:, 2 * dk + dv :], (1, 0))
    ranked = dot(xn, rank_down, (1, 0))
    logits = dot(ranked, up_own, (1, 0), HIGHEST) + bias_own
    decays = (jax.nn.log_sigmoid(logits) / GATE_NORM).astype(BF16)

    def blocks(x):
        return x.reshape(heads, micro, rows, x.shape[-1])

    qkv_b, og_b, decays_b = blocks(qkv), blocks(og), blocks(decays)
    gain_row = head_gain.reshape(1, dv)
    keep = 1.0 - jnp.broadcast_to(starts.T[:, :, None, None], (heads, micro, 1, dk)).astype(F32)
    o_b, gated, through, kept, all_cot = attention_forward(
        keep, qkv_b, decays_b, og_b, gain_row, cotangent.reshape(micro * rows, width)
    )

    source = tokens.astype(F32).reshape(micro * rows, width)
    hidden = source + dot(gated, w_out, (1, 1))
    inv_ffn = rms(hidden, 1e-6)
    plain_ffn = hidden * inv_ffn
    h2 = (plain_ffn * ffn_gain).astype(BF16)

    g_h2, ffn_part, grads = feed_forward(h2, all_cot, later, hidden_units, heads)

    back_ffn, g_ffn_gain = norm_back(g_h2, ffn_gain, plain_ffn, inv_ffn)
    g_hidden = cotangent.astype(F32).reshape(micro * rows, width) + back_ffn
    g_mixed = g_hidden.astype(BF16)
    grads = scatter_grad(weight_grad(g_mixed, gated, grads, later.shape[1], 0, dv))
    g_gated = dot(g_mixed, w_out, (1, 0)).astype(BF16)
    g_proj_b, g_logits_b, g_head_gain, ffn_out = attention_back(
        keep, g_gated, og_b, o_b, qkv_b, decays_b, blocks(logits), through, gain_row, kept, ffn_part.reshape(group, width),
    )
    output = (hidden + ffn_out).astype(BF16)
    g_proj, g_logits = g_proj_b.reshape(group, proj_width), g_logits_b.reshape(group, dk)
    input_grad, grad_in, *small, g_rank_down = finish(
        xn, g_proj, w_in, g_logits, ranked, up_own, rank_down, tokens.reshape(micro * rows, width),
        g_hidden, norm_gain.reshape(1, width), g_ffn_gain.reshape(1, width), g_head_gain,
    )
    g_norm_gain, g_ffn_gain, g_head_gain, g_bias, g_rank_up = small
    slab = width // (seq * heads)
    grad_in, grads = lax.optimization_barrier((grad_in, grads))
    grad_ffn = grads[:, vals:]
    grad_out = lax.all_to_all(
        grads[:, :vals].reshape(heads, slab, vals), "head", split_axis=0, concat_axis=0, tiled=True
    )
    grad_out = grad_out.astype(F32).sum(0)
    return (
        output.reshape(tokens.shape),
        input_grad.reshape(tokens.shape),
        grad_in,
        grad_out,
        grad_ffn[:, : 2 * hidden_units].astype(F32).reshape(-1, 2, hidden_units),
        grad_ffn[:, 2 * hidden_units :].astype(F32),
        g_norm_gain.reshape(norm_gain.shape),
        g_ffn_gain.reshape(ffn_gain.shape),
        g_head_gain.reshape(head_gain.shape),
        g_rank_down.T,
        g_rank_up,
        g_bias.reshape(gate_bias.shape),
    )


def solution(mesh):
    rows = P(None, ("seq", "head"), None)
    return jax.shard_map(
        on_device,
        mesh=mesh,
        in_specs=(
            rows, P(None, "seq"), rows, P("seq", None), P("seq", None),
            P("seq", None, "head"), P("seq", "head"), P(), P(), P(), P(), P(), P(),
        ),
        out_specs=(
            rows, rows, P(("seq", "head"), None), P(("seq", "head"), None),
            P("seq", None, "head"), P("seq", "head"), P(), P(), P(), P(), P(), P(),
        ),
        check_vma=False,
    )
```

```python
import functools

import jax
import jax.numpy as jnp
from jax import lax
from jax.experimental import pallas as pl
from jax.experimental.pallas import tpu as pltpu
from jax.sharding import PartitionSpec as P

HIGHEST = lax.Precision.HIGHEST
GATE_NORM = 16.0
BF16 = jnp.bfloat16
F32 = jnp.float32


def mm(a, b, contract, precision=HIGHEST):
    return lax.dot_general(
        a, b, ((contract[:1], contract[1:]), ((), ())),
        precision=precision, preferred_element_type=F32,
    )


def split(x):
    high = x.astype(BF16)
    return high, (x - high.astype(F32)).astype(BF16)


def mms(left, right, contract):
    total = mm(left[0], right[0], contract, None)
    if len(right) > 1:
        total += mm(left[0], right[1], contract, None)
    if len(left) > 1:
        total += mm(left[1], right[0], contract, None)
    return total


def lower_ones(size):
    rows = lax.broadcasted_iota(jnp.int32, (size, size), 0)
    cols = lax.broadcasted_iota(jnp.int32, (size, size), 1)
    return rows >= cols


def running(decay_low):
    ones = lower_ones(decay_low.shape[0]).astype(F32).astype(BF16)
    return mm(ones, decay_low, (1, 0), None)


def sigmoid(x):
    return 1.0 / (1.0 + jnp.exp(-x))


def cost(micros):
    return pl.CostEstimate(flops=0, bytes_accessed=int(micros * 3.0e6), transcendentals=0)


def greet(axes):
    barrier = pltpu.get_barrier_semaphore()
    met = 0
    for axis in axes:
        me, count = lax.axis_index(axis), lax.axis_size(axis)
        for hop in range(1, count):
            pl.semaphore_signal(
                barrier, inc=1, device_id={axis: lax.rem(me + hop, count)},
                device_id_type=pl.DeviceIdType.MESH,
            )
        met += count - 1
    pl.semaphore_wait(barrier, met)


def push(src, dst, send, recv, to, axis="head"):
    return pltpu.make_async_remote_copy(
        src_ref=src, dst_ref=dst, send_sem=send, recv_sem=recv,
        device_id={axis: to}, device_id_type=pl.DeviceIdType.MESH,
    )


def near_order(z, count, i):
    both = jnp.minimum(z, count - 1 - z)
    left = z > count - 1 - z
    paired = jnp.where(i % 2 == 1, z - (i + 1) // 2, z + i // 2)
    single = jnp.where(left, z - (i - both), z + (i - both))
    return jnp.where(i <= 2 * both, paired, single)


class Line:
    def __init__(self, own, all_rows, send, recv):
        self.own, self.all, self.send, self.recv = own, all_rows, send, recv
        self.z, self.count, self.rows = lax.axis_index("head"), lax.axis_size("head"), own.shape[0]
        z, count = self.z, self.count
        self.right = push(own, self.at(z), send.at[0], recv.at[z], lax.rem(z + 1, count))
        self.left = push(own, self.at(z), send.at[1], recv.at[z], lax.rem(z + count - 1, count))

    def chunk(self, b):
        return pl.ds(pl.multiple_of(b * self.rows, self.rows), self.rows)

    def at(self, b):
        return self.all.at[self.chunk(b)]

    def start(self):
        pl.when(self.z < self.count - 1)(self.right.start)
        pl.when(self.z > 0)(self.left.start)

    def passing(self, i, b):
        z, count = self.z, self.count
        to = jnp.where(b < z, z + 1, z - 1)
        going = ((b < z) & (z < count - 1)) | ((b > z) & (z > 0))
        copy = push(
            self.at(b), self.at(b), self.send.at[i + 1], self.recv.at[b], lax.rem(to + count, count)
        )
        return copy, going

    def receive(self, i, b):
        copy, going = self.passing(i, b)
        copy.wait_recv()
        pl.when(going)(copy.start)

    def finish(self):
        def sent(i, _):
            copy, going = self.passing(i, near_order(self.z, self.count, i))
            pl.when(going)(copy.wait_send)
            return 0

        lax.fori_loop(1, self.count, sent, 0)
        pl.when(self.z < self.count - 1)(self.right.wait_send)
        pl.when(self.z > 0)(self.left.wait_send)


class LineSum:
    def __init__(self, parts, landed, send, recv, rows):
        self.parts, self.landed, self.send, self.recv = parts, landed, send, recv
        self.z, self.count = lax.axis_index("head"), lax.axis_size("head")
        self.rows, self.pieces = rows, send.shape[1]
        self.deep = rows // self.pieces
        self.inner = (self.z > 0) & (self.z < self.count - 1)
        self.far_end = jnp.where(self.z < self.count - 1 - self.z, self.count - 1, 0)

    def piece(self, b, p):
        return pl.ds(pl.multiple_of(b * self.rows + p * self.deep, self.deep), self.deep)

    def onward(self, b, p):
        z, count = self.z, self.count
        to = jnp.where(b > z, z + 1, z - 1)
        slot = jnp.where((to == b) & (z > b), count, b)
        return push(
            self.parts.at[self.piece(b, p)], self.landed.at[self.piece(slot, p)],
            self.send.at[b, p], self.recv.at[slot, p], lax.rem(to + count, count),
        )

    def send_all(self):
        @pl.when(jnp.logical_not(self.inner))
        def _():
            for i in range(1, self.count):
                b = jnp.where(self.z == 0, self.count - i, i - 1)
                for p in range(self.pieces):
                    self.onward(b, p).start()

    def arrived(self, slot, p):
        at = self.piece(slot, p)
        push(
            self.landed.at[at], self.landed.at[at], self.send.at[0, p], self.recv.at[slot, p],
            lax.rem(self.z + 1, self.count),
        ).wait_recv()
        return self.landed[at, :].astype(F32)

    def relay(self, b, p):
        at = self.piece(b, p)
        self.parts[at, :] = (self.parts[at, :].astype(F32) + self.arrived(b, p)).astype(BF16)
        self.onward(b, p).start()

    def relay_in_turn(self, j):
        pieces = self.pieces

        @pl.when(self.inner & (j < pieces))
        def _():
            self.relay(self.count - 1 - self.z, j)

        @pl.when(self.inner & (j >= pieces))
        def _():
            self.relay(self.far_end, j - pieces)

        @pl.when(self.inner & (j > pieces))
        def _():
            self.relay(self.count - 1 - self.far_end, j - pieces - 1)

    def relay_last(self):
        @pl.when(self.inner)
        def _():
            self.relay(self.count - 1 - self.far_end, self.pieces - 1)

    def result(self, out):
        z, count = self.z, self.count
        for p in range(self.pieces):
            here = pl.ds(p * self.deep, self.deep)
            out[here, :] = self.parts[self.piece(z, p), :].astype(F32)

            @pl.when(z > 0)
            def _():
                out[here, :] += self.arrived(z, p)

            @pl.when(z < count - 1)
            def _():
                out[here, :] += self.arrived(count, p)

    def finish(self):
        def sent(i, _):
            b = near_order(self.z, self.count, i)
            for p in range(self.pieces):
                self.onward(b, p).wait_send()
            return 0

        lax.fori_loop(1, self.count, sent, 0)


class PairSum:
    def __init__(self, mine, paired, inbox, pair_send, pair_recv, send, recv):
        self.mine, self.paired, self.inbox = mine, paired, inbox
        self.pair_send, self.pair_recv, self.send, self.recv = pair_send, pair_recv, send, recv
        self.s, self.pairs = lax.axis_index("seq"), lax.axis_size("seq") // 2
        self.side, self.own = lax.rem(self.s, 2), self.s // 2
        self.deep, self.half = mine.shape[1], mine.shape[2] // 2
        self.levels = self.pairs.bit_length() - 1
        assert self.pairs == 1 << self.levels

    def block(self, k, other=False):
        i = 2 * k + (1 - self.side if other else self.side)
        return pl.ds(pl.multiple_of(i * self.deep, self.deep), self.deep)

    def to_partner(self, src, k):
        return push(
            src, self.paired.at[k], self.pair_send.at[k], self.pair_recv.at[k],
            self.s + 1 - 2 * self.side, "seq",
        )

    def bit(self, i, level):
        return lax.rem(i // (1 << level), 2)

    def move(self, side, slot, k, level):
        columns = pl.ds(side * self.half, self.half)
        to = self.s + (1 - 2 * self.bit(self.own, level)) * (2 << level)
        return push(
            self.mine.at[k, :, columns], self.inbox.at[slot, :, columns],
            self.send.at[side, slot], self.recv.at[side, slot], to, "seq",
        )

    def moves(self, side, step):
        order = list(range(self.levels))
        if side:
            order.reverse()
        level, free = order[step], sorted(order[step + 1 :])
        fixed = sum((self.bit(self.own, d) * (1 << d) for d in order[:step]), 0)
        offset = self.pairs - (1 << (self.levels - step))
        here = self.bit(self.own, level) * (1 << level)
        for c in range(1 << len(free)):
            rest = fixed + sum(((c >> j) & 1) << d for j, d in enumerate(free))
            yield offset + c, rest + here, rest + (1 << level) - here, level

    def pass_on(self, k):
        top = 1 << (self.levels - 1)
        pl.when(self.bit(k, 0) != self.bit(self.own, 0))(self.move(0, k // 2, k, 0).start)
        pl.when(k // top != self.own // top)(
            self.move(1, lax.rem(k, top), k, self.levels - 1).start
        )

    def advance(self, step):
        for side in range(2):
            columns = slice(side * self.half, (side + 1) * self.half)
            for slot, keep, gone, level in self.moves(side, step):
                self.move(side, slot, gone, level).wait_recv()
                self.mine[keep, :, columns] = (
                    self.mine[keep, :, columns].astype(F32)
                    + self.inbox[slot, :, columns].astype(F32)
                ).astype(BF16)
            if step + 1 < self.levels:
                for slot, keep, gone, level in self.moves(side, step + 1):
                    self.move(side, slot, gone, level).start()

    def finish(self, src):
        for k in range(self.pairs):
            self.to_partner(src(k), k).wait_send()
        for side in range(2):
            for step in range(self.levels):
                for slot, keep, gone, level in self.moves(side, step):
                    self.move(side, slot, gone, level).wait_send()


def gather_norm_kernel(own, gain, shard, normed, rows_of_all, rows_all, here_sem, send, recv,
                       w_sem, w_peer, w_pair, w_recv):
    z, count, rows = lax.axis_index("head"), lax.axis_size("head"), own.shape[0]
    greet(("seq", "head"))
    line = Line(own, rows_all, send, recv)
    line.start()
    here = pltpu.make_async_copy(own, line.at(z), here_sem)
    here.start()

    s, deep = lax.axis_index("seq"), shard.shape[0]
    side, pairs, own_pair = lax.rem(s, 2), lax.axis_size("seq") // 2, s // 2
    partner = s + 1 - 2 * side

    def shard_at(i):
        return rows_of_all.at[pl.ds(pl.multiple_of(i * deep, deep), deep)]

    def to_peer(k):
        return push(shard, shard_at(s), w_peer.at[k], w_recv.at[s], 2 * k + side, "seq")

    def from_peer(k):
        i = 2 * k + side
        return push(shard, shard_at(i), w_peer.at[k], w_recv.at[i], partner, "seq")

    def to_partner(k):
        i = 2 * k + side
        return push(shard_at(i), shard_at(i), w_pair.at[k], w_recv.at[i], partner, "seq")

    def from_partner(k):
        i = 2 * k + 1 - side
        return push(shard_at(i), shard_at(i), w_pair.at[k], w_recv.at[i], partner, "seq")

    mine = pltpu.make_async_copy(shard, shard_at(s), w_sem)
    mine.start()
    for k in range(pairs):
        pl.when(own_pair != k)(to_peer(k).start)
    mine.wait()
    to_partner(own_pair).start()
    here.wait()
    band = 16

    def step(i, _):
        b = near_order(z, count, i)
        pl.when(i > 0)(lambda: line.receive(i, b))

        def norm(r, _):
            at = pl.ds(pl.multiple_of(b * rows + r * band, band), band)
            x = rows_all[at, :].astype(F32)
            inv = lax.rsqrt(jnp.mean(x * x, axis=-1, keepdims=True) + 1e-6)
            normed[at, :] = (x * inv * gain[...]).astype(BF16)
            return 0

        lax.fori_loop(0, rows // band, norm, 0)
        return 0

    lax.fori_loop(0, count, step, 0)
    for k in range(pairs):

        @pl.when(own_pair != k)
        def _():
            from_peer(k).wait_recv()
            to_partner(k).start()

    for k in range(pairs):
        from_partner(k).wait_recv()
    for k in range(pairs):
        to_partner(k).wait_send()
        pl.when(own_pair != k)(to_peer(k).wait_send)
    line.finish()


def gather_norm(x, gain, shard):
    rows, width = x.shape
    seq = lax.axis_size("seq")
    anywhere = pl.BlockSpec(memory_space=pl.ANY)
    count = lax.axis_size("head")
    vmem = pl.BlockSpec(memory_space=pltpu.VMEM)
    dma = pltpu.SemaphoreType.DMA
    return pl.pallas_call(
        gather_norm_kernel,
        out_shape=(
            jax.ShapeDtypeStruct((count * rows, width), BF16),
            jax.ShapeDtypeStruct((seq * shard.shape[0], shard.shape[1]), BF16),
        ),
        in_specs=[vmem, vmem, anywhere],
        out_specs=(vmem, anywhere),
        scratch_shapes=[
            pltpu.VMEM((count * rows, width), BF16), dma(()), dma((count + 1,)), dma((count,)),
            dma(()), dma((seq // 2,)), dma((seq // 2,)), dma((seq,)),
        ],
        compiler_params=pltpu.CompilerParams(
            collective_id=1, has_side_effects=True, vmem_limit_bytes=32 << 20
        ),
        cost_estimate=cost(50),
        name="gather_norm",
    )(x, gain, shard)


def swap_slices(own, got, send, recv):
    side = lax.rem(lax.axis_index("seq"), 2)
    me, count = lax.axis_index("seq") // 2, lax.axis_size("seq") // 2

    def copy(hop, index):
        to = lax.rem(me + hop, count)
        return push(own.at[to], got.at[index], send.at[hop], recv.at[index], 2 * to + side, "seq")

    def start(hop, _):
        copy(hop, me).start()
        return 0

    def wait_recv(hop, _):
        copy(hop, lax.rem(me + hop, count)).wait_recv()
        return 0

    def wait_send(hop, _):
        copy(hop, me).wait_send()
        return 0

    def begin():
        lax.fori_loop(1, count, start, 0)
        got[me] = own[me]

    def end():
        lax.fori_loop(1, count, wait_recv, 0)

    def drain():
        lax.fori_loop(1, count, wait_send, 0)

    return begin, end, drain


def to_mate(src, dst, send, recv):
    s = lax.axis_index("seq")
    return push(src, dst, send, recv, s + 1 - 2 * lax.rem(s, 2), "seq")


def sided(own, mate):
    first = lax.rem(lax.axis_index("seq"), 2) == 0
    return jnp.where(first, own, mate), jnp.where(first, mate, own)


def scan_states(reverse, own, through, out):
    count, part = out.shape[0], out.shape[2]

    def step(k, state):
        j = count - 1 - k if reverse else k
        out[j] = state.astype(BF16)
        decay = through[j, :, 0:1, :].astype(F32) + through[j, :, 1:2, :].astype(F32)
        return decay * state + own[j, :, :part, :].astype(F32)

    lax.fori_loop(0, count, step, jnp.zeros(out.shape[1:], F32))


def front_kernel(keep, qkv, decay, og, gain, rows_own,
                 o_out, gated, through, pair_through, kept_out, rows_all,
                 kept, runs, state, sending, got, scanned, before, leaving, mate_out, mate_in,
                 back_out, back_in, first_state,
                 here_sem, go, come, s_send, s_recv, b_send, b_recv, z_send, z_recv, k_sem, m_sem):
    h, head = lax.axis_index("head"), lax.axis_size("head")
    count, micro, rows, dk = decay.shape
    dv = og.shape[-1]
    slices, part = scanned.shape[0], scanned.shape[2]
    scale = dk ** (-0.5)
    greet(("seq", "head"))
    line = Line(rows_own, rows_all, go, come)
    line.start()
    here = pltpu.make_async_copy(rows_own, line.at(h), here_sem)
    here.start()

    state[...] = jnp.zeros_like(state)
    passed = [jnp.zeros((1, dk), F32)] * micro
    alive = [jnp.ones((1, dk), F32)] * micro
    for b in range(count):
        for m in range(micro):
            run = running(decay[b, m])
            runs[b, m] = run
            last = run[rows - 1 : rows, :]
            carried = qkv[b, m, :, dk : 2 * dk].astype(F32) * jnp.exp(last - run)
            fresh = mms((qkv[b, m, :, 2 * dk :],), split(carried), (0, 0))
            kept[b, m] = fresh
            state[m] = jnp.exp(last) * (state[m] * keep[b, m]) + fresh
            passed[m] = passed[m] + last
            alive[m] = alive[m] * keep[b, m]
    tail = sending.shape[2] - part
    at = lax.broadcasted_iota(jnp.int32, (tail, dk), 0)
    half = dv // 2
    side = lax.rem(lax.axis_index("seq"), 2)
    own_half = pl.ds(pl.multiple_of(side * half, half), half)
    mate_half = pl.ds(pl.multiple_of((1 - side) * half, half), half)

    def as_rows(value):
        high, low = split(value)
        return jnp.where(at == 0, high.astype(F32), jnp.where(at == 1, low.astype(F32), 0.0))

    own_rows = [as_rows(jnp.exp(passed[m]) * alive[m]) for m in range(micro)]
    for m in range(micro):
        mate_out[m, :half, :] = state[m, mate_half, :].astype(BF16)
        mate_out[m, half:, :] = own_rows[m].astype(BF16)
    swap = to_mate(mate_out, mate_in, m_sem.at[0], m_sem.at[1])
    swap.start()
    swap.wait_recv()
    first_through = []
    for m in range(micro):
        firsts, seconds = sided(own_rows[m], mate_in[m, half:, :].astype(F32))
        pair_through[0, m], pair_through[1, m] = firsts.astype(BF16), seconds.astype(BF16)
        first, second = firsts[0:1] + firsts[1:2], seconds[0:1] + seconds[1:2]
        first_through.append(first)
        start, after = sided(state[m, own_half, :], mate_in[m, :half, :].astype(F32))
        first_state[m] = start
        pair = second * start + after
        both = as_rows(first * second).astype(BF16)
        for i in range(slices):
            sending[i, m, :part, :] = pair[i * part : (i + 1) * part, :].astype(BF16)
            sending[i, m, part:, :] = both
    begin, end, drain = swap_slices(sending, got, s_send, s_recv)
    begin()
    causal = lower_ones(rows)

    def inside(b, _):
        for m in range(micro):
            run = runs[b, m]
            queried = split(qkv[b, m, :, :dk].astype(F32) * (jnp.exp(run) * scale))
            keyed = split(qkv[b, m, :, dk : 2 * dk].astype(F32) * jnp.exp(-run))
            scores = jnp.where(causal, mms(queried, keyed, (1, 1)), 0.0)
            o_out[b, m] = mms(split(scores), (qkv[b, m, :, 2 * dk :],), (1, 0))
        return 0

    lax.fori_loop(0, count, inside, 0)
    line.receive(1, near_order(h, head, 1))
    end()
    through[...] = got[:, :, part:, :]
    scan_states(False, got, through, scanned)
    begin_back, end_back, drain_back = swap_slices(scanned, before, b_send, b_recv)
    begin_back()
    line.receive(2, near_order(h, head, 2))
    end_back()
    for m in range(micro):
        entry = before[:, m].astype(F32).reshape(half, dk)
        own, mate = sided(entry, first_through[m] * entry + first_state[m])
        state[m, own_half, :] = own
        back_out[m] = mate.astype(BF16)
    swap_back = to_mate(back_out, back_in, m_sem.at[2], m_sem.at[3])
    swap_back.start()
    swap_back.wait_recv()
    for m in range(micro):
        state[m, mate_half, :] = back_in[m].astype(F32)

    def to_owner(b):
        columns = gated.at[:, pl.ds(pl.multiple_of(h * dv, dv), dv)]
        return push(leaving.at[b], columns, z_send.at[b], z_recv.at[h], b)

    def save(b):
        return pltpu.make_async_copy(kept.at[b], kept_out.at[b], k_sem.at[b])

    def across(b, _):
        for m in range(micro):
            run = runs[b, m]
            queried = split(qkv[b, m, :, :dk].astype(F32) * (jnp.exp(run) * scale))
            entry = state[m] * keep[b, m]
            state[m] = jnp.exp(run[rows - 1 : rows, :]) * entry + kept[b, m]
            kept[b, m] = entry
            o = o_out[b, m] + mms(queried, split(entry), (1, 1))
            o_out[b, m] = o
            inv = lax.rsqrt(jnp.mean(o * o, axis=-1, keepdims=True) + 1e-5)
            normed = (o * inv * gain[...]).astype(BF16).astype(F32)
            gate = og[b, m]
            leaving[b, m * rows : (m + 1) * rows, :] = (normed * gate * sigmoid(gate)).astype(BF16)
        save(b).start()
        pl.when(b != h)(to_owner(b).start)

        @pl.when(b == 1)
        def _():
            line.receive(3, near_order(h, head, 3))

        return 0

    lax.fori_loop(0, count, across, 0)
    gated[:, pl.ds(pl.multiple_of(h * dv, dv), dv)] = leaving[h]
    for hop in range(1, head):
        other = lax.rem(h + hop, head)
        columns = gated.at[:, pl.ds(pl.multiple_of(other * dv, dv), dv)]
        push(leaving.at[other], columns, z_send.at[other], z_recv.at[other], other).wait_recv()
        to_owner(other).wait_send()
    for b in range(count):
        save(b).wait()
    here.wait()
    line.finish()
    drain()
    drain_back()
    swap.wait_send()
    swap_back.wait_send()


def attention_forward(keep, qkv, decays, og, gain, rows_own):
    blocks, micro, rows, width = qkv.shape
    dk, dv = decays.shape[-1], og.shape[-1]
    head, seq = lax.axis_size("head"), lax.axis_size("seq")
    assert blocks == head and head == 4
    pairs, half, tail = seq // 2, dv // 2, 16
    part = half // pairs
    own_rows = micro * rows
    vmem, anywhere = pl.BlockSpec(memory_space=pltpu.VMEM), pl.BlockSpec(memory_space=pl.ANY)
    dma = pltpu.SemaphoreType.DMA
    states, wider = (pairs, micro, part, dk), (pairs, micro, part + tail, dk)
    return pl.pallas_call(
        front_kernel,
        out_shape=(
            jax.ShapeDtypeStruct((blocks, micro, rows, dv), F32),
            jax.ShapeDtypeStruct((own_rows, head * dv), BF16),
            jax.ShapeDtypeStruct((pairs, micro, tail, dk), BF16),
            jax.ShapeDtypeStruct((2, micro, tail, dk), BF16),
            jax.ShapeDtypeStruct((blocks, micro, dv, dk), F32),
            jax.ShapeDtypeStruct((head * rows_own.shape[0], rows_own.shape[1]), BF16),
        ),
        in_specs=[vmem] * 5 + [anywhere],
        out_specs=(vmem,) * 4 + (anywhere,) * 2,
        scratch_shapes=[
            pltpu.VMEM((blocks, micro, dv, dk), F32), pltpu.VMEM((blocks, micro, rows, dk), F32),
            pltpu.VMEM((micro, dv, dk), F32), pltpu.VMEM(wider, BF16), pltpu.VMEM(wider, BF16),
            pltpu.VMEM(states, BF16), pltpu.VMEM(states, BF16),
            pltpu.VMEM((blocks, own_rows, dv), BF16),
            pltpu.VMEM((micro, half + tail, dk), BF16), pltpu.VMEM((micro, half + tail, dk), BF16),
            pltpu.VMEM((micro, half, dk), BF16), pltpu.VMEM((micro, half, dk), BF16),
            pltpu.VMEM((micro, half, dk), F32),
            dma(()), dma((head + 1,)), dma((head,)), dma((pairs,)), dma((pairs,)), dma((pairs,)),
            dma((pairs,)), dma((head,)), dma((head,)), dma((blocks,)), dma((4,)),
        ],
        compiler_params=pltpu.CompilerParams(
            collective_id=2, has_side_effects=True, vmem_limit_bytes=40 << 20
        ),
        cost_estimate=cost(90),
        name="attention_forward",
    )(keep, qkv, decays, og, gain, rows_own)


def ffn_kernel(count, x_own, c_all, w, g_x, f_parts, grad,
               wv, xs, cs, act, lin, parts, landed, turned, turned_c, tiles,
               w_sem, own_sem, go_sem, x_sem, p_sem, q_sem, o_sem):
    z = lax.axis_index("head")
    rows, width = x_own.shape
    hidden = act.shape[1] // 3
    chunk = lambda b: pl.ds(pl.multiple_of(b * rows, rows), rows)

    weights = [
        pltpu.make_async_copy(
            w.at[:, pl.ds(k * hidden, hidden)], wv.at[:, pl.ds(k * hidden, hidden)], w_sem.at[k]
        )
        for k in range(3)
    ]
    own = [
        pltpu.make_async_copy(x_own, xs.at[chunk(z)], own_sem.at[0]),
        pltpu.make_async_copy(c_all, cs, own_sem.at[1]),
    ]
    for copy in own + weights:
        copy.start()
    greet(("head",))
    line = Line(x_own, xs, go_sem, x_sem)
    line.start()
    for copy in own + weights:
        copy.wait()

    total = LineSum(parts, landed, p_sem, q_sem, rows)

    def step(i, _):
        b = near_order(z, count, i)

        pl.when(i > 0)(lambda: line.receive(i, b))

        at = chunk(b)
        x = xs[at, :]
        lin[0] = jnp.dot(x, wv[:, :hidden], preferred_element_type=F32)
        lin[1] = jnp.dot(x, wv[:, hidden : 2 * hidden], preferred_element_type=F32)
        lin[2] = jnp.dot(cs[at, :], wv[:, 2 * hidden :], preferred_element_type=F32)
        band = 16

        def act_rows(r, _):
            here = pl.ds(pl.multiple_of(r * band, band), band)
            there = pl.ds(pl.multiple_of(b * rows + r * band, band), band)
            gate, up, g_product = lin[0, here, :], lin[1, here, :], lin[2, here, :]
            sig = sigmoid(gate)
            gated = gate * sig
            act[there, :hidden] = (g_product * up * sig * (1.0 + gate * (1.0 - sig))).astype(BF16)
            act[there, hidden : 2 * hidden] = (g_product * gated).astype(BF16)
            act[there, 2 * hidden :] = (gated * up).astype(BF16)
            return 0

        lax.fori_loop(0, rows // band, act_rows, 0)
        parts[at, :] = mm(act[at, : 2 * hidden], wv[:, : 2 * hidden], (1, 1), None).astype(BF16)

        @pl.when((i > 0) & jnp.logical_not(total.inner))
        def _():
            for p in range(total.pieces):
                total.onward(b, p).start()

        return 0

    lax.fori_loop(0, count, step, 0)

    high = tiles.shape[1]
    steps = width // high
    first = grad.shape[1] - 3 * hidden

    def store(t, r, k):
        down = pl.ds(pl.multiple_of(r * high, high), high)
        into = grad.at[down, pl.ds(first + k * hidden, hidden)]
        return pltpu.make_async_copy(tiles.at[lax.rem(t, 2)], into, o_sem.at[lax.rem(t, 2)])

    turned[...] = xs[...].T
    turned_c[...] = cs[...].T

    def tile(r, k):
        t = 3 * r + k

        @pl.when(t >= 2)
        def _():
            store(t, r, k).wait()

        left_rows = (turned_c if k == 2 else turned)[
            pl.ds(pl.multiple_of(r * high, high), high), :
        ]
        tiles[lax.rem(t, 2)] = jnp.dot(
            left_rows, act[:, k * hidden : (k + 1) * hidden], preferred_element_type=F32
        ).astype(BF16)
        store(t, r, k).start()

    def slab(r, _):
        tile(r, 0)
        tile(r, 1)
        total.relay_in_turn(2 * r)
        tile(r, 2)
        at = chunk(r)
        f_parts[r] = mm(act[at, 2 * hidden :], wv[:, 2 * hidden :], (1, 1), None).astype(BF16)
        total.relay_in_turn(2 * r + 1)
        return 0

    lax.fori_loop(0, steps, slab, 0)
    total.relay_last()
    total.result(g_x)
    total.finish()
    line.finish()
    store(3 * steps - 2, 0, 0).wait()
    store(3 * steps - 1, 0, 0).wait()


def feed_forward(x_own, c_all, w, hidden, count):
    rows, width = x_own.shape
    group = rows * count
    assert count == 4 and width % 4 == 0 and rows % 64 == 0
    anywhere = pl.BlockSpec(memory_space=pl.ANY)
    vmem = pl.BlockSpec(memory_space=pltpu.VMEM)
    dma = pltpu.SemaphoreType.DMA
    return pl.pallas_call(
        functools.partial(ffn_kernel, count),
        out_shape=(
            jax.ShapeDtypeStruct((rows, width), F32),
            jax.ShapeDtypeStruct((count, rows, width), BF16),
            jax.ShapeDtypeStruct(w.shape, BF16),
        ),
        in_specs=[anywhere] * 3,
        out_specs=(vmem, vmem, anywhere),
        scratch_shapes=[
            pltpu.VMEM((width, 3 * hidden), BF16),
            pltpu.VMEM((group, width), BF16),
            pltpu.VMEM((group, width), BF16),
            pltpu.VMEM((group, 3 * hidden), BF16),
            pltpu.VMEM((3, rows, hidden), F32),
            pltpu.VMEM((group, width), BF16),
            pltpu.VMEM((group + rows, width), BF16),
            pltpu.VMEM((width, group), BF16),
            pltpu.VMEM((width, group), BF16),
            pltpu.VMEM((2, width // 4, hidden), BF16),
            dma((3,)), dma((2,)), dma((count + 1,)), dma((count,)),
            dma((count, 4)), dma((count + 1, 4)), dma((2,)),
        ],
        compiler_params=pltpu.CompilerParams(
            collective_id=0, has_side_effects=True, vmem_limit_bytes=60 << 20
        ),
        cost_estimate=cost(100),
        name="feed_forward",
    )(x_own, c_all, w)


def back_kernel(keep, gated_own, og, o_in, qkv, decay, logits, through, pair_through, gain,
                kept_in, parts_in,
                g_proj, g_logits, g_gain, f_out,
                gated_all, go, runs, g_queried, g_keyed, g_values, pulls, weights, kept,
                parts, landed, state, sending, got, scanned, after, mate_out, mate_in,
                back_out, back_in, second_state, m_sem, in_sem, z_send, z_recv, s_send, s_recv, b_send, b_recv, p_sem, q_sem):
    h, head = lax.axis_index("head"), lax.axis_size("head")
    count, micro, rows, dk = decay.shape
    dv = og.shape[-1]
    width = qkv.shape[-1]
    slices, part = sending.shape[0], sending.shape[2]
    scale = dk ** (-0.5)
    loads = [
        pltpu.make_async_copy(parts_in, parts, in_sem.at[0]),
        pltpu.make_async_copy(kept_in, kept, in_sem.at[1]),
    ]
    for load in loads:
        load.start()
    greet(("seq", "head"))

    def to_head(hop, slot):
        to = lax.rem(h + hop, head)
        columns = gated_own.at[:, pl.ds(pl.multiple_of(to * dv, dv), dv)]
        return push(columns, gated_all.at[slot], z_send.at[hop], z_recv.at[slot], to)

    for hop in range(1, head):
        to_head(hop, h).start()
    gated_all[h] = gated_own[:, pl.ds(pl.multiple_of(h * dv, dv), dv)]

    causal = lower_ones(rows)
    before = [jnp.zeros((1, dk), F32)] * micro
    alive = [jnp.ones((1, dk), F32)] * micro
    for b in range(count):
        for m in range(micro):
            run = running(decay[b, m])
            runs[b, m] = run
            alive[m] = alive[m] * keep[b, m]
            weights[b, m] = jnp.exp(before[m]) * alive[m]
            before[m] = before[m] + run[rows - 1 : rows, :]
    g_gain[...] = jnp.zeros_like(g_gain)
    state[...] = jnp.zeros_like(state)

    def gates(i, _):
        b = near_order(h, head, i)
        pl.when(i > 0)(lambda: to_head(lax.rem(b - h + head, head), b).wait_recv())
        for m in range(micro):
            gate, o = og[b, m], o_in[b, m]
            grad = gated_all[b, m * rows : (m + 1) * rows, :].astype(F32)
            sig = sigmoid(gate)
            inv = lax.rsqrt(jnp.mean(o * o, axis=-1, keepdims=True) + 1e-5)
            plain = o * inv
            normed = (plain * gain[...]).astype(BF16).astype(F32)
            g_on = (grad * gate * sig).astype(BF16).astype(F32)
            g_proj[b, m, :, width:] = (
                grad * normed * sig * (1.0 + gate * (1.0 - sig))
            ).astype(BF16)
            scaled = g_on * gain[...]
            g_o = inv * (scaled - plain * jnp.mean(scaled * plain, axis=-1, keepdims=True))
            go[b, m] = g_o
            g_gain[0:1, :] += jnp.sum(g_on * plain, axis=0, keepdims=True)
            queried = qkv[b, m, :, :dk].astype(F32) * (jnp.exp(runs[b, m]) * scale)
            pull = mms(split(g_o), split(queried), (0, 0))
            pulls[b, m] = pull
            state[m] += pull * weights[b, m]
        return 0

    lax.fori_loop(0, head, gates, 0)
    half = dv // 2
    side = lax.rem(lax.axis_index("seq"), 2)
    own_half = pl.ds(pl.multiple_of(side * half, half), half)
    mate_half = pl.ds(pl.multiple_of((1 - side) * half, half), half)
    mate_out[...] = state[:, mate_half, :].astype(BF16)
    swap = to_mate(mate_out, mate_in, m_sem.at[0], m_sem.at[1])
    swap.start()
    swap.wait_recv()
    passes = pair_through[:, :, 0:1, :].astype(F32) + pair_through[:, :, 1:2, :].astype(F32)
    for m in range(micro):
        start, later_state = sided(state[m, own_half, :], mate_in[m].astype(F32))
        second_state[m] = later_state
        pair = passes[0, m] * later_state + start
        for i in range(slices):
            sending[i, m] = pair[i * part : (i + 1) * part, :].astype(BF16)
    begin, end, drain = swap_slices(sending, got, s_send, s_recv)
    begin()
    for load in loads:
        load.wait()
    total = LineSum(parts, landed, p_sem, q_sem, f_out.shape[0])
    total.send_all()

    def inside(b, _):
        for m in range(micro):
            q = qkv[b, m, :, :dk].astype(F32)
            k = qkv[b, m, :, dk : 2 * dk].astype(F32)
            v = (qkv[b, m, :, 2 * dk :],)
            run = runs[b, m]
            queried, keyed = split(q * (jnp.exp(run) * scale)), split(k * jnp.exp(-run))
            g_o, entry = split(go[b, m]), split(kept[b, m])
            scores = split(jnp.where(causal, mms(queried, keyed, (1, 1)), 0.0))
            g_scores = split(jnp.where(causal, mms(g_o, v, (1, 1)), 0.0))
            g_queried[b, m] = mms(g_scores, keyed, (1, 0)) + mms(g_o, entry, (1, 0))
            g_keyed[b, m] = mms(g_scores, queried, (0, 0))
            g_values[b, m] = mms(scores, g_o, (0, 0))
        pl.when(total.inner)(lambda: total.relay(total.far_end, b))
        return 0

    lax.fori_loop(0, count, inside, 0)
    end()
    scan_states(True, got, through, scanned)
    begin_back, end_back, drain_back = swap_slices(scanned, after, b_send, b_recv)
    begin_back()

    @pl.when(total.inner)
    def _():
        for p in range(total.pieces):
            total.relay(head - 1 - total.far_end, p)
        for p in range(total.pieces):
            total.relay(head - 1 - h, p)

    end_back()
    for m in range(micro):
        leave = after[:, m].astype(F32).reshape(half, dk)
        firsts = passes[1, m] * leave + second_state[m]
        own, _ = sided(firsts, leave)
        mate, _ = sided(leave, firsts)
        state[m, own_half, :] = own
        back_out[m] = mate.astype(BF16)
    swap_back = to_mate(back_out, back_in, m_sem.at[2], m_sem.at[3])
    swap_back.start()
    swap_back.wait_recv()
    for m in range(micro):
        state[m, mate_half, :] = back_in[m].astype(F32)

    def across(step, _):
        b = count - 1 - step
        for m in range(micro):
            q = qkv[b, m, :, :dk].astype(F32)
            k = qkv[b, m, :, dk : 2 * dk].astype(F32)
            v = (qkv[b, m, :, 2 * dk :],)
            run = runs[b, m]
            last = run[rows - 1 : rows, :]
            up, down, rest = jnp.exp(run) * scale, jnp.exp(-run), jnp.exp(last - run)
            decayed = jnp.exp(last)
            gs = state[m]
            gs_parts = split(gs)
            carried = k * rest
            g_v = g_values[b, m] + mms(split(carried), gs_parts, (1, 1))
            g_carried = mms(v, gs_parts, (1, 0))
            from_carried = g_carried * carried
            g_total = jnp.sum(decayed * kept[b, m] * gs, axis=0, keepdims=True) + jnp.sum(
                from_carried, axis=0, keepdims=True
            )
            state[m] = (decayed * gs + pulls[b, m]) * keep[b, m]
            gq, gk = g_queried[b, m], g_keyed[b, m]
            g_run = gq * (q * up) - gk * (k * down) - from_carried
            later = mms((causal.astype(F32).astype(BF16),), split(g_run), (0, 0)) + g_total
            g_proj[b, m, :, :dk] = (gq * up).astype(BF16)
            g_proj[b, m, :, dk : 2 * dk] = (gk * down + g_carried * rest).astype(BF16)
            g_proj[b, m, :, 2 * dk : width] = g_v.astype(BF16)
            g_logits[b, m] = (
                later.astype(BF16).astype(F32) * sigmoid(-logits[b, m]) * (1.0 / GATE_NORM)
            )
        return 0

    lax.fori_loop(0, count, across, 0)
    total.result(f_out)
    total.finish()
    drain()
    drain_back()
    swap.wait_send()
    swap_back.wait_send()
    for hop in range(1, head):
        to_head(hop, h).wait_send()


def attention_back(
    keep, gated_own, og, o, qkv, decays, logits, through, pair_through, gain, kept, parts
):
    blocks, micro, rows, width = qkv.shape
    dk, dv = decays.shape[-1], og.shape[-1]
    head, seq = lax.axis_size("head"), lax.axis_size("seq")
    own_rows = parts.shape[0] // head
    vmem, anywhere = pl.BlockSpec(memory_space=pltpu.VMEM), pl.BlockSpec(memory_space=pl.ANY)
    dma = pltpu.SemaphoreType.DMA
    blocked = lambda w, kind: pltpu.VMEM((blocks, micro, rows, w), kind)
    pairs, half = seq // 2, dv // 2
    states = (pairs, micro, half // pairs, dk)
    halves = (micro, half, dk)
    return pl.pallas_call(
        back_kernel,
        out_shape=(
            jax.ShapeDtypeStruct((blocks, micro, rows, width + dv), BF16),
            jax.ShapeDtypeStruct((blocks, micro, rows, dk), F32),
            jax.ShapeDtypeStruct((8, dv), F32),
            jax.ShapeDtypeStruct((own_rows, parts.shape[1]), F32),
        ),
        in_specs=[vmem] * 10 + [anywhere] * 2,
        out_specs=(vmem,) * 4,
        scratch_shapes=[
            pltpu.VMEM((blocks, micro * rows, dv), BF16), blocked(dv, F32), blocked(dk, F32),
            blocked(dk, F32), blocked(dk, F32), blocked(dv, F32),
            pltpu.VMEM((blocks, micro, dv, dk), F32), pltpu.VMEM((blocks, micro, 1, dk), F32),
            pltpu.VMEM((blocks, micro, dv, dk), F32),
            pltpu.VMEM(parts.shape, BF16),
            pltpu.VMEM((parts.shape[0] + own_rows, parts.shape[1]), BF16),
            pltpu.VMEM((micro, dv, dk), F32),
            pltpu.VMEM(states, BF16), pltpu.VMEM(states, BF16), pltpu.VMEM(states, BF16),
            pltpu.VMEM(states, BF16), pltpu.VMEM(halves, BF16), pltpu.VMEM(halves, BF16),
            pltpu.VMEM(halves, BF16), pltpu.VMEM(halves, BF16), pltpu.VMEM(halves, F32), dma((4,)),
            dma((2,)), dma((head,)), dma((head,)), dma((pairs,)), dma((pairs,)), dma((pairs,)),
            dma((pairs,)), dma((head, 4)), dma((head + 1, 4)),
        ],
        compiler_params=pltpu.CompilerParams(
            collective_id=3, has_side_effects=True, vmem_limit_bytes=60 << 20
        ),
        cost_estimate=cost(80),
        name="attention_back",
    )(keep, gated_own, og, o, qkv, decays, logits, through, pair_through, gain, kept,
      parts)


def finish_kernel(xn_in, proj_in, w_in, g_logits, ranked, up_own, rank_down, source,
                  gain, g_ffn, g_head,
                  g_x, grad, norm_sum, ffn_sum, head_sum, bias_sum, up_sum, down_sum,
                  turned, proj, w, outgoing, mine, paired, inbox, heads_in, parts, landed,
                  slim_high, slim_low, small, small_in, small_part,
                  small_heads, small_all, rows_sum, in_sem, pair_send, pair_recv, send, recv, x_send, x_recv,
                  p_sem, q_sem, a_send, a_recv, b_send, b_recv, c_send, c_recv):
    h, head = lax.axis_index("head"), lax.axis_size("head")
    rows, width = g_x.shape
    deep = grad.shape[0] * head
    pairs = lax.axis_size("seq") // 2

    loads = [
        pltpu.make_async_copy(proj_in, proj, in_sem.at[0]),
        pltpu.make_async_copy(w_in, w, in_sem.at[1]),
        pltpu.make_async_copy(xn_in, landed.at[pl.ds(0, xn_in.shape[0])], in_sem.at[2]),
    ]
    for load in loads:
        load.start()
    sums = PairSum(mine, paired, inbox, pair_send, pair_recv, send, recv)
    for load in loads:
        load.wait()
    turned[...] = landed[: xn_in.shape[0], :].T
    greet(("seq", "head"))
    total = LineSum(parts, landed, p_sem, q_sem, rows)
    logit_parts = split(g_logits[...])
    g_ranked = mms(logit_parts, split(up_own[...]), (1, 1))
    slim = split(g_ranked)
    slim_high[...], slim_low[...] = slim

    def chunk(i, _):
        b = near_order(h, head, head - 1 - i)
        at = pl.ds(pl.multiple_of(b * rows, rows), rows)
        rank_part = mms((slim_high[at, :], slim_low[at, :]), (rank_down[...],), (1, 1))
        parts[at, :] = (mm(proj[at, :], w[...], (1, 1), None) + rank_part).astype(BF16)

        @pl.when((b != h) & jnp.logical_not(total.inner))
        def _():
            for p in range(total.pieces):
                total.onward(b, p).start()

        return 0

    lax.fori_loop(0, head, chunk, 0)

    def gone(k, _):
        outgoing[k] = jnp.dot(
            turned[sums.block(k, True), :], proj[...], preferred_element_type=F32
        ).astype(BF16)
        sums.to_partner(outgoing.at[k], k).start()
        return 0

    lax.fori_loop(0, pairs, gone, 0)

    def kept(k, _):
        here = jnp.dot(turned[sums.block(k), :], proj[...], preferred_element_type=F32)
        sums.to_partner(outgoing.at[k], k).wait_recv()
        mine[k] = (here + paired[k].astype(F32)).astype(BF16)
        sums.pass_on(k)

        @pl.when(total.inner & (k < total.pieces))
        def _():
            total.relay(total.far_end, k)

        @pl.when(total.inner & (k > 0) & (k <= total.pieces))
        def _():
            total.relay(head - 1 - total.far_end, k - 1)

        return 0

    lax.fori_loop(0, pairs, kept, 0)

    @pl.when(total.inner)
    def _():
        for p in range(pairs, total.pieces + 1):
            if p < total.pieces:
                total.relay(total.far_end, p)
            total.relay(head - 1 - total.far_end, p - 1)
        for p in range(total.pieces):
            total.relay(head - 1 - h, p)

    thin = grad.shape[0]

    def to_head(hop, slot):
        to = lax.rem(h + hop, head)
        at = pl.ds(pl.multiple_of(to * thin, thin), thin)
        return push(mine.at[sums.own, at, :], heads_in.at[slot], x_send.at[hop], x_recv.at[slot], to)

    sums.advance(0)

    total.result(g_x)
    rows_sum[...] = jnp.zeros_like(rows_sum)
    band = rows_sum.shape[0]

    def norm_rows(r, _):
        at = pl.ds(pl.multiple_of(r * band, band), band)
        x = source[at, :].astype(F32)
        inv = lax.rsqrt(jnp.mean(x * x, axis=-1, keepdims=True) + 1e-6)
        plain, g = x * inv, g_x[at, :]
        scaled = g * gain[...]
        inner = jnp.mean(scaled * plain, axis=-1, keepdims=True)
        rows_sum[...] += g * plain
        g_x[at, :] = inv * (scaled - plain * inner)
        return 0

    lax.fori_loop(0, rows // band, norm_rows, 0)
    rank, dk = up_own.shape
    low, keys = rank // 2, up_sum.shape[1]
    g_down = mms(slim, (turned[...],), (0, 1))
    g_up = mms(split(ranked[...]), logit_parts, (0, 0))
    small[...] = jnp.zeros_like(small)
    small[:low, :width] = g_down[:low]
    small[:low, width:] = g_down[low:]
    own_keys = pl.multiple_of(h * dk, dk)
    small[low:, pl.ds(own_keys, dk)] = g_up[:low]
    small[low:, pl.ds(keys + own_keys, dk)] = g_up[low:]
    small[low : low + 1, width:] = jnp.sum(rows_sum[...], axis=0, keepdims=True)
    small[low + 1 : low + 2, width:] = g_ffn[...]
    small[low + 2 : low + 3, width : width + g_head.shape[1]] = g_head[0:1, :]
    small[low + 3 : low + 4, pl.ds(width + own_keys, dk)] = jnp.sum(
        g_logits[...], axis=0, keepdims=True
    )
    s, seq = lax.axis_index("seq"), lax.axis_size("seq")
    wide = small.shape[1] // seq

    def piece(ref, i):
        return ref.at[:, pl.ds(pl.multiple_of(i * wide, wide), wide)]

    def begin_small(axis, me, count, copy):
        for hop in range(1, count):
            copy(hop, me, lax.rem(me + hop, count)).start()

    def end_small(axis, me, count, copy):
        for hop in range(1, count):
            other = lax.rem(me + hop, count)
            copy(hop, other, other).wait_recv()

    def scatter(hop, slot, to):
        return push(
            piece(small, to), small_in.at[slot], a_send.at[hop], a_recv.at[slot], to, "seq"
        )

    def between(hop, slot, to):
        return push(small_part, small_heads.at[slot], b_send.at[hop], b_recv.at[slot], to)

    def spread(hop, slot, to):
        return push(
            small_part, piece(small_all, slot), c_send.at[hop], c_recv.at[slot], to, "seq"
        )

    begin_small("seq", s, seq, scatter)
    small_in[s] = small[:, pl.ds(pl.multiple_of(s * wide, wide), wide)]
    for step in range(1, sums.levels):
        sums.advance(step)
    for hop in range(1, head):
        to_head(hop, h).start()
    own_rows = pl.ds(pl.multiple_of(h * thin, thin), thin)
    heads_in[h] = mine[sums.own, own_rows, :]
    end_small("seq", s, seq, scatter)
    small_part[...] = jnp.sum(small_in[...], axis=0)
    begin_small("head", h, head, between)
    small_heads[h] = small_part[...]
    end_small("head", h, head, between)
    for hop in range(1, head):
        between(hop, h, lax.rem(h + hop, head)).wait_send()
    small_part[...] = jnp.sum(small_heads[...], axis=0)
    begin_small("seq", s, seq, spread)
    small_all[:, pl.ds(pl.multiple_of(s * wide, wide), wide)] = small_part[...]
    for hop in range(1, head):
        to_head(hop, lax.rem(h + hop, head)).wait_recv()
    dv = mine.shape[2] // 2 - dk
    for j in range(head):
        at, start = 0, 0
        for size in (dk, dk, dv, dv):
            grad[:, start + j * size : start + (j + 1) * size] = heads_in[j, :, at : at + size]
            at, start = at + size, start + head * size
    end_small("seq", s, seq, spread)
    down_sum[:low, :] = small_all[:low, :width]
    down_sum[low:, :] = small_all[:low, width:]
    up_sum[:low, :] = small_all[low:, :keys]
    up_sum[low:, :] = small_all[low:, keys : 2 * keys]
    norm_sum[...] = small_all[low : low + 1, width:]
    ffn_sum[...] = small_all[low + 1 : low + 2, width:]
    head_sum[...] = small_all[low + 2 : low + 3, width : width + head_sum.shape[1]]
    bias_sum[...] = small_all[low + 3 : low + 4, width : width + keys]
    for hop in range(1, seq):
        scatter(hop, s, lax.rem(s + hop, seq)).wait_send()
        spread(hop, s, lax.rem(s + hop, seq)).wait_send()
    sums.finish(lambda k: outgoing.at[k])
    for hop in range(1, head):
        to_head(hop, h).wait_send()
    total.finish()


def finish(
    xn, g_proj, w_in, g_logits, ranked, up_own, rank_down, source, gain, g_ffn, g_head
):
    seq, head = lax.axis_size("seq"), lax.axis_size("head")
    group, width = xn.shape
    columns, rank = w_in.shape[1], ranked.shape[1]
    deep, rows, pairs = width // seq, group // head, seq // 2
    dk = up_own.shape[1]
    vmem, anywhere = pl.BlockSpec(memory_space=pltpu.VMEM), pl.BlockSpec(memory_space=pl.ANY)
    dma = pltpu.SemaphoreType.DMA
    blocks = lambda count, w: pltpu.VMEM((count, deep, w), BF16)
    ends = lambda w: pltpu.VMEM((head, deep // head, w), BF16)
    moves = dma((2, pairs - 1))
    return pl.pallas_call(
        finish_kernel,
        out_shape=(
            jax.ShapeDtypeStruct((rows, width), F32),
            jax.ShapeDtypeStruct((deep // head, columns * head), BF16),
            jax.ShapeDtypeStruct((1, width), F32),
            jax.ShapeDtypeStruct((1, width), F32),
            jax.ShapeDtypeStruct((1, g_head.shape[1]), F32),
            jax.ShapeDtypeStruct((1, dk * head), F32),
            jax.ShapeDtypeStruct((rank, dk * head), F32),
            jax.ShapeDtypeStruct((rank, width), F32),
        ),
        in_specs=[anywhere] * 3 + [vmem] * 8,
        out_specs=(vmem,) * 8,
        scratch_shapes=[
            pltpu.VMEM((width, group), BF16), pltpu.VMEM(g_proj.shape, BF16),
            pltpu.VMEM(w_in.shape, BF16), blocks(pairs, columns), blocks(pairs, columns),
            blocks(pairs, columns), blocks(pairs - 1, columns), ends(columns),
            pltpu.VMEM((group, width), BF16), pltpu.VMEM((group + rows, width), BF16),
            pltpu.VMEM(ranked.shape, BF16), pltpu.VMEM(ranked.shape, BF16),
            pltpu.VMEM((rank, 2 * width), F32), pltpu.VMEM((seq, rank, 2 * width // seq), F32),
            pltpu.VMEM((rank, 2 * width // seq), F32),
            pltpu.VMEM((head, rank, 2 * width // seq), F32),
            pltpu.VMEM((rank, 2 * width), F32), pltpu.VMEM((16, width), F32),
            dma((3,)), dma((pairs,)), dma((pairs,)), moves, moves, dma((head,)), dma((head,)),
            dma((head, 4)), dma((head + 1, 4)),
            dma((seq,)), dma((seq,)), dma((head,)), dma((head,)), dma((seq,)), dma((seq,)),
        ],
        compiler_params=pltpu.CompilerParams(
            collective_id=5, has_side_effects=True, vmem_limit_bytes=60 << 20
        ),
        cost_estimate=cost(95),
        name="finish",
    )(xn, g_proj, w_in, g_logits, ranked, up_own, rank_down, source, gain, g_ffn, g_head)


def weight_grad_kernel(left, right, *rest):
    out, turned = rest[-2:]

    @pl.when(pl.program_id(1) == 0)
    def _():
        turned[...] = left[...].T

    out[...] = jnp.dot(turned[...], right[...], preferred_element_type=F32).astype(BF16)


def weight_grad(left, right, into, columns, start, tile):
    depth, rows = left.shape
    high = min(rows, 512)
    first = start // tile
    given = () if into is None else (into,)
    return pl.pallas_call(
        weight_grad_kernel,
        out_shape=jax.ShapeDtypeStruct((rows, columns), BF16),
        grid=(rows // high, right.shape[1] // tile),
        in_specs=[
            pl.BlockSpec((depth, high), lambda i, j: (0, i)),
            pl.BlockSpec((depth, tile), lambda i, j: (0, j)),
        ]
        + [pl.BlockSpec(memory_space=pl.ANY) for _ in given],
        out_specs=pl.BlockSpec((high, tile), lambda i, j: (i, first + j)),
        scratch_shapes=[pltpu.VMEM((high, depth), BF16)],
        input_output_aliases={2: 0} if given else {},
        compiler_params=pltpu.CompilerParams(
            dimension_semantics=("arbitrary", "arbitrary"), vmem_limit_bytes=48 << 20
        ),
        cost_estimate=pl.CostEstimate(
            flops=2 * depth * rows * right.shape[1],
            bytes_accessed=2 * (depth * rows + (depth + rows) * right.shape[1]),
            transcendentals=0,
        ),
        name="weight_grad",
    )(left, right, *given)


def gather_weight(w):
    return lax.all_gather(w, "seq", axis=0, tiled=True)


def scatter_grad(g):
    return lax.psum_scatter(g.astype(BF16), "seq", scatter_dimension=0, tiled=True)


def dot(a, b, contract, precision=None):
    return lax.dot_general(
        a, b, (((contract[0],), (contract[1],)), ((), ())),
        precision=precision, preferred_element_type=F32,
    )


def rms(x, epsilon):
    return lax.rsqrt(jnp.mean(x * x, axis=-1, keepdims=True) + epsilon)


def norm_back(grad, gain, normed, inv):
    scaled = grad * gain
    inner = jnp.mean(scaled * normed, axis=-1, keepdims=True)
    return inv * (scaled - normed * inner), jnp.sum(grad * normed, axis=0)


def on_device(
    tokens, starts, cotangent, mix_in, mix_out, gate_up, down_proj,
    norm_gain, ffn_gain, head_gain, rank_down, rank_up, gate_bias,
):
    micro, rows, width = tokens.shape
    heads, seq = lax.axis_size("head"), lax.axis_size("seq")
    head = lax.axis_index("head")
    keys, dv = rank_up.shape[1], head_gain.shape[0]
    dk, vals = keys // heads, dv * heads
    hidden_units = down_proj.shape[1]
    group = heads * micro * rows
    proj_width = 2 * dk + 2 * dv

    def own_columns(w, start, size):
        return lax.dynamic_slice_in_dim(w, start + head * size, size, 1)

    w_in_own = jnp.concatenate(
        [
            own_columns(mix_in, 0, dk),
            own_columns(mix_in, keys, dk),
            own_columns(mix_in, 2 * keys, dv),
            own_columns(mix_in, 2 * keys + vals, dv),
        ],
        axis=1,
    )
    later = gather_weight(
        jnp.concatenate(
            [gate_up.reshape(gate_up.shape[0], 2 * hidden_units), down_proj, mix_out], axis=1
        )
    )
    w_out = later[:, 3 * hidden_units :]
    up_own = own_columns(rank_up, 0, dk)
    bias_own = lax.dynamic_slice_in_dim(gate_bias, head * dk, dk, 0)

    xn, w_in = gather_norm(
        tokens.reshape(micro * rows, width), norm_gain.reshape(1, width), w_in_own
    )
    qkv = dot(xn, w_in[:, : 2 * dk + dv], (1, 0)).astype(BF16)
    og = dot(xn, w_in[:, 2 * dk + dv :], (1, 0))
    ranked = dot(xn, rank_down, (1, 0))
    logits = dot(ranked, up_own, (1, 0), HIGHEST) + bias_own
    decays = (jax.nn.log_sigmoid(logits) / GATE_NORM).astype(BF16)

    def blocks(x):
        return x.reshape(heads, micro, rows, x.shape[-1])

    qkv_b, og_b, decays_b = blocks(qkv), blocks(og), blocks(decays)
    gain_row = head_gain.reshape(1, dv)
    keep = 1.0 - jnp.broadcast_to(starts.T[:, :, None, None], (heads, micro, 1, dk)).astype(F32)
    o_b, gated, through, pair_through, kept, all_cot = attention_forward(
        keep, qkv_b, decays_b, og_b, gain_row, cotangent.reshape(micro * rows, width)
    )

    source = tokens.astype(F32).reshape(micro * rows, width)
    hidden = source + dot(gated, w_out, (1, 1))
    inv_ffn = rms(hidden, 1e-6)
    plain_ffn = hidden * inv_ffn
    h2 = (plain_ffn * ffn_gain).astype(BF16)

    g_h2, ffn_part, grads = feed_forward(h2, all_cot, later, hidden_units, heads)

    back_ffn, g_ffn_gain = norm_back(g_h2, ffn_gain, plain_ffn, inv_ffn)
    g_hidden = cotangent.astype(F32).reshape(micro * rows, width) + back_ffn
    g_mixed = g_hidden.astype(BF16)
    grads = scatter_grad(weight_grad(g_mixed, gated, grads, later.shape[1], 0, vals))
    g_gated = dot(g_mixed, w_out, (1, 0)).astype(BF16)
    g_proj_b, g_logits_b, g_head_gain, ffn_out = attention_back(
        keep, g_gated, og_b, o_b, qkv_b, decays_b, blocks(logits), through, pair_through, gain_row, kept, ffn_part.reshape(group, width),
    )
    output = (hidden + ffn_out).astype(BF16)
    g_proj, g_logits = g_proj_b.reshape(group, proj_width), g_logits_b.reshape(group, dk)
    back_in, grad_in, *small, g_rank_down = finish(
        xn, g_proj, w_in, g_logits, ranked, up_own, rank_down, tokens.reshape(micro * rows, width),
        norm_gain.reshape(1, width), g_ffn_gain.reshape(1, width), g_head_gain,
    )
    g_norm_gain, g_ffn_gain, g_head_gain, g_bias, g_rank_up = small
    input_grad = g_hidden + back_in
    slab = width // (seq * heads)
    grad_in, grads = lax.optimization_barrier((grad_in, grads))
    grad_ffn = grads[:, vals:]
    grad_out = lax.all_to_all(
        grads[:, :vals].reshape(heads, slab, vals), "head", split_axis=0, concat_axis=0, tiled=True
    )
    grad_out = grad_out.astype(F32).sum(0)
    return (
        output.reshape(tokens.shape),
        input_grad.reshape(tokens.shape),
        grad_in.astype(F32),
        grad_out,
        grad_ffn[:, : 2 * hidden_units].astype(F32).reshape(-1, 2, hidden_units),
        grad_ffn[:, 2 * hidden_units :].astype(F32),
        g_norm_gain.reshape(norm_gain.shape),
        g_ffn_gain.reshape(ffn_gain.shape),
        g_head_gain.reshape(head_gain.shape),
        g_rank_down.T,
        g_rank_up,
        g_bias.reshape(gate_bias.shape),
    )


def solution(mesh):
    rows = P(None, ("seq", "head"), None)
    return jax.shard_map(
        on_device,
        mesh=mesh,
        in_specs=(
            rows, P(None, "seq"), rows, P("seq", None), P("seq", None),
            P("seq", None, "head"), P("seq", "head"), P(), P(), P(), P(), P(), P(),
        ),
        out_specs=(
            rows, rows, P(("seq", "head"), None), P(("seq", "head"), None),
            P("seq", None, "head"), P("seq", "head"), P(), P(), P(), P(), P(), P(),
        ),
        check_vma=False,
    )
```

```python
import functools

import jax
import jax.numpy as jnp
from jax import lax
from jax.experimental import pallas as pl
from jax.experimental.pallas import tpu as pltpu
from jax.sharding import PartitionSpec as P

HIGHEST = lax.Precision.HIGHEST
GATE_NORM = 16.0
BF16 = jnp.bfloat16
F32 = jnp.float32


def mm(a, b, contract, precision=HIGHEST):
    return lax.dot_general(
        a, b, ((contract[:1], contract[1:]), ((), ())),
        precision=precision, preferred_element_type=F32,
    )


def split(x):
    high = x.astype(BF16)
    return high, (x - high.astype(F32)).astype(BF16)


def mms(left, right, contract):
    total = mm(left[0], right[0], contract, None)
    if len(right) > 1:
        total += mm(left[0], right[1], contract, None)
    if len(left) > 1:
        total += mm(left[1], right[0], contract, None)
    return total


def lower_ones(size):
    rows = lax.broadcasted_iota(jnp.int32, (size, size), 0)
    cols = lax.broadcasted_iota(jnp.int32, (size, size), 1)
    return rows >= cols


def running(decay_low):
    ones = lower_ones(decay_low.shape[0]).astype(F32).astype(BF16)
    return mm(ones, decay_low, (1, 0), None)


def sigmoid(x):
    return 1.0 / (1.0 + jnp.exp(-x))


def cost(micros):
    return pl.CostEstimate(flops=0, bytes_accessed=int(micros * 3.0e6), transcendentals=0)


def greet(axes):
    barrier = pltpu.get_barrier_semaphore()
    met = 0
    for axis in axes:
        me, count = lax.axis_index(axis), lax.axis_size(axis)
        for hop in range(1, count):
            pl.semaphore_signal(
                barrier, inc=1, device_id={axis: lax.rem(me + hop, count)},
                device_id_type=pl.DeviceIdType.MESH,
            )
        met += count - 1
    pl.semaphore_wait(barrier, met)


def push(src, dst, send, recv, to, axis="head"):
    return pltpu.make_async_remote_copy(
        src_ref=src, dst_ref=dst, send_sem=send, recv_sem=recv,
        device_id={axis: to}, device_id_type=pl.DeviceIdType.MESH,
    )


def near_order(z, count, i):
    both = jnp.minimum(z, count - 1 - z)
    left = z > count - 1 - z
    paired = jnp.where(i % 2 == 1, z - (i + 1) // 2, z + i // 2)
    single = jnp.where(left, z - (i - both), z + (i - both))
    return jnp.where(i <= 2 * both, paired, single)


class Line:
    def __init__(self, own, all_rows, send, recv):
        self.own, self.all, self.send, self.recv = own, all_rows, send, recv
        self.z, self.count = lax.axis_index("head"), lax.axis_size("head")
        self.rows, self.parts = own.shape[0], recv.shape[1]
        self.deep = self.rows // self.parts

    def at(self, b):
        return self.all.at[pl.ds(pl.multiple_of(b * self.rows, self.rows), self.rows)]

    def part(self, b, p):
        start = b * self.rows + p * self.deep
        return self.all.at[pl.ds(pl.multiple_of(start, self.deep), self.deep)]

    def first(self, way, p):
        to = lax.rem(self.z + (1 if way == 0 else self.count - 1), self.count)
        src = self.own.at[pl.ds(p * self.deep, self.deep)]
        return push(
            src, self.part(self.z, p), self.send.at[way, p], self.recv.at[self.z, p], to
        )

    def each_first(self, act):
        for p in range(self.parts):
            pl.when(self.z < self.count - 1)(lambda p=p: act(self.first(0, p)))
            pl.when(self.z > 0)(lambda p=p: act(self.first(1, p)))

    def start(self):
        self.each_first(lambda copy: copy.start())

    def passing(self, i, b, p):
        z, count = self.z, self.count
        to = jnp.where(b < z, z + 1, z - 1)
        going = ((b < z) & (z < count - 1)) | ((b > z) & (z > 0))
        copy = push(
            self.part(b, p), self.part(b, p), self.send.at[i + 1, p], self.recv.at[b, p],
            lax.rem(to + count, count),
        )
        return copy, going

    def receive(self, i, b, p=0):
        copy, going = self.passing(i, b, p)
        copy.wait_recv()
        pl.when(going)(copy.start)

    def finish(self):
        def sent(i, _):
            for p in range(self.parts):
                copy, going = self.passing(i, near_order(self.z, self.count, i), p)
                pl.when(going)(copy.wait_send)
            return 0

        lax.fori_loop(1, self.count, sent, 0)
        self.each_first(lambda copy: copy.wait_send())


class LineSum:
    def __init__(self, parts, landed, send, recv, rows):
        self.parts, self.landed, self.send, self.recv = parts, landed, send, recv
        self.z, self.count = lax.axis_index("head"), lax.axis_size("head")
        self.rows, self.pieces = rows, send.shape[1]
        self.deep = rows // self.pieces
        self.inner = (self.z > 0) & (self.z < self.count - 1)
        self.far_end = jnp.where(self.z < self.count - 1 - self.z, self.count - 1, 0)

    def piece(self, b, p):
        return pl.ds(pl.multiple_of(b * self.rows + p * self.deep, self.deep), self.deep)

    def onward(self, b, p):
        z, count = self.z, self.count
        to = jnp.where(b > z, z + 1, z - 1)
        slot = jnp.where((to == b) & (z > b), count, b)
        return push(
            self.parts.at[self.piece(b, p)], self.landed.at[self.piece(slot, p)],
            self.send.at[b, p], self.recv.at[slot, p], lax.rem(to + count, count),
        )

    def send_all(self):
        @pl.when(jnp.logical_not(self.inner))
        def _():
            for i in range(1, self.count):
                b = jnp.where(self.z == 0, self.count - i, i - 1)
                for p in range(self.pieces):
                    self.onward(b, p).start()

    def arrived(self, slot, p):
        at = self.piece(slot, p)
        push(
            self.landed.at[at], self.landed.at[at], self.send.at[0, p], self.recv.at[slot, p],
            lax.rem(self.z + 1, self.count),
        ).wait_recv()
        return self.landed[at, :].astype(F32)

    def relay(self, b, p):
        at = self.piece(b, p)
        self.parts[at, :] = (self.parts[at, :].astype(F32) + self.arrived(b, p)).astype(BF16)
        self.onward(b, p).start()

    def relay_in_turn(self, j):
        pieces = self.pieces

        @pl.when(self.inner & (j < pieces))
        def _():
            self.relay(self.count - 1 - self.z, j)

        @pl.when(self.inner & (j >= pieces))
        def _():
            self.relay(self.far_end, j - pieces)

        @pl.when(self.inner & (j > pieces))
        def _():
            self.relay(self.count - 1 - self.far_end, j - pieces - 1)

    def relay_last(self):
        @pl.when(self.inner)
        def _():
            self.relay(self.count - 1 - self.far_end, self.pieces - 1)

    def result(self, out):
        z, count = self.z, self.count
        for p in range(self.pieces):
            here = pl.ds(p * self.deep, self.deep)
            out[here, :] = self.parts[self.piece(z, p), :].astype(F32)

            @pl.when(z > 0)
            def _():
                out[here, :] += self.arrived(z, p)

            @pl.when(z < count - 1)
            def _():
                out[here, :] += self.arrived(count, p)

    def finish(self):
        def sent(i, _):
            b = near_order(self.z, self.count, i)
            for p in range(self.pieces):
                self.onward(b, p).wait_send()
            return 0

        lax.fori_loop(1, self.count, sent, 0)


class PairSum:
    def __init__(self, mine, paired, inbox, pair_send, pair_recv, send, recv):
        self.mine, self.paired, self.inbox = mine, paired, inbox
        self.pair_send, self.pair_recv, self.send, self.recv = pair_send, pair_recv, send, recv
        self.s, self.pairs = lax.axis_index("seq"), lax.axis_size("seq") // 2
        self.side, self.own = lax.rem(self.s, 2), self.s // 2
        self.deep, self.half = mine.shape[1], mine.shape[2] // 2
        self.levels = self.pairs.bit_length() - 1
        assert self.pairs == 1 << self.levels

    def block(self, k, other=False):
        i = 2 * k + (1 - self.side if other else self.side)
        return pl.ds(pl.multiple_of(i * self.deep, self.deep), self.deep)

    def to_partner(self, src, k):
        return push(
            src, self.paired.at[k], self.pair_send.at[k], self.pair_recv.at[k],
            self.s + 1 - 2 * self.side, "seq",
        )

    def bit(self, i, level):
        return lax.rem(i // (1 << level), 2)

    def move(self, side, slot, k, level):
        columns = pl.ds(side * self.half, self.half)
        to = self.s + (1 - 2 * self.bit(self.own, level)) * (2 << level)
        return push(
            self.mine.at[k, :, columns], self.inbox.at[slot, :, columns],
            self.send.at[side, slot], self.recv.at[side, slot], to, "seq",
        )

    def moves(self, side, step):
        order = list(range(self.levels))
        if side:
            order.reverse()
        level, free = order[step], sorted(order[step + 1 :])
        fixed = sum((self.bit(self.own, d) * (1 << d) for d in order[:step]), 0)
        offset = self.pairs - (1 << (self.levels - step))
        here = self.bit(self.own, level) * (1 << level)
        for c in range(1 << len(free)):
            rest = fixed + sum(((c >> j) & 1) << d for j, d in enumerate(free))
            yield offset + c, rest + here, rest + (1 << level) - here, level

    def pass_on(self, k):
        top = 1 << (self.levels - 1)
        pl.when(self.bit(k, 0) != self.bit(self.own, 0))(self.move(0, k // 2, k, 0).start)
        pl.when(k // top != self.own // top)(
            self.move(1, lax.rem(k, top), k, self.levels - 1).start
        )

    def advance(self, step):
        for side in range(2):
            columns = slice(side * self.half, (side + 1) * self.half)
            for slot, keep, gone, level in self.moves(side, step):
                self.move(side, slot, gone, level).wait_recv()
                self.mine[keep, :, columns] = (
                    self.mine[keep, :, columns].astype(F32)
                    + self.inbox[slot, :, columns].astype(F32)
                ).astype(BF16)
            if step + 1 < self.levels:
                for slot, keep, gone, level in self.moves(side, step + 1):
                    self.move(side, slot, gone, level).start()

    def finish(self, src):
        for k in range(self.pairs):
            self.to_partner(src(k), k).wait_send()
        for side in range(2):
            for step in range(self.levels):
                for slot, keep, gone, level in self.moves(side, step):
                    self.move(side, slot, gone, level).wait_send()


def gather_norm_kernel(own, gain, shard, normed, rows_of_all, rows_all, here_sem, send, recv,
                       w_sem, w_peer, w_pair, w_recv):
    z, count, rows = lax.axis_index("head"), lax.axis_size("head"), own.shape[0]
    greet(("seq", "head"))
    line = Line(own, rows_all, send, recv)
    line.start()
    here = pltpu.make_async_copy(own, line.at(z), here_sem)
    here.start()

    s, deep = lax.axis_index("seq"), shard.shape[0]
    side, pairs, own_pair = lax.rem(s, 2), lax.axis_size("seq") // 2, s // 2
    partner = s + 1 - 2 * side

    def shard_at(i):
        return rows_of_all.at[pl.ds(pl.multiple_of(i * deep, deep), deep)]

    def to_peer(k):
        return push(shard, shard_at(s), w_peer.at[k], w_recv.at[s], 2 * k + side, "seq")

    def from_peer(k):
        i = 2 * k + side
        return push(shard, shard_at(i), w_peer.at[k], w_recv.at[i], partner, "seq")

    def to_partner(k):
        i = 2 * k + side
        return push(shard_at(i), shard_at(i), w_pair.at[k], w_recv.at[i], partner, "seq")

    def from_partner(k):
        i = 2 * k + 1 - side
        return push(shard_at(i), shard_at(i), w_pair.at[k], w_recv.at[i], partner, "seq")

    mine = pltpu.make_async_copy(shard, shard_at(s), w_sem)
    mine.start()
    for k in range(pairs):
        pl.when(own_pair != k)(to_peer(k).start)
    mine.wait()
    to_partner(own_pair).start()
    here.wait()
    band = 16

    def step(i, _):
        b = near_order(z, count, i)
        pl.when(i > 0)(lambda: line.receive(i, b))

        def norm(r, _):
            at = pl.ds(pl.multiple_of(b * rows + r * band, band), band)
            x = rows_all[at, :].astype(F32)
            inv = lax.rsqrt(jnp.mean(x * x, axis=-1, keepdims=True) + 1e-6)
            normed[at, :] = (x * inv * gain[...]).astype(BF16)
            return 0

        lax.fori_loop(0, rows // band, norm, 0)
        return 0

    lax.fori_loop(0, count, step, 0)
    for k in range(pairs):

        @pl.when(own_pair != k)
        def _():
            from_peer(k).wait_recv()
            to_partner(k).start()

    for k in range(pairs):
        from_partner(k).wait_recv()
    for k in range(pairs):
        to_partner(k).wait_send()
        pl.when(own_pair != k)(to_peer(k).wait_send)
    line.finish()


def gather_norm(x, gain, shard):
    rows, width = x.shape
    seq = lax.axis_size("seq")
    anywhere = pl.BlockSpec(memory_space=pl.ANY)
    count = lax.axis_size("head")
    vmem = pl.BlockSpec(memory_space=pltpu.VMEM)
    dma = pltpu.SemaphoreType.DMA
    return pl.pallas_call(
        gather_norm_kernel,
        out_shape=(
            jax.ShapeDtypeStruct((count * rows, width), BF16),
            jax.ShapeDtypeStruct((seq * shard.shape[0], shard.shape[1]), BF16),
        ),
        in_specs=[vmem, vmem, anywhere],
        out_specs=(vmem, anywhere),
        scratch_shapes=[
            pltpu.VMEM((count * rows, width), BF16), dma(()), dma((count + 1, 1)), dma((count, 1)),
            dma(()), dma((seq // 2,)), dma((seq // 2,)), dma((seq,)),
        ],
        compiler_params=pltpu.CompilerParams(
            collective_id=1, has_side_effects=True, vmem_limit_bytes=32 << 20
        ),
        cost_estimate=cost(50),
        name="gather_norm",
    )(x, gain, shard)


def swap_slices(own, got, send, recv):
    side = lax.rem(lax.axis_index("seq"), 2)
    me, count = lax.axis_index("seq") // 2, lax.axis_size("seq") // 2

    def copy(hop, index):
        to = lax.rem(me + hop, count)
        return push(own.at[to], got.at[index], send.at[hop], recv.at[index], 2 * to + side, "seq")

    def start(hop, _):
        copy(hop, me).start()
        return 0

    def wait_recv(hop, _):
        copy(hop, lax.rem(me + hop, count)).wait_recv()
        return 0

    def wait_send(hop, _):
        copy(hop, me).wait_send()
        return 0

    def begin():
        lax.fori_loop(1, count, start, 0)
        got[me] = own[me]

    def end():
        lax.fori_loop(1, count, wait_recv, 0)

    def drain():
        lax.fori_loop(1, count, wait_send, 0)

    return begin, end, drain


def to_mate(src, dst, send, recv):
    s = lax.axis_index("seq")
    return push(src, dst, send, recv, s + 1 - 2 * lax.rem(s, 2), "seq")


def sided(own, mate):
    first = lax.rem(lax.axis_index("seq"), 2) == 0
    return jnp.where(first, own, mate), jnp.where(first, mate, own)


def scan_states(reverse, own, through, out):
    count, part = out.shape[0], out.shape[2]

    def step(k, state):
        j = count - 1 - k if reverse else k
        out[j] = state.astype(BF16)
        decay = through[j, :, 0:1, :].astype(F32) + through[j, :, 1:2, :].astype(F32)
        return decay * state + own[j, :, :part, :].astype(F32)

    lax.fori_loop(0, count, step, jnp.zeros(out.shape[1:], F32))


def front_kernel(keep, qkv, decay, og, gain, rows_own,
                 o_out, gated, through, pair_through, kept_out, rows_all,
                 kept, runs, state, sending, got, scanned, before, leaving, mate_out, mate_in,
                 back_out, back_in, first_state,
                 here_sem, go, come, s_send, s_recv, b_send, b_recv, z_send, z_recv, k_sem, m_sem):
    h, head = lax.axis_index("head"), lax.axis_size("head")
    count, micro, rows, dk = decay.shape
    dv = og.shape[-1]
    slices, part = scanned.shape[0], scanned.shape[2]
    scale = dk ** (-0.5)
    greet(("seq", "head"))
    line = Line(rows_own, rows_all, go, come)
    line.start()
    here = pltpu.make_async_copy(rows_own, line.at(h), here_sem)
    here.start()

    state[...] = jnp.zeros_like(state)
    passed = [jnp.zeros((1, dk), F32)] * micro
    alive = [jnp.ones((1, dk), F32)] * micro
    for b in range(count):
        for m in range(micro):
            run = running(decay[b, m])
            runs[b, m] = run
            last = run[rows - 1 : rows, :]
            carried = qkv[b, m, :, dk : 2 * dk].astype(F32) * jnp.exp(last - run)
            fresh = mms((qkv[b, m, :, 2 * dk :],), split(carried), (0, 0))
            kept[b, m] = fresh
            state[m] = jnp.exp(last) * (state[m] * keep[b, m]) + fresh
            passed[m] = passed[m] + last
            alive[m] = alive[m] * keep[b, m]
    tail = sending.shape[2] - part
    at = lax.broadcasted_iota(jnp.int32, (tail, dk), 0)
    half = dv // 2
    side = lax.rem(lax.axis_index("seq"), 2)
    own_half = pl.ds(pl.multiple_of(side * half, half), half)
    mate_half = pl.ds(pl.multiple_of((1 - side) * half, half), half)

    def as_rows(value):
        high, low = split(value)
        return jnp.where(at == 0, high.astype(F32), jnp.where(at == 1, low.astype(F32), 0.0))

    own_rows = [as_rows(jnp.exp(passed[m]) * alive[m]) for m in range(micro)]
    for m in range(micro):
        mate_out[m, :half, :] = state[m, mate_half, :].astype(BF16)
        mate_out[m, half:, :] = own_rows[m].astype(BF16)
    swap = to_mate(mate_out, mate_in, m_sem.at[0], m_sem.at[1])
    swap.start()
    swap.wait_recv()
    first_through = []
    for m in range(micro):
        firsts, seconds = sided(own_rows[m], mate_in[m, half:, :].astype(F32))
        pair_through[0, m], pair_through[1, m] = firsts.astype(BF16), seconds.astype(BF16)
        first, second = firsts[0:1] + firsts[1:2], seconds[0:1] + seconds[1:2]
        first_through.append(first)
        start, after = sided(state[m, own_half, :], mate_in[m, :half, :].astype(F32))
        first_state[m] = start
        pair = second * start + after
        both = as_rows(first * second).astype(BF16)
        for i in range(slices):
            sending[i, m, :part, :] = pair[i * part : (i + 1) * part, :].astype(BF16)
            sending[i, m, part:, :] = both
    begin, end, drain = swap_slices(sending, got, s_send, s_recv)
    begin()
    causal = lower_ones(rows)

    def inside(b, _):
        for m in range(micro):
            run = runs[b, m]
            queried = split(qkv[b, m, :, :dk].astype(F32) * (jnp.exp(run) * scale))
            keyed = split(qkv[b, m, :, dk : 2 * dk].astype(F32) * jnp.exp(-run))
            scores = jnp.where(causal, mms(queried, keyed, (1, 1)), 0.0)
            o_out[b, m] = mms(split(scores), (qkv[b, m, :, 2 * dk :],), (1, 0))
        return 0

    lax.fori_loop(0, count, inside, 0)
    line.receive(1, near_order(h, head, 1))
    end()
    through[...] = got[:, :, part:, :]
    scan_states(False, got, through, scanned)
    begin_back, end_back, drain_back = swap_slices(scanned, before, b_send, b_recv)
    begin_back()
    line.receive(2, near_order(h, head, 2))
    end_back()
    for m in range(micro):
        entry = before[:, m].astype(F32).reshape(half, dk)
        own, mate = sided(entry, first_through[m] * entry + first_state[m])
        state[m, own_half, :] = own
        back_out[m] = mate.astype(BF16)
    swap_back = to_mate(back_out, back_in, m_sem.at[2], m_sem.at[3])
    swap_back.start()
    swap_back.wait_recv()
    for m in range(micro):
        state[m, mate_half, :] = back_in[m].astype(F32)

    def to_owner(b):
        columns = gated.at[:, pl.ds(pl.multiple_of(h * dv, dv), dv)]
        return push(leaving.at[b], columns, z_send.at[b], z_recv.at[h], b)

    def save(b):
        return pltpu.make_async_copy(kept.at[b], kept_out.at[b], k_sem.at[b])

    def across(b, _):
        for m in range(micro):
            run = runs[b, m]
            queried = split(qkv[b, m, :, :dk].astype(F32) * (jnp.exp(run) * scale))
            entry = state[m] * keep[b, m]
            state[m] = jnp.exp(run[rows - 1 : rows, :]) * entry + kept[b, m]
            kept[b, m] = entry
            o = o_out[b, m] + mms(queried, split(entry), (1, 1))
            o_out[b, m] = o
            inv = lax.rsqrt(jnp.mean(o * o, axis=-1, keepdims=True) + 1e-5)
            normed = (o * inv * gain[...]).astype(BF16).astype(F32)
            gate = og[b, m]
            leaving[b, m * rows : (m + 1) * rows, :] = (normed * gate * sigmoid(gate)).astype(BF16)
        save(b).start()
        pl.when(b != h)(to_owner(b).start)

        @pl.when(b == 1)
        def _():
            line.receive(3, near_order(h, head, 3))

        return 0

    lax.fori_loop(0, count, across, 0)
    gated[:, pl.ds(pl.multiple_of(h * dv, dv), dv)] = leaving[h]
    for hop in range(1, head):
        other = lax.rem(h + hop, head)
        columns = gated.at[:, pl.ds(pl.multiple_of(other * dv, dv), dv)]
        push(leaving.at[other], columns, z_send.at[other], z_recv.at[other], other).wait_recv()
        to_owner(other).wait_send()
    for b in range(count):
        save(b).wait()
    here.wait()
    line.finish()
    drain()
    drain_back()
    swap.wait_send()
    swap_back.wait_send()


def attention_forward(keep, qkv, decays, og, gain, rows_own):
    blocks, micro, rows, width = qkv.shape
    dk, dv = decays.shape[-1], og.shape[-1]
    head, seq = lax.axis_size("head"), lax.axis_size("seq")
    assert blocks == head and head == 4
    pairs, half, tail = seq // 2, dv // 2, 16
    part = half // pairs
    own_rows = micro * rows
    vmem, anywhere = pl.BlockSpec(memory_space=pltpu.VMEM), pl.BlockSpec(memory_space=pl.ANY)
    dma = pltpu.SemaphoreType.DMA
    states, wider = (pairs, micro, part, dk), (pairs, micro, part + tail, dk)
    return pl.pallas_call(
        front_kernel,
        out_shape=(
            jax.ShapeDtypeStruct((blocks, micro, rows, dv), F32),
            jax.ShapeDtypeStruct((own_rows, head * dv), BF16),
            jax.ShapeDtypeStruct((pairs, micro, tail, dk), BF16),
            jax.ShapeDtypeStruct((2, micro, tail, dk), BF16),
            jax.ShapeDtypeStruct((blocks, micro, dv, dk), F32),
            jax.ShapeDtypeStruct((head * rows_own.shape[0], rows_own.shape[1]), BF16),
        ),
        in_specs=[vmem] * 5 + [anywhere],
        out_specs=(vmem,) * 4 + (anywhere,) * 2,
        scratch_shapes=[
            pltpu.VMEM((blocks, micro, dv, dk), F32), pltpu.VMEM((blocks, micro, rows, dk), F32),
            pltpu.VMEM((micro, dv, dk), F32), pltpu.VMEM(wider, BF16), pltpu.VMEM(wider, BF16),
            pltpu.VMEM(states, BF16), pltpu.VMEM(states, BF16),
            pltpu.VMEM((blocks, own_rows, dv), BF16),
            pltpu.VMEM((micro, half + tail, dk), BF16), pltpu.VMEM((micro, half + tail, dk), BF16),
            pltpu.VMEM((micro, half, dk), BF16), pltpu.VMEM((micro, half, dk), BF16),
            pltpu.VMEM((micro, half, dk), F32),
            dma(()), dma((head + 1, 1)), dma((head, 1)), dma((pairs,)), dma((pairs,)), dma((pairs,)),
            dma((pairs,)), dma((head,)), dma((head,)), dma((blocks,)), dma((4,)),
        ],
        compiler_params=pltpu.CompilerParams(
            collective_id=2, has_side_effects=True, vmem_limit_bytes=40 << 20
        ),
        cost_estimate=cost(90),
        name="attention_forward",
    )(keep, qkv, decays, og, gain, rows_own)


def ffn_kernel(count, x_own, c_all, w, g_x, f_parts, grad,
               wv, xs, cs, act, lin, parts, landed, turned, turned_c, tiles,
               w_sem, own_sem, go_sem, x_sem, p_sem, q_sem, o_sem):
    z = lax.axis_index("head")
    rows, width = x_own.shape
    hidden = act.shape[1] // 3
    chunk = lambda b: pl.ds(pl.multiple_of(b * rows, rows), rows)

    weights = [
        pltpu.make_async_copy(
            w.at[:, pl.ds(k * hidden, hidden)], wv.at[:, pl.ds(k * hidden, hidden)], w_sem.at[k]
        )
        for k in range(3)
    ]
    own = [
        pltpu.make_async_copy(x_own, xs.at[chunk(z)], own_sem.at[0]),
        pltpu.make_async_copy(c_all, cs, own_sem.at[1]),
    ]
    for copy in own + weights:
        copy.start()
    greet(("head",))
    line = Line(x_own, xs, go_sem, x_sem)
    line.start()
    for copy in own + weights:
        copy.wait()

    total = LineSum(parts, landed, p_sem, q_sem, rows)

    halves = x_sem.shape[1]
    deep = rows // halves
    each = total.pieces // halves

    def step(t, _):
        i, half = t // halves, lax.rem(t, halves)
        b = near_order(z, count, i)
        pl.when(i > 0)(lambda: line.receive(i, b, half))
        start = b * rows + half * deep
        at = pl.ds(pl.multiple_of(start, deep), deep)
        x = xs[at, :]
        lin[0] = jnp.dot(x, wv[:, :hidden], preferred_element_type=F32)
        lin[1] = jnp.dot(x, wv[:, hidden : 2 * hidden], preferred_element_type=F32)
        lin[2] = jnp.dot(cs[at, :], wv[:, 2 * hidden :], preferred_element_type=F32)
        band = 16

        def act_rows(r, _):
            here = pl.ds(pl.multiple_of(r * band, band), band)
            there = pl.ds(pl.multiple_of(start + r * band, band), band)
            gate, up, g_product = lin[0, here, :], lin[1, here, :], lin[2, here, :]
            sig = sigmoid(gate)
            gated = gate * sig
            act[there, :hidden] = (g_product * up * sig * (1.0 + gate * (1.0 - sig))).astype(BF16)
            act[there, hidden : 2 * hidden] = (g_product * gated).astype(BF16)
            act[there, 2 * hidden :] = (gated * up).astype(BF16)
            return 0

        lax.fori_loop(0, deep // band, act_rows, 0)
        parts[at, :] = mm(act[at, : 2 * hidden], wv[:, : 2 * hidden], (1, 1), None).astype(BF16)

        @pl.when((i > 0) & jnp.logical_not(total.inner))
        def _():
            for p in range(each):
                total.onward(b, half * each + p).start()

        return 0

    lax.fori_loop(0, count * halves, step, 0)

    high = tiles.shape[1]
    steps = width // high
    first = grad.shape[1] - 3 * hidden

    def store(t, r, k):
        down = pl.ds(pl.multiple_of(r * high, high), high)
        into = grad.at[down, pl.ds(first + k * hidden, hidden)]
        return pltpu.make_async_copy(tiles.at[lax.rem(t, 2)], into, o_sem.at[lax.rem(t, 2)])

    turned[...] = xs[...].T
    turned_c[...] = cs[...].T

    def tile(r, k):
        t = 3 * r + k

        @pl.when(t >= 2)
        def _():
            store(t, r, k).wait()

        left_rows = (turned_c if k == 2 else turned)[
            pl.ds(pl.multiple_of(r * high, high), high), :
        ]
        tiles[lax.rem(t, 2)] = jnp.dot(
            left_rows, act[:, k * hidden : (k + 1) * hidden], preferred_element_type=F32
        ).astype(BF16)
        store(t, r, k).start()

    def slab(r, _):
        tile(r, 0)
        tile(r, 1)
        total.relay_in_turn(2 * r)
        tile(r, 2)
        at = chunk(r)
        f_parts[r] = mm(act[at, 2 * hidden :], wv[:, 2 * hidden :], (1, 1), None).astype(BF16)
        total.relay_in_turn(2 * r + 1)
        return 0

    lax.fori_loop(0, steps, slab, 0)
    total.relay_last()
    total.result(g_x)
    total.finish()
    line.finish()
    store(3 * steps - 2, 0, 0).wait()
    store(3 * steps - 1, 0, 0).wait()


def feed_forward(x_own, c_all, w, hidden, count):
    rows, width = x_own.shape
    group = rows * count
    assert count == 4 and width % 4 == 0 and rows % 64 == 0
    anywhere = pl.BlockSpec(memory_space=pl.ANY)
    vmem = pl.BlockSpec(memory_space=pltpu.VMEM)
    dma = pltpu.SemaphoreType.DMA
    return pl.pallas_call(
        functools.partial(ffn_kernel, count),
        out_shape=(
            jax.ShapeDtypeStruct((rows, width), F32),
            jax.ShapeDtypeStruct((count, rows, width), BF16),
            jax.ShapeDtypeStruct(w.shape, BF16),
        ),
        in_specs=[anywhere] * 3,
        out_specs=(vmem, vmem, anywhere),
        scratch_shapes=[
            pltpu.VMEM((width, 3 * hidden), BF16),
            pltpu.VMEM((group, width), BF16),
            pltpu.VMEM((group, width), BF16),
            pltpu.VMEM((group, 3 * hidden), BF16),
            pltpu.VMEM((3, rows // 2, hidden), F32),
            pltpu.VMEM((group, width), BF16),
            pltpu.VMEM((group + rows, width), BF16),
            pltpu.VMEM((width, group), BF16),
            pltpu.VMEM((width, group), BF16),
            pltpu.VMEM((2, width // 4, hidden), BF16),
            dma((3,)), dma((2,)), dma((count + 1, 2)), dma((count, 2)),
            dma((count, 4)), dma((count + 1, 4)), dma((2,)),
        ],
        compiler_params=pltpu.CompilerParams(
            collective_id=0, has_side_effects=True, vmem_limit_bytes=60 << 20
        ),
        cost_estimate=cost(100),
        name="feed_forward",
    )(x_own, c_all, w)


def back_kernel(keep, gated_own, og, o_in, qkv, decay, logits, through, pair_through, gain,
                kept_in, parts_in,
                g_proj, g_logits, g_gain, f_out,
                gated_all, go, runs, g_queried, g_keyed, g_values, pulls, weights, kept,
                parts, landed, state, sending, got, scanned, after, mate_out, mate_in,
                back_out, back_in, second_state, m_sem, in_sem, z_send, z_recv, s_send, s_recv, b_send, b_recv, p_sem, q_sem):
    h, head = lax.axis_index("head"), lax.axis_size("head")
    count, micro, rows, dk = decay.shape
    dv = og.shape[-1]
    width = qkv.shape[-1]
    slices, part = sending.shape[0], sending.shape[2]
    scale = dk ** (-0.5)
    loads = [
        pltpu.make_async_copy(parts_in, parts, in_sem.at[0]),
        pltpu.make_async_copy(kept_in, kept, in_sem.at[1]),
    ]
    for load in loads:
        load.start()
    greet(("seq", "head"))

    def to_head(hop, slot):
        to = lax.rem(h + hop, head)
        columns = gated_own.at[:, pl.ds(pl.multiple_of(to * dv, dv), dv)]
        return push(columns, gated_all.at[slot], z_send.at[hop], z_recv.at[slot], to)

    for hop in range(1, head):
        to_head(hop, h).start()
    gated_all[h] = gated_own[:, pl.ds(pl.multiple_of(h * dv, dv), dv)]

    causal = lower_ones(rows)
    before = [jnp.zeros((1, dk), F32)] * micro
    alive = [jnp.ones((1, dk), F32)] * micro
    for b in range(count):
        for m in range(micro):
            run = running(decay[b, m])
            runs[b, m] = run
            alive[m] = alive[m] * keep[b, m]
            weights[b, m] = jnp.exp(before[m]) * alive[m]
            before[m] = before[m] + run[rows - 1 : rows, :]
    g_gain[...] = jnp.zeros_like(g_gain)
    state[...] = jnp.zeros_like(state)

    def gates(i, _):
        b = near_order(h, head, i)
        pl.when(i > 0)(lambda: to_head(lax.rem(b - h + head, head), b).wait_recv())
        for m in range(micro):
            gate, o = og[b, m], o_in[b, m]
            grad = gated_all[b, m * rows : (m + 1) * rows, :].astype(F32)
            sig = sigmoid(gate)
            inv = lax.rsqrt(jnp.mean(o * o, axis=-1, keepdims=True) + 1e-5)
            plain = o * inv
            normed = (plain * gain[...]).astype(BF16).astype(F32)
            g_on = (grad * gate * sig).astype(BF16).astype(F32)
            g_proj[b, m, :, width:] = (
                grad * normed * sig * (1.0 + gate * (1.0 - sig))
            ).astype(BF16)
            scaled = g_on * gain[...]
            g_o = inv * (scaled - plain * jnp.mean(scaled * plain, axis=-1, keepdims=True))
            go[b, m] = g_o
            g_gain[0:1, :] += jnp.sum(g_on * plain, axis=0, keepdims=True)
            queried = qkv[b, m, :, :dk].astype(F32) * (jnp.exp(runs[b, m]) * scale)
            pull = mms(split(g_o), split(queried), (0, 0))
            pulls[b, m] = pull
            state[m] += pull * weights[b, m]
        return 0

    lax.fori_loop(0, head, gates, 0)
    loads[0].wait()
    total = LineSum(parts, landed, p_sem, q_sem, f_out.shape[0])
    total.send_all()
    half = dv // 2
    side = lax.rem(lax.axis_index("seq"), 2)
    own_half = pl.ds(pl.multiple_of(side * half, half), half)
    mate_half = pl.ds(pl.multiple_of((1 - side) * half, half), half)
    mate_out[...] = state[:, mate_half, :].astype(BF16)
    swap = to_mate(mate_out, mate_in, m_sem.at[0], m_sem.at[1])
    swap.start()
    swap.wait_recv()
    passes = pair_through[:, :, 0:1, :].astype(F32) + pair_through[:, :, 1:2, :].astype(F32)
    for m in range(micro):
        start, later_state = sided(state[m, own_half, :], mate_in[m].astype(F32))
        second_state[m] = later_state
        pair = passes[0, m] * later_state + start
        for i in range(slices):
            sending[i, m] = pair[i * part : (i + 1) * part, :].astype(BF16)
    begin, end, drain = swap_slices(sending, got, s_send, s_recv)
    begin()
    loads[1].wait()

    def inside(b, _):
        for m in range(micro):
            q = qkv[b, m, :, :dk].astype(F32)
            k = qkv[b, m, :, dk : 2 * dk].astype(F32)
            v = (qkv[b, m, :, 2 * dk :],)
            run = runs[b, m]
            queried, keyed = split(q * (jnp.exp(run) * scale)), split(k * jnp.exp(-run))
            g_o, entry = split(go[b, m]), split(kept[b, m])
            scores = split(jnp.where(causal, mms(queried, keyed, (1, 1)), 0.0))
            g_scores = split(jnp.where(causal, mms(g_o, v, (1, 1)), 0.0))
            g_queried[b, m] = mms(g_scores, keyed, (1, 0)) + mms(g_o, entry, (1, 0))
            g_keyed[b, m] = mms(g_scores, queried, (0, 0))
            g_values[b, m] = mms(scores, g_o, (0, 0))
        pl.when(total.inner)(lambda: total.relay(total.far_end, b))
        return 0

    lax.fori_loop(0, count, inside, 0)
    end()
    scan_states(True, got, through, scanned)
    begin_back, end_back, drain_back = swap_slices(scanned, after, b_send, b_recv)
    begin_back()

    @pl.when(total.inner)
    def _():
        for p in range(total.pieces):
            total.relay(head - 1 - total.far_end, p)
        for p in range(total.pieces):
            total.relay(head - 1 - h, p)

    end_back()
    for m in range(micro):
        leave = after[:, m].astype(F32).reshape(half, dk)
        firsts = passes[1, m] * leave + second_state[m]
        own, _ = sided(firsts, leave)
        mate, _ = sided(leave, firsts)
        state[m, own_half, :] = own
        back_out[m] = mate.astype(BF16)
    swap_back = to_mate(back_out, back_in, m_sem.at[2], m_sem.at[3])
    swap_back.start()
    swap_back.wait_recv()
    for m in range(micro):
        state[m, mate_half, :] = back_in[m].astype(F32)

    def across(step, _):
        b = count - 1 - step
        for m in range(micro):
            q = qkv[b, m, :, :dk].astype(F32)
            k = qkv[b, m, :, dk : 2 * dk].astype(F32)
            v = (qkv[b, m, :, 2 * dk :],)
            run = runs[b, m]
            last = run[rows - 1 : rows, :]
            up, down, rest = jnp.exp(run) * scale, jnp.exp(-run), jnp.exp(last - run)
            decayed = jnp.exp(last)
            gs = state[m]
            gs_parts = split(gs)
            carried = k * rest
            g_v = g_values[b, m] + mms(split(carried), gs_parts, (1, 1))
            g_carried = mms(v, gs_parts, (1, 0))
            from_carried = g_carried * carried
            g_total = jnp.sum(decayed * kept[b, m] * gs, axis=0, keepdims=True) + jnp.sum(
                from_carried, axis=0, keepdims=True
            )
            state[m] = (decayed * gs + pulls[b, m]) * keep[b, m]
            gq, gk = g_queried[b, m], g_keyed[b, m]
            g_run = gq * (q * up) - gk * (k * down) - from_carried
            later = mms((causal.astype(F32).astype(BF16),), split(g_run), (0, 0)) + g_total
            g_proj[b, m, :, :dk] = (gq * up).astype(BF16)
            g_proj[b, m, :, dk : 2 * dk] = (gk * down + g_carried * rest).astype(BF16)
            g_proj[b, m, :, 2 * dk : width] = g_v.astype(BF16)
            g_logits[b, m] = (
                later.astype(BF16).astype(F32) * sigmoid(-logits[b, m]) * (1.0 / GATE_NORM)
            )
        return 0

    lax.fori_loop(0, count, across, 0)
    total.result(f_out)
    total.finish()
    drain()
    drain_back()
    swap.wait_send()
    swap_back.wait_send()
    for hop in range(1, head):
        to_head(hop, h).wait_send()


def attention_back(
    keep, gated_own, og, o, qkv, decays, logits, through, pair_through, gain, kept, parts
):
    blocks, micro, rows, width = qkv.shape
    dk, dv = decays.shape[-1], og.shape[-1]
    head, seq = lax.axis_size("head"), lax.axis_size("seq")
    own_rows = parts.shape[0] // head
    vmem, anywhere = pl.BlockSpec(memory_space=pltpu.VMEM), pl.BlockSpec(memory_space=pl.ANY)
    dma = pltpu.SemaphoreType.DMA
    blocked = lambda w, kind: pltpu.VMEM((blocks, micro, rows, w), kind)
    pairs, half = seq // 2, dv // 2
    states = (pairs, micro, half // pairs, dk)
    halves = (micro, half, dk)
    return pl.pallas_call(
        back_kernel,
        out_shape=(
            jax.ShapeDtypeStruct((blocks, micro, rows, width + dv), BF16),
            jax.ShapeDtypeStruct((blocks, micro, rows, dk), F32),
            jax.ShapeDtypeStruct((8, dv), F32),
            jax.ShapeDtypeStruct((own_rows, parts.shape[1]), F32),
        ),
        in_specs=[vmem] * 10 + [anywhere] * 2,
        out_specs=(vmem,) * 4,
        scratch_shapes=[
            pltpu.VMEM((blocks, micro * rows, dv), BF16), blocked(dv, F32), blocked(dk, F32),
            blocked(dk, F32), blocked(dk, F32), blocked(dv, F32),
            pltpu.VMEM((blocks, micro, dv, dk), F32), pltpu.VMEM((blocks, micro, 1, dk), F32),
            pltpu.VMEM((blocks, micro, dv, dk), F32),
            pltpu.VMEM(parts.shape, BF16),
            pltpu.VMEM((parts.shape[0] + own_rows, parts.shape[1]), BF16),
            pltpu.VMEM((micro, dv, dk), F32),
            pltpu.VMEM(states, BF16), pltpu.VMEM(states, BF16), pltpu.VMEM(states, BF16),
            pltpu.VMEM(states, BF16), pltpu.VMEM(halves, BF16), pltpu.VMEM(halves, BF16),
            pltpu.VMEM(halves, BF16), pltpu.VMEM(halves, BF16), pltpu.VMEM(halves, F32), dma((4,)),
            dma((2,)), dma((head,)), dma((head,)), dma((pairs,)), dma((pairs,)), dma((pairs,)),
            dma((pairs,)), dma((head, 4)), dma((head + 1, 4)),
        ],
        compiler_params=pltpu.CompilerParams(
            collective_id=3, has_side_effects=True, vmem_limit_bytes=60 << 20
        ),
        cost_estimate=cost(80),
        name="attention_back",
    )(keep, gated_own, og, o, qkv, decays, logits, through, pair_through, gain, kept,
      parts)


def finish_kernel(xn_in, proj_in, w_in, g_logits, ranked, up_own, rank_down, source,
                  gain, g_ffn, g_head,
                  g_x, grad, norm_sum, ffn_sum, head_sum, bias_sum, up_sum, down_sum,
                  turned, proj, w, outgoing, mine, paired, inbox, heads_in, parts, landed,
                  slim_high, slim_low, small, small_in, small_part,
                  small_heads, small_all, rows_sum, in_sem, pair_send, pair_recv, send, recv, x_send, x_recv,
                  p_sem, q_sem, a_send, a_recv, b_send, b_recv, c_send, c_recv):
    h, head = lax.axis_index("head"), lax.axis_size("head")
    rows, width = g_x.shape
    deep = grad.shape[0] * head
    pairs = lax.axis_size("seq") // 2

    loads = [
        pltpu.make_async_copy(proj_in, proj, in_sem.at[0]),
        pltpu.make_async_copy(w_in, w, in_sem.at[1]),
        pltpu.make_async_copy(xn_in, landed.at[pl.ds(0, xn_in.shape[0])], in_sem.at[2]),
    ]
    for load in loads:
        load.start()
    sums = PairSum(mine, paired, inbox, pair_send, pair_recv, send, recv)
    for load in loads:
        load.wait()
    turned[...] = landed[: xn_in.shape[0], :].T
    greet(("seq", "head"))
    total = LineSum(parts, landed, p_sem, q_sem, rows)
    logit_parts = split(g_logits[...])
    g_ranked = mms(logit_parts, split(up_own[...]), (1, 1))
    slim = split(g_ranked)
    slim_high[...], slim_low[...] = slim

    def chunk(i, _):
        b = near_order(h, head, head - 1 - i)
        at = pl.ds(pl.multiple_of(b * rows, rows), rows)
        rank_part = mms((slim_high[at, :], slim_low[at, :]), (rank_down[...],), (1, 1))
        parts[at, :] = (mm(proj[at, :], w[...], (1, 1), None) + rank_part).astype(BF16)

        @pl.when((b != h) & jnp.logical_not(total.inner))
        def _():
            for p in range(total.pieces):
                total.onward(b, p).start()

        return 0

    lax.fori_loop(0, head, chunk, 0)

    def gone(k, _):
        outgoing[k] = jnp.dot(
            turned[sums.block(k, True), :], proj[...], preferred_element_type=F32
        ).astype(BF16)
        sums.to_partner(outgoing.at[k], k).start()
        return 0

    lax.fori_loop(0, pairs, gone, 0)

    def kept(k, _):
        here = jnp.dot(turned[sums.block(k), :], proj[...], preferred_element_type=F32)
        sums.to_partner(outgoing.at[k], k).wait_recv()
        mine[k] = (here + paired[k].astype(F32)).astype(BF16)
        sums.pass_on(k)

        @pl.when(total.inner & (k < total.pieces))
        def _():
            total.relay(total.far_end, k)

        @pl.when(total.inner & (k > 0) & (k <= total.pieces))
        def _():
            total.relay(head - 1 - total.far_end, k - 1)

        return 0

    lax.fori_loop(0, pairs, kept, 0)

    @pl.when(total.inner)
    def _():
        for p in range(pairs, total.pieces + 1):
            if p < total.pieces:
                total.relay(total.far_end, p)
            total.relay(head - 1 - total.far_end, p - 1)
        for p in range(total.pieces):
            total.relay(head - 1 - h, p)

    thin = grad.shape[0]

    def to_head(hop, slot):
        to = lax.rem(h + hop, head)
        at = pl.ds(pl.multiple_of(to * thin, thin), thin)
        return push(mine.at[sums.own, at, :], heads_in.at[slot], x_send.at[hop], x_recv.at[slot], to)

    sums.advance(0)

    total.result(g_x)
    rows_sum[...] = jnp.zeros_like(rows_sum)
    band = rows_sum.shape[0]

    def norm_rows(r, _):
        at = pl.ds(pl.multiple_of(r * band, band), band)
        x = source[at, :].astype(F32)
        inv = lax.rsqrt(jnp.mean(x * x, axis=-1, keepdims=True) + 1e-6)
        plain, g = x * inv, g_x[at, :]
        scaled = g * gain[...]
        inner = jnp.mean(scaled * plain, axis=-1, keepdims=True)
        rows_sum[...] += g * plain
        g_x[at, :] = inv * (scaled - plain * inner)
        return 0

    lax.fori_loop(0, rows // band, norm_rows, 0)
    rank, dk = up_own.shape
    low, keys = rank // 2, up_sum.shape[1]
    g_down = mms(slim, (turned[...],), (0, 1))
    g_up = mms(split(ranked[...]), logit_parts, (0, 0))
    small[...] = jnp.zeros_like(small)
    small[:low, :width] = g_down[:low]
    small[:low, width:] = g_down[low:]
    own_keys = pl.multiple_of(h * dk, dk)
    small[low:, pl.ds(own_keys, dk)] = g_up[:low]
    small[low:, pl.ds(keys + own_keys, dk)] = g_up[low:]
    small[low : low + 1, width:] = jnp.sum(rows_sum[...], axis=0, keepdims=True)
    small[low + 1 : low + 2, width:] = g_ffn[...]
    small[low + 2 : low + 3, width : width + g_head.shape[1]] = g_head[0:1, :]
    small[low + 3 : low + 4, pl.ds(width + own_keys, dk)] = jnp.sum(
        g_logits[...], axis=0, keepdims=True
    )
    s, seq = lax.axis_index("seq"), lax.axis_size("seq")
    wide = small.shape[1] // seq

    def piece(ref, i):
        return ref.at[:, pl.ds(pl.multiple_of(i * wide, wide), wide)]

    def begin_small(axis, me, count, copy):
        for hop in range(1, count):
            copy(hop, me, lax.rem(me + hop, count)).start()

    def end_small(axis, me, count, copy):
        for hop in range(1, count):
            other = lax.rem(me + hop, count)
            copy(hop, other, other).wait_recv()

    def scatter(hop, slot, to):
        return push(
            piece(small, to), small_in.at[slot], a_send.at[hop], a_recv.at[slot], to, "seq"
        )

    def between(hop, slot, to):
        return push(small_part, small_heads.at[slot], b_send.at[hop], b_recv.at[slot], to)

    def spread(hop, slot, to):
        return push(
            small_part, piece(small_all, slot), c_send.at[hop], c_recv.at[slot], to, "seq"
        )

    begin_small("seq", s, seq, scatter)
    small_in[s] = small[:, pl.ds(pl.multiple_of(s * wide, wide), wide)]
    for step in range(1, sums.levels):
        sums.advance(step)
    for hop in range(1, head):
        to_head(hop, h).start()
    own_rows = pl.ds(pl.multiple_of(h * thin, thin), thin)
    heads_in[h] = mine[sums.own, own_rows, :]
    end_small("seq", s, seq, scatter)
    small_part[...] = jnp.sum(small_in[...], axis=0)
    begin_small("head", h, head, between)
    small_heads[h] = small_part[...]
    end_small("head", h, head, between)
    for hop in range(1, head):
        between(hop, h, lax.rem(h + hop, head)).wait_send()
    small_part[...] = jnp.sum(small_heads[...], axis=0)
    begin_small("seq", s, seq, spread)
    small_all[:, pl.ds(pl.multiple_of(s * wide, wide), wide)] = small_part[...]
    for hop in range(1, head):
        to_head(hop, lax.rem(h + hop, head)).wait_recv()
    dv = mine.shape[2] // 2 - dk
    for j in range(head):
        at, start = 0, 0
        for size in (dk, dk, dv, dv):
            grad[:, start + j * size : start + (j + 1) * size] = heads_in[j, :, at : at + size]
            at, start = at + size, start + head * size
    end_small("seq", s, seq, spread)
    down_sum[:low, :] = small_all[:low, :width]
    down_sum[low:, :] = small_all[:low, width:]
    up_sum[:low, :] = small_all[low:, :keys]
    up_sum[low:, :] = small_all[low:, keys : 2 * keys]
    norm_sum[...] = small_all[low : low + 1, width:]
    ffn_sum[...] = small_all[low + 1 : low + 2, width:]
    head_sum[...] = small_all[low + 2 : low + 3, width : width + head_sum.shape[1]]
    bias_sum[...] = small_all[low + 3 : low + 4, width : width + keys]
    for hop in range(1, seq):
        scatter(hop, s, lax.rem(s + hop, seq)).wait_send()
        spread(hop, s, lax.rem(s + hop, seq)).wait_send()
    sums.finish(lambda k: outgoing.at[k])
    for hop in range(1, head):
        to_head(hop, h).wait_send()
    total.finish()


def finish(
    xn, g_proj, w_in, g_logits, ranked, up_own, rank_down, source, gain, g_ffn, g_head
):
    seq, head = lax.axis_size("seq"), lax.axis_size("head")
    group, width = xn.shape
    columns, rank = w_in.shape[1], ranked.shape[1]
    deep, rows, pairs = width // seq, group // head, seq // 2
    dk = up_own.shape[1]
    vmem, anywhere = pl.BlockSpec(memory_space=pltpu.VMEM), pl.BlockSpec(memory_space=pl.ANY)
    dma = pltpu.SemaphoreType.DMA
    blocks = lambda count, w: pltpu.VMEM((count, deep, w), BF16)
    ends = lambda w: pltpu.VMEM((head, deep // head, w), BF16)
    moves = dma((2, pairs - 1))
    return pl.pallas_call(
        finish_kernel,
        out_shape=(
            jax.ShapeDtypeStruct((rows, width), F32),
            jax.ShapeDtypeStruct((deep // head, columns * head), BF16),
            jax.ShapeDtypeStruct((1, width), F32),
            jax.ShapeDtypeStruct((1, width), F32),
            jax.ShapeDtypeStruct((1, g_head.shape[1]), F32),
            jax.ShapeDtypeStruct((1, dk * head), F32),
            jax.ShapeDtypeStruct((rank, dk * head), F32),
            jax.ShapeDtypeStruct((rank, width), F32),
        ),
        in_specs=[anywhere] * 3 + [vmem] * 8,
        out_specs=(vmem,) * 8,
        scratch_shapes=[
            pltpu.VMEM((width, group), BF16), pltpu.VMEM(g_proj.shape, BF16),
            pltpu.VMEM(w_in.shape, BF16), blocks(pairs, columns), blocks(pairs, columns),
            blocks(pairs, columns), blocks(pairs - 1, columns), ends(columns),
            pltpu.VMEM((group, width), BF16), pltpu.VMEM((group + rows, width), BF16),
            pltpu.VMEM(ranked.shape, BF16), pltpu.VMEM(ranked.shape, BF16),
            pltpu.VMEM((rank, 2 * width), F32), pltpu.VMEM((seq, rank, 2 * width // seq), F32),
            pltpu.VMEM((rank, 2 * width // seq), F32),
            pltpu.VMEM((head, rank, 2 * width // seq), F32),
            pltpu.VMEM((rank, 2 * width), F32), pltpu.VMEM((16, width), F32),
            dma((3,)), dma((pairs,)), dma((pairs,)), moves, moves, dma((head,)), dma((head,)),
            dma((head, 4)), dma((head + 1, 4)),
            dma((seq,)), dma((seq,)), dma((head,)), dma((head,)), dma((seq,)), dma((seq,)),
        ],
        compiler_params=pltpu.CompilerParams(
            collective_id=5, has_side_effects=True, vmem_limit_bytes=60 << 20
        ),
        cost_estimate=cost(95),
        name="finish",
    )(xn, g_proj, w_in, g_logits, ranked, up_own, rank_down, source, gain, g_ffn, g_head)


def weight_grad_kernel(left, right, *rest):
    out, turned = rest[-2:]

    @pl.when(pl.program_id(1) == 0)
    def _():
        turned[...] = left[...].T

    out[...] = jnp.dot(turned[...], right[...], preferred_element_type=F32).astype(BF16)


def weight_grad(left, right, into, columns, start, tile):
    depth, rows = left.shape
    high = min(rows, 512)
    first = start // tile
    given = () if into is None else (into,)
    return pl.pallas_call(
        weight_grad_kernel,
        out_shape=jax.ShapeDtypeStruct((rows, columns), BF16),
        grid=(rows // high, right.shape[1] // tile),
        in_specs=[
            pl.BlockSpec((depth, high), lambda i, j: (0, i)),
            pl.BlockSpec((depth, tile), lambda i, j: (0, j)),
        ]
        + [pl.BlockSpec(memory_space=pl.ANY) for _ in given],
        out_specs=pl.BlockSpec((high, tile), lambda i, j: (i, first + j)),
        scratch_shapes=[pltpu.VMEM((high, depth), BF16)],
        input_output_aliases={2: 0} if given else {},
        compiler_params=pltpu.CompilerParams(
            dimension_semantics=("arbitrary", "arbitrary"), vmem_limit_bytes=48 << 20
        ),
        cost_estimate=pl.CostEstimate(
            flops=2 * depth * rows * right.shape[1],
            bytes_accessed=2 * (depth * rows + (depth + rows) * right.shape[1]),
            transcendentals=0,
        ),
        name="weight_grad",
    )(left, right, *given)


def gather_weight(w):
    return lax.all_gather(w, "seq", axis=0, tiled=True)


def scatter_grad(g):
    return lax.psum_scatter(g.astype(BF16), "seq", scatter_dimension=0, tiled=True)


def dot(a, b, contract, precision=None):
    return lax.dot_general(
        a, b, (((contract[0],), (contract[1],)), ((), ())),
        precision=precision, preferred_element_type=F32,
    )


def rms(x, epsilon):
    return lax.rsqrt(jnp.mean(x * x, axis=-1, keepdims=True) + epsilon)


def norm_back(grad, gain, normed, inv):
    scaled = grad * gain
    inner = jnp.mean(scaled * normed, axis=-1, keepdims=True)
    return inv * (scaled - normed * inner), jnp.sum(grad * normed, axis=0)


def on_device(
    tokens, starts, cotangent, mix_in, mix_out, gate_up, down_proj,
    norm_gain, ffn_gain, head_gain, rank_down, rank_up, gate_bias,
):
    micro, rows, width = tokens.shape
    heads, seq = lax.axis_size("head"), lax.axis_size("seq")
    head = lax.axis_index("head")
    keys, dv = rank_up.shape[1], head_gain.shape[0]
    dk, vals = keys // heads, dv * heads
    hidden_units = down_proj.shape[1]
    group = heads * micro * rows
    proj_width = 2 * dk + 2 * dv

    def own_columns(w, start, size):
        return lax.dynamic_slice_in_dim(w, start + head * size, size, 1)

    w_in_own = jnp.concatenate(
        [
            own_columns(mix_in, 0, dk),
            own_columns(mix_in, keys, dk),
            own_columns(mix_in, 2 * keys, dv),
            own_columns(mix_in, 2 * keys + vals, dv),
        ],
        axis=1,
    )
    later = gather_weight(
        jnp.concatenate(
            [gate_up.reshape(gate_up.shape[0], 2 * hidden_units), down_proj, mix_out], axis=1
        )
    )
    w_out = later[:, 3 * hidden_units :]
    up_own = own_columns(rank_up, 0, dk)
    bias_own = lax.dynamic_slice_in_dim(gate_bias, head * dk, dk, 0)

    xn, w_in = gather_norm(
        tokens.reshape(micro * rows, width), norm_gain.reshape(1, width), w_in_own
    )
    qkv = dot(xn, w_in[:, : 2 * dk + dv], (1, 0)).astype(BF16)
    og = dot(xn, w_in[:, 2 * dk + dv :], (1, 0))
    ranked = dot(xn, rank_down, (1, 0))
    logits = dot(ranked, up_own, (1, 0), HIGHEST) + bias_own
    decays = (jax.nn.log_sigmoid(logits) / GATE_NORM).astype(BF16)

    def blocks(x):
        return x.reshape(heads, micro, rows, x.shape[-1])

    qkv_b, og_b, decays_b = blocks(qkv), blocks(og), blocks(decays)
    gain_row = head_gain.reshape(1, dv)
    keep = 1.0 - jnp.broadcast_to(starts.T[:, :, None, None], (heads, micro, 1, dk)).astype(F32)
    o_b, gated, through, pair_through, kept, all_cot = attention_forward(
        keep, qkv_b, decays_b, og_b, gain_row, cotangent.reshape(micro * rows, width)
    )

    source = tokens.astype(F32).reshape(micro * rows, width)
    hidden = source + dot(gated, w_out, (1, 1))
    inv_ffn = rms(hidden, 1e-6)
    plain_ffn = hidden * inv_ffn
    h2 = (plain_ffn * ffn_gain).astype(BF16)

    g_h2, ffn_part, grads = feed_forward(h2, all_cot, later, hidden_units, heads)

    back_ffn, g_ffn_gain = norm_back(g_h2, ffn_gain, plain_ffn, inv_ffn)
    g_hidden = cotangent.astype(F32).reshape(micro * rows, width) + back_ffn
    g_mixed = g_hidden.astype(BF16)
    grads = scatter_grad(weight_grad(g_mixed, gated, grads, later.shape[1], 0, vals))
    g_gated = dot(g_mixed, w_out, (1, 0)).astype(BF16)
    g_proj_b, g_logits_b, g_head_gain, ffn_out = attention_back(
        keep, g_gated, og_b, o_b, qkv_b, decays_b, blocks(logits), through, pair_through, gain_row, kept, ffn_part.reshape(group, width),
    )
    output = (hidden + ffn_out).astype(BF16)
    g_proj, g_logits = g_proj_b.reshape(group, proj_width), g_logits_b.reshape(group, dk)
    back_in, grad_in, *small, g_rank_down = finish(
        xn, g_proj, w_in, g_logits, ranked, up_own, rank_down, tokens.reshape(micro * rows, width),
        norm_gain.reshape(1, width), g_ffn_gain.reshape(1, width), g_head_gain,
    )
    g_norm_gain, g_ffn_gain, g_head_gain, g_bias, g_rank_up = small
    input_grad = g_hidden + back_in
    slab = width // (seq * heads)
    grad_in, grads = lax.optimization_barrier((grad_in, grads))
    grad_ffn = grads[:, vals:]
    grad_out = lax.all_to_all(
        grads[:, :vals].reshape(heads, slab, vals), "head", split_axis=0, concat_axis=0, tiled=True
    )
    grad_out = grad_out.astype(F32).sum(0)
    return (
        output.reshape(tokens.shape),
        input_grad.reshape(tokens.shape),
        grad_in.astype(F32),
        grad_out,
        grad_ffn[:, : 2 * hidden_units].astype(F32).reshape(-1, 2, hidden_units),
        grad_ffn[:, 2 * hidden_units :].astype(F32),
        g_norm_gain.reshape(norm_gain.shape),
        g_ffn_gain.reshape(ffn_gain.shape),
        g_head_gain.reshape(head_gain.shape),
        g_rank_down.T,
        g_rank_up,
        g_bias.reshape(gate_bias.shape),
    )


def solution(mesh):
    rows = P(None, ("seq", "head"), None)
    return jax.shard_map(
        on_device,
        mesh=mesh,
        in_specs=(
            rows, P(None, "seq"), rows, P("seq", None), P("seq", None),
            P("seq", None, "head"), P("seq", "head"), P(), P(), P(), P(), P(), P(),
        ),
        out_specs=(
            rows, rows, P(("seq", "head"), None), P(("seq", "head"), None),
            P("seq", None, "head"), P("seq", "head"), P(), P(), P(), P(), P(), P(),
        ),
        check_vma=False,
    )
```

```python
import functools

import jax
import jax.numpy as jnp
from jax import lax
from jax.experimental import pallas as pl
from jax.experimental.pallas import tpu as pltpu
from jax.sharding import PartitionSpec as P

HIGHEST = lax.Precision.HIGHEST
GATE_NORM = 16.0
BF16 = jnp.bfloat16
F32 = jnp.float32


def mm(a, b, contract, precision=HIGHEST):
    return lax.dot_general(
        a, b, ((contract[:1], contract[1:]), ((), ())),
        precision=precision, preferred_element_type=F32,
    )


def split(x):
    high = x.astype(BF16)
    return high, (x - high.astype(F32)).astype(BF16)


def mms(left, right, contract):
    total = mm(left[0], right[0], contract, None)
    if len(right) > 1:
        total += mm(left[0], right[1], contract, None)
    if len(left) > 1:
        total += mm(left[1], right[0], contract, None)
    return total


def lower_ones(size):
    rows = lax.broadcasted_iota(jnp.int32, (size, size), 0)
    cols = lax.broadcasted_iota(jnp.int32, (size, size), 1)
    return rows >= cols


def running(decay_low):
    ones = lower_ones(decay_low.shape[0]).astype(F32).astype(BF16)
    return mm(ones, decay_low, (1, 0), None)


def sigmoid(x):
    return 1.0 / (1.0 + jnp.exp(-x))


def cost(micros):
    return pl.CostEstimate(flops=0, bytes_accessed=int(micros * 3.0e6), transcendentals=0)


def greet(axes):
    barrier = pltpu.get_barrier_semaphore()
    met = 0
    for axis in axes:
        me, count = lax.axis_index(axis), lax.axis_size(axis)
        for hop in range(1, count):
            pl.semaphore_signal(
                barrier, inc=1, device_id={axis: lax.rem(me + hop, count)},
                device_id_type=pl.DeviceIdType.MESH,
            )
        met += count - 1
    pl.semaphore_wait(barrier, met)


def push(src, dst, send, recv, to, axis="head"):
    return pltpu.make_async_remote_copy(
        src_ref=src, dst_ref=dst, send_sem=send, recv_sem=recv,
        device_id={axis: to}, device_id_type=pl.DeviceIdType.MESH,
    )


def near_order(z, count, i):
    both = jnp.minimum(z, count - 1 - z)
    left = z > count - 1 - z
    paired = jnp.where(i % 2 == 1, z - (i + 1) // 2, z + i // 2)
    single = jnp.where(left, z - (i - both), z + (i - both))
    return jnp.where(i <= 2 * both, paired, single)


class Line:
    def __init__(self, own, all_rows, send, recv):
        self.own, self.all, self.send, self.recv = own, all_rows, send, recv
        self.z, self.count = lax.axis_index("head"), lax.axis_size("head")
        self.rows, self.parts = own.shape[0], recv.shape[1]
        self.deep = self.rows // self.parts

    def at(self, b):
        return self.all.at[pl.ds(pl.multiple_of(b * self.rows, self.rows), self.rows)]

    def part(self, b, p):
        start = b * self.rows + p * self.deep
        return self.all.at[pl.ds(pl.multiple_of(start, self.deep), self.deep)]

    def first(self, way, p):
        to = lax.rem(self.z + (1 if way == 0 else self.count - 1), self.count)
        src = self.own.at[pl.ds(p * self.deep, self.deep)]
        return push(
            src, self.part(self.z, p), self.send.at[way, p], self.recv.at[self.z, p], to
        )

    def each_first(self, act):
        for p in range(self.parts):
            pl.when(self.z < self.count - 1)(lambda p=p: act(self.first(0, p)))
            pl.when(self.z > 0)(lambda p=p: act(self.first(1, p)))

    def start(self):
        self.each_first(lambda copy: copy.start())

    def passing(self, i, b, p):
        z, count = self.z, self.count
        to = jnp.where(b < z, z + 1, z - 1)
        going = ((b < z) & (z < count - 1)) | ((b > z) & (z > 0))
        copy = push(
            self.part(b, p), self.part(b, p), self.send.at[i + 1, p], self.recv.at[b, p],
            lax.rem(to + count, count),
        )
        return copy, going

    def receive(self, i, b, p=0):
        copy, going = self.passing(i, b, p)
        copy.wait_recv()
        pl.when(going)(copy.start)

    def finish(self):
        def sent(i, _):
            for p in range(self.parts):
                copy, going = self.passing(i, near_order(self.z, self.count, i), p)
                pl.when(going)(copy.wait_send)
            return 0

        lax.fori_loop(1, self.count, sent, 0)
        self.each_first(lambda copy: copy.wait_send())


class LineSum:
    def __init__(self, parts, landed, send, recv, rows):
        self.parts, self.landed, self.send, self.recv = parts, landed, send, recv
        self.z, self.count = lax.axis_index("head"), lax.axis_size("head")
        self.rows, self.pieces = rows, send.shape[1]
        self.deep = rows // self.pieces
        self.inner = (self.z > 0) & (self.z < self.count - 1)
        self.far_end = jnp.where(self.z < self.count - 1 - self.z, self.count - 1, 0)

    def piece(self, b, p):
        return pl.ds(pl.multiple_of(b * self.rows + p * self.deep, self.deep), self.deep)

    def onward(self, b, p):
        z, count = self.z, self.count
        to = jnp.where(b > z, z + 1, z - 1)
        slot = jnp.where((to == b) & (z > b), count, b)
        return push(
            self.parts.at[self.piece(b, p)], self.landed.at[self.piece(slot, p)],
            self.send.at[b, p], self.recv.at[slot, p], lax.rem(to + count, count),
        )

    def send_all(self):
        @pl.when(jnp.logical_not(self.inner))
        def _():
            for i in range(1, self.count):
                b = jnp.where(self.z == 0, self.count - i, i - 1)
                for p in range(self.pieces):
                    self.onward(b, p).start()

    def arrived(self, slot, p):
        at = self.piece(slot, p)
        push(
            self.landed.at[at], self.landed.at[at], self.send.at[0, p], self.recv.at[slot, p],
            lax.rem(self.z + 1, self.count),
        ).wait_recv()
        return self.landed[at, :].astype(F32)

    def relay(self, b, p):
        at = self.piece(b, p)
        self.parts[at, :] = (self.parts[at, :].astype(F32) + self.arrived(b, p)).astype(BF16)
        self.onward(b, p).start()

    def relay_in_turn(self, j):
        pieces = self.pieces

        @pl.when(self.inner & (j < pieces))
        def _():
            self.relay(self.count - 1 - self.z, j)

        @pl.when(self.inner & (j >= pieces))
        def _():
            self.relay(self.far_end, j - pieces)

        @pl.when(self.inner & (j > pieces))
        def _():
            self.relay(self.count - 1 - self.far_end, j - pieces - 1)

    def relay_last(self):
        @pl.when(self.inner)
        def _():
            self.relay(self.count - 1 - self.far_end, self.pieces - 1)

    def result(self, out):
        z, count = self.z, self.count
        for p in range(self.pieces):
            here = pl.ds(p * self.deep, self.deep)
            out[here, :] = self.parts[self.piece(z, p), :].astype(F32)

            @pl.when(z > 0)
            def _():
                out[here, :] += self.arrived(z, p)

            @pl.when(z < count - 1)
            def _():
                out[here, :] += self.arrived(count, p)

    def finish(self):
        def sent(i, _):
            b = near_order(self.z, self.count, i)
            for p in range(self.pieces):
                self.onward(b, p).wait_send()
            return 0

        lax.fori_loop(1, self.count, sent, 0)


class PairSum:
    def __init__(self, mine, paired, inbox, pair_send, pair_recv, send, recv):
        self.mine, self.paired, self.inbox = mine, paired, inbox
        self.pair_send, self.pair_recv, self.send, self.recv = pair_send, pair_recv, send, recv
        self.s, self.pairs = lax.axis_index("seq"), lax.axis_size("seq") // 2
        self.side, self.own = lax.rem(self.s, 2), self.s // 2
        self.deep, self.half = mine.shape[1], mine.shape[2] // 2
        self.levels = self.pairs.bit_length() - 1
        assert self.pairs == 1 << self.levels

    def block(self, k, other=False):
        i = 2 * k + (1 - self.side if other else self.side)
        return pl.ds(pl.multiple_of(i * self.deep, self.deep), self.deep)

    def to_partner(self, src, k):
        return push(
            src, self.paired.at[k], self.pair_send.at[k], self.pair_recv.at[k],
            self.s + 1 - 2 * self.side, "seq",
        )

    def bit(self, i, level):
        return lax.rem(i // (1 << level), 2)

    def move(self, side, slot, k, level):
        columns = pl.ds(side * self.half, self.half)
        to = self.s + (1 - 2 * self.bit(self.own, level)) * (2 << level)
        return push(
            self.mine.at[k, :, columns], self.inbox.at[slot, :, columns],
            self.send.at[side, slot], self.recv.at[side, slot], to, "seq",
        )

    def moves(self, side, step):
        order = list(range(self.levels))
        if side:
            order.reverse()
        level, free = order[step], sorted(order[step + 1 :])
        fixed = sum((self.bit(self.own, d) * (1 << d) for d in order[:step]), 0)
        offset = self.pairs - (1 << (self.levels - step))
        here = self.bit(self.own, level) * (1 << level)
        for c in range(1 << len(free)):
            rest = fixed + sum(((c >> j) & 1) << d for j, d in enumerate(free))
            yield offset + c, rest + here, rest + (1 << level) - here, level

    def pass_on(self, k):
        top = 1 << (self.levels - 1)
        pl.when(self.bit(k, 0) != self.bit(self.own, 0))(self.move(0, k // 2, k, 0).start)
        pl.when(k // top != self.own // top)(
            self.move(1, lax.rem(k, top), k, self.levels - 1).start
        )

    def advance(self, step):
        for side in range(2):
            columns = slice(side * self.half, (side + 1) * self.half)
            for slot, keep, gone, level in self.moves(side, step):
                self.move(side, slot, gone, level).wait_recv()
                self.mine[keep, :, columns] = (
                    self.mine[keep, :, columns].astype(F32)
                    + self.inbox[slot, :, columns].astype(F32)
                ).astype(BF16)
            if step + 1 < self.levels:
                for slot, keep, gone, level in self.moves(side, step + 1):
                    self.move(side, slot, gone, level).start()

    def finish(self, src):
        for k in range(self.pairs):
            self.to_partner(src(k), k).wait_send()
        for side in range(2):
            for step in range(self.levels):
                for slot, keep, gone, level in self.moves(side, step):
                    self.move(side, slot, gone, level).wait_send()


def gather_norm_kernel(own, gain, shard, normed, rows_of_all, rows_all, here_sem, send, recv,
                       w_sem, w_peer, w_pair, w_recv):
    z, count, rows = lax.axis_index("head"), lax.axis_size("head"), own.shape[0]
    greet(("seq", "head"))
    line = Line(own, rows_all, send, recv)
    line.start()
    here = pltpu.make_async_copy(own, line.at(z), here_sem)
    here.start()

    s, deep = lax.axis_index("seq"), shard.shape[0]
    side, pairs, own_pair = lax.rem(s, 2), lax.axis_size("seq") // 2, s // 2
    partner = s + 1 - 2 * side

    def shard_at(i):
        return rows_of_all.at[pl.ds(pl.multiple_of(i * deep, deep), deep)]

    def to_peer(k):
        return push(shard, shard_at(s), w_peer.at[k], w_recv.at[s], 2 * k + side, "seq")

    def from_peer(k):
        i = 2 * k + side
        return push(shard, shard_at(i), w_peer.at[k], w_recv.at[i], partner, "seq")

    def to_partner(k):
        i = 2 * k + side
        return push(shard_at(i), shard_at(i), w_pair.at[k], w_recv.at[i], partner, "seq")

    def from_partner(k):
        i = 2 * k + 1 - side
        return push(shard_at(i), shard_at(i), w_pair.at[k], w_recv.at[i], partner, "seq")

    mine = pltpu.make_async_copy(shard, shard_at(s), w_sem)
    mine.start()
    for k in range(pairs):
        pl.when(own_pair != k)(to_peer(k).start)
    mine.wait()
    to_partner(own_pair).start()
    here.wait()
    band = 16

    def step(i, _):
        b = near_order(z, count, i)
        pl.when(i > 0)(lambda: line.receive(i, b))

        def norm(r, _):
            at = pl.ds(pl.multiple_of(b * rows + r * band, band), band)
            x = rows_all[at, :].astype(F32)
            inv = lax.rsqrt(jnp.mean(x * x, axis=-1, keepdims=True) + 1e-6)
            normed[at, :] = (x * inv * gain[...]).astype(BF16)
            return 0

        lax.fori_loop(0, rows // band, norm, 0)
        return 0

    lax.fori_loop(0, count, step, 0)
    for k in range(pairs):

        @pl.when(own_pair != k)
        def _():
            from_peer(k).wait_recv()
            to_partner(k).start()

    for k in range(pairs):
        from_partner(k).wait_recv()
    for k in range(pairs):
        to_partner(k).wait_send()
        pl.when(own_pair != k)(to_peer(k).wait_send)
    line.finish()


def gather_norm(x, gain, shard):
    rows, width = x.shape
    seq = lax.axis_size("seq")
    anywhere = pl.BlockSpec(memory_space=pl.ANY)
    count = lax.axis_size("head")
    vmem = pl.BlockSpec(memory_space=pltpu.VMEM)
    dma = pltpu.SemaphoreType.DMA
    return pl.pallas_call(
        gather_norm_kernel,
        out_shape=(
            jax.ShapeDtypeStruct((count * rows, width), BF16),
            jax.ShapeDtypeStruct((seq * shard.shape[0], shard.shape[1]), BF16),
        ),
        in_specs=[vmem, vmem, anywhere],
        out_specs=(vmem, anywhere),
        scratch_shapes=[
            pltpu.VMEM((count * rows, width), BF16), dma(()), dma((count + 1, 1)), dma((count, 1)),
            dma(()), dma((seq // 2,)), dma((seq // 2,)), dma((seq,)),
        ],
        compiler_params=pltpu.CompilerParams(
            collective_id=1, has_side_effects=True, vmem_limit_bytes=32 << 20
        ),
        cost_estimate=cost(50),
        name="gather_norm",
    )(x, gain, shard)


def swap_slices(own, got, send, recv):
    side = lax.rem(lax.axis_index("seq"), 2)
    me, count = lax.axis_index("seq") // 2, lax.axis_size("seq") // 2

    def copy(hop, index):
        to = lax.rem(me + hop, count)
        return push(own.at[to], got.at[index], send.at[hop], recv.at[index], 2 * to + side, "seq")

    def start(hop, _):
        copy(hop, me).start()
        return 0

    def wait_recv(hop, _):
        copy(hop, lax.rem(me + hop, count)).wait_recv()
        return 0

    def wait_send(hop, _):
        copy(hop, me).wait_send()
        return 0

    def begin():
        lax.fori_loop(1, count, start, 0)
        got[me] = own[me]

    def end():
        lax.fori_loop(1, count, wait_recv, 0)

    def drain():
        lax.fori_loop(1, count, wait_send, 0)

    return begin, end, drain


def to_mate(src, dst, send, recv):
    s = lax.axis_index("seq")
    return push(src, dst, send, recv, s + 1 - 2 * lax.rem(s, 2), "seq")


def sided(own, mate):
    first = lax.rem(lax.axis_index("seq"), 2) == 0
    return jnp.where(first, own, mate), jnp.where(first, mate, own)


def scan_states(reverse, own, through, out):
    count, part = out.shape[0], out.shape[2]

    def step(k, state):
        j = count - 1 - k if reverse else k
        out[j] = state.astype(BF16)
        decay = through[j, :, 0:1, :].astype(F32) + through[j, :, 1:2, :].astype(F32)
        return decay * state + own[j, :, :part, :].astype(F32)

    lax.fori_loop(0, count, step, jnp.zeros(out.shape[1:], F32))


def front_kernel(keep, qkv, decay, og, gain, rows_own,
                 o_out, gated, through, pair_through, kept_out, rows_all,
                 kept, runs, state, sending, got, scanned, before, leaving, mate_out, mate_in,
                 back_out, back_in, first_state,
                 here_sem, go, come, s_send, s_recv, b_send, b_recv, z_send, z_recv, k_sem, m_sem):
    h, head = lax.axis_index("head"), lax.axis_size("head")
    count, micro, rows, dk = decay.shape
    dv = og.shape[-1]
    slices, part = scanned.shape[0], scanned.shape[2]
    scale = dk ** (-0.5)
    greet(("seq", "head"))
    line = Line(rows_own, rows_all, go, come)
    line.start()
    here = pltpu.make_async_copy(rows_own, line.at(h), here_sem)
    here.start()

    state[...] = jnp.zeros_like(state)
    passed = [jnp.zeros((1, dk), F32)] * micro
    alive = [jnp.ones((1, dk), F32)] * micro
    for b in range(count):
        for m in range(micro):
            run = running(decay[b, m])
            runs[b, m] = run
            last = run[rows - 1 : rows, :]
            carried = qkv[b, m, :, dk : 2 * dk].astype(F32) * jnp.exp(last - run)
            fresh = mms((qkv[b, m, :, 2 * dk :],), split(carried), (0, 0))
            kept[b, m] = fresh
            state[m] = jnp.exp(last) * (state[m] * keep[b, m]) + fresh
            passed[m] = passed[m] + last
            alive[m] = alive[m] * keep[b, m]
    tail = sending.shape[2] - part
    at = lax.broadcasted_iota(jnp.int32, (tail, dk), 0)
    half = dv // 2
    side = lax.rem(lax.axis_index("seq"), 2)
    own_half = pl.ds(pl.multiple_of(side * half, half), half)
    mate_half = pl.ds(pl.multiple_of((1 - side) * half, half), half)

    def as_rows(value):
        high, low = split(value)
        return jnp.where(at == 0, high.astype(F32), jnp.where(at == 1, low.astype(F32), 0.0))

    own_rows = [as_rows(jnp.exp(passed[m]) * alive[m]) for m in range(micro)]
    for m in range(micro):
        mate_out[m, :half, :] = state[m, mate_half, :].astype(BF16)
        mate_out[m, half:, :] = own_rows[m].astype(BF16)
    swap = to_mate(mate_out, mate_in, m_sem.at[0], m_sem.at[1])
    swap.start()
    swap.wait_recv()
    first_through = []
    for m in range(micro):
        firsts, seconds = sided(own_rows[m], mate_in[m, half:, :].astype(F32))
        pair_through[0, m], pair_through[1, m] = firsts.astype(BF16), seconds.astype(BF16)
        first, second = firsts[0:1] + firsts[1:2], seconds[0:1] + seconds[1:2]
        first_through.append(first)
        start, after = sided(state[m, own_half, :], mate_in[m, :half, :].astype(F32))
        first_state[m] = start
        pair = second * start + after
        both = as_rows(first * second).astype(BF16)
        for i in range(slices):
            sending[i, m, :part, :] = pair[i * part : (i + 1) * part, :].astype(BF16)
            sending[i, m, part:, :] = both
    begin, end, drain = swap_slices(sending, got, s_send, s_recv)
    begin()
    causal = lower_ones(rows)

    def inside(b, _):
        for m in range(micro):
            run = runs[b, m]
            queried = split(qkv[b, m, :, :dk].astype(F32) * (jnp.exp(run) * scale))
            keyed = split(qkv[b, m, :, dk : 2 * dk].astype(F32) * jnp.exp(-run))
            scores = jnp.where(causal, mms(queried, keyed, (1, 1)), 0.0)
            o_out[b, m] = mms(split(scores), (qkv[b, m, :, 2 * dk :],), (1, 0))
        return 0

    lax.fori_loop(0, count, inside, 0)
    line.receive(1, near_order(h, head, 1))
    end()
    through[...] = got[:, :, part:, :]
    scan_states(False, got, through, scanned)
    begin_back, end_back, drain_back = swap_slices(scanned, before, b_send, b_recv)
    begin_back()
    line.receive(2, near_order(h, head, 2))
    end_back()
    for m in range(micro):
        entry = before[:, m].astype(F32).reshape(half, dk)
        own, mate = sided(entry, first_through[m] * entry + first_state[m])
        state[m, own_half, :] = own
        back_out[m] = mate.astype(BF16)
    swap_back = to_mate(back_out, back_in, m_sem.at[2], m_sem.at[3])
    swap_back.start()
    swap_back.wait_recv()
    for m in range(micro):
        state[m, mate_half, :] = back_in[m].astype(F32)

    def to_owner(b):
        columns = gated.at[:, pl.ds(pl.multiple_of(h * dv, dv), dv)]
        return push(leaving.at[b], columns, z_send.at[b], z_recv.at[h], b)

    def save(b):
        return pltpu.make_async_copy(kept.at[b], kept_out.at[b], k_sem.at[b])

    def across(b, _):
        for m in range(micro):
            run = runs[b, m]
            queried = split(qkv[b, m, :, :dk].astype(F32) * (jnp.exp(run) * scale))
            entry = state[m] * keep[b, m]
            state[m] = jnp.exp(run[rows - 1 : rows, :]) * entry + kept[b, m]
            kept[b, m] = entry
            o = o_out[b, m] + mms(queried, split(entry), (1, 1))
            o_out[b, m] = o
            inv = lax.rsqrt(jnp.mean(o * o, axis=-1, keepdims=True) + 1e-5)
            normed = (o * inv * gain[...]).astype(BF16).astype(F32)
            gate = og[b, m]
            leaving[b, m * rows : (m + 1) * rows, :] = (normed * gate * sigmoid(gate)).astype(BF16)
        save(b).start()
        pl.when(b != h)(to_owner(b).start)

        @pl.when(b == 1)
        def _():
            line.receive(3, near_order(h, head, 3))

        return 0

    lax.fori_loop(0, count, across, 0)
    gated[:, pl.ds(pl.multiple_of(h * dv, dv), dv)] = leaving[h]
    for hop in range(1, head):
        other = lax.rem(h + hop, head)
        columns = gated.at[:, pl.ds(pl.multiple_of(other * dv, dv), dv)]
        push(leaving.at[other], columns, z_send.at[other], z_recv.at[other], other).wait_recv()
        to_owner(other).wait_send()
    for b in range(count):
        save(b).wait()
    here.wait()
    line.finish()
    drain()
    drain_back()
    swap.wait_send()
    swap_back.wait_send()


def attention_forward(keep, qkv, decays, og, gain, rows_own):
    blocks, micro, rows, width = qkv.shape
    dk, dv = decays.shape[-1], og.shape[-1]
    head, seq = lax.axis_size("head"), lax.axis_size("seq")
    assert blocks == head and head == 4
    pairs, half, tail = seq // 2, dv // 2, 16
    part = half // pairs
    own_rows = micro * rows
    vmem, anywhere = pl.BlockSpec(memory_space=pltpu.VMEM), pl.BlockSpec(memory_space=pl.ANY)
    dma = pltpu.SemaphoreType.DMA
    states, wider = (pairs, micro, part, dk), (pairs, micro, part + tail, dk)
    return pl.pallas_call(
        front_kernel,
        out_shape=(
            jax.ShapeDtypeStruct((blocks, micro, rows, dv), F32),
            jax.ShapeDtypeStruct((own_rows, head * dv), BF16),
            jax.ShapeDtypeStruct((pairs, micro, tail, dk), BF16),
            jax.ShapeDtypeStruct((2, micro, tail, dk), BF16),
            jax.ShapeDtypeStruct((blocks, micro, dv, dk), F32),
            jax.ShapeDtypeStruct((head * rows_own.shape[0], rows_own.shape[1]), BF16),
        ),
        in_specs=[vmem] * 5 + [anywhere],
        out_specs=(vmem,) * 4 + (anywhere,) * 2,
        scratch_shapes=[
            pltpu.VMEM((blocks, micro, dv, dk), F32), pltpu.VMEM((blocks, micro, rows, dk), F32),
            pltpu.VMEM((micro, dv, dk), F32), pltpu.VMEM(wider, BF16), pltpu.VMEM(wider, BF16),
            pltpu.VMEM(states, BF16), pltpu.VMEM(states, BF16),
            pltpu.VMEM((blocks, own_rows, dv), BF16),
            pltpu.VMEM((micro, half + tail, dk), BF16), pltpu.VMEM((micro, half + tail, dk), BF16),
            pltpu.VMEM((micro, half, dk), BF16), pltpu.VMEM((micro, half, dk), BF16),
            pltpu.VMEM((micro, half, dk), F32),
            dma(()), dma((head + 1, 1)), dma((head, 1)), dma((pairs,)), dma((pairs,)), dma((pairs,)),
            dma((pairs,)), dma((head,)), dma((head,)), dma((blocks,)), dma((4,)),
        ],
        compiler_params=pltpu.CompilerParams(
            collective_id=2, has_side_effects=True, vmem_limit_bytes=40 << 20
        ),
        cost_estimate=cost(90),
        name="attention_forward",
    )(keep, qkv, decays, og, gain, rows_own)


def ffn_kernel(count, x_own, c_all, w, g_x, f_parts, grad,
               wv, xs, cs, act, lin, parts, landed, turned, turned_c, tiles,
               w_sem, own_sem, go_sem, x_sem, p_sem, q_sem, o_sem):
    z = lax.axis_index("head")
    rows, width = x_own.shape
    hidden = act.shape[1] // 3
    chunk = lambda b: pl.ds(pl.multiple_of(b * rows, rows), rows)

    weights = [
        pltpu.make_async_copy(
            w.at[:, pl.ds(k * hidden, hidden)], wv.at[:, pl.ds(k * hidden, hidden)], w_sem.at[k]
        )
        for k in range(3)
    ]
    own = [
        pltpu.make_async_copy(x_own, xs.at[chunk(z)], own_sem.at[0]),
        pltpu.make_async_copy(c_all, cs, own_sem.at[1]),
    ]
    for copy in own + weights:
        copy.start()
    greet(("head",))
    line = Line(x_own, xs, go_sem, x_sem)
    line.start()
    for copy in own + weights:
        copy.wait()

    total = LineSum(parts, landed, p_sem, q_sem, rows)

    halves = x_sem.shape[1]
    deep = rows // halves
    each = total.pieces // halves

    def step(t, _):
        i, half = t // halves, lax.rem(t, halves)
        b = near_order(z, count, i)
        pl.when(i > 0)(lambda: line.receive(i, b, half))
        start = b * rows + half * deep
        at = pl.ds(pl.multiple_of(start, deep), deep)
        x = xs[at, :]
        lin[0] = jnp.dot(x, wv[:, :hidden], preferred_element_type=F32)
        lin[1] = jnp.dot(x, wv[:, hidden : 2 * hidden], preferred_element_type=F32)
        lin[2] = jnp.dot(cs[at, :], wv[:, 2 * hidden :], preferred_element_type=F32)
        band = 16

        def act_rows(r, _):
            here = pl.ds(pl.multiple_of(r * band, band), band)
            there = pl.ds(pl.multiple_of(start + r * band, band), band)
            gate, up, g_product = lin[0, here, :], lin[1, here, :], lin[2, here, :]
            sig = sigmoid(gate)
            gated = gate * sig
            act[there, :hidden] = (g_product * up * sig * (1.0 + gate * (1.0 - sig))).astype(BF16)
            act[there, hidden : 2 * hidden] = (g_product * gated).astype(BF16)
            act[there, 2 * hidden :] = (gated * up).astype(BF16)
            return 0

        lax.fori_loop(0, deep // band, act_rows, 0)
        parts[at, :] = mm(act[at, : 2 * hidden], wv[:, : 2 * hidden], (1, 1), None).astype(BF16)

        @pl.when((i > 0) & jnp.logical_not(total.inner))
        def _():
            for p in range(each):
                total.onward(b, half * each + p).start()

        return 0

    lax.fori_loop(0, count * halves, step, 0)

    high = tiles.shape[1]
    steps = width // high
    first = grad.shape[1] - 3 * hidden

    def store(t, r, k):
        down = pl.ds(pl.multiple_of(r * high, high), high)
        into = grad.at[down, pl.ds(first + k * hidden, hidden)]
        return pltpu.make_async_copy(tiles.at[lax.rem(t, 2)], into, o_sem.at[lax.rem(t, 2)])

    turned[...] = xs[...].T
    turned_c[...] = cs[...].T

    def tile(r, k):
        t = 3 * r + k

        @pl.when(t >= 2)
        def _():
            store(t, r, k).wait()

        left_rows = (turned_c if k == 2 else turned)[
            pl.ds(pl.multiple_of(r * high, high), high), :
        ]
        tiles[lax.rem(t, 2)] = jnp.dot(
            left_rows, act[:, k * hidden : (k + 1) * hidden], preferred_element_type=F32
        ).astype(BF16)
        store(t, r, k).start()

    def slab(r, _):
        tile(r, 0)
        tile(r, 1)
        total.relay_in_turn(2 * r)
        tile(r, 2)
        at = chunk(r)
        f_parts[r] = mm(act[at, 2 * hidden :], wv[:, 2 * hidden :], (1, 1), None).astype(BF16)
        total.relay_in_turn(2 * r + 1)
        return 0

    lax.fori_loop(0, steps, slab, 0)
    total.relay_last()
    total.result(g_x)
    total.finish()
    line.finish()
    store(3 * steps - 2, 0, 0).wait()
    store(3 * steps - 1, 0, 0).wait()


def feed_forward(x_own, c_all, w, hidden, count):
    rows, width = x_own.shape
    group = rows * count
    assert count == 4 and width % 4 == 0 and rows % 64 == 0
    anywhere = pl.BlockSpec(memory_space=pl.ANY)
    vmem = pl.BlockSpec(memory_space=pltpu.VMEM)
    dma = pltpu.SemaphoreType.DMA
    return pl.pallas_call(
        functools.partial(ffn_kernel, count),
        out_shape=(
            jax.ShapeDtypeStruct((rows, width), F32),
            jax.ShapeDtypeStruct((count, rows, width), BF16),
            jax.ShapeDtypeStruct(w.shape, BF16),
        ),
        in_specs=[anywhere] * 3,
        out_specs=(vmem, vmem, anywhere),
        scratch_shapes=[
            pltpu.VMEM((width, 3 * hidden), BF16),
            pltpu.VMEM((group, width), BF16),
            pltpu.VMEM((group, width), BF16),
            pltpu.VMEM((group, 3 * hidden), BF16),
            pltpu.VMEM((3, rows, hidden), F32),
            pltpu.VMEM((group, width), BF16),
            pltpu.VMEM((group + rows, width), BF16),
            pltpu.VMEM((width, group), BF16),
            pltpu.VMEM((width, group), BF16),
            pltpu.VMEM((2, width // 4, hidden), BF16),
            dma((3,)), dma((2,)), dma((count + 1, 1)), dma((count, 1)),
            dma((count, 4)), dma((count + 1, 4)), dma((2,)),
        ],
        compiler_params=pltpu.CompilerParams(
            collective_id=0, has_side_effects=True, vmem_limit_bytes=60 << 20
        ),
        cost_estimate=cost(100),
        name="feed_forward",
    )(x_own, c_all, w)


def back_kernel(keep, gated_own, og, o_in, qkv, decay, logits, through, pair_through, gain,
                kept_in, parts_in,
                g_proj, g_logits, g_gain, f_out,
                gated_all, go, runs, g_queried, g_keyed, g_values, pulls, weights, kept,
                parts, landed, state, sending, got, scanned, after, mate_out, mate_in,
                back_out, back_in, second_state, m_sem, in_sem, z_send, z_recv, s_send, s_recv, b_send, b_recv, p_sem, q_sem):
    h, head = lax.axis_index("head"), lax.axis_size("head")
    count, micro, rows, dk = decay.shape
    dv = og.shape[-1]
    width = qkv.shape[-1]
    slices, part = sending.shape[0], sending.shape[2]
    scale = dk ** (-0.5)
    loads = [
        pltpu.make_async_copy(parts_in, parts, in_sem.at[0]),
        pltpu.make_async_copy(kept_in, kept, in_sem.at[1]),
    ]
    for load in loads:
        load.start()
    greet(("seq", "head"))

    def to_head(hop, slot):
        to = lax.rem(h + hop, head)
        columns = gated_own.at[:, pl.ds(pl.multiple_of(to * dv, dv), dv)]
        return push(columns, gated_all.at[slot], z_send.at[hop], z_recv.at[slot], to)

    for hop in range(1, head):
        to_head(hop, h).start()
    gated_all[h] = gated_own[:, pl.ds(pl.multiple_of(h * dv, dv), dv)]

    causal = lower_ones(rows)
    before = [jnp.zeros((1, dk), F32)] * micro
    alive = [jnp.ones((1, dk), F32)] * micro
    for b in range(count):
        for m in range(micro):
            run = running(decay[b, m])
            runs[b, m] = run
            alive[m] = alive[m] * keep[b, m]
            weights[b, m] = jnp.exp(before[m]) * alive[m]
            before[m] = before[m] + run[rows - 1 : rows, :]
    g_gain[...] = jnp.zeros_like(g_gain)
    state[...] = jnp.zeros_like(state)

    def gates(i, _):
        b = near_order(h, head, i)
        pl.when(i > 0)(lambda: to_head(lax.rem(b - h + head, head), b).wait_recv())
        for m in range(micro):
            gate, o = og[b, m], o_in[b, m]
            grad = gated_all[b, m * rows : (m + 1) * rows, :].astype(F32)
            sig = sigmoid(gate)
            inv = lax.rsqrt(jnp.mean(o * o, axis=-1, keepdims=True) + 1e-5)
            plain = o * inv
            normed = (plain * gain[...]).astype(BF16).astype(F32)
            g_on = (grad * gate * sig).astype(BF16).astype(F32)
            g_proj[b, m, :, width:] = (
                grad * normed * sig * (1.0 + gate * (1.0 - sig))
            ).astype(BF16)
            scaled = g_on * gain[...]
            g_o = inv * (scaled - plain * jnp.mean(scaled * plain, axis=-1, keepdims=True))
            go[b, m] = g_o
            g_gain[0:1, :] += jnp.sum(g_on * plain, axis=0, keepdims=True)
            queried = qkv[b, m, :, :dk].astype(F32) * (jnp.exp(runs[b, m]) * scale)
            pull = mms(split(g_o), split(queried), (0, 0))
            pulls[b, m] = pull
            state[m] += pull * weights[b, m]
        return 0

    lax.fori_loop(0, head, gates, 0)
    loads[0].wait()
    total = LineSum(parts, landed, p_sem, q_sem, f_out.shape[0])
    total.send_all()
    half = dv // 2
    side = lax.rem(lax.axis_index("seq"), 2)
    own_half = pl.ds(pl.multiple_of(side * half, half), half)
    mate_half = pl.ds(pl.multiple_of((1 - side) * half, half), half)
    mate_out[...] = state[:, mate_half, :].astype(BF16)
    swap = to_mate(mate_out, mate_in, m_sem.at[0], m_sem.at[1])
    swap.start()
    swap.wait_recv()
    passes = pair_through[:, :, 0:1, :].astype(F32) + pair_through[:, :, 1:2, :].astype(F32)
    for m in range(micro):
        start, later_state = sided(state[m, own_half, :], mate_in[m].astype(F32))
        second_state[m] = later_state
        pair = passes[0, m] * later_state + start
        for i in range(slices):
            sending[i, m] = pair[i * part : (i + 1) * part, :].astype(BF16)
    begin, end, drain = swap_slices(sending, got, s_send, s_recv)
    begin()
    loads[1].wait()

    def inside(b, _):
        for m in range(micro):
            q = qkv[b, m, :, :dk].astype(F32)
            k = qkv[b, m, :, dk : 2 * dk].astype(F32)
            v = (qkv[b, m, :, 2 * dk :],)
            run = runs[b, m]
            queried, keyed = split(q * (jnp.exp(run) * scale)), split(k * jnp.exp(-run))
            g_o, entry = split(go[b, m]), split(kept[b, m])
            scores = split(jnp.where(causal, mms(queried, keyed, (1, 1)), 0.0))
            g_scores = split(jnp.where(causal, mms(g_o, v, (1, 1)), 0.0))
            g_queried[b, m] = mms(g_scores, keyed, (1, 0)) + mms(g_o, entry, (1, 0))
            g_keyed[b, m] = mms(g_scores, queried, (0, 0))
            g_values[b, m] = mms(scores, g_o, (0, 0))
        pl.when(total.inner)(lambda: total.relay(total.far_end, b))
        return 0

    lax.fori_loop(0, count, inside, 0)
    end()
    scan_states(True, got, through, scanned)
    begin_back, end_back, drain_back = swap_slices(scanned, after, b_send, b_recv)
    begin_back()

    @pl.when(total.inner)
    def _():
        for p in range(total.pieces):
            total.relay(head - 1 - total.far_end, p)
        for p in range(total.pieces):
            total.relay(head - 1 - h, p)

    end_back()
    for m in range(micro):
        leave = after[:, m].astype(F32).reshape(half, dk)
        firsts = passes[1, m] * leave + second_state[m]
        own, _ = sided(firsts, leave)
        mate, _ = sided(leave, firsts)
        state[m, own_half, :] = own
        back_out[m] = mate.astype(BF16)
    swap_back = to_mate(back_out, back_in, m_sem.at[2], m_sem.at[3])
    swap_back.start()
    swap_back.wait_recv()
    for m in range(micro):
        state[m, mate_half, :] = back_in[m].astype(F32)

    def across(step, _):
        b = count - 1 - step
        for m in range(micro):
            q = qkv[b, m, :, :dk].astype(F32)
            k = qkv[b, m, :, dk : 2 * dk].astype(F32)
            v = (qkv[b, m, :, 2 * dk :],)
            run = runs[b, m]
            last = run[rows - 1 : rows, :]
            up, down, rest = jnp.exp(run) * scale, jnp.exp(-run), jnp.exp(last - run)
            decayed = jnp.exp(last)
            gs = state[m]
            gs_parts = split(gs)
            carried = k * rest
            g_v = g_values[b, m] + mms(split(carried), gs_parts, (1, 1))
            g_carried = mms(v, gs_parts, (1, 0))
            from_carried = g_carried * carried
            g_total = jnp.sum(decayed * kept[b, m] * gs, axis=0, keepdims=True) + jnp.sum(
                from_carried, axis=0, keepdims=True
            )
            state[m] = (decayed * gs + pulls[b, m]) * keep[b, m]
            gq, gk = g_queried[b, m], g_keyed[b, m]
            g_run = gq * (q * up) - gk * (k * down) - from_carried
            later = mms((causal.astype(F32).astype(BF16),), split(g_run), (0, 0)) + g_total
            g_proj[b, m, :, :dk] = (gq * up).astype(BF16)
            g_proj[b, m, :, dk : 2 * dk] = (gk * down + g_carried * rest).astype(BF16)
            g_proj[b, m, :, 2 * dk : width] = g_v.astype(BF16)
            g_logits[b, m] = (
                later.astype(BF16).astype(F32) * sigmoid(-logits[b, m]) * (1.0 / GATE_NORM)
            )
        return 0

    lax.fori_loop(0, count, across, 0)
    total.result(f_out)
    total.finish()
    drain()
    drain_back()
    swap.wait_send()
    swap_back.wait_send()
    for hop in range(1, head):
        to_head(hop, h).wait_send()


def attention_back(
    keep, gated_own, og, o, qkv, decays, logits, through, pair_through, gain, kept, parts
):
    blocks, micro, rows, width = qkv.shape
    dk, dv = decays.shape[-1], og.shape[-1]
    head, seq = lax.axis_size("head"), lax.axis_size("seq")
    own_rows = parts.shape[0] // head
    vmem, anywhere = pl.BlockSpec(memory_space=pltpu.VMEM), pl.BlockSpec(memory_space=pl.ANY)
    dma = pltpu.SemaphoreType.DMA
    blocked = lambda w, kind: pltpu.VMEM((blocks, micro, rows, w), kind)
    pairs, half = seq // 2, dv // 2
    states = (pairs, micro, half // pairs, dk)
    halves = (micro, half, dk)
    return pl.pallas_call(
        back_kernel,
        out_shape=(
            jax.ShapeDtypeStruct((blocks, micro, rows, width + dv), BF16),
            jax.ShapeDtypeStruct((blocks, micro, rows, dk), F32),
            jax.ShapeDtypeStruct((8, dv), F32),
            jax.ShapeDtypeStruct((own_rows, parts.shape[1]), F32),
        ),
        in_specs=[vmem] * 10 + [anywhere] * 2,
        out_specs=(vmem,) * 4,
        scratch_shapes=[
            pltpu.VMEM((blocks, micro * rows, dv), BF16), blocked(dv, F32), blocked(dk, F32),
            blocked(dk, F32), blocked(dk, F32), blocked(dv, F32),
            pltpu.VMEM((blocks, micro, dv, dk), F32), pltpu.VMEM((blocks, micro, 1, dk), F32),
            pltpu.VMEM((blocks, micro, dv, dk), F32),
            pltpu.VMEM(parts.shape, BF16),
            pltpu.VMEM((parts.shape[0] + own_rows, parts.shape[1]), BF16),
            pltpu.VMEM((micro, dv, dk), F32),
            pltpu.VMEM(states, BF16), pltpu.VMEM(states, BF16), pltpu.VMEM(states, BF16),
            pltpu.VMEM(states, BF16), pltpu.VMEM(halves, BF16), pltpu.VMEM(halves, BF16),
            pltpu.VMEM(halves, BF16), pltpu.VMEM(halves, BF16), pltpu.VMEM(halves, F32), dma((4,)),
            dma((2,)), dma((head,)), dma((head,)), dma((pairs,)), dma((pairs,)), dma((pairs,)),
            dma((pairs,)), dma((head, 4)), dma((head + 1, 4)),
        ],
        compiler_params=pltpu.CompilerParams(
            collective_id=3, has_side_effects=True, vmem_limit_bytes=60 << 20
        ),
        cost_estimate=cost(80),
        name="attention_back",
    )(keep, gated_own, og, o, qkv, decays, logits, through, pair_through, gain, kept,
      parts)


def finish_kernel(xn_in, proj_in, w_in, g_logits, ranked, up_own, rank_down, source,
                  gain, g_ffn, g_head,
                  g_x, grad, norm_sum, ffn_sum, head_sum, bias_sum, up_sum, down_sum,
                  turned, proj, w, outgoing, mine, paired, inbox, heads_in, parts, landed,
                  slim_high, slim_low, small, small_in, small_part,
                  small_heads, small_all, rows_sum, in_sem, pair_send, pair_recv, send, recv, x_send, x_recv,
                  p_sem, q_sem, a_send, a_recv, b_send, b_recv, c_send, c_recv):
    h, head = lax.axis_index("head"), lax.axis_size("head")
    rows, width = g_x.shape
    deep = grad.shape[0] * head
    pairs = lax.axis_size("seq") // 2

    loads = [
        pltpu.make_async_copy(proj_in, proj, in_sem.at[0]),
        pltpu.make_async_copy(w_in, w, in_sem.at[1]),
        pltpu.make_async_copy(xn_in, landed.at[pl.ds(0, xn_in.shape[0])], in_sem.at[2]),
    ]
    for load in loads:
        load.start()
    sums = PairSum(mine, paired, inbox, pair_send, pair_recv, send, recv)
    for load in loads:
        load.wait()
    turned[...] = landed[: xn_in.shape[0], :].T
    greet(("seq", "head"))
    total = LineSum(parts, landed, p_sem, q_sem, rows)
    logit_parts = split(g_logits[...])
    g_ranked = mms(logit_parts, split(up_own[...]), (1, 1))
    slim = split(g_ranked)
    slim_high[...], slim_low[...] = slim

    def chunk(i, _):
        b = near_order(h, head, head - 1 - i)
        at = pl.ds(pl.multiple_of(b * rows, rows), rows)
        rank_part = mms((slim_high[at, :], slim_low[at, :]), (rank_down[...],), (1, 1))
        parts[at, :] = (mm(proj[at, :], w[...], (1, 1), None) + rank_part).astype(BF16)

        @pl.when((b != h) & jnp.logical_not(total.inner))
        def _():
            for p in range(total.pieces):
                total.onward(b, p).start()

        return 0

    lax.fori_loop(0, head, chunk, 0)

    def gone(k, _):
        outgoing[k] = jnp.dot(
            turned[sums.block(k, True), :], proj[...], preferred_element_type=F32
        ).astype(BF16)
        sums.to_partner(outgoing.at[k], k).start()
        return 0

    lax.fori_loop(0, pairs, gone, 0)

    def kept(k, _):
        here = jnp.dot(turned[sums.block(k), :], proj[...], preferred_element_type=F32)
        sums.to_partner(outgoing.at[k], k).wait_recv()
        mine[k] = (here + paired[k].astype(F32)).astype(BF16)
        sums.pass_on(k)

        @pl.when(total.inner & (k < total.pieces))
        def _():
            total.relay(total.far_end, k)

        @pl.when(total.inner & (k > 0) & (k <= total.pieces))
        def _():
            total.relay(head - 1 - total.far_end, k - 1)

        return 0

    lax.fori_loop(0, pairs, kept, 0)

    @pl.when(total.inner)
    def _():
        for p in range(pairs, total.pieces + 1):
            if p < total.pieces:
                total.relay(total.far_end, p)
            total.relay(head - 1 - total.far_end, p - 1)
        for p in range(total.pieces):
            total.relay(head - 1 - h, p)

    thin = grad.shape[0]

    def to_head(hop, slot):
        to = lax.rem(h + hop, head)
        at = pl.ds(pl.multiple_of(to * thin, thin), thin)
        return push(mine.at[sums.own, at, :], heads_in.at[slot], x_send.at[hop], x_recv.at[slot], to)

    sums.advance(0)

    total.result(g_x)
    rows_sum[...] = jnp.zeros_like(rows_sum)
    band = rows_sum.shape[0]

    def norm_rows(r, _):
        at = pl.ds(pl.multiple_of(r * band, band), band)
        x = source[at, :].astype(F32)
        inv = lax.rsqrt(jnp.mean(x * x, axis=-1, keepdims=True) + 1e-6)
        plain, g = x * inv, g_x[at, :]
        scaled = g * gain[...]
        inner = jnp.mean(scaled * plain, axis=-1, keepdims=True)
        rows_sum[...] += g * plain
        g_x[at, :] = inv * (scaled - plain * inner)
        return 0

    lax.fori_loop(0, rows // band, norm_rows, 0)
    rank, dk = up_own.shape
    low, keys = rank // 2, up_sum.shape[1]
    g_down = mms(slim, (turned[...],), (0, 1))
    g_up = mms(split(ranked[...]), logit_parts, (0, 0))
    small[...] = jnp.zeros_like(small)
    small[:low, :width] = g_down[:low]
    small[:low, width:] = g_down[low:]
    own_keys = pl.multiple_of(h * dk, dk)
    small[low:, pl.ds(own_keys, dk)] = g_up[:low]
    small[low:, pl.ds(keys + own_keys, dk)] = g_up[low:]
    small[low : low + 1, width:] = jnp.sum(rows_sum[...], axis=0, keepdims=True)
    small[low + 1 : low + 2, width:] = g_ffn[...]
    small[low + 2 : low + 3, width : width + g_head.shape[1]] = g_head[0:1, :]
    small[low + 3 : low + 4, pl.ds(width + own_keys, dk)] = jnp.sum(
        g_logits[...], axis=0, keepdims=True
    )
    s, seq = lax.axis_index("seq"), lax.axis_size("seq")
    wide = small.shape[1] // seq

    def piece(ref, i):
        return ref.at[:, pl.ds(pl.multiple_of(i * wide, wide), wide)]

    def begin_small(axis, me, count, copy):
        for hop in range(1, count):
            copy(hop, me, lax.rem(me + hop, count)).start()

    def end_small(axis, me, count, copy):
        for hop in range(1, count):
            other = lax.rem(me + hop, count)
            copy(hop, other, other).wait_recv()

    def scatter(hop, slot, to):
        return push(
            piece(small, to), small_in.at[slot], a_send.at[hop], a_recv.at[slot], to, "seq"
        )

    def between(hop, slot, to):
        return push(small_part, small_heads.at[slot], b_send.at[hop], b_recv.at[slot], to)

    def spread(hop, slot, to):
        return push(
            small_part, piece(small_all, slot), c_send.at[hop], c_recv.at[slot], to, "seq"
        )

    begin_small("seq", s, seq, scatter)
    small_in[s] = small[:, pl.ds(pl.multiple_of(s * wide, wide), wide)]
    for step in range(1, sums.levels):
        sums.advance(step)
    for hop in range(1, head):
        to_head(hop, h).start()
    own_rows = pl.ds(pl.multiple_of(h * thin, thin), thin)
    heads_in[h] = mine[sums.own, own_rows, :]
    end_small("seq", s, seq, scatter)
    small_part[...] = jnp.sum(small_in[...], axis=0)
    begin_small("head", h, head, between)
    small_heads[h] = small_part[...]
    end_small("head", h, head, between)
    for hop in range(1, head):
        between(hop, h, lax.rem(h + hop, head)).wait_send()
    small_part[...] = jnp.sum(small_heads[...], axis=0)
    begin_small("seq", s, seq, spread)
    small_all[:, pl.ds(pl.multiple_of(s * wide, wide), wide)] = small_part[...]
    for hop in range(1, head):
        to_head(hop, lax.rem(h + hop, head)).wait_recv()
    dv = mine.shape[2] // 2 - dk
    for j in range(head):
        at, start = 0, 0
        for size in (dk, dk, dv, dv):
            grad[:, start + j * size : start + (j + 1) * size] = heads_in[j, :, at : at + size]
            at, start = at + size, start + head * size
    end_small("seq", s, seq, spread)
    down_sum[:low, :] = small_all[:low, :width]
    down_sum[low:, :] = small_all[:low, width:]
    up_sum[:low, :] = small_all[low:, :keys]
    up_sum[low:, :] = small_all[low:, keys : 2 * keys]
    norm_sum[...] = small_all[low : low + 1, width:]
    ffn_sum[...] = small_all[low + 1 : low + 2, width:]
    head_sum[...] = small_all[low + 2 : low + 3, width : width + head_sum.shape[1]]
    bias_sum[...] = small_all[low + 3 : low + 4, width : width + keys]
    for hop in range(1, seq):
        scatter(hop, s, lax.rem(s + hop, seq)).wait_send()
        spread(hop, s, lax.rem(s + hop, seq)).wait_send()
    sums.finish(lambda k: outgoing.at[k])
    for hop in range(1, head):
        to_head(hop, h).wait_send()
    total.finish()


def finish(
    xn, g_proj, w_in, g_logits, ranked, up_own, rank_down, source, gain, g_ffn, g_head
):
    seq, head = lax.axis_size("seq"), lax.axis_size("head")
    group, width = xn.shape
    columns, rank = w_in.shape[1], ranked.shape[1]
    deep, rows, pairs = width // seq, group // head, seq // 2
    dk = up_own.shape[1]
    vmem, anywhere = pl.BlockSpec(memory_space=pltpu.VMEM), pl.BlockSpec(memory_space=pl.ANY)
    dma = pltpu.SemaphoreType.DMA
    blocks = lambda count, w: pltpu.VMEM((count, deep, w), BF16)
    ends = lambda w: pltpu.VMEM((head, deep // head, w), BF16)
    moves = dma((2, pairs - 1))
    return pl.pallas_call(
        finish_kernel,
        out_shape=(
            jax.ShapeDtypeStruct((rows, width), F32),
            jax.ShapeDtypeStruct((deep // head, columns * head), BF16),
            jax.ShapeDtypeStruct((1, width), F32),
            jax.ShapeDtypeStruct((1, width), F32),
            jax.ShapeDtypeStruct((1, g_head.shape[1]), F32),
            jax.ShapeDtypeStruct((1, dk * head), F32),
            jax.ShapeDtypeStruct((rank, dk * head), F32),
            jax.ShapeDtypeStruct((rank, width), F32),
        ),
        in_specs=[anywhere] * 3 + [vmem] * 8,
        out_specs=(vmem,) * 8,
        scratch_shapes=[
            pltpu.VMEM((width, group), BF16), pltpu.VMEM(g_proj.shape, BF16),
            pltpu.VMEM(w_in.shape, BF16), blocks(pairs, columns), blocks(pairs, columns),
            blocks(pairs, columns), blocks(pairs - 1, columns), ends(columns),
            pltpu.VMEM((group, width), BF16), pltpu.VMEM((group + rows, width), BF16),
            pltpu.VMEM(ranked.shape, BF16), pltpu.VMEM(ranked.shape, BF16),
            pltpu.VMEM((rank, 2 * width), F32), pltpu.VMEM((seq, rank, 2 * width // seq), F32),
            pltpu.VMEM((rank, 2 * width // seq), F32),
            pltpu.VMEM((head, rank, 2 * width // seq), F32),
            pltpu.VMEM((rank, 2 * width), F32), pltpu.VMEM((16, width), F32),
            dma((3,)), dma((pairs,)), dma((pairs,)), moves, moves, dma((head,)), dma((head,)),
            dma((head, 4)), dma((head + 1, 4)),
            dma((seq,)), dma((seq,)), dma((head,)), dma((head,)), dma((seq,)), dma((seq,)),
        ],
        compiler_params=pltpu.CompilerParams(
            collective_id=5, has_side_effects=True, vmem_limit_bytes=60 << 20
        ),
        cost_estimate=cost(95),
        name="finish",
    )(xn, g_proj, w_in, g_logits, ranked, up_own, rank_down, source, gain, g_ffn, g_head)


def weight_grad_kernel(left, right, *rest):
    out, turned = rest[-2:]

    @pl.when(pl.program_id(1) == 0)
    def _():
        turned[...] = left[...].T

    out[...] = jnp.dot(turned[...], right[...], preferred_element_type=F32).astype(BF16)


def weight_grad(left, right, into, columns, start, tile):
    depth, rows = left.shape
    high = min(rows, 512)
    first = start // tile
    given = () if into is None else (into,)
    return pl.pallas_call(
        weight_grad_kernel,
        out_shape=jax.ShapeDtypeStruct((rows, columns), BF16),
        grid=(rows // high, right.shape[1] // tile),
        in_specs=[
            pl.BlockSpec((depth, high), lambda i, j: (0, i)),
            pl.BlockSpec((depth, tile), lambda i, j: (0, j)),
        ]
        + [pl.BlockSpec(memory_space=pl.ANY) for _ in given],
        out_specs=pl.BlockSpec((high, tile), lambda i, j: (i, first + j)),
        scratch_shapes=[pltpu.VMEM((high, depth), BF16)],
        input_output_aliases={2: 0} if given else {},
        compiler_params=pltpu.CompilerParams(
            dimension_semantics=("arbitrary", "arbitrary"), vmem_limit_bytes=48 << 20
        ),
        cost_estimate=pl.CostEstimate(
            flops=2 * depth * rows * right.shape[1],
            bytes_accessed=2 * (depth * rows + (depth + rows) * right.shape[1]),
            transcendentals=0,
        ),
        name="weight_grad",
    )(left, right, *given)


def gather_weight(w):
    return lax.all_gather(w, "seq", axis=0, tiled=True)


def scatter_grad(g):
    return lax.psum_scatter(g.astype(BF16), "seq", scatter_dimension=0, tiled=True)


def dot(a, b, contract, precision=None):
    return lax.dot_general(
        a, b, (((contract[0],), (contract[1],)), ((), ())),
        precision=precision, preferred_element_type=F32,
    )


def rms(x, epsilon):
    return lax.rsqrt(jnp.mean(x * x, axis=-1, keepdims=True) + epsilon)


def norm_back(grad, gain, normed, inv):
    scaled = grad * gain
    inner = jnp.mean(scaled * normed, axis=-1, keepdims=True)
    return inv * (scaled - normed * inner), jnp.sum(grad * normed, axis=0)


def on_device(
    tokens, starts, cotangent, mix_in, mix_out, gate_up, down_proj,
    norm_gain, ffn_gain, head_gain, rank_down, rank_up, gate_bias,
):
    micro, rows, width = tokens.shape
    heads, seq = lax.axis_size("head"), lax.axis_size("seq")
    head = lax.axis_index("head")
    keys, dv = rank_up.shape[1], head_gain.shape[0]
    dk, vals = keys // heads, dv * heads
    hidden_units = down_proj.shape[1]
    group = heads * micro * rows
    proj_width = 2 * dk + 2 * dv

    def own_columns(w, start, size):
        return lax.dynamic_slice_in_dim(w, start + head * size, size, 1)

    w_in_own = jnp.concatenate(
        [
            own_columns(mix_in, 0, dk),
            own_columns(mix_in, keys, dk),
            own_columns(mix_in, 2 * keys, dv),
            own_columns(mix_in, 2 * keys + vals, dv),
        ],
        axis=1,
    )
    later = gather_weight(
        jnp.concatenate(
            [gate_up.reshape(gate_up.shape[0], 2 * hidden_units), down_proj, mix_out], axis=1
        )
    )
    w_out = later[:, 3 * hidden_units :]
    up_own = own_columns(rank_up, 0, dk)
    bias_own = lax.dynamic_slice_in_dim(gate_bias, head * dk, dk, 0)

    xn, w_in = gather_norm(
        tokens.reshape(micro * rows, width), norm_gain.reshape(1, width), w_in_own
    )
    qkv = dot(xn, w_in[:, : 2 * dk + dv], (1, 0)).astype(BF16)
    og = dot(xn, w_in[:, 2 * dk + dv :], (1, 0))
    ranked = dot(xn, rank_down, (1, 0))
    logits = dot(ranked, up_own, (1, 0), HIGHEST) + bias_own
    decays = (jax.nn.log_sigmoid(logits) / GATE_NORM).astype(BF16)

    def blocks(x):
        return x.reshape(heads, micro, rows, x.shape[-1])

    qkv_b, og_b, decays_b = blocks(qkv), blocks(og), blocks(decays)
    gain_row = head_gain.reshape(1, dv)
    keep = 1.0 - jnp.broadcast_to(starts.T[:, :, None, None], (heads, micro, 1, dk)).astype(F32)
    o_b, gated, through, pair_through, kept, all_cot = attention_forward(
        keep, qkv_b, decays_b, og_b, gain_row, cotangent.reshape(micro * rows, width)
    )

    source = tokens.astype(F32).reshape(micro * rows, width)
    hidden = source + dot(gated, w_out, (1, 1))
    inv_ffn = rms(hidden, 1e-6)
    plain_ffn = hidden * inv_ffn
    h2 = (plain_ffn * ffn_gain).astype(BF16)

    g_h2, ffn_part, grads = feed_forward(h2, all_cot, later, hidden_units, heads)

    back_ffn, g_ffn_gain = norm_back(g_h2, ffn_gain, plain_ffn, inv_ffn)
    g_hidden = cotangent.astype(F32).reshape(micro * rows, width) + back_ffn
    g_mixed = g_hidden.astype(BF16)
    grads = scatter_grad(weight_grad(g_mixed, gated, grads, later.shape[1], 0, vals))
    g_gated = dot(g_mixed, w_out, (1, 0)).astype(BF16)
    g_proj_b, g_logits_b, g_head_gain, ffn_out = attention_back(
        keep, g_gated, og_b, o_b, qkv_b, decays_b, blocks(logits), through, pair_through, gain_row, kept, ffn_part.reshape(group, width),
    )
    output = (hidden + ffn_out).astype(BF16)
    g_proj, g_logits = g_proj_b.reshape(group, proj_width), g_logits_b.reshape(group, dk)
    back_in, grad_in, *small, g_rank_down = finish(
        xn, g_proj, w_in, g_logits, ranked, up_own, rank_down, tokens.reshape(micro * rows, width),
        norm_gain.reshape(1, width), g_ffn_gain.reshape(1, width), g_head_gain,
    )
    g_norm_gain, g_ffn_gain, g_head_gain, g_bias, g_rank_up = small
    input_grad = g_hidden + back_in
    slab = width // (seq * heads)
    grad_in, grads = lax.optimization_barrier((grad_in, grads))
    grad_ffn = grads[:, vals:]
    grad_out = lax.all_to_all(
        grads[:, :vals].reshape(heads, slab, vals), "head", split_axis=0, concat_axis=0, tiled=True
    )
    grad_out = grad_out.astype(F32).sum(0)
    return (
        output.reshape(tokens.shape),
        input_grad.reshape(tokens.shape),
        grad_in.astype(F32),
        grad_out,
        grad_ffn[:, : 2 * hidden_units].astype(F32).reshape(-1, 2, hidden_units),
        grad_ffn[:, 2 * hidden_units :].astype(F32),
        g_norm_gain.reshape(norm_gain.shape),
        g_ffn_gain.reshape(ffn_gain.shape),
        g_head_gain.reshape(head_gain.shape),
        g_rank_down.T,
        g_rank_up,
        g_bias.reshape(gate_bias.shape),
    )


def solution(mesh):
    rows = P(None, ("seq", "head"), None)
    return jax.shard_map(
        on_device,
        mesh=mesh,
        in_specs=(
            rows, P(None, "seq"), rows, P("seq", None), P("seq", None),
            P("seq", None, "head"), P("seq", "head"), P(), P(), P(), P(), P(), P(),
        ),
        out_specs=(
            rows, rows, P(("seq", "head"), None), P(("seq", "head"), None),
            P("seq", None, "head"), P("seq", "head"), P(), P(), P(), P(), P(), P(),
        ),
        check_vma=False,
    )
```

```python
import functools

import jax
import jax.numpy as jnp
from jax import lax
from jax.experimental import pallas as pl
from jax.experimental.pallas import tpu as pltpu
from jax.sharding import PartitionSpec as P

HIGHEST = lax.Precision.HIGHEST
GATE_NORM = 16.0
BF16 = jnp.bfloat16
F32 = jnp.float32


def mm(a, b, contract, precision=HIGHEST):
    return lax.dot_general(
        a, b, ((contract[:1], contract[1:]), ((), ())),
        precision=precision, preferred_element_type=F32,
    )


def split(x):
    high = x.astype(BF16)
    return high, (x - high.astype(F32)).astype(BF16)


def mms(left, right, contract):
    total = mm(left[0], right[0], contract, None)
    if len(right) > 1:
        total += mm(left[0], right[1], contract, None)
    if len(left) > 1:
        total += mm(left[1], right[0], contract, None)
    return total


def lower_ones(size):
    rows = lax.broadcasted_iota(jnp.int32, (size, size), 0)
    cols = lax.broadcasted_iota(jnp.int32, (size, size), 1)
    return rows >= cols


def running(decay_low):
    ones = lower_ones(decay_low.shape[0]).astype(F32).astype(BF16)
    return mm(ones, decay_low, (1, 0), None)


def sigmoid(x):
    return 1.0 / (1.0 + jnp.exp(-x))


def cost(micros):
    return pl.CostEstimate(flops=0, bytes_accessed=int(micros * 3.0e6), transcendentals=0)


def greet(axes):
    barrier = pltpu.get_barrier_semaphore()
    met = 0
    for axis in axes:
        me, count = lax.axis_index(axis), lax.axis_size(axis)
        for hop in range(1, count):
            pl.semaphore_signal(
                barrier, inc=1, device_id={axis: lax.rem(me + hop, count)},
                device_id_type=pl.DeviceIdType.MESH,
            )
        met += count - 1
    pl.semaphore_wait(barrier, met)


def push(src, dst, send, recv, to, axis="head"):
    return pltpu.make_async_remote_copy(
        src_ref=src, dst_ref=dst, send_sem=send, recv_sem=recv,
        device_id={axis: to}, device_id_type=pl.DeviceIdType.MESH,
    )


def near_order(z, count, i):
    both = jnp.minimum(z, count - 1 - z)
    left = z > count - 1 - z
    paired = jnp.where(i % 2 == 1, z - (i + 1) // 2, z + i // 2)
    single = jnp.where(left, z - (i - both), z + (i - both))
    return jnp.where(i <= 2 * both, paired, single)


class Line:
    def __init__(self, own, all_rows, send, recv):
        self.own, self.all, self.send, self.recv = own, all_rows, send, recv
        self.z, self.count = lax.axis_index("head"), lax.axis_size("head")
        self.rows, self.parts = own.shape[0], recv.shape[1]
        self.deep = self.rows // self.parts

    def at(self, b):
        return self.all.at[pl.ds(pl.multiple_of(b * self.rows, self.rows), self.rows)]

    def part(self, b, p):
        start = b * self.rows + p * self.deep
        return self.all.at[pl.ds(pl.multiple_of(start, self.deep), self.deep)]

    def first(self, way, p):
        to = lax.rem(self.z + (1 if way == 0 else self.count - 1), self.count)
        src = self.own.at[pl.ds(p * self.deep, self.deep)]
        return push(
            src, self.part(self.z, p), self.send.at[way, p], self.recv.at[self.z, p], to
        )

    def each_first(self, act):
        for p in range(self.parts):
            pl.when(self.z < self.count - 1)(lambda p=p: act(self.first(0, p)))
            pl.when(self.z > 0)(lambda p=p: act(self.first(1, p)))

    def start(self):
        self.each_first(lambda copy: copy.start())

    def passing(self, i, b, p):
        z, count = self.z, self.count
        to = jnp.where(b < z, z + 1, z - 1)
        going = ((b < z) & (z < count - 1)) | ((b > z) & (z > 0))
        copy = push(
            self.part(b, p), self.part(b, p), self.send.at[i + 1, p], self.recv.at[b, p],
            lax.rem(to + count, count),
        )
        return copy, going

    def receive(self, i, b, p=0):
        copy, going = self.passing(i, b, p)
        copy.wait_recv()
        pl.when(going)(copy.start)

    def finish(self):
        def sent(i, _):
            for p in range(self.parts):
                copy, going = self.passing(i, near_order(self.z, self.count, i), p)
                pl.when(going)(copy.wait_send)
            return 0

        lax.fori_loop(1, self.count, sent, 0)
        self.each_first(lambda copy: copy.wait_send())


class LineSum:
    def __init__(self, parts, landed, send, recv, rows):
        self.parts, self.landed, self.send, self.recv = parts, landed, send, recv
        self.z, self.count = lax.axis_index("head"), lax.axis_size("head")
        self.rows, self.pieces = rows, send.shape[1]
        self.deep = rows // self.pieces
        self.inner = (self.z > 0) & (self.z < self.count - 1)
        self.far_end = jnp.where(self.z < self.count - 1 - self.z, self.count - 1, 0)

    def piece(self, b, p):
        return pl.ds(pl.multiple_of(b * self.rows + p * self.deep, self.deep), self.deep)

    def onward(self, b, p):
        z, count = self.z, self.count
        to = jnp.where(b > z, z + 1, z - 1)
        slot = jnp.where((to == b) & (z > b), count, b)
        return push(
            self.parts.at[self.piece(b, p)], self.landed.at[self.piece(slot, p)],
            self.send.at[b, p], self.recv.at[slot, p], lax.rem(to + count, count),
        )

    def send_all(self):
        @pl.when(jnp.logical_not(self.inner))
        def _():
            for i in range(1, self.count):
                b = jnp.where(self.z == 0, self.count - i, i - 1)
                for p in range(self.pieces):
                    self.onward(b, p).start()

    def arrived(self, slot, p):
        at = self.piece(slot, p)
        push(
            self.landed.at[at], self.landed.at[at], self.send.at[0, p], self.recv.at[slot, p],
            lax.rem(self.z + 1, self.count),
        ).wait_recv()
        return self.landed[at, :].astype(F32)

    def relay(self, b, p):
        at = self.piece(b, p)
        self.parts[at, :] = (self.parts[at, :].astype(F32) + self.arrived(b, p)).astype(BF16)
        self.onward(b, p).start()

    def relay_in_turn(self, j):
        pieces = self.pieces

        @pl.when(self.inner & (j < pieces))
        def _():
            self.relay(self.count - 1 - self.z, j)

        @pl.when(self.inner & (j >= pieces))
        def _():
            self.relay(self.far_end, j - pieces)

        @pl.when(self.inner & (j > pieces))
        def _():
            self.relay(self.count - 1 - self.far_end, j - pieces - 1)

    def relay_last(self):
        @pl.when(self.inner)
        def _():
            self.relay(self.count - 1 - self.far_end, self.pieces - 1)

    def result(self, out):
        z, count = self.z, self.count
        for p in range(self.pieces):
            here = pl.ds(p * self.deep, self.deep)
            out[here, :] = self.parts[self.piece(z, p), :].astype(F32)

            @pl.when(z > 0)
            def _():
                out[here, :] += self.arrived(z, p)

            @pl.when(z < count - 1)
            def _():
                out[here, :] += self.arrived(count, p)

    def finish(self):
        def sent(i, _):
            b = near_order(self.z, self.count, i)
            for p in range(self.pieces):
                self.onward(b, p).wait_send()
            return 0

        lax.fori_loop(1, self.count, sent, 0)


class PairSum:
    def __init__(self, mine, paired, inbox, pair_send, pair_recv, send, recv):
        self.mine, self.paired, self.inbox = mine, paired, inbox
        self.pair_send, self.pair_recv, self.send, self.recv = pair_send, pair_recv, send, recv
        self.s, self.pairs = lax.axis_index("seq"), lax.axis_size("seq") // 2
        self.side, self.own = lax.rem(self.s, 2), self.s // 2
        self.deep, self.half = mine.shape[1], mine.shape[2] // 2
        self.levels = self.pairs.bit_length() - 1
        assert self.pairs == 1 << self.levels

    def block(self, k, other=False):
        i = 2 * k + (1 - self.side if other else self.side)
        return pl.ds(pl.multiple_of(i * self.deep, self.deep), self.deep)

    def to_partner(self, src, k):
        return push(
            src, self.paired.at[k], self.pair_send.at[k], self.pair_recv.at[k],
            self.s + 1 - 2 * self.side, "seq",
        )

    def bit(self, i, level):
        return lax.rem(i // (1 << level), 2)

    def move(self, side, slot, k, level):
        columns = pl.ds(side * self.half, self.half)
        to = self.s + (1 - 2 * self.bit(self.own, level)) * (2 << level)
        return push(
            self.mine.at[k, :, columns], self.inbox.at[slot, :, columns],
            self.send.at[side, slot], self.recv.at[side, slot], to, "seq",
        )

    def moves(self, side, step):
        order = list(range(self.levels))
        if side:
            order.reverse()
        level, free = order[step], sorted(order[step + 1 :])
        fixed = sum((self.bit(self.own, d) * (1 << d) for d in order[:step]), 0)
        offset = self.pairs - (1 << (self.levels - step))
        here = self.bit(self.own, level) * (1 << level)
        for c in range(1 << len(free)):
            rest = fixed + sum(((c >> j) & 1) << d for j, d in enumerate(free))
            yield offset + c, rest + here, rest + (1 << level) - here, level

    def pass_on(self, k):
        top = 1 << (self.levels - 1)
        pl.when(self.bit(k, 0) != self.bit(self.own, 0))(self.move(0, k // 2, k, 0).start)
        pl.when(k // top != self.own // top)(
            self.move(1, lax.rem(k, top), k, self.levels - 1).start
        )

    def advance(self, step):
        for side in range(2):
            columns = slice(side * self.half, (side + 1) * self.half)
            for slot, keep, gone, level in self.moves(side, step):
                self.move(side, slot, gone, level).wait_recv()
                self.mine[keep, :, columns] = (
                    self.mine[keep, :, columns].astype(F32)
                    + self.inbox[slot, :, columns].astype(F32)
                ).astype(BF16)
            if step + 1 < self.levels:
                for slot, keep, gone, level in self.moves(side, step + 1):
                    self.move(side, slot, gone, level).start()

    def finish(self, src):
        for k in range(self.pairs):
            self.to_partner(src(k), k).wait_send()
        for side in range(2):
            for step in range(self.levels):
                for slot, keep, gone, level in self.moves(side, step):
                    self.move(side, slot, gone, level).wait_send()


def gather_norm_kernel(own, gain, shard, normed, rows_of_all, rows_all, here_sem, send, recv,
                       w_sem, w_peer, w_pair, w_recv):
    z, count, rows = lax.axis_index("head"), lax.axis_size("head"), own.shape[0]
    greet(("seq", "head"))
    line = Line(own, rows_all, send, recv)
    line.start()
    here = pltpu.make_async_copy(own, line.at(z), here_sem)
    here.start()

    s, deep = lax.axis_index("seq"), shard.shape[0]
    side, pairs, own_pair = lax.rem(s, 2), lax.axis_size("seq") // 2, s // 2
    partner = s + 1 - 2 * side

    def shard_at(i):
        return rows_of_all.at[pl.ds(pl.multiple_of(i * deep, deep), deep)]

    def to_peer(k):
        return push(shard, shard_at(s), w_peer.at[k], w_recv.at[s], 2 * k + side, "seq")

    def from_peer(k):
        i = 2 * k + side
        return push(shard, shard_at(i), w_peer.at[k], w_recv.at[i], partner, "seq")

    def to_partner(k):
        i = 2 * k + side
        return push(shard_at(i), shard_at(i), w_pair.at[k], w_recv.at[i], partner, "seq")

    def from_partner(k):
        i = 2 * k + 1 - side
        return push(shard_at(i), shard_at(i), w_pair.at[k], w_recv.at[i], partner, "seq")

    mine = pltpu.make_async_copy(shard, shard_at(s), w_sem)
    mine.start()
    for k in range(pairs):
        pl.when(own_pair != k)(to_peer(k).start)
    mine.wait()
    to_partner(own_pair).start()
    here.wait()
    band = 16

    def step(i, _):
        b = near_order(z, count, i)
        pl.when(i > 0)(lambda: line.receive(i, b))

        def norm(r, _):
            at = pl.ds(pl.multiple_of(b * rows + r * band, band), band)
            x = rows_all[at, :].astype(F32)
            inv = lax.rsqrt(jnp.mean(x * x, axis=-1, keepdims=True) + 1e-6)
            normed[at, :] = (x * inv * gain[...]).astype(BF16)
            return 0

        lax.fori_loop(0, rows // band, norm, 0)
        return 0

    lax.fori_loop(0, count, step, 0)
    for k in range(pairs):

        @pl.when(own_pair != k)
        def _():
            from_peer(k).wait_recv()
            to_partner(k).start()

    for k in range(pairs):
        from_partner(k).wait_recv()
    for k in range(pairs):
        to_partner(k).wait_send()
        pl.when(own_pair != k)(to_peer(k).wait_send)
    line.finish()


def gather_norm(x, gain, shard):
    rows, width = x.shape
    seq = lax.axis_size("seq")
    anywhere = pl.BlockSpec(memory_space=pl.ANY)
    count = lax.axis_size("head")
    vmem = pl.BlockSpec(memory_space=pltpu.VMEM)
    dma = pltpu.SemaphoreType.DMA
    return pl.pallas_call(
        gather_norm_kernel,
        out_shape=(
            jax.ShapeDtypeStruct((count * rows, width), BF16),
            jax.ShapeDtypeStruct((seq * shard.shape[0], shard.shape[1]), BF16),
        ),
        in_specs=[vmem, vmem, anywhere],
        out_specs=(vmem, anywhere),
        scratch_shapes=[
            pltpu.VMEM((count * rows, width), BF16), dma(()), dma((count + 1, 1)), dma((count, 1)),
            dma(()), dma((seq // 2,)), dma((seq // 2,)), dma((seq,)),
        ],
        compiler_params=pltpu.CompilerParams(
            collective_id=1, has_side_effects=True, vmem_limit_bytes=32 << 20
        ),
        cost_estimate=cost(50),
        name="gather_norm",
    )(x, gain, shard)


def swap_slices(own, got, send, recv):
    side = lax.rem(lax.axis_index("seq"), 2)
    me, count = lax.axis_index("seq") // 2, lax.axis_size("seq") // 2

    def copy(hop, index):
        to = lax.rem(me + hop, count)
        return push(own.at[to], got.at[index], send.at[hop], recv.at[index], 2 * to + side, "seq")

    def start(hop, _):
        copy(hop, me).start()
        return 0

    def wait_recv(hop, _):
        copy(hop, lax.rem(me + hop, count)).wait_recv()
        return 0

    def wait_send(hop, _):
        copy(hop, me).wait_send()
        return 0

    def begin():
        lax.fori_loop(1, count, start, 0)
        got[me] = own[me]

    def end():
        lax.fori_loop(1, count, wait_recv, 0)

    def drain():
        lax.fori_loop(1, count, wait_send, 0)

    return begin, end, drain


def to_mate(src, dst, send, recv):
    s = lax.axis_index("seq")
    return push(src, dst, send, recv, s + 1 - 2 * lax.rem(s, 2), "seq")


def sided(own, mate):
    first = lax.rem(lax.axis_index("seq"), 2) == 0
    return jnp.where(first, own, mate), jnp.where(first, mate, own)


def scan_states(reverse, own, through, out):
    count, part = out.shape[0], out.shape[2]

    def step(k, state):
        j = count - 1 - k if reverse else k
        out[j] = state.astype(BF16)
        decay = through[j, :, 0:1, :].astype(F32) + through[j, :, 1:2, :].astype(F32)
        return decay * state + own[j, :, :part, :].astype(F32)

    lax.fori_loop(0, count, step, jnp.zeros(out.shape[1:], F32))


def front_kernel(keep, qkv, decay, og, gain, rows_own,
                 o_out, gated, through, pair_through, kept_out, rows_all,
                 kept, runs, state, sending, got, scanned, before, leaving, mate_out, mate_in,
                 back_out, back_in, first_state,
                 here_sem, go, come, s_send, s_recv, b_send, b_recv, z_send, z_recv, k_sem, m_sem):
    h, head = lax.axis_index("head"), lax.axis_size("head")
    count, micro, rows, dk = decay.shape
    dv = og.shape[-1]
    slices, part = scanned.shape[0], scanned.shape[2]
    scale = dk ** (-0.5)
    greet(("seq", "head"))
    line = Line(rows_own, rows_all, go, come)
    line.start()
    here = pltpu.make_async_copy(rows_own, line.at(h), here_sem)
    here.start()

    state[...] = jnp.zeros_like(state)
    passed = [jnp.zeros((1, dk), F32)] * micro
    alive = [jnp.ones((1, dk), F32)] * micro
    for b in range(count):
        for m in range(micro):
            run = running(decay[b, m])
            runs[b, m] = run
            last = run[rows - 1 : rows, :]
            carried = qkv[b, m, :, dk : 2 * dk].astype(F32) * jnp.exp(last - run)
            fresh = mms((qkv[b, m, :, 2 * dk :],), split(carried), (0, 0))
            kept[b, m] = fresh
            state[m] = jnp.exp(last) * (state[m] * keep[b, m]) + fresh
            passed[m] = passed[m] + last
            alive[m] = alive[m] * keep[b, m]
    tail = sending.shape[2] - part
    at = lax.broadcasted_iota(jnp.int32, (tail, dk), 0)
    half = dv // 2
    side = lax.rem(lax.axis_index("seq"), 2)
    own_half = pl.ds(pl.multiple_of(side * half, half), half)
    mate_half = pl.ds(pl.multiple_of((1 - side) * half, half), half)

    def as_rows(value):
        high, low = split(value)
        return jnp.where(at == 0, high.astype(F32), jnp.where(at == 1, low.astype(F32), 0.0))

    own_rows = [as_rows(jnp.exp(passed[m]) * alive[m]) for m in range(micro)]
    for m in range(micro):
        mate_out[m, :half, :] = state[m, mate_half, :].astype(BF16)
        mate_out[m, half:, :] = own_rows[m].astype(BF16)
    swap = to_mate(mate_out, mate_in, m_sem.at[0], m_sem.at[1])
    swap.start()
    swap.wait_recv()
    first_through = []
    for m in range(micro):
        firsts, seconds = sided(own_rows[m], mate_in[m, half:, :].astype(F32))
        pair_through[0, m], pair_through[1, m] = firsts.astype(BF16), seconds.astype(BF16)
        first, second = firsts[0:1] + firsts[1:2], seconds[0:1] + seconds[1:2]
        first_through.append(first)
        start, after = sided(state[m, own_half, :], mate_in[m, :half, :].astype(F32))
        first_state[m] = start
        pair = second * start + after
        both = as_rows(first * second).astype(BF16)
        for i in range(slices):
            sending[i, m, :part, :] = pair[i * part : (i + 1) * part, :].astype(BF16)
            sending[i, m, part:, :] = both
    begin, end, drain = swap_slices(sending, got, s_send, s_recv)
    begin()
    causal = lower_ones(rows)

    def inside(b, _):
        for m in range(micro):
            run = runs[b, m]
            queried = split(qkv[b, m, :, :dk].astype(F32) * (jnp.exp(run) * scale))
            keyed = split(qkv[b, m, :, dk : 2 * dk].astype(F32) * jnp.exp(-run))
            scores = jnp.where(causal, mms(queried, keyed, (1, 1)), 0.0)
            o_out[b, m] = mms(split(scores), (qkv[b, m, :, 2 * dk :],), (1, 0))
        return 0

    lax.fori_loop(0, count, inside, 0)
    line.receive(1, near_order(h, head, 1))
    end()
    through[...] = got[:, :, part:, :]
    scan_states(False, got, through, scanned)
    begin_back, end_back, drain_back = swap_slices(scanned, before, b_send, b_recv)
    begin_back()
    line.receive(2, near_order(h, head, 2))
    end_back()
    for m in range(micro):
        entry = before[:, m].astype(F32).reshape(half, dk)
        own, mate = sided(entry, first_through[m] * entry + first_state[m])
        state[m, own_half, :] = own
        back_out[m] = mate.astype(BF16)
    swap_back = to_mate(back_out, back_in, m_sem.at[2], m_sem.at[3])
    swap_back.start()
    swap_back.wait_recv()
    for m in range(micro):
        state[m, mate_half, :] = back_in[m].astype(F32)

    def to_owner(b):
        columns = gated.at[:, pl.ds(pl.multiple_of(h * dv, dv), dv)]
        return push(leaving.at[b], columns, z_send.at[b], z_recv.at[h], b)

    def save(b):
        return pltpu.make_async_copy(kept.at[b], kept_out.at[b], k_sem.at[b])

    def across(b, _):
        for m in range(micro):
            run = runs[b, m]
            queried = split(qkv[b, m, :, :dk].astype(F32) * (jnp.exp(run) * scale))
            entry = state[m] * keep[b, m]
            state[m] = jnp.exp(run[rows - 1 : rows, :]) * entry + kept[b, m]
            kept[b, m] = entry
            o = o_out[b, m] + mms(queried, split(entry), (1, 1))
            o_out[b, m] = o
            inv = lax.rsqrt(jnp.mean(o * o, axis=-1, keepdims=True) + 1e-5)
            normed = (o * inv * gain[...]).astype(BF16).astype(F32)
            gate = og[b, m]
            leaving[b, m * rows : (m + 1) * rows, :] = (normed * gate * sigmoid(gate)).astype(BF16)
        save(b).start()
        pl.when(b != h)(to_owner(b).start)

        @pl.when(b == 1)
        def _():
            line.receive(3, near_order(h, head, 3))

        return 0

    lax.fori_loop(0, count, across, 0)
    gated[:, pl.ds(pl.multiple_of(h * dv, dv), dv)] = leaving[h]
    for hop in range(1, head):
        other = lax.rem(h + hop, head)
        columns = gated.at[:, pl.ds(pl.multiple_of(other * dv, dv), dv)]
        push(leaving.at[other], columns, z_send.at[other], z_recv.at[other], other).wait_recv()
        to_owner(other).wait_send()
    for b in range(count):
        save(b).wait()
    here.wait()
    line.finish()
    drain()
    drain_back()
    swap.wait_send()
    swap_back.wait_send()


def attention_forward(keep, qkv, decays, og, gain, rows_own):
    blocks, micro, rows, width = qkv.shape
    dk, dv = decays.shape[-1], og.shape[-1]
    head, seq = lax.axis_size("head"), lax.axis_size("seq")
    assert blocks == head and head == 4
    pairs, half, tail = seq // 2, dv // 2, 16
    part = half // pairs
    own_rows = micro * rows
    vmem, anywhere = pl.BlockSpec(memory_space=pltpu.VMEM), pl.BlockSpec(memory_space=pl.ANY)
    dma = pltpu.SemaphoreType.DMA
    states, wider = (pairs, micro, part, dk), (pairs, micro, part + tail, dk)
    return pl.pallas_call(
        front_kernel,
        out_shape=(
            jax.ShapeDtypeStruct((blocks, micro, rows, dv), F32),
            jax.ShapeDtypeStruct((own_rows, head * dv), BF16),
            jax.ShapeDtypeStruct((pairs, micro, tail, dk), BF16),
            jax.ShapeDtypeStruct((2, micro, tail, dk), BF16),
            jax.ShapeDtypeStruct((blocks, micro, dv, dk), F32),
            jax.ShapeDtypeStruct((head * rows_own.shape[0], rows_own.shape[1]), BF16),
        ),
        in_specs=[vmem] * 5 + [anywhere],
        out_specs=(vmem,) * 4 + (anywhere,) * 2,
        scratch_shapes=[
            pltpu.VMEM((blocks, micro, dv, dk), F32), pltpu.VMEM((blocks, micro, rows, dk), F32),
            pltpu.VMEM((micro, dv, dk), F32), pltpu.VMEM(wider, BF16), pltpu.VMEM(wider, BF16),
            pltpu.VMEM(states, BF16), pltpu.VMEM(states, BF16),
            pltpu.VMEM((blocks, own_rows, dv), BF16),
            pltpu.VMEM((micro, half + tail, dk), BF16), pltpu.VMEM((micro, half + tail, dk), BF16),
            pltpu.VMEM((micro, half, dk), BF16), pltpu.VMEM((micro, half, dk), BF16),
            pltpu.VMEM((micro, half, dk), F32),
            dma(()), dma((head + 1, 1)), dma((head, 1)), dma((pairs,)), dma((pairs,)), dma((pairs,)),
            dma((pairs,)), dma((head,)), dma((head,)), dma((blocks,)), dma((4,)),
        ],
        compiler_params=pltpu.CompilerParams(
            collective_id=2, has_side_effects=True, vmem_limit_bytes=60 << 20
        ),
        cost_estimate=cost(90),
        name="attention_forward",
    )(keep, qkv, decays, og, gain, rows_own)


def ffn_kernel(count, x_own, c_all, w, g_x, f_parts, grad,
               wv, xs, cs, act, lin, parts, landed, turned, turned_c, tiles,
               w_sem, own_sem, go_sem, x_sem, p_sem, q_sem, o_sem):
    z = lax.axis_index("head")
    rows, width = x_own.shape
    hidden = act.shape[1] // 3
    chunk = lambda b: pl.ds(pl.multiple_of(b * rows, rows), rows)

    weights = [
        pltpu.make_async_copy(
            w.at[:, pl.ds(w.shape[1] + (k - 3) * hidden, hidden)],
            wv.at[:, pl.ds(k * hidden, hidden)],
            w_sem.at[k],
        )
        for k in range(3)
    ]
    own = [
        pltpu.make_async_copy(x_own, xs.at[chunk(z)], own_sem.at[0]),
        pltpu.make_async_copy(c_all, cs, own_sem.at[1]),
    ]
    for copy in own + weights:
        copy.start()
    greet(("head",))
    line = Line(x_own, xs, go_sem, x_sem)
    line.start()
    for copy in own + weights:
        copy.wait()

    total = LineSum(parts, landed, p_sem, q_sem, rows)

    halves = x_sem.shape[1]
    deep = rows // halves
    each = total.pieces // halves

    def step(t, _):
        i, half = t // halves, lax.rem(t, halves)
        b = near_order(z, count, i)
        pl.when(i > 0)(lambda: line.receive(i, b, half))
        start = b * rows + half * deep
        at = pl.ds(pl.multiple_of(start, deep), deep)
        x = xs[at, :]
        lin[0] = jnp.dot(x, wv[:, :hidden], preferred_element_type=F32)
        lin[1] = jnp.dot(x, wv[:, hidden : 2 * hidden], preferred_element_type=F32)
        lin[2] = jnp.dot(cs[at, :], wv[:, 2 * hidden :], preferred_element_type=F32)
        band = 16

        def act_rows(r, _):
            here = pl.ds(pl.multiple_of(r * band, band), band)
            there = pl.ds(pl.multiple_of(start + r * band, band), band)
            gate, up, g_product = lin[0, here, :], lin[1, here, :], lin[2, here, :]
            sig = sigmoid(gate)
            gated = gate * sig
            act[there, :hidden] = (g_product * up * sig * (1.0 + gate * (1.0 - sig))).astype(BF16)
            act[there, hidden : 2 * hidden] = (g_product * gated).astype(BF16)
            act[there, 2 * hidden :] = (gated * up).astype(BF16)
            return 0

        lax.fori_loop(0, deep // band, act_rows, 0)
        parts[at, :] = mm(act[at, : 2 * hidden], wv[:, : 2 * hidden], (1, 1), None).astype(BF16)

        @pl.when((i > 0) & jnp.logical_not(total.inner))
        def _():
            for p in range(each):
                total.onward(b, half * each + p).start()

        return 0

    lax.fori_loop(0, count * halves, step, 0)

    high = tiles.shape[1]
    steps = width // high
    first = grad.shape[1] - 3 * hidden

    def store(t, r, k):
        down = pl.ds(pl.multiple_of(r * high, high), high)
        into = grad.at[down, pl.ds(first + k * hidden, hidden)]
        return pltpu.make_async_copy(tiles.at[lax.rem(t, 2)], into, o_sem.at[lax.rem(t, 2)])

    turned[...] = xs[...].T
    turned_c[...] = cs[...].T

    def tile(r, k):
        t = 3 * r + k

        @pl.when(t >= 2)
        def _():
            store(t, r, k).wait()

        left_rows = (turned_c if k == 2 else turned)[
            pl.ds(pl.multiple_of(r * high, high), high), :
        ]
        tiles[lax.rem(t, 2)] = jnp.dot(
            left_rows, act[:, k * hidden : (k + 1) * hidden], preferred_element_type=F32
        ).astype(BF16)
        store(t, r, k).start()

    def slab(r, _):
        tile(r, 0)
        tile(r, 1)
        total.relay_in_turn(2 * r)
        tile(r, 2)
        at = chunk(r)
        f_parts[r] = mm(act[at, 2 * hidden :], wv[:, 2 * hidden :], (1, 1), None).astype(BF16)
        total.relay_in_turn(2 * r + 1)
        return 0

    lax.fori_loop(0, steps, slab, 0)
    total.relay_last()
    total.result(g_x)
    total.finish()
    line.finish()
    store(3 * steps - 2, 0, 0).wait()
    store(3 * steps - 1, 0, 0).wait()


def feed_forward(x_own, c_all, w, hidden, count):
    rows, width = x_own.shape
    group = rows * count
    assert count == 4 and width % 4 == 0 and rows % 64 == 0
    anywhere = pl.BlockSpec(memory_space=pl.ANY)
    vmem = pl.BlockSpec(memory_space=pltpu.VMEM)
    dma = pltpu.SemaphoreType.DMA
    return pl.pallas_call(
        functools.partial(ffn_kernel, count),
        out_shape=(
            jax.ShapeDtypeStruct((rows, width), F32),
            jax.ShapeDtypeStruct((count, rows, width), BF16),
            jax.ShapeDtypeStruct(w.shape, BF16),
        ),
        in_specs=[anywhere] * 3,
        out_specs=(vmem, vmem, anywhere),
        scratch_shapes=[
            pltpu.VMEM((width, 3 * hidden), BF16),
            pltpu.VMEM((group, width), BF16),
            pltpu.VMEM((group, width), BF16),
            pltpu.VMEM((group, 3 * hidden), BF16),
            pltpu.VMEM((3, rows, hidden), F32),
            pltpu.VMEM((group, width), BF16),
            pltpu.VMEM((group + rows, width), BF16),
            pltpu.VMEM((width, group), BF16),
            pltpu.VMEM((width, group), BF16),
            pltpu.VMEM((2, width // 4, hidden), BF16),
            dma((3,)), dma((2,)), dma((count + 1, 1)), dma((count, 1)),
            dma((count, 4)), dma((count + 1, 4)), dma((2,)),
        ],
        compiler_params=pltpu.CompilerParams(
            collective_id=0, has_side_effects=True, vmem_limit_bytes=60 << 20
        ),
        cost_estimate=cost(100),
        name="feed_forward",
    )(x_own, c_all, w)


def back_kernel(keep, gated_own, og, o_in, qkv, decay, logits, through, pair_through, gain,
                kept_in, parts_in,
                g_proj, g_logits, g_gain, f_out,
                gated_all, go, runs, g_queried, g_keyed, g_values, pulls, weights, kept,
                parts, landed, state, sending, got, scanned, after, mate_out, mate_in,
                back_out, back_in, second_state, m_sem, in_sem, z_send, z_recv, s_send, s_recv, b_send, b_recv, p_sem, q_sem):
    h, head = lax.axis_index("head"), lax.axis_size("head")
    count, micro, rows, dk = decay.shape
    dv = og.shape[-1]
    width = qkv.shape[-1]
    slices, part = sending.shape[0], sending.shape[2]
    scale = dk ** (-0.5)
    loads = [
        pltpu.make_async_copy(parts_in, parts, in_sem.at[0]),
        pltpu.make_async_copy(kept_in, kept, in_sem.at[1]),
    ]
    for load in loads:
        load.start()
    greet(("seq", "head"))

    def to_head(hop, slot):
        to = lax.rem(h + hop, head)
        columns = gated_own.at[:, pl.ds(pl.multiple_of(to * dv, dv), dv)]
        return push(columns, gated_all.at[slot], z_send.at[hop], z_recv.at[slot], to)

    for hop in range(1, head):
        to_head(hop, h).start()
    gated_all[h] = gated_own[:, pl.ds(pl.multiple_of(h * dv, dv), dv)]

    causal = lower_ones(rows)
    before = [jnp.zeros((1, dk), F32)] * micro
    alive = [jnp.ones((1, dk), F32)] * micro
    for b in range(count):
        for m in range(micro):
            run = running(decay[b, m])
            runs[b, m] = run
            alive[m] = alive[m] * keep[b, m]
            weights[b, m] = jnp.exp(before[m]) * alive[m]
            before[m] = before[m] + run[rows - 1 : rows, :]
    g_gain[...] = jnp.zeros_like(g_gain)
    state[...] = jnp.zeros_like(state)

    def gates(i, _):
        b = near_order(h, head, i)
        pl.when(i > 0)(lambda: to_head(lax.rem(b - h + head, head), b).wait_recv())
        for m in range(micro):
            gate, o = og[b, m], o_in[b, m]
            grad = gated_all[b, m * rows : (m + 1) * rows, :].astype(F32)
            sig = sigmoid(gate)
            inv = lax.rsqrt(jnp.mean(o * o, axis=-1, keepdims=True) + 1e-5)
            plain = o * inv
            normed = (plain * gain[...]).astype(BF16).astype(F32)
            g_on = (grad * gate * sig).astype(BF16).astype(F32)
            g_proj[b, m, :, width:] = (
                grad * normed * sig * (1.0 + gate * (1.0 - sig))
            ).astype(BF16)
            scaled = g_on * gain[...]
            g_o = inv * (scaled - plain * jnp.mean(scaled * plain, axis=-1, keepdims=True))
            go[b, m] = g_o
            g_gain[0:1, :] += jnp.sum(g_on * plain, axis=0, keepdims=True)
            queried = qkv[b, m, :, :dk].astype(F32) * (jnp.exp(runs[b, m]) * scale)
            pull = mms(split(g_o), split(queried), (0, 0))
            pulls[b, m] = pull
            state[m] += pull * weights[b, m]
        return 0

    lax.fori_loop(0, head, gates, 0)
    loads[0].wait()
    total = LineSum(parts, landed, p_sem, q_sem, f_out.shape[0])
    total.send_all()
    half = dv // 2
    side = lax.rem(lax.axis_index("seq"), 2)
    own_half = pl.ds(pl.multiple_of(side * half, half), half)
    mate_half = pl.ds(pl.multiple_of((1 - side) * half, half), half)
    mate_out[...] = state[:, mate_half, :].astype(BF16)
    swap = to_mate(mate_out, mate_in, m_sem.at[0], m_sem.at[1])
    swap.start()
    swap.wait_recv()
    passes = pair_through[:, :, 0:1, :].astype(F32) + pair_through[:, :, 1:2, :].astype(F32)
    for m in range(micro):
        start, later_state = sided(state[m, own_half, :], mate_in[m].astype(F32))
        second_state[m] = later_state
        pair = passes[0, m] * later_state + start
        for i in range(slices):
            sending[i, m] = pair[i * part : (i + 1) * part, :].astype(BF16)
    begin, end, drain = swap_slices(sending, got, s_send, s_recv)
    begin()
    loads[1].wait()

    def inside(b, _):
        for m in range(micro):
            q = qkv[b, m, :, :dk].astype(F32)
            k = qkv[b, m, :, dk : 2 * dk].astype(F32)
            v = (qkv[b, m, :, 2 * dk :],)
            run = runs[b, m]
            queried, keyed = split(q * (jnp.exp(run) * scale)), split(k * jnp.exp(-run))
            g_o, entry = split(go[b, m]), split(kept[b, m])
            scores = split(jnp.where(causal, mms(queried, keyed, (1, 1)), 0.0))
            g_scores = split(jnp.where(causal, mms(g_o, v, (1, 1)), 0.0))
            g_queried[b, m] = mms(g_scores, keyed, (1, 0)) + mms(g_o, entry, (1, 0))
            g_keyed[b, m] = mms(g_scores, queried, (0, 0))
            g_values[b, m] = mms(scores, g_o, (0, 0))
        pl.when(total.inner)(lambda: total.relay(total.far_end, b))
        return 0

    lax.fori_loop(0, count, inside, 0)
    end()
    scan_states(True, got, through, scanned)
    begin_back, end_back, drain_back = swap_slices(scanned, after, b_send, b_recv)
    begin_back()

    @pl.when(total.inner)
    def _():
        for p in range(total.pieces):
            total.relay(head - 1 - total.far_end, p)
        for p in range(total.pieces):
            total.relay(head - 1 - h, p)

    end_back()
    for m in range(micro):
        leave = after[:, m].astype(F32).reshape(half, dk)
        firsts = passes[1, m] * leave + second_state[m]
        own, _ = sided(firsts, leave)
        mate, _ = sided(leave, firsts)
        state[m, own_half, :] = own
        back_out[m] = mate.astype(BF16)
    swap_back = to_mate(back_out, back_in, m_sem.at[2], m_sem.at[3])
    swap_back.start()
    swap_back.wait_recv()
    for m in range(micro):
        state[m, mate_half, :] = back_in[m].astype(F32)

    def across(step, _):
        b = count - 1 - step
        for m in range(micro):
            q = qkv[b, m, :, :dk].astype(F32)
            k = qkv[b, m, :, dk : 2 * dk].astype(F32)
            v = (qkv[b, m, :, 2 * dk :],)
            run = runs[b, m]
            last = run[rows - 1 : rows, :]
            up, down, rest = jnp.exp(run) * scale, jnp.exp(-run), jnp.exp(last - run)
            decayed = jnp.exp(last)
            gs = state[m]
            gs_parts = split(gs)
            carried = k * rest
            g_v = g_values[b, m] + mms(split(carried), gs_parts, (1, 1))
            g_carried = mms(v, gs_parts, (1, 0))
            from_carried = g_carried * carried
            g_total = jnp.sum(decayed * kept[b, m] * gs, axis=0, keepdims=True) + jnp.sum(
                from_carried, axis=0, keepdims=True
            )
            state[m] = (decayed * gs + pulls[b, m]) * keep[b, m]
            gq, gk = g_queried[b, m], g_keyed[b, m]
            g_run = gq * (q * up) - gk * (k * down) - from_carried
            later = mms((causal.astype(F32).astype(BF16),), split(g_run), (0, 0)) + g_total
            g_proj[b, m, :, :dk] = (gq * up).astype(BF16)
            g_proj[b, m, :, dk : 2 * dk] = (gk * down + g_carried * rest).astype(BF16)
            g_proj[b, m, :, 2 * dk : width] = g_v.astype(BF16)
            g_logits[b, m] = (
                later.astype(BF16).astype(F32) * sigmoid(-logits[b, m]) * (1.0 / GATE_NORM)
            )
        return 0

    lax.fori_loop(0, count, across, 0)
    total.result(f_out)
    total.finish()
    drain()
    drain_back()
    swap.wait_send()
    swap_back.wait_send()
    for hop in range(1, head):
        to_head(hop, h).wait_send()


def attention_back(
    keep, gated_own, og, o, qkv, decays, logits, through, pair_through, gain, kept, parts
):
    blocks, micro, rows, width = qkv.shape
    dk, dv = decays.shape[-1], og.shape[-1]
    head, seq = lax.axis_size("head"), lax.axis_size("seq")
    own_rows = parts.shape[0] // head
    vmem, anywhere = pl.BlockSpec(memory_space=pltpu.VMEM), pl.BlockSpec(memory_space=pl.ANY)
    dma = pltpu.SemaphoreType.DMA
    blocked = lambda w, kind: pltpu.VMEM((blocks, micro, rows, w), kind)
    pairs, half = seq // 2, dv // 2
    states = (pairs, micro, half // pairs, dk)
    halves = (micro, half, dk)
    return pl.pallas_call(
        back_kernel,
        out_shape=(
            jax.ShapeDtypeStruct((blocks, micro, rows, width + dv), BF16),
            jax.ShapeDtypeStruct((blocks, micro, rows, dk), F32),
            jax.ShapeDtypeStruct((8, dv), F32),
            jax.ShapeDtypeStruct((own_rows, parts.shape[1]), F32),
        ),
        in_specs=[vmem] * 10 + [anywhere] * 2,
        out_specs=(vmem,) * 4,
        scratch_shapes=[
            pltpu.VMEM((blocks, micro * rows, dv), BF16), blocked(dv, F32), blocked(dk, F32),
            blocked(dk, F32), blocked(dk, F32), blocked(dv, F32),
            pltpu.VMEM((blocks, micro, dv, dk), F32), pltpu.VMEM((blocks, micro, 1, dk), F32),
            pltpu.VMEM((blocks, micro, dv, dk), F32),
            pltpu.VMEM(parts.shape, BF16),
            pltpu.VMEM((parts.shape[0] + own_rows, parts.shape[1]), BF16),
            pltpu.VMEM((micro, dv, dk), F32),
            pltpu.VMEM(states, BF16), pltpu.VMEM(states, BF16), pltpu.VMEM(states, BF16),
            pltpu.VMEM(states, BF16), pltpu.VMEM(halves, BF16), pltpu.VMEM(halves, BF16),
            pltpu.VMEM(halves, BF16), pltpu.VMEM(halves, BF16), pltpu.VMEM(halves, F32), dma((4,)),
            dma((2,)), dma((head,)), dma((head,)), dma((pairs,)), dma((pairs,)), dma((pairs,)),
            dma((pairs,)), dma((head, 4)), dma((head + 1, 4)),
        ],
        compiler_params=pltpu.CompilerParams(
            collective_id=3, has_side_effects=True, vmem_limit_bytes=60 << 20
        ),
        cost_estimate=cost(80),
        name="attention_back",
    )(keep, gated_own, og, o, qkv, decays, logits, through, pair_through, gain, kept,
      parts)


def finish_kernel(xn_in, proj_in, w_in, g_logits, ranked, up_own, rank_down, source,
                  gain, g_ffn, g_head,
                  g_x, grad, norm_sum, ffn_sum, head_sum, bias_sum, up_sum, down_sum,
                  turned, proj, w, outgoing, mine, paired, inbox, heads_in, parts, landed,
                  slim_high, slim_low, small, small_in, small_part,
                  small_heads, small_all, rows_sum, in_sem, pair_send, pair_recv, send, recv, x_send, x_recv,
                  p_sem, q_sem, a_send, a_recv, b_send, b_recv, c_send, c_recv):
    h, head = lax.axis_index("head"), lax.axis_size("head")
    rows, width = g_x.shape
    deep = grad.shape[0] * head
    pairs = lax.axis_size("seq") // 2

    loads = [
        pltpu.make_async_copy(proj_in, proj, in_sem.at[0]),
        pltpu.make_async_copy(w_in, w, in_sem.at[1]),
        pltpu.make_async_copy(xn_in, landed.at[pl.ds(0, xn_in.shape[0])], in_sem.at[2]),
    ]
    for load in loads:
        load.start()
    sums = PairSum(mine, paired, inbox, pair_send, pair_recv, send, recv)
    for load in loads:
        load.wait()
    turned[...] = landed[: xn_in.shape[0], :].T
    greet(("seq", "head"))
    total = LineSum(parts, landed, p_sem, q_sem, rows)
    logit_parts = split(g_logits[...])
    g_ranked = mms(logit_parts, split(up_own[...]), (1, 1))
    slim = split(g_ranked)
    slim_high[...], slim_low[...] = slim

    def chunk(i, _):
        b = near_order(h, head, head - 1 - i)
        at = pl.ds(pl.multiple_of(b * rows, rows), rows)
        rank_part = mms((slim_high[at, :], slim_low[at, :]), (rank_down[...],), (1, 1))
        parts[at, :] = (mm(proj[at, :], w[...], (1, 1), None) + rank_part).astype(BF16)

        @pl.when((b != h) & jnp.logical_not(total.inner))
        def _():
            for p in range(total.pieces):
                total.onward(b, p).start()

        return 0

    lax.fori_loop(0, head, chunk, 0)

    def gone(k, _):
        outgoing[k] = jnp.dot(
            turned[sums.block(k, True), :], proj[...], preferred_element_type=F32
        ).astype(BF16)
        sums.to_partner(outgoing.at[k], k).start()
        return 0

    lax.fori_loop(0, pairs, gone, 0)

    def kept(k, _):
        here = jnp.dot(turned[sums.block(k), :], proj[...], preferred_element_type=F32)
        sums.to_partner(outgoing.at[k], k).wait_recv()
        mine[k] = (here + paired[k].astype(F32)).astype(BF16)
        sums.pass_on(k)

        @pl.when(total.inner & (k < total.pieces))
        def _():
            total.relay(total.far_end, k)

        @pl.when(total.inner & (k > 0) & (k <= total.pieces))
        def _():
            total.relay(head - 1 - total.far_end, k - 1)

        return 0

    lax.fori_loop(0, pairs, kept, 0)

    @pl.when(total.inner)
    def _():
        for p in range(pairs, total.pieces + 1):
            if p < total.pieces:
                total.relay(total.far_end, p)
            total.relay(head - 1 - total.far_end, p - 1)
        for p in range(total.pieces):
            total.relay(head - 1 - h, p)

    thin = grad.shape[0]

    def to_head(hop, slot):
        to = lax.rem(h + hop, head)
        at = pl.ds(pl.multiple_of(to * thin, thin), thin)
        return push(mine.at[sums.own, at, :], heads_in.at[slot], x_send.at[hop], x_recv.at[slot], to)

    sums.advance(0)

    total.result(g_x)
    rows_sum[...] = jnp.zeros_like(rows_sum)
    band = rows_sum.shape[0]

    def norm_rows(r, _):
        at = pl.ds(pl.multiple_of(r * band, band), band)
        x = source[at, :].astype(F32)
        inv = lax.rsqrt(jnp.mean(x * x, axis=-1, keepdims=True) + 1e-6)
        plain, g = x * inv, g_x[at, :]
        scaled = g * gain[...]
        inner = jnp.mean(scaled * plain, axis=-1, keepdims=True)
        rows_sum[...] += g * plain
        g_x[at, :] = inv * (scaled - plain * inner)
        return 0

    lax.fori_loop(0, rows // band, norm_rows, 0)
    rank, dk = up_own.shape
    low, keys = rank // 2, up_sum.shape[1]
    g_down = mms(slim, (turned[...],), (0, 1))
    g_up = mms(split(ranked[...]), logit_parts, (0, 0))
    small[...] = jnp.zeros_like(small)
    small[:low, :width] = g_down[:low]
    small[:low, width:] = g_down[low:]
    own_keys = pl.multiple_of(h * dk, dk)
    small[low:, pl.ds(own_keys, dk)] = g_up[:low]
    small[low:, pl.ds(keys + own_keys, dk)] = g_up[low:]
    small[low : low + 1, width:] = jnp.sum(rows_sum[...], axis=0, keepdims=True)
    small[low + 1 : low + 2, width:] = g_ffn[...]
    small[low + 2 : low + 3, width : width + g_head.shape[1]] = g_head[0:1, :]
    small[low + 3 : low + 4, pl.ds(width + own_keys, dk)] = jnp.sum(
        g_logits[...], axis=0, keepdims=True
    )
    s, seq = lax.axis_index("seq"), lax.axis_size("seq")
    wide = small.shape[1] // seq

    def piece(ref, i):
        return ref.at[:, pl.ds(pl.multiple_of(i * wide, wide), wide)]

    def begin_small(axis, me, count, copy):
        for hop in range(1, count):
            copy(hop, me, lax.rem(me + hop, count)).start()

    def end_small(axis, me, count, copy):
        for hop in range(1, count):
            other = lax.rem(me + hop, count)
            copy(hop, other, other).wait_recv()

    def scatter(hop, slot, to):
        return push(
            piece(small, to), small_in.at[slot], a_send.at[hop], a_recv.at[slot], to, "seq"
        )

    def between(hop, slot, to):
        return push(small_part, small_heads.at[slot], b_send.at[hop], b_recv.at[slot], to)

    def spread(hop, slot, to):
        return push(
            small_part, piece(small_all, slot), c_send.at[hop], c_recv.at[slot], to, "seq"
        )

    begin_small("seq", s, seq, scatter)
    small_in[s] = small[:, pl.ds(pl.multiple_of(s * wide, wide), wide)]
    for step in range(1, sums.levels):
        sums.advance(step)
    for hop in range(1, head):
        to_head(hop, h).start()
    own_rows = pl.ds(pl.multiple_of(h * thin, thin), thin)
    heads_in[h] = mine[sums.own, own_rows, :]
    end_small("seq", s, seq, scatter)
    small_part[...] = jnp.sum(small_in[...], axis=0)
    begin_small("head", h, head, between)
    small_heads[h] = small_part[...]
    end_small("head", h, head, between)
    for hop in range(1, head):
        between(hop, h, lax.rem(h + hop, head)).wait_send()
    small_part[...] = jnp.sum(small_heads[...], axis=0)
    begin_small("seq", s, seq, spread)
    small_all[:, pl.ds(pl.multiple_of(s * wide, wide), wide)] = small_part[...]
    for hop in range(1, head):
        to_head(hop, lax.rem(h + hop, head)).wait_recv()
    dv = mine.shape[2] // 2 - dk
    for j in range(head):
        at, start = 0, 0
        for size in (dk, dk, dv, dv):
            grad[:, start + j * size : start + (j + 1) * size] = heads_in[j, :, at : at + size]
            at, start = at + size, start + head * size
    end_small("seq", s, seq, spread)
    down_sum[:low, :] = small_all[:low, :width]
    down_sum[low:, :] = small_all[:low, width:]
    up_sum[:low, :] = small_all[low:, :keys]
    up_sum[low:, :] = small_all[low:, keys : 2 * keys]
    norm_sum[...] = small_all[low : low + 1, width:]
    ffn_sum[...] = small_all[low + 1 : low + 2, width:]
    head_sum[...] = small_all[low + 2 : low + 3, width : width + head_sum.shape[1]]
    bias_sum[...] = small_all[low + 3 : low + 4, width : width + keys]
    for hop in range(1, seq):
        scatter(hop, s, lax.rem(s + hop, seq)).wait_send()
        spread(hop, s, lax.rem(s + hop, seq)).wait_send()
    sums.finish(lambda k: outgoing.at[k])
    for hop in range(1, head):
        to_head(hop, h).wait_send()
    total.finish()


def finish(
    xn, g_proj, w_in, g_logits, ranked, up_own, rank_down, source, gain, g_ffn, g_head
):
    seq, head = lax.axis_size("seq"), lax.axis_size("head")
    group, width = xn.shape
    columns, rank = w_in.shape[1], ranked.shape[1]
    deep, rows, pairs = width // seq, group // head, seq // 2
    dk = up_own.shape[1]
    vmem, anywhere = pl.BlockSpec(memory_space=pltpu.VMEM), pl.BlockSpec(memory_space=pl.ANY)
    dma = pltpu.SemaphoreType.DMA
    blocks = lambda count, w: pltpu.VMEM((count, deep, w), BF16)
    ends = lambda w: pltpu.VMEM((head, deep // head, w), BF16)
    moves = dma((2, pairs - 1))
    return pl.pallas_call(
        finish_kernel,
        out_shape=(
            jax.ShapeDtypeStruct((rows, width), F32),
            jax.ShapeDtypeStruct((deep // head, columns * head), BF16),
            jax.ShapeDtypeStruct((1, width), F32),
            jax.ShapeDtypeStruct((1, width), F32),
            jax.ShapeDtypeStruct((1, g_head.shape[1]), F32),
            jax.ShapeDtypeStruct((1, dk * head), F32),
            jax.ShapeDtypeStruct((rank, dk * head), F32),
            jax.ShapeDtypeStruct((rank, width), F32),
        ),
        in_specs=[anywhere] * 3 + [vmem] * 8,
        out_specs=(vmem,) * 8,
        scratch_shapes=[
            pltpu.VMEM((width, group), BF16), pltpu.VMEM(g_proj.shape, BF16),
            pltpu.VMEM(w_in.shape, BF16), blocks(pairs, columns), blocks(pairs, columns),
            blocks(pairs, columns), blocks(pairs - 1, columns), ends(columns),
            pltpu.VMEM((group, width), BF16), pltpu.VMEM((group + rows, width), BF16),
            pltpu.VMEM(ranked.shape, BF16), pltpu.VMEM(ranked.shape, BF16),
            pltpu.VMEM((rank, 2 * width), F32), pltpu.VMEM((seq, rank, 2 * width // seq), F32),
            pltpu.VMEM((rank, 2 * width // seq), F32),
            pltpu.VMEM((head, rank, 2 * width // seq), F32),
            pltpu.VMEM((rank, 2 * width), F32), pltpu.VMEM((16, width), F32),
            dma((3,)), dma((pairs,)), dma((pairs,)), moves, moves, dma((head,)), dma((head,)),
            dma((head, 4)), dma((head + 1, 4)),
            dma((seq,)), dma((seq,)), dma((head,)), dma((head,)), dma((seq,)), dma((seq,)),
        ],
        compiler_params=pltpu.CompilerParams(
            collective_id=5, has_side_effects=True, vmem_limit_bytes=60 << 20
        ),
        cost_estimate=cost(95),
        name="finish",
    )(xn, g_proj, w_in, g_logits, ranked, up_own, rank_down, source, gain, g_ffn, g_head)


def weight_grad_kernel(left, right, *rest):
    out, turned = rest[-2:]

    @pl.when(pl.program_id(1) == 0)
    def _():
        turned[...] = left[...].T

    out[...] = jnp.dot(turned[...], right[...], preferred_element_type=F32).astype(BF16)


def weight_grad(left, right, into, columns, start, tile):
    depth, rows = left.shape
    high = min(rows, 512)
    first = start // tile
    given = () if into is None else (into,)
    return pl.pallas_call(
        weight_grad_kernel,
        out_shape=jax.ShapeDtypeStruct((rows, columns), BF16),
        grid=(rows // high, right.shape[1] // tile),
        in_specs=[
            pl.BlockSpec((depth, high), lambda i, j: (0, i)),
            pl.BlockSpec((depth, tile), lambda i, j: (0, j)),
        ]
        + [pl.BlockSpec(memory_space=pl.ANY) for _ in given],
        out_specs=pl.BlockSpec((high, tile), lambda i, j: (i, first + j)),
        scratch_shapes=[pltpu.VMEM((high, depth), BF16)],
        input_output_aliases={2: 0} if given else {},
        compiler_params=pltpu.CompilerParams(
            dimension_semantics=("arbitrary", "arbitrary"), vmem_limit_bytes=48 << 20
        ),
        cost_estimate=pl.CostEstimate(
            flops=2 * depth * rows * right.shape[1],
            bytes_accessed=2 * (depth * rows + (depth + rows) * right.shape[1]),
            transcendentals=0,
        ),
        name="weight_grad",
    )(left, right, *given)


def product_kernel(left, right, out):
    out[...] = jnp.dot(left[...], right[...], preferred_element_type=F32).astype(BF16)


def rows_by_columns(left, right, columns):
    rows, depth = left.shape
    tile = 512
    return pl.pallas_call(
        product_kernel,
        out_shape=jax.ShapeDtypeStruct((rows, columns), BF16),
        grid=(columns // tile,),
        in_specs=[
            pl.BlockSpec((rows, depth), lambda j: (0, 0)),
            pl.BlockSpec((depth, tile), lambda j: (0, j)),
        ],
        out_specs=pl.BlockSpec((rows, tile), lambda j: (0, j)),
        compiler_params=pltpu.CompilerParams(
            dimension_semantics=("arbitrary",), vmem_limit_bytes=32 << 20
        ),
        cost_estimate=cost(5),
        name="product",
    )(left, right)


def gather_weight(w):
    return lax.all_gather(w, "seq", axis=0, tiled=True)


def scatter_grad(g):
    return lax.psum_scatter(g.astype(BF16), "seq", scatter_dimension=0, tiled=True)


def dot(a, b, contract, precision=None):
    return lax.dot_general(
        a, b, (((contract[0],), (contract[1],)), ((), ())),
        precision=precision, preferred_element_type=F32,
    )


def rms(x, epsilon):
    return lax.rsqrt(jnp.mean(x * x, axis=-1, keepdims=True) + epsilon)


def norm_back(grad, gain, normed, inv):
    scaled = grad * gain
    inner = jnp.mean(scaled * normed, axis=-1, keepdims=True)
    return inv * (scaled - normed * inner), jnp.sum(grad * normed, axis=0)


def on_device(
    tokens, starts, cotangent, mix_in, mix_out, gate_up, down_proj,
    norm_gain, ffn_gain, head_gain, rank_down, rank_up, gate_bias,
):
    micro, rows, width = tokens.shape
    heads, seq = lax.axis_size("head"), lax.axis_size("seq")
    head = lax.axis_index("head")
    keys, dv = rank_up.shape[1], head_gain.shape[0]
    dk, vals = keys // heads, dv * heads
    hidden_units = down_proj.shape[1]
    group = heads * micro * rows
    proj_width = 2 * dk + 2 * dv

    def own_columns(w, start, size):
        return lax.dynamic_slice_in_dim(w, start + head * size, size, 1)

    w_in_own = jnp.concatenate(
        [
            own_columns(mix_in, 0, dk),
            own_columns(mix_in, keys, dk),
            own_columns(mix_in, 2 * keys, dv),
            own_columns(mix_in, 2 * keys + vals, dv),
        ],
        axis=1,
    )
    later = gather_weight(
        jnp.concatenate(
            [mix_out, gate_up.reshape(gate_up.shape[0], 2 * hidden_units), down_proj], axis=1
        )
    )
    w_out = later[:, :vals]
    up_own = own_columns(rank_up, 0, dk)
    bias_own = lax.dynamic_slice_in_dim(gate_bias, head * dk, dk, 0)

    xn, w_in = gather_norm(
        tokens.reshape(micro * rows, width), norm_gain.reshape(1, width), w_in_own
    )
    qkv = dot(xn, w_in[:, : 2 * dk + dv], (1, 0)).astype(BF16)
    og = dot(xn, w_in[:, 2 * dk + dv :], (1, 0))
    ranked = dot(xn, rank_down, (1, 0))
    logits = dot(ranked, up_own, (1, 0), HIGHEST) + bias_own
    decays = (jax.nn.log_sigmoid(logits) / GATE_NORM).astype(BF16)

    def blocks(x):
        return x.reshape(heads, micro, rows, x.shape[-1])

    qkv_b, og_b, decays_b = blocks(qkv), blocks(og), blocks(decays)
    gain_row = head_gain.reshape(1, dv)
    keep = 1.0 - jnp.broadcast_to(starts.T[:, :, None, None], (heads, micro, 1, dk)).astype(F32)
    o_b, gated, through, pair_through, kept, all_cot = attention_forward(
        keep, qkv_b, decays_b, og_b, gain_row, cotangent.reshape(micro * rows, width)
    )

    source = tokens.astype(F32).reshape(micro * rows, width)
    hidden = source + dot(gated, w_out, (1, 1))
    inv_ffn = rms(hidden, 1e-6)
    plain_ffn = hidden * inv_ffn
    h2 = (plain_ffn * ffn_gain).astype(BF16)

    g_h2, ffn_part, grads = feed_forward(h2, all_cot, later, hidden_units, heads)

    back_ffn, g_ffn_gain = norm_back(g_h2, ffn_gain, plain_ffn, inv_ffn)
    g_hidden = cotangent.astype(F32).reshape(micro * rows, width) + back_ffn
    g_mixed = g_hidden.astype(BF16)
    grads = scatter_grad(weight_grad(g_mixed, gated, grads, later.shape[1], 0, vals))
    g_gated = rows_by_columns(g_mixed, later, vals)
    g_proj_b, g_logits_b, g_head_gain, ffn_out = attention_back(
        keep, g_gated, og_b, o_b, qkv_b, decays_b, blocks(logits), through, pair_through, gain_row, kept, ffn_part.reshape(group, width),
    )
    output = (hidden + ffn_out).astype(BF16)
    g_proj, g_logits = g_proj_b.reshape(group, proj_width), g_logits_b.reshape(group, dk)
    back_in, grad_in, *small, g_rank_down = finish(
        xn, g_proj, w_in, g_logits, ranked, up_own, rank_down, tokens.reshape(micro * rows, width),
        norm_gain.reshape(1, width), g_ffn_gain.reshape(1, width), g_head_gain,
    )
    g_norm_gain, g_ffn_gain, g_head_gain, g_bias, g_rank_up = small
    input_grad = g_hidden + back_in
    slab = width // (seq * heads)
    grad_in, grads = lax.optimization_barrier((grad_in, grads))
    grad_ffn = grads[:, vals:]
    grad_out = lax.all_to_all(
        grads[:, :vals].reshape(heads, slab, vals), "head", split_axis=0, concat_axis=0, tiled=True
    )
    grad_out = grad_out.astype(F32).sum(0)
    return (
        output.reshape(tokens.shape),
        input_grad.reshape(tokens.shape),
        grad_in.astype(F32),
        grad_out,
        grad_ffn[:, : 2 * hidden_units].astype(F32).reshape(-1, 2, hidden_units),
        grad_ffn[:, 2 * hidden_units :].astype(F32),
        g_norm_gain.reshape(norm_gain.shape),
        g_ffn_gain.reshape(ffn_gain.shape),
        g_head_gain.reshape(head_gain.shape),
        g_rank_down.T,
        g_rank_up,
        g_bias.reshape(gate_bias.shape),
    )


def solution(mesh):
    rows = P(None, ("seq", "head"), None)
    return jax.shard_map(
        on_device,
        mesh=mesh,
        in_specs=(
            rows, P(None, "seq"), rows, P("seq", None), P("seq", None),
            P("seq", None, "head"), P("seq", "head"), P(), P(), P(), P(), P(), P(),
        ),
        out_specs=(
            rows, rows, P(("seq", "head"), None), P(("seq", "head"), None),
            P("seq", None, "head"), P("seq", "head"), P(), P(), P(), P(), P(), P(),
        ),
        check_vma=False,
    )
```

```python
import functools

import jax
import jax.numpy as jnp
from jax import lax
from jax.experimental import pallas as pl
from jax.experimental.pallas import tpu as pltpu
from jax.sharding import PartitionSpec as P

HIGHEST = lax.Precision.HIGHEST
GATE_NORM = 16.0
BF16 = jnp.bfloat16
F32 = jnp.float32


def mm(a, b, contract, precision=HIGHEST):
    return lax.dot_general(
        a, b, ((contract[:1], contract[1:]), ((), ())),
        precision=precision, preferred_element_type=F32,
    )


def split(x):
    high = x.astype(BF16)
    return high, (x - high.astype(F32)).astype(BF16)


def mms(left, right, contract):
    total = mm(left[0], right[0], contract, None)
    if len(right) > 1:
        total += mm(left[0], right[1], contract, None)
    if len(left) > 1:
        total += mm(left[1], right[0], contract, None)
    return total


def lower_ones(size):
    rows = lax.broadcasted_iota(jnp.int32, (size, size), 0)
    cols = lax.broadcasted_iota(jnp.int32, (size, size), 1)
    return rows >= cols


def running(decay_low):
    ones = lower_ones(decay_low.shape[0]).astype(F32).astype(BF16)
    return mm(ones, decay_low, (1, 0), None)


def sigmoid(x):
    return 1.0 / (1.0 + jnp.exp(-x))


def cost(micros):
    return pl.CostEstimate(flops=0, bytes_accessed=int(micros * 3.0e6), transcendentals=0)


def greet(axes):
    barrier = pltpu.get_barrier_semaphore()
    met = 0
    for axis in axes:
        me, count = lax.axis_index(axis), lax.axis_size(axis)
        for hop in range(1, count):
            pl.semaphore_signal(
                barrier, inc=1, device_id={axis: lax.rem(me + hop, count)},
                device_id_type=pl.DeviceIdType.MESH,
            )
        met += count - 1
    pl.semaphore_wait(barrier, met)


def push(src, dst, send, recv, to, axis="head"):
    return pltpu.make_async_remote_copy(
        src_ref=src, dst_ref=dst, send_sem=send, recv_sem=recv,
        device_id={axis: to}, device_id_type=pl.DeviceIdType.MESH,
    )


def near_order(z, count, i):
    both = jnp.minimum(z, count - 1 - z)
    left = z > count - 1 - z
    paired = jnp.where(i % 2 == 1, z - (i + 1) // 2, z + i // 2)
    single = jnp.where(left, z - (i - both), z + (i - both))
    return jnp.where(i <= 2 * both, paired, single)


class Line:
    def __init__(self, own, all_rows, send, recv):
        self.own, self.all, self.send, self.recv = own, all_rows, send, recv
        self.z, self.count = lax.axis_index("head"), lax.axis_size("head")
        self.rows, self.parts = own.shape[0], recv.shape[1]
        self.deep = self.rows // self.parts

    def at(self, b):
        return self.all.at[pl.ds(pl.multiple_of(b * self.rows, self.rows), self.rows)]

    def part(self, b, p):
        start = b * self.rows + p * self.deep
        return self.all.at[pl.ds(pl.multiple_of(start, self.deep), self.deep)]

    def first(self, way, p):
        to = lax.rem(self.z + (1 if way == 0 else self.count - 1), self.count)
        src = self.own.at[pl.ds(p * self.deep, self.deep)]
        return push(
            src, self.part(self.z, p), self.send.at[way, p], self.recv.at[self.z, p], to
        )

    def each_first(self, act):
        for p in range(self.parts):
            pl.when(self.z < self.count - 1)(lambda p=p: act(self.first(0, p)))
            pl.when(self.z > 0)(lambda p=p: act(self.first(1, p)))

    def start(self):
        self.each_first(lambda copy: copy.start())

    def passing(self, i, b, p):
        z, count = self.z, self.count
        to = jnp.where(b < z, z + 1, z - 1)
        going = ((b < z) & (z < count - 1)) | ((b > z) & (z > 0))
        copy = push(
            self.part(b, p), self.part(b, p), self.send.at[i + 1, p], self.recv.at[b, p],
            lax.rem(to + count, count),
        )
        return copy, going

    def receive(self, i, b, p=0):
        copy, going = self.passing(i, b, p)
        copy.wait_recv()
        pl.when(going)(copy.start)

    def finish(self):
        def sent(i, _):
            for p in range(self.parts):
                copy, going = self.passing(i, near_order(self.z, self.count, i), p)
                pl.when(going)(copy.wait_send)
            return 0

        lax.fori_loop(1, self.count, sent, 0)
        self.each_first(lambda copy: copy.wait_send())


class LineSum:
    def __init__(self, parts, landed, send, recv, rows):
        self.parts, self.landed, self.send, self.recv = parts, landed, send, recv
        self.z, self.count = lax.axis_index("head"), lax.axis_size("head")
        self.rows, self.pieces = rows, send.shape[1]
        self.deep = rows // self.pieces
        self.inner = (self.z > 0) & (self.z < self.count - 1)
        self.far_end = jnp.where(self.z < self.count - 1 - self.z, self.count - 1, 0)

    def piece(self, b, p):
        return pl.ds(pl.multiple_of(b * self.rows + p * self.deep, self.deep), self.deep)

    def onward(self, b, p):
        z, count = self.z, self.count
        to = jnp.where(b > z, z + 1, z - 1)
        slot = jnp.where((to == b) & (z > b), count, b)
        return push(
            self.parts.at[self.piece(b, p)], self.landed.at[self.piece(slot, p)],
            self.send.at[b, p], self.recv.at[slot, p], lax.rem(to + count, count),
        )

    def send_all(self):
        @pl.when(jnp.logical_not(self.inner))
        def _():
            for i in range(1, self.count):
                b = jnp.where(self.z == 0, self.count - i, i - 1)
                for p in range(self.pieces):
                    self.onward(b, p).start()

    def arrived(self, slot, p):
        at = self.piece(slot, p)
        push(
            self.landed.at[at], self.landed.at[at], self.send.at[0, p], self.recv.at[slot, p],
            lax.rem(self.z + 1, self.count),
        ).wait_recv()
        return self.landed[at, :].astype(F32)

    def relay(self, b, p):
        at = self.piece(b, p)
        self.parts[at, :] = (self.parts[at, :].astype(F32) + self.arrived(b, p)).astype(BF16)
        self.onward(b, p).start()

    def relay_in_turn(self, j):
        pieces = self.pieces

        @pl.when(self.inner & (j < pieces))
        def _():
            self.relay(self.count - 1 - self.z, j)

        @pl.when(self.inner & (j >= pieces))
        def _():
            self.relay(self.far_end, j - pieces)

        @pl.when(self.inner & (j > pieces))
        def _():
            self.relay(self.count - 1 - self.far_end, j - pieces - 1)

    def relay_last(self):
        @pl.when(self.inner)
        def _():
            self.relay(self.count - 1 - self.far_end, self.pieces - 1)

    def result(self, out):
        z, count = self.z, self.count
        for p in range(self.pieces):
            here = pl.ds(p * self.deep, self.deep)
            out[here, :] = self.parts[self.piece(z, p), :].astype(F32)

            @pl.when(z > 0)
            def _():
                out[here, :] += self.arrived(z, p)

            @pl.when(z < count - 1)
            def _():
                out[here, :] += self.arrived(count, p)

    def finish(self):
        def sent(i, _):
            b = near_order(self.z, self.count, i)
            for p in range(self.pieces):
                self.onward(b, p).wait_send()
            return 0

        lax.fori_loop(1, self.count, sent, 0)


class PairSum:
    def __init__(self, mine, paired, inbox, pair_send, pair_recv, send, recv):
        self.mine, self.paired, self.inbox = mine, paired, inbox
        self.pair_send, self.pair_recv, self.send, self.recv = pair_send, pair_recv, send, recv
        self.s, self.pairs = lax.axis_index("seq"), lax.axis_size("seq") // 2
        self.side, self.own = lax.rem(self.s, 2), self.s // 2
        self.deep, self.half = mine.shape[1], mine.shape[2] // 2
        self.levels = self.pairs.bit_length() - 1
        assert self.pairs == 1 << self.levels

    def block(self, k, other=False):
        i = 2 * k + (1 - self.side if other else self.side)
        return pl.ds(pl.multiple_of(i * self.deep, self.deep), self.deep)

    def to_partner(self, src, k):
        return push(
            src, self.paired.at[k], self.pair_send.at[k], self.pair_recv.at[k],
            self.s + 1 - 2 * self.side, "seq",
        )

    def bit(self, i, level):
        return lax.rem(i // (1 << level), 2)

    def move(self, side, slot, k, level):
        columns = pl.ds(side * self.half, self.half)
        to = self.s + (1 - 2 * self.bit(self.own, level)) * (2 << level)
        return push(
            self.mine.at[k, :, columns], self.inbox.at[slot, :, columns],
            self.send.at[side, slot], self.recv.at[side, slot], to, "seq",
        )

    def moves(self, side, step):
        order = list(range(self.levels))
        if side:
            order.reverse()
        level, free = order[step], sorted(order[step + 1 :])
        fixed = sum((self.bit(self.own, d) * (1 << d) for d in order[:step]), 0)
        offset = self.pairs - (1 << (self.levels - step))
        here = self.bit(self.own, level) * (1 << level)
        for c in range(1 << len(free)):
            rest = fixed + sum(((c >> j) & 1) << d for j, d in enumerate(free))
            yield offset + c, rest + here, rest + (1 << level) - here, level

    def pass_on(self, k):
        top = 1 << (self.levels - 1)
        pl.when(self.bit(k, 0) != self.bit(self.own, 0))(self.move(0, k // 2, k, 0).start)
        pl.when(k // top != self.own // top)(
            self.move(1, lax.rem(k, top), k, self.levels - 1).start
        )

    def advance(self, step):
        for side in range(2):
            columns = slice(side * self.half, (side + 1) * self.half)
            for slot, keep, gone, level in self.moves(side, step):
                self.move(side, slot, gone, level).wait_recv()
                self.mine[keep, :, columns] = (
                    self.mine[keep, :, columns].astype(F32)
                    + self.inbox[slot, :, columns].astype(F32)
                ).astype(BF16)
            if step + 1 < self.levels:
                for slot, keep, gone, level in self.moves(side, step + 1):
                    self.move(side, slot, gone, level).start()

    def finish(self, src):
        for k in range(self.pairs):
            self.to_partner(src(k), k).wait_send()
        for side in range(2):
            for step in range(self.levels):
                for slot, keep, gone, level in self.moves(side, step):
                    self.move(side, slot, gone, level).wait_send()


def gather_norm_kernel(own, gain, shard, normed, rows_of_all, rows_all, here_sem, send, recv,
                       w_sem, w_send, w_recv, w_pair, w_pair_recv):
    z, count, rows = lax.axis_index("head"), lax.axis_size("head"), own.shape[0]
    greet(("seq", "head"))
    line = Line(own, rows_all, send, recv)
    line.start()
    here = pltpu.make_async_copy(own, line.at(z), here_sem)
    here.start()

    s, deep, half = lax.axis_index("seq"), shard.shape[0], shard.shape[1] // 2
    side, pairs, own_pair = lax.rem(s, 2), lax.axis_size("seq") // 2, s // 2
    levels = pairs.bit_length() - 1
    assert pairs == 1 << levels
    orders = list(range(levels)), list(reversed(range(levels)))

    def bit(level):
        return lax.rem(own_pair // (1 << level), 2) * (1 << level)

    def block(k, of_side):
        return pl.ds(pl.multiple_of((2 * k + of_side) * deep, deep), deep)

    def across(part, step):
        level = orders[part][step]
        return own_pair + (1 << level) - 2 * bit(level)

    def known(part, step, start):
        done = orders[part][:step]
        base = start - sum((bit(d) for d in done), 0)
        for c in range(1 << step):
            yield base + sum(((c >> n) & 1) << d for n, d in enumerate(done))

    def hop(part, step, k):
        at = rows_of_all.at[block(k, side), pl.ds(part * half, half)]
        to = 2 * across(part, step) + side
        return push(at, at, w_send.at[part, step, k], w_recv.at[part, k], to, "seq")

    def begin(step):
        for part in range(2):
            for k in known(part, step, own_pair):
                hop(part, step, k).start()

    def advance(step):
        for part in range(2):
            for k in known(part, step, across(part, step)):
                hop(part, step, k).wait_recv()
        if step + 1 < levels:
            begin(step + 1)

    def to_partner(k, of_side):
        at = rows_of_all.at[block(k, of_side)]
        return push(at, at, w_pair.at[k], w_pair_recv.at[k], s + 1 - 2 * side, "seq")

    mine = pltpu.make_async_copy(shard, rows_of_all.at[block(own_pair, side)], w_sem)
    mine.start()
    mine.wait()
    begin(0)
    to_partner(own_pair, side).start()
    here.wait()
    band = 16

    def step(i, _):
        b = near_order(z, count, i)
        pl.when(i > 0)(lambda: line.receive(i, b))
        pl.when(i == 1)(lambda: advance(0))

        def norm(r, _):
            at = pl.ds(pl.multiple_of(b * rows + r * band, band), band)
            x = rows_all[at, :].astype(F32)
            inv = lax.rsqrt(jnp.mean(x * x, axis=-1, keepdims=True) + 1e-6)
            normed[at, :] = (x * inv * gain[...]).astype(BF16)
            return 0

        lax.fori_loop(0, rows // band, norm, 0)
        return 0

    lax.fori_loop(0, count, step, 0)
    for later in range(1, levels):
        advance(later)
    for k in range(pairs):
        pl.when(own_pair != k)(to_partner(k, side).start)
    for k in range(pairs):
        to_partner(k, 1 - side).wait_recv()
    for k in range(pairs):
        to_partner(k, side).wait_send()
    for part in range(2):
        for late in range(levels):
            for k in known(part, late, own_pair):
                hop(part, late, k).wait_send()
    line.finish()


def gather_norm(x, gain, shard):
    rows, width = x.shape
    seq = lax.axis_size("seq")
    anywhere = pl.BlockSpec(memory_space=pl.ANY)
    count = lax.axis_size("head")
    vmem = pl.BlockSpec(memory_space=pltpu.VMEM)
    dma = pltpu.SemaphoreType.DMA
    return pl.pallas_call(
        gather_norm_kernel,
        out_shape=(
            jax.ShapeDtypeStruct((count * rows, width), BF16),
            jax.ShapeDtypeStruct((seq * shard.shape[0], shard.shape[1]), BF16),
        ),
        in_specs=[vmem, vmem, anywhere],
        out_specs=(vmem, anywhere),
        scratch_shapes=[
            pltpu.VMEM((count * rows, width), BF16), dma(()), dma((count + 1, 1)), dma((count, 1)),
            dma(()), dma((2, (seq // 2).bit_length() - 1, seq // 2)), dma((2, seq // 2)),
            dma((seq // 2,)), dma((seq // 2,)),
        ],
        compiler_params=pltpu.CompilerParams(
            collective_id=1, has_side_effects=True, vmem_limit_bytes=32 << 20
        ),
        cost_estimate=cost(50),
        name="gather_norm",
    )(x, gain, shard)


def swap_slices(own, got, send, recv):
    side = lax.rem(lax.axis_index("seq"), 2)
    me, count = lax.axis_index("seq") // 2, lax.axis_size("seq") // 2

    def copy(hop, index):
        to = lax.rem(me + hop, count)
        return push(own.at[to], got.at[index], send.at[hop], recv.at[index], 2 * to + side, "seq")

    def start(hop, _):
        copy(hop, me).start()
        return 0

    def wait_recv(hop, _):
        copy(hop, lax.rem(me + hop, count)).wait_recv()
        return 0

    def wait_send(hop, _):
        copy(hop, me).wait_send()
        return 0

    def begin():
        lax.fori_loop(1, count, start, 0)
        got[me] = own[me]

    def end():
        lax.fori_loop(1, count, wait_recv, 0)

    def drain():
        lax.fori_loop(1, count, wait_send, 0)

    return begin, end, drain


def to_mate(src, dst, send, recv):
    s = lax.axis_index("seq")
    return push(src, dst, send, recv, s + 1 - 2 * lax.rem(s, 2), "seq")


def sided(own, mate):
    first = lax.rem(lax.axis_index("seq"), 2) == 0
    return jnp.where(first, own, mate), jnp.where(first, mate, own)


def scan_states(reverse, own, through, out):
    count, part = out.shape[0], out.shape[2]

    def step(k, state):
        j = count - 1 - k if reverse else k
        out[j] = state.astype(BF16)
        decay = through[j, :, 0:1, :].astype(F32) + through[j, :, 1:2, :].astype(F32)
        return decay * state + own[j, :, :part, :].astype(F32)

    lax.fori_loop(0, count, step, jnp.zeros(out.shape[1:], F32))


def front_kernel(keep, qkv, decay, og, gain, rows_own,
                 o_out, gated, through, pair_through, kept_out, rows_all,
                 kept, runs, state, sending, got, scanned, before, leaving, mate_out, mate_in,
                 back_out, back_in, first_state,
                 here_sem, go, come, s_send, s_recv, b_send, b_recv, z_send, z_recv, k_sem, m_sem):
    h, head = lax.axis_index("head"), lax.axis_size("head")
    count, micro, rows, dk = decay.shape
    dv = og.shape[-1]
    slices, part = scanned.shape[0], scanned.shape[2]
    scale = dk ** (-0.5)
    greet(("seq", "head"))
    line = Line(rows_own, rows_all, go, come)
    line.start()
    here = pltpu.make_async_copy(rows_own, line.at(h), here_sem)
    here.start()

    state[...] = jnp.zeros_like(state)
    passed = [jnp.zeros((1, dk), F32)] * micro
    alive = [jnp.ones((1, dk), F32)] * micro
    for b in range(count):
        for m in range(micro):
            run = running(decay[b, m])
            runs[b, m] = run
            last = run[rows - 1 : rows, :]
            carried = qkv[b, m, :, dk : 2 * dk].astype(F32) * jnp.exp(last - run)
            fresh = mms((qkv[b, m, :, 2 * dk :],), split(carried), (0, 0))
            kept[b, m] = fresh
            state[m] = jnp.exp(last) * (state[m] * keep[b, m]) + fresh
            passed[m] = passed[m] + last
            alive[m] = alive[m] * keep[b, m]
    tail = sending.shape[2] - part
    at = lax.broadcasted_iota(jnp.int32, (tail, dk), 0)
    half = dv // 2
    side = lax.rem(lax.axis_index("seq"), 2)
    own_half = pl.ds(pl.multiple_of(side * half, half), half)
    mate_half = pl.ds(pl.multiple_of((1 - side) * half, half), half)

    def as_rows(value):
        high, low = split(value)
        return jnp.where(at == 0, high.astype(F32), jnp.where(at == 1, low.astype(F32), 0.0))

    own_rows = [as_rows(jnp.exp(passed[m]) * alive[m]) for m in range(micro)]
    for m in range(micro):
        mate_out[m, :half, :] = state[m, mate_half, :].astype(BF16)
        mate_out[m, half:, :] = own_rows[m].astype(BF16)
    swap = to_mate(mate_out, mate_in, m_sem.at[0], m_sem.at[1])
    swap.start()
    swap.wait_recv()
    first_through = []
    for m in range(micro):
        firsts, seconds = sided(own_rows[m], mate_in[m, half:, :].astype(F32))
        pair_through[0, m], pair_through[1, m] = firsts.astype(BF16), seconds.astype(BF16)
        first, second = firsts[0:1] + firsts[1:2], seconds[0:1] + seconds[1:2]
        first_through.append(first)
        start, after = sided(state[m, own_half, :], mate_in[m, :half, :].astype(F32))
        first_state[m] = start
        pair = second * start + after
        both = as_rows(first * second).astype(BF16)
        for i in range(slices):
            sending[i, m, :part, :] = pair[i * part : (i + 1) * part, :].astype(BF16)
            sending[i, m, part:, :] = both
    begin, end, drain = swap_slices(sending, got, s_send, s_recv)
    begin()
    causal = lower_ones(rows)

    def inside(b, _):
        for m in range(micro):
            run = runs[b, m]
            queried = split(qkv[b, m, :, :dk].astype(F32) * (jnp.exp(run) * scale))
            keyed = split(qkv[b, m, :, dk : 2 * dk].astype(F32) * jnp.exp(-run))
            scores = jnp.where(causal, mms(queried, keyed, (1, 1)), 0.0)
            o_out[b, m] = mms(split(scores), (qkv[b, m, :, 2 * dk :],), (1, 0))
        return 0

    lax.fori_loop(0, count, inside, 0)
    line.receive(1, near_order(h, head, 1))
    end()
    through[...] = got[:, :, part:, :]
    scan_states(False, got, through, scanned)
    begin_back, end_back, drain_back = swap_slices(scanned, before, b_send, b_recv)
    begin_back()
    line.receive(2, near_order(h, head, 2))
    end_back()
    for m in range(micro):
        entry = before[:, m].astype(F32).reshape(half, dk)
        own, mate = sided(entry, first_through[m] * entry + first_state[m])
        state[m, own_half, :] = own
        back_out[m] = mate.astype(BF16)
    swap_back = to_mate(back_out, back_in, m_sem.at[2], m_sem.at[3])
    swap_back.start()
    swap_back.wait_recv()
    for m in range(micro):
        state[m, mate_half, :] = back_in[m].astype(F32)

    def to_owner(b):
        columns = gated.at[:, pl.ds(pl.multiple_of(h * dv, dv), dv)]
        return push(leaving.at[b], columns, z_send.at[b], z_recv.at[h], b)

    def save(b):
        return pltpu.make_async_copy(kept.at[b], kept_out.at[b], k_sem.at[b])

    def across(b, _):
        for m in range(micro):
            run = runs[b, m]
            queried = split(qkv[b, m, :, :dk].astype(F32) * (jnp.exp(run) * scale))
            entry = state[m] * keep[b, m]
            state[m] = jnp.exp(run[rows - 1 : rows, :]) * entry + kept[b, m]
            kept[b, m] = entry
            o = o_out[b, m] + mms(queried, split(entry), (1, 1))
            o_out[b, m] = o
            inv = lax.rsqrt(jnp.mean(o * o, axis=-1, keepdims=True) + 1e-5)
            normed = (o * inv * gain[...]).astype(BF16).astype(F32)
            gate = og[b, m]
            leaving[b, m * rows : (m + 1) * rows, :] = (normed * gate * sigmoid(gate)).astype(BF16)
        save(b).start()
        pl.when(b != h)(to_owner(b).start)

        @pl.when(b == 1)
        def _():
            line.receive(3, near_order(h, head, 3))

        return 0

    lax.fori_loop(0, count, across, 0)
    gated[:, pl.ds(pl.multiple_of(h * dv, dv), dv)] = leaving[h]
    for hop in range(1, head):
        other = lax.rem(h + hop, head)
        columns = gated.at[:, pl.ds(pl.multiple_of(other * dv, dv), dv)]
        push(leaving.at[other], columns, z_send.at[other], z_recv.at[other], other).wait_recv()
        to_owner(other).wait_send()
    for b in range(count):
        save(b).wait()
    here.wait()
    line.finish()
    drain()
    drain_back()
    swap.wait_send()
    swap_back.wait_send()


def attention_forward(keep, qkv, decays, og, gain, rows_own):
    blocks, micro, rows, width = qkv.shape
    dk, dv = decays.shape[-1], og.shape[-1]
    head, seq = lax.axis_size("head"), lax.axis_size("seq")
    assert blocks == head and head == 4
    pairs, half, tail = seq // 2, dv // 2, 16
    part = half // pairs
    own_rows = micro * rows
    vmem, anywhere = pl.BlockSpec(memory_space=pltpu.VMEM), pl.BlockSpec(memory_space=pl.ANY)
    dma = pltpu.SemaphoreType.DMA
    states, wider = (pairs, micro, part, dk), (pairs, micro, part + tail, dk)
    return pl.pallas_call(
        front_kernel,
        out_shape=(
            jax.ShapeDtypeStruct((blocks, micro, rows, dv), F32),
            jax.ShapeDtypeStruct((own_rows, head * dv), BF16),
            jax.ShapeDtypeStruct((pairs, micro, tail, dk), BF16),
            jax.ShapeDtypeStruct((2, micro, tail, dk), BF16),
            jax.ShapeDtypeStruct((blocks, micro, dv, dk), F32),
            jax.ShapeDtypeStruct((head * rows_own.shape[0], rows_own.shape[1]), BF16),
        ),
        in_specs=[vmem] * 5 + [anywhere],
        out_specs=(vmem,) * 4 + (anywhere,) * 2,
        scratch_shapes=[
            pltpu.VMEM((blocks, micro, dv, dk), F32), pltpu.VMEM((blocks, micro, rows, dk), F32),
            pltpu.VMEM((micro, dv, dk), F32), pltpu.VMEM(wider, BF16), pltpu.VMEM(wider, BF16),
            pltpu.VMEM(states, BF16), pltpu.VMEM(states, BF16),
            pltpu.VMEM((blocks, own_rows, dv), BF16),
            pltpu.VMEM((micro, half + tail, dk), BF16), pltpu.VMEM((micro, half + tail, dk), BF16),
            pltpu.VMEM((micro, half, dk), BF16), pltpu.VMEM((micro, half, dk), BF16),
            pltpu.VMEM((micro, half, dk), F32),
            dma(()), dma((head + 1, 1)), dma((head, 1)), dma((pairs,)), dma((pairs,)), dma((pairs,)),
            dma((pairs,)), dma((head,)), dma((head,)), dma((blocks,)), dma((4,)),
        ],
        compiler_params=pltpu.CompilerParams(
            collective_id=2, has_side_effects=True, vmem_limit_bytes=40 << 20
        ),
        cost_estimate=cost(90),
        name="attention_forward",
    )(keep, qkv, decays, og, gain, rows_own)


def ffn_kernel(count, x_own, c_all, w, g_x, f_parts, grad,
               wv, xs, cs, act, lin, parts, landed, turned, turned_c, tiles,
               w_sem, own_sem, go_sem, x_sem, p_sem, q_sem, o_sem):
    z = lax.axis_index("head")
    rows, width = x_own.shape
    hidden = act.shape[1] // 3
    chunk = lambda b: pl.ds(pl.multiple_of(b * rows, rows), rows)

    weights = [
        pltpu.make_async_copy(
            w.at[:, pl.ds(k * hidden, hidden)], wv.at[:, pl.ds(k * hidden, hidden)], w_sem.at[k]
        )
        for k in range(3)
    ]
    own = [
        pltpu.make_async_copy(x_own, xs.at[chunk(z)], own_sem.at[0]),
        pltpu.make_async_copy(c_all, cs, own_sem.at[1]),
    ]
    for copy in own + weights:
        copy.start()
    greet(("head",))
    line = Line(x_own, xs, go_sem, x_sem)
    line.start()
    for copy in own + weights:
        copy.wait()

    total = LineSum(parts, landed, p_sem, q_sem, rows)

    halves = x_sem.shape[1]
    deep = rows // halves
    each = total.pieces // halves

    def step(t, _):
        i, half = t // halves, lax.rem(t, halves)
        b = near_order(z, count, i)
        pl.when(i > 0)(lambda: line.receive(i, b, half))
        start = b * rows + half * deep
        at = pl.ds(pl.multiple_of(start, deep), deep)
        x = xs[at, :]
        lin[0] = jnp.dot(x, wv[:, :hidden], preferred_element_type=F32)
        lin[1] = jnp.dot(x, wv[:, hidden : 2 * hidden], preferred_element_type=F32)
        lin[2] = jnp.dot(cs[at, :], wv[:, 2 * hidden :], preferred_element_type=F32)
        band = 16

        def act_rows(r, _):
            here = pl.ds(pl.multiple_of(r * band, band), band)
            there = pl.ds(pl.multiple_of(start + r * band, band), band)
            gate, up, g_product = lin[0, here, :], lin[1, here, :], lin[2, here, :]
            sig = sigmoid(gate)
            gated = gate * sig
            act[there, :hidden] = (g_product * up * sig * (1.0 + gate * (1.0 - sig))).astype(BF16)
            act[there, hidden : 2 * hidden] = (g_product * gated).astype(BF16)
            act[there, 2 * hidden :] = (gated * up).astype(BF16)
            return 0

        lax.fori_loop(0, deep // band, act_rows, 0)
        parts[at, :] = mm(act[at, : 2 * hidden], wv[:, : 2 * hidden], (1, 1), None).astype(BF16)

        @pl.when((i > 0) & jnp.logical_not(total.inner))
        def _():
            for p in range(each):
                total.onward(b, half * each + p).start()

        return 0

    lax.fori_loop(0, count * halves, step, 0)

    high = tiles.shape[1]
    steps = width // high
    first = grad.shape[1] - 3 * hidden

    def store(t, r, k):
        down = pl.ds(pl.multiple_of(r * high, high), high)
        into = grad.at[down, pl.ds(first + k * hidden, hidden)]
        return pltpu.make_async_copy(tiles.at[lax.rem(t, 2)], into, o_sem.at[lax.rem(t, 2)])

    turned[...] = xs[...].T
    turned_c[...] = cs[...].T

    def tile(r, k):
        t = 3 * r + k

        @pl.when(t >= 2)
        def _():
            store(t, r, k).wait()

        left_rows = (turned_c if k == 2 else turned)[
            pl.ds(pl.multiple_of(r * high, high), high), :
        ]
        tiles[lax.rem(t, 2)] = jnp.dot(
            left_rows, act[:, k * hidden : (k + 1) * hidden], preferred_element_type=F32
        ).astype(BF16)
        store(t, r, k).start()

    def slab(r, _):
        tile(r, 0)
        tile(r, 1)
        total.relay_in_turn(2 * r)
        tile(r, 2)
        at = chunk(r)
        f_parts[r] = mm(act[at, 2 * hidden :], wv[:, 2 * hidden :], (1, 1), None).astype(BF16)
        total.relay_in_turn(2 * r + 1)
        return 0

    lax.fori_loop(0, steps, slab, 0)
    total.relay_last()
    total.result(g_x)
    total.finish()
    line.finish()
    store(3 * steps - 2, 0, 0).wait()
    store(3 * steps - 1, 0, 0).wait()


def feed_forward(x_own, c_all, w, hidden, count):
    rows, width = x_own.shape
    group = rows * count
    assert count == 4 and width % 4 == 0 and rows % 64 == 0
    anywhere = pl.BlockSpec(memory_space=pl.ANY)
    vmem = pl.BlockSpec(memory_space=pltpu.VMEM)
    dma = pltpu.SemaphoreType.DMA
    return pl.pallas_call(
        functools.partial(ffn_kernel, count),
        out_shape=(
            jax.ShapeDtypeStruct((rows, width), F32),
            jax.ShapeDtypeStruct((count, rows, width), BF16),
            jax.ShapeDtypeStruct(w.shape, BF16),
        ),
        in_specs=[anywhere] * 3,
        out_specs=(vmem, vmem, anywhere),
        scratch_shapes=[
            pltpu.VMEM((width, 3 * hidden), BF16),
            pltpu.VMEM((group, width), BF16),
            pltpu.VMEM((group, width), BF16),
            pltpu.VMEM((group, 3 * hidden), BF16),
            pltpu.VMEM((3, rows, hidden), F32),
            pltpu.VMEM((group, width), BF16),
            pltpu.VMEM((group + rows, width), BF16),
            pltpu.VMEM((width, group), BF16),
            pltpu.VMEM((width, group), BF16),
            pltpu.VMEM((2, width // 4, hidden), BF16),
            dma((3,)), dma((2,)), dma((count + 1, 1)), dma((count, 1)),
            dma((count, 4)), dma((count + 1, 4)), dma((2,)),
        ],
        compiler_params=pltpu.CompilerParams(
            collective_id=0, has_side_effects=True, vmem_limit_bytes=60 << 20
        ),
        cost_estimate=cost(100),
        name="feed_forward",
    )(x_own, c_all, w)


def back_kernel(keep, gated_own, og, o_in, qkv, decay, logits, through, pair_through, gain,
                kept_in, parts_in,
                g_proj, g_logits, g_gain, f_out,
                gated_all, go, runs, g_queried, g_keyed, g_values, pulls, weights, kept,
                parts, landed, state, sending, got, scanned, after, mate_out, mate_in,
                back_out, back_in, second_state, m_sem, in_sem, z_send, z_recv, s_send, s_recv, b_send, b_recv, p_sem, q_sem):
    h, head = lax.axis_index("head"), lax.axis_size("head")
    count, micro, rows, dk = decay.shape
    dv = og.shape[-1]
    width = qkv.shape[-1]
    slices, part = sending.shape[0], sending.shape[2]
    scale = dk ** (-0.5)
    loads = [
        pltpu.make_async_copy(parts_in, parts, in_sem.at[0]),
        pltpu.make_async_copy(kept_in, kept, in_sem.at[1]),
    ]
    for load in loads:
        load.start()
    greet(("seq", "head"))

    def to_head(hop, slot):
        to = lax.rem(h + hop, head)
        columns = gated_own.at[:, pl.ds(pl.multiple_of(to * dv, dv), dv)]
        return push(columns, gated_all.at[slot], z_send.at[hop], z_recv.at[slot], to)

    for hop in range(1, head):
        to_head(hop, h).start()
    gated_all[h] = gated_own[:, pl.ds(pl.multiple_of(h * dv, dv), dv)]

    causal = lower_ones(rows)
    before = [jnp.zeros((1, dk), F32)] * micro
    alive = [jnp.ones((1, dk), F32)] * micro
    for b in range(count):
        for m in range(micro):
            run = running(decay[b, m])
            runs[b, m] = run
            alive[m] = alive[m] * keep[b, m]
            weights[b, m] = jnp.exp(before[m]) * alive[m]
            before[m] = before[m] + run[rows - 1 : rows, :]
    g_gain[...] = jnp.zeros_like(g_gain)
    state[...] = jnp.zeros_like(state)

    def gates(i, _):
        b = near_order(h, head, i)
        pl.when(i > 0)(lambda: to_head(lax.rem(b - h + head, head), b).wait_recv())
        for m in range(micro):
            gate, o = og[b, m], o_in[b, m]
            grad = gated_all[b, m * rows : (m + 1) * rows, :].astype(F32)
            sig = sigmoid(gate)
            inv = lax.rsqrt(jnp.mean(o * o, axis=-1, keepdims=True) + 1e-5)
            plain = o * inv
            normed = (plain * gain[...]).astype(BF16).astype(F32)
            g_on = (grad * gate * sig).astype(BF16).astype(F32)
            g_proj[b, m, :, width:] = (
                grad * normed * sig * (1.0 + gate * (1.0 - sig))
            ).astype(BF16)
            scaled = g_on * gain[...]
            g_o = inv * (scaled - plain * jnp.mean(scaled * plain, axis=-1, keepdims=True))
            go[b, m] = g_o
            g_gain[0:1, :] += jnp.sum(g_on * plain, axis=0, keepdims=True)
            queried = qkv[b, m, :, :dk].astype(F32) * (jnp.exp(runs[b, m]) * scale)
            pull = mms(split(g_o), split(queried), (0, 0))
            pulls[b, m] = pull
            state[m] += pull * weights[b, m]
        return 0

    lax.fori_loop(0, head, gates, 0)
    loads[0].wait()
    total = LineSum(parts, landed, p_sem, q_sem, f_out.shape[0])
    total.send_all()
    half = dv // 2
    side = lax.rem(lax.axis_index("seq"), 2)
    own_half = pl.ds(pl.multiple_of(side * half, half), half)
    mate_half = pl.ds(pl.multiple_of((1 - side) * half, half), half)
    mate_out[...] = state[:, mate_half, :].astype(BF16)
    swap = to_mate(mate_out, mate_in, m_sem.at[0], m_sem.at[1])
    swap.start()
    swap.wait_recv()
    passes = pair_through[:, :, 0:1, :].astype(F32) + pair_through[:, :, 1:2, :].astype(F32)
    for m in range(micro):
        start, later_state = sided(state[m, own_half, :], mate_in[m].astype(F32))
        second_state[m] = later_state
        pair = passes[0, m] * later_state + start
        for i in range(slices):
            sending[i, m] = pair[i * part : (i + 1) * part, :].astype(BF16)
    begin, end, drain = swap_slices(sending, got, s_send, s_recv)
    begin()
    loads[1].wait()

    def inside(b, _):
        for m in range(micro):
            q = qkv[b, m, :, :dk].astype(F32)
            k = qkv[b, m, :, dk : 2 * dk].astype(F32)
            v = (qkv[b, m, :, 2 * dk :],)
            run = runs[b, m]
            queried, keyed = split(q * (jnp.exp(run) * scale)), split(k * jnp.exp(-run))
            g_o, entry = split(go[b, m]), split(kept[b, m])
            scores = split(jnp.where(causal, mms(queried, keyed, (1, 1)), 0.0))
            g_scores = split(jnp.where(causal, mms(g_o, v, (1, 1)), 0.0))
            g_queried[b, m] = mms(g_scores, keyed, (1, 0)) + mms(g_o, entry, (1, 0))
            g_keyed[b, m] = mms(g_scores, queried, (0, 0))
            g_values[b, m] = mms(scores, g_o, (0, 0))
        pl.when(total.inner)(lambda: total.relay(total.far_end, b))
        return 0

    lax.fori_loop(0, count, inside, 0)
    end()
    scan_states(True, got, through, scanned)
    begin_back, end_back, drain_back = swap_slices(scanned, after, b_send, b_recv)
    begin_back()

    @pl.when(total.inner)
    def _():
        for p in range(total.pieces):
            total.relay(head - 1 - total.far_end, p)
        for p in range(total.pieces):
            total.relay(head - 1 - h, p)

    end_back()
    for m in range(micro):
        leave = after[:, m].astype(F32).reshape(half, dk)
        firsts = passes[1, m] * leave + second_state[m]
        own, _ = sided(firsts, leave)
        mate, _ = sided(leave, firsts)
        state[m, own_half, :] = own
        back_out[m] = mate.astype(BF16)
    swap_back = to_mate(back_out, back_in, m_sem.at[2], m_sem.at[3])
    swap_back.start()
    swap_back.wait_recv()
    for m in range(micro):
        state[m, mate_half, :] = back_in[m].astype(F32)

    def across(step, _):
        b = count - 1 - step
        for m in range(micro):
            q = qkv[b, m, :, :dk].astype(F32)
            k = qkv[b, m, :, dk : 2 * dk].astype(F32)
            v = (qkv[b, m, :, 2 * dk :],)
            run = runs[b, m]
            last = run[rows - 1 : rows, :]
            up, down, rest = jnp.exp(run) * scale, jnp.exp(-run), jnp.exp(last - run)
            decayed = jnp.exp(last)
            gs = state[m]
            gs_parts = split(gs)
            carried = k * rest
            g_v = g_values[b, m] + mms(split(carried), gs_parts, (1, 1))
            g_carried = mms(v, gs_parts, (1, 0))
            from_carried = g_carried * carried
            g_total = jnp.sum(decayed * kept[b, m] * gs, axis=0, keepdims=True) + jnp.sum(
                from_carried, axis=0, keepdims=True
            )
            state[m] = (decayed * gs + pulls[b, m]) * keep[b, m]
            gq, gk = g_queried[b, m], g_keyed[b, m]
            g_run = gq * (q * up) - gk * (k * down) - from_carried
            later = mms((causal.astype(F32).astype(BF16),), split(g_run), (0, 0)) + g_total
            g_proj[b, m, :, :dk] = (gq * up).astype(BF16)
            g_proj[b, m, :, dk : 2 * dk] = (gk * down + g_carried * rest).astype(BF16)
            g_proj[b, m, :, 2 * dk : width] = g_v.astype(BF16)
            g_logits[b, m] = (
                later.astype(BF16).astype(F32) * sigmoid(-logits[b, m]) * (1.0 / GATE_NORM)
            )
        return 0

    lax.fori_loop(0, count, across, 0)
    total.result(f_out)
    total.finish()
    drain()
    drain_back()
    swap.wait_send()
    swap_back.wait_send()
    for hop in range(1, head):
        to_head(hop, h).wait_send()


def attention_back(
    keep, gated_own, og, o, qkv, decays, logits, through, pair_through, gain, kept, parts
):
    blocks, micro, rows, width = qkv.shape
    dk, dv = decays.shape[-1], og.shape[-1]
    head, seq = lax.axis_size("head"), lax.axis_size("seq")
    own_rows = parts.shape[0] // head
    vmem, anywhere = pl.BlockSpec(memory_space=pltpu.VMEM), pl.BlockSpec(memory_space=pl.ANY)
    dma = pltpu.SemaphoreType.DMA
    blocked = lambda w, kind: pltpu.VMEM((blocks, micro, rows, w), kind)
    pairs, half = seq // 2, dv // 2
    states = (pairs, micro, half // pairs, dk)
    halves = (micro, half, dk)
    return pl.pallas_call(
        back_kernel,
        out_shape=(
            jax.ShapeDtypeStruct((blocks, micro, rows, width + dv), BF16),
            jax.ShapeDtypeStruct((blocks, micro, rows, dk), F32),
            jax.ShapeDtypeStruct((8, dv), F32),
            jax.ShapeDtypeStruct((own_rows, parts.shape[1]), F32),
        ),
        in_specs=[vmem] * 10 + [anywhere] * 2,
        out_specs=(vmem,) * 4,
        scratch_shapes=[
            pltpu.VMEM((blocks, micro * rows, dv), BF16), blocked(dv, F32), blocked(dk, F32),
            blocked(dk, F32), blocked(dk, F32), blocked(dv, F32),
            pltpu.VMEM((blocks, micro, dv, dk), F32), pltpu.VMEM((blocks, micro, 1, dk), F32),
            pltpu.VMEM((blocks, micro, dv, dk), F32),
            pltpu.VMEM(parts.shape, BF16),
            pltpu.VMEM((parts.shape[0] + own_rows, parts.shape[1]), BF16),
            pltpu.VMEM((micro, dv, dk), F32),
            pltpu.VMEM(states, BF16), pltpu.VMEM(states, BF16), pltpu.VMEM(states, BF16),
            pltpu.VMEM(states, BF16), pltpu.VMEM(halves, BF16), pltpu.VMEM(halves, BF16),
            pltpu.VMEM(halves, BF16), pltpu.VMEM(halves, BF16), pltpu.VMEM(halves, F32), dma((4,)),
            dma((2,)), dma((head,)), dma((head,)), dma((pairs,)), dma((pairs,)), dma((pairs,)),
            dma((pairs,)), dma((head, 4)), dma((head + 1, 4)),
        ],
        compiler_params=pltpu.CompilerParams(
            collective_id=3, has_side_effects=True, vmem_limit_bytes=60 << 20
        ),
        cost_estimate=cost(80),
        name="attention_back",
    )(keep, gated_own, og, o, qkv, decays, logits, through, pair_through, gain, kept,
      parts)


def finish_kernel(xn_in, proj_in, w_in, g_logits, ranked, up_own, rank_down, source,
                  gain, g_ffn, g_head,
                  g_x, grad, norm_sum, ffn_sum, head_sum, bias_sum, up_sum, down_sum,
                  turned, proj, w, outgoing, mine, paired, inbox, heads_in, parts, landed,
                  slim_high, slim_low, small, small_in, small_part,
                  small_heads, small_all, rows_sum, in_sem, pair_send, pair_recv, send, recv, x_send, x_recv,
                  p_sem, q_sem, a_send, a_recv, b_send, b_recv, c_send, c_recv):
    h, head = lax.axis_index("head"), lax.axis_size("head")
    rows, width = g_x.shape
    deep = grad.shape[0] * head
    pairs = lax.axis_size("seq") // 2

    loads = [
        pltpu.make_async_copy(proj_in, proj, in_sem.at[0]),
        pltpu.make_async_copy(w_in, w, in_sem.at[1]),
        pltpu.make_async_copy(xn_in, landed.at[pl.ds(0, xn_in.shape[0])], in_sem.at[2]),
    ]
    for load in loads:
        load.start()
    sums = PairSum(mine, paired, inbox, pair_send, pair_recv, send, recv)
    for load in loads:
        load.wait()
    turned[...] = landed[: xn_in.shape[0], :].T
    greet(("seq", "head"))
    total = LineSum(parts, landed, p_sem, q_sem, rows)
    logit_parts = split(g_logits[...])
    g_ranked = mms(logit_parts, split(up_own[...]), (1, 1))
    slim = split(g_ranked)
    slim_high[...], slim_low[...] = slim

    def chunk(i, _):
        b = near_order(h, head, head - 1 - i)
        at = pl.ds(pl.multiple_of(b * rows, rows), rows)
        rank_part = mms((slim_high[at, :], slim_low[at, :]), (rank_down[...],), (1, 1))
        parts[at, :] = (mm(proj[at, :], w[...], (1, 1), None) + rank_part).astype(BF16)

        @pl.when((b != h) & jnp.logical_not(total.inner))
        def _():
            for p in range(total.pieces):
                total.onward(b, p).start()

        return 0

    lax.fori_loop(0, head, chunk, 0)

    def gone(k, _):
        outgoing[k] = jnp.dot(
            turned[sums.block(k, True), :], proj[...], preferred_element_type=F32
        ).astype(BF16)
        sums.to_partner(outgoing.at[k], k).start()
        return 0

    lax.fori_loop(0, pairs, gone, 0)

    def kept(k, _):
        here = jnp.dot(turned[sums.block(k), :], proj[...], preferred_element_type=F32)
        sums.to_partner(outgoing.at[k], k).wait_recv()
        mine[k] = (here + paired[k].astype(F32)).astype(BF16)
        sums.pass_on(k)

        @pl.when(total.inner & (k < total.pieces))
        def _():
            total.relay(total.far_end, k)

        @pl.when(total.inner & (k > 0) & (k <= total.pieces))
        def _():
            total.relay(head - 1 - total.far_end, k - 1)

        return 0

    lax.fori_loop(0, pairs, kept, 0)

    @pl.when(total.inner)
    def _():
        for p in range(pairs, total.pieces + 1):
            if p < total.pieces:
                total.relay(total.far_end, p)
            total.relay(head - 1 - total.far_end, p - 1)
        for p in range(total.pieces):
            total.relay(head - 1 - h, p)

    thin = grad.shape[0]

    def to_head(hop, slot):
        to = lax.rem(h + hop, head)
        at = pl.ds(pl.multiple_of(to * thin, thin), thin)
        return push(mine.at[sums.own, at, :], heads_in.at[slot], x_send.at[hop], x_recv.at[slot], to)

    sums.advance(0)

    total.result(g_x)
    rows_sum[...] = jnp.zeros_like(rows_sum)
    band = rows_sum.shape[0]

    def norm_rows(r, _):
        at = pl.ds(pl.multiple_of(r * band, band), band)
        x = source[at, :].astype(F32)
        inv = lax.rsqrt(jnp.mean(x * x, axis=-1, keepdims=True) + 1e-6)
        plain, g = x * inv, g_x[at, :]
        scaled = g * gain[...]
        inner = jnp.mean(scaled * plain, axis=-1, keepdims=True)
        rows_sum[...] += g * plain
        g_x[at, :] = inv * (scaled - plain * inner)
        return 0

    lax.fori_loop(0, rows // band, norm_rows, 0)
    rank, dk = up_own.shape
    low, keys = rank // 2, up_sum.shape[1]
    g_down = mms(slim, (turned[...],), (0, 1))
    g_up = mms(split(ranked[...]), logit_parts, (0, 0))
    small[...] = jnp.zeros_like(small)
    small[:low, :width] = g_down[:low]
    small[:low, width:] = g_down[low:]
    own_keys = pl.multiple_of(h * dk, dk)
    small[low:, pl.ds(own_keys, dk)] = g_up[:low]
    small[low:, pl.ds(keys + own_keys, dk)] = g_up[low:]
    small[low : low + 1, width:] = jnp.sum(rows_sum[...], axis=0, keepdims=True)
    small[low + 1 : low + 2, width:] = g_ffn[...]
    small[low + 2 : low + 3, width : width + g_head.shape[1]] = g_head[0:1, :]
    small[low + 3 : low + 4, pl.ds(width + own_keys, dk)] = jnp.sum(
        g_logits[...], axis=0, keepdims=True
    )
    s, seq = lax.axis_index("seq"), lax.axis_size("seq")
    wide = small.shape[1] // seq

    def piece(ref, i):
        return ref.at[:, pl.ds(pl.multiple_of(i * wide, wide), wide)]

    def begin_small(axis, me, count, copy):
        for hop in range(1, count):
            copy(hop, me, lax.rem(me + hop, count)).start()

    def end_small(axis, me, count, copy):
        for hop in range(1, count):
            other = lax.rem(me + hop, count)
            copy(hop, other, other).wait_recv()

    def scatter(hop, slot, to):
        return push(
            piece(small, to), small_in.at[slot], a_send.at[hop], a_recv.at[slot], to, "seq"
        )

    def between(hop, slot, to):
        return push(small_part, small_heads.at[slot], b_send.at[hop], b_recv.at[slot], to)

    def spread(hop, slot, to):
        return push(
            small_part, piece(small_all, slot), c_send.at[hop], c_recv.at[slot], to, "seq"
        )

    begin_small("seq", s, seq, scatter)
    small_in[s] = small[:, pl.ds(pl.multiple_of(s * wide, wide), wide)]
    for step in range(1, sums.levels):
        sums.advance(step)
    for hop in range(1, head):
        to_head(hop, h).start()
    own_rows = pl.ds(pl.multiple_of(h * thin, thin), thin)
    heads_in[h] = mine[sums.own, own_rows, :]
    end_small("seq", s, seq, scatter)
    small_part[...] = jnp.sum(small_in[...], axis=0)
    begin_small("head", h, head, between)
    small_heads[h] = small_part[...]
    end_small("head", h, head, between)
    for hop in range(1, head):
        between(hop, h, lax.rem(h + hop, head)).wait_send()
    small_part[...] = jnp.sum(small_heads[...], axis=0)
    begin_small("seq", s, seq, spread)
    small_all[:, pl.ds(pl.multiple_of(s * wide, wide), wide)] = small_part[...]
    for hop in range(1, head):
        to_head(hop, lax.rem(h + hop, head)).wait_recv()
    dv = mine.shape[2] // 2 - dk
    for j in range(head):
        at, start = 0, 0
        for size in (dk, dk, dv, dv):
            grad[:, start + j * size : start + (j + 1) * size] = heads_in[j, :, at : at + size]
            at, start = at + size, start + head * size
    end_small("seq", s, seq, spread)
    down_sum[:low, :] = small_all[:low, :width]
    down_sum[low:, :] = small_all[:low, width:]
    up_sum[:low, :] = small_all[low:, :keys]
    up_sum[low:, :] = small_all[low:, keys : 2 * keys]
    norm_sum[...] = small_all[low : low + 1, width:]
    ffn_sum[...] = small_all[low + 1 : low + 2, width:]
    head_sum[...] = small_all[low + 2 : low + 3, width : width + head_sum.shape[1]]
    bias_sum[...] = small_all[low + 3 : low + 4, width : width + keys]
    for hop in range(1, seq):
        scatter(hop, s, lax.rem(s + hop, seq)).wait_send()
        spread(hop, s, lax.rem(s + hop, seq)).wait_send()
    sums.finish(lambda k: outgoing.at[k])
    for hop in range(1, head):
        to_head(hop, h).wait_send()
    total.finish()


def finish(
    xn, g_proj, w_in, g_logits, ranked, up_own, rank_down, source, gain, g_ffn, g_head
):
    seq, head = lax.axis_size("seq"), lax.axis_size("head")
    group, width = xn.shape
    columns, rank = w_in.shape[1], ranked.shape[1]
    deep, rows, pairs = width // seq, group // head, seq // 2
    dk = up_own.shape[1]
    vmem, anywhere = pl.BlockSpec(memory_space=pltpu.VMEM), pl.BlockSpec(memory_space=pl.ANY)
    dma = pltpu.SemaphoreType.DMA
    blocks = lambda count, w: pltpu.VMEM((count, deep, w), BF16)
    ends = lambda w: pltpu.VMEM((head, deep // head, w), BF16)
    moves = dma((2, pairs - 1))
    return pl.pallas_call(
        finish_kernel,
        out_shape=(
            jax.ShapeDtypeStruct((rows, width), F32),
            jax.ShapeDtypeStruct((deep // head, columns * head), BF16),
            jax.ShapeDtypeStruct((1, width), F32),
            jax.ShapeDtypeStruct((1, width), F32),
            jax.ShapeDtypeStruct((1, g_head.shape[1]), F32),
            jax.ShapeDtypeStruct((1, dk * head), F32),
            jax.ShapeDtypeStruct((rank, dk * head), F32),
            jax.ShapeDtypeStruct((rank, width), F32),
        ),
        in_specs=[anywhere] * 3 + [vmem] * 8,
        out_specs=(vmem,) * 8,
        scratch_shapes=[
            pltpu.VMEM((width, group), BF16), pltpu.VMEM(g_proj.shape, BF16),
            pltpu.VMEM(w_in.shape, BF16), blocks(pairs, columns), blocks(pairs, columns),
            blocks(pairs, columns), blocks(pairs - 1, columns), ends(columns),
            pltpu.VMEM((group, width), BF16), pltpu.VMEM((group + rows, width), BF16),
            pltpu.VMEM(ranked.shape, BF16), pltpu.VMEM(ranked.shape, BF16),
            pltpu.VMEM((rank, 2 * width), F32), pltpu.VMEM((seq, rank, 2 * width // seq), F32),
            pltpu.VMEM((rank, 2 * width // seq), F32),
            pltpu.VMEM((head, rank, 2 * width // seq), F32),
            pltpu.VMEM((rank, 2 * width), F32), pltpu.VMEM((16, width), F32),
            dma((3,)), dma((pairs,)), dma((pairs,)), moves, moves, dma((head,)), dma((head,)),
            dma((head, 4)), dma((head + 1, 4)),
            dma((seq,)), dma((seq,)), dma((head,)), dma((head,)), dma((seq,)), dma((seq,)),
        ],
        compiler_params=pltpu.CompilerParams(
            collective_id=5, has_side_effects=True, vmem_limit_bytes=60 << 20
        ),
        cost_estimate=cost(95),
        name="finish",
    )(xn, g_proj, w_in, g_logits, ranked, up_own, rank_down, source, gain, g_ffn, g_head)


def weight_grad_kernel(left, right, *rest):
    out, turned = rest[-2:]

    @pl.when(pl.program_id(1) == 0)
    def _():
        turned[...] = left[...].T

    out[...] = jnp.dot(turned[...], right[...], preferred_element_type=F32).astype(BF16)


def weight_grad(left, right, into, columns, start, tile):
    depth, rows = left.shape
    high = min(rows, 512)
    first = start // tile
    given = () if into is None else (into,)
    return pl.pallas_call(
        weight_grad_kernel,
        out_shape=jax.ShapeDtypeStruct((rows, columns), BF16),
        grid=(rows // high, right.shape[1] // tile),
        in_specs=[
            pl.BlockSpec((depth, high), lambda i, j: (0, i)),
            pl.BlockSpec((depth, tile), lambda i, j: (0, j)),
        ]
        + [pl.BlockSpec(memory_space=pl.ANY) for _ in given],
        out_specs=pl.BlockSpec((high, tile), lambda i, j: (i, first + j)),
        scratch_shapes=[pltpu.VMEM((high, depth), BF16)],
        input_output_aliases={2: 0} if given else {},
        compiler_params=pltpu.CompilerParams(
            dimension_semantics=("arbitrary", "arbitrary"), vmem_limit_bytes=48 << 20
        ),
        cost_estimate=pl.CostEstimate(
            flops=2 * depth * rows * right.shape[1],
            bytes_accessed=2 * (depth * rows + (depth + rows) * right.shape[1]),
            transcendentals=0,
        ),
        name="weight_grad",
    )(left, right, *given)


def gather_weight(w):
    return lax.all_gather(w, "seq", axis=0, tiled=True)


def scatter_grad(g):
    return lax.psum_scatter(g.astype(BF16), "seq", scatter_dimension=0, tiled=True)


def dot(a, b, contract, precision=None):
    return lax.dot_general(
        a, b, (((contract[0],), (contract[1],)), ((), ())),
        precision=precision, preferred_element_type=F32,
    )


def rms(x, epsilon):
    return lax.rsqrt(jnp.mean(x * x, axis=-1, keepdims=True) + epsilon)


def norm_back(grad, gain, normed, inv):
    scaled = grad * gain
    inner = jnp.mean(scaled * normed, axis=-1, keepdims=True)
    return inv * (scaled - normed * inner), jnp.sum(grad * normed, axis=0)


def on_device(
    tokens, starts, cotangent, mix_in, mix_out, gate_up, down_proj,
    norm_gain, ffn_gain, head_gain, rank_down, rank_up, gate_bias,
):
    micro, rows, width = tokens.shape
    heads, seq = lax.axis_size("head"), lax.axis_size("seq")
    head = lax.axis_index("head")
    keys, dv = rank_up.shape[1], head_gain.shape[0]
    dk, vals = keys // heads, dv * heads
    hidden_units = down_proj.shape[1]
    group = heads * micro * rows
    proj_width = 2 * dk + 2 * dv

    def own_columns(w, start, size):
        return lax.dynamic_slice_in_dim(w, start + head * size, size, 1)

    w_in_own = jnp.concatenate(
        [
            own_columns(mix_in, 0, dk),
            own_columns(mix_in, keys, dk),
            own_columns(mix_in, 2 * keys, dv),
            own_columns(mix_in, 2 * keys + vals, dv),
        ],
        axis=1,
    )
    later = gather_weight(
        jnp.concatenate(
            [gate_up.reshape(gate_up.shape[0], 2 * hidden_units), down_proj, mix_out], axis=1
        )
    )
    w_out = later[:, 3 * hidden_units :]
    up_own = own_columns(rank_up, 0, dk)
    bias_own = lax.dynamic_slice_in_dim(gate_bias, head * dk, dk, 0)

    xn, w_in = gather_norm(
        tokens.reshape(micro * rows, width), norm_gain.reshape(1, width), w_in_own
    )
    qkv = dot(xn, w_in[:, : 2 * dk + dv], (1, 0)).astype(BF16)
    og = dot(xn, w_in[:, 2 * dk + dv :], (1, 0))
    ranked = dot(xn, rank_down, (1, 0))
    logits = dot(ranked, up_own, (1, 0), HIGHEST) + bias_own
    decays = (jax.nn.log_sigmoid(logits) / GATE_NORM).astype(BF16)

    def blocks(x):
        return x.reshape(heads, micro, rows, x.shape[-1])

    qkv_b, og_b, decays_b = blocks(qkv), blocks(og), blocks(decays)
    gain_row = head_gain.reshape(1, dv)
    keep = 1.0 - jnp.broadcast_to(starts.T[:, :, None, None], (heads, micro, 1, dk)).astype(F32)
    o_b, gated, through, pair_through, kept, all_cot = attention_forward(
        keep, qkv_b, decays_b, og_b, gain_row, cotangent.reshape(micro * rows, width)
    )

    source = tokens.astype(F32).reshape(micro * rows, width)
    hidden = source + dot(gated, w_out, (1, 1))
    inv_ffn = rms(hidden, 1e-6)
    plain_ffn = hidden * inv_ffn
    h2 = (plain_ffn * ffn_gain).astype(BF16)

    g_h2, ffn_part, grads = feed_forward(h2, all_cot, later, hidden_units, heads)

    back_ffn, g_ffn_gain = norm_back(g_h2, ffn_gain, plain_ffn, inv_ffn)
    g_hidden = cotangent.astype(F32).reshape(micro * rows, width) + back_ffn
    g_mixed = g_hidden.astype(BF16)
    grads = scatter_grad(weight_grad(g_mixed, gated, grads, later.shape[1], 0, vals))
    g_gated = dot(g_mixed, w_out, (1, 0)).astype(BF16)
    g_proj_b, g_logits_b, g_head_gain, ffn_out = attention_back(
        keep, g_gated, og_b, o_b, qkv_b, decays_b, blocks(logits), through, pair_through, gain_row, kept, ffn_part.reshape(group, width),
    )
    output = (hidden + ffn_out).astype(BF16)
    g_proj, g_logits = g_proj_b.reshape(group, proj_width), g_logits_b.reshape(group, dk)
    back_in, grad_in, *small, g_rank_down = finish(
        xn, g_proj, w_in, g_logits, ranked, up_own, rank_down, tokens.reshape(micro * rows, width),
        norm_gain.reshape(1, width), g_ffn_gain.reshape(1, width), g_head_gain,
    )
    g_norm_gain, g_ffn_gain, g_head_gain, g_bias, g_rank_up = small
    input_grad = g_hidden + back_in
    slab = width // (seq * heads)
    grad_in, grads = lax.optimization_barrier((grad_in, grads))
    grad_ffn = grads[:, vals:]
    grad_out = lax.all_to_all(
        grads[:, :vals].reshape(heads, slab, vals), "head", split_axis=0, concat_axis=0, tiled=True
    )
    grad_out = grad_out.astype(F32).sum(0)
    return (
        output.reshape(tokens.shape),
        input_grad.reshape(tokens.shape),
        grad_in.astype(F32),
        grad_out,
        grad_ffn[:, : 2 * hidden_units].astype(F32).reshape(-1, 2, hidden_units),
        grad_ffn[:, 2 * hidden_units :].astype(F32),
        g_norm_gain.reshape(norm_gain.shape),
        g_ffn_gain.reshape(ffn_gain.shape),
        g_head_gain.reshape(head_gain.shape),
        g_rank_down.T,
        g_rank_up,
        g_bias.reshape(gate_bias.shape),
    )


def solution(mesh):
    rows = P(None, ("seq", "head"), None)
    return jax.shard_map(
        on_device,
        mesh=mesh,
        in_specs=(
            rows, P(None, "seq"), rows, P("seq", None), P("seq", None),
            P("seq", None, "head"), P("seq", "head"), P(), P(), P(), P(), P(), P(),
        ),
        out_specs=(
            rows, rows, P(("seq", "head"), None), P(("seq", "head"), None),
            P("seq", None, "head"), P("seq", "head"), P(), P(), P(), P(), P(), P(),
        ),
        check_vma=False,
    )
```

```python
import functools

import jax
import jax.numpy as jnp
from jax import lax
from jax.experimental import pallas as pl
from jax.experimental.pallas import tpu as pltpu
from jax.sharding import PartitionSpec as P

HIGHEST = lax.Precision.HIGHEST
GATE_NORM = 16.0
BF16 = jnp.bfloat16
F32 = jnp.float32


def mm(a, b, contract, precision=HIGHEST):
    return lax.dot_general(
        a, b, ((contract[:1], contract[1:]), ((), ())),
        precision=precision, preferred_element_type=F32,
    )


def split(x):
    high = x.astype(BF16)
    return high, (x - high.astype(F32)).astype(BF16)


def mms(left, right, contract):
    total = mm(left[0], right[0], contract, None)
    if len(right) > 1:
        total += mm(left[0], right[1], contract, None)
    if len(left) > 1:
        total += mm(left[1], right[0], contract, None)
    return total


def lower_ones(size):
    rows = lax.broadcasted_iota(jnp.int32, (size, size), 0)
    cols = lax.broadcasted_iota(jnp.int32, (size, size), 1)
    return rows >= cols


def running(decay_low):
    ones = lower_ones(decay_low.shape[0]).astype(F32).astype(BF16)
    return mm(ones, decay_low, (1, 0), None)


def sigmoid(x):
    return 1.0 / (1.0 + jnp.exp(-x))


def cost(micros):
    return pl.CostEstimate(flops=0, bytes_accessed=int(micros * 3.0e6), transcendentals=0)


def greet(axes):
    barrier = pltpu.get_barrier_semaphore()
    met = 0
    for axis in axes:
        me, count = lax.axis_index(axis), lax.axis_size(axis)
        for hop in range(1, count):
            pl.semaphore_signal(
                barrier, inc=1, device_id={axis: lax.rem(me + hop, count)},
                device_id_type=pl.DeviceIdType.MESH,
            )
        met += count - 1
    pl.semaphore_wait(barrier, met)


def push(src, dst, send, recv, to, axis="head"):
    return pltpu.make_async_remote_copy(
        src_ref=src, dst_ref=dst, send_sem=send, recv_sem=recv,
        device_id={axis: to}, device_id_type=pl.DeviceIdType.MESH,
    )


def near_order(z, count, i):
    both = jnp.minimum(z, count - 1 - z)
    left = z > count - 1 - z
    paired = jnp.where(i % 2 == 1, z - (i + 1) // 2, z + i // 2)
    single = jnp.where(left, z - (i - both), z + (i - both))
    return jnp.where(i <= 2 * both, paired, single)


class Line:
    def __init__(self, own, all_rows, send, recv):
        self.own, self.all, self.send, self.recv = own, all_rows, send, recv
        self.z, self.count = lax.axis_index("head"), lax.axis_size("head")
        self.rows, self.parts = own.shape[0], recv.shape[1]
        self.deep = self.rows // self.parts

    def at(self, b):
        return self.all.at[pl.ds(pl.multiple_of(b * self.rows, self.rows), self.rows)]

    def part(self, b, p):
        start = b * self.rows + p * self.deep
        return self.all.at[pl.ds(pl.multiple_of(start, self.deep), self.deep)]

    def first(self, way, p):
        to = lax.rem(self.z + (1 if way == 0 else self.count - 1), self.count)
        src = self.own.at[pl.ds(p * self.deep, self.deep)]
        return push(
            src, self.part(self.z, p), self.send.at[way, p], self.recv.at[self.z, p], to
        )

    def each_first(self, act):
        for p in range(self.parts):
            pl.when(self.z < self.count - 1)(lambda p=p: act(self.first(0, p)))
            pl.when(self.z > 0)(lambda p=p: act(self.first(1, p)))

    def start(self):
        self.each_first(lambda copy: copy.start())

    def passing(self, i, b, p):
        z, count = self.z, self.count
        to = jnp.where(b < z, z + 1, z - 1)
        going = ((b < z) & (z < count - 1)) | ((b > z) & (z > 0))
        copy = push(
            self.part(b, p), self.part(b, p), self.send.at[i + 1, p], self.recv.at[b, p],
            lax.rem(to + count, count),
        )
        return copy, going

    def receive(self, i, b, p=0):
        copy, going = self.passing(i, b, p)
        copy.wait_recv()
        pl.when(going)(copy.start)

    def finish(self):
        def sent(i, _):
            for p in range(self.parts):
                copy, going = self.passing(i, near_order(self.z, self.count, i), p)
                pl.when(going)(copy.wait_send)
            return 0

        lax.fori_loop(1, self.count, sent, 0)
        self.each_first(lambda copy: copy.wait_send())


class LineSum:
    def __init__(self, parts, landed, send, recv, rows):
        self.parts, self.landed, self.send, self.recv = parts, landed, send, recv
        self.z, self.count = lax.axis_index("head"), lax.axis_size("head")
        self.rows, self.pieces = rows, send.shape[1]
        self.deep = rows // self.pieces
        self.inner = (self.z > 0) & (self.z < self.count - 1)
        self.far_end = jnp.where(self.z < self.count - 1 - self.z, self.count - 1, 0)

    def piece(self, b, p):
        return pl.ds(pl.multiple_of(b * self.rows + p * self.deep, self.deep), self.deep)

    def onward(self, b, p):
        z, count = self.z, self.count
        to = jnp.where(b > z, z + 1, z - 1)
        slot = jnp.where((to == b) & (z > b), count, b)
        return push(
            self.parts.at[self.piece(b, p)], self.landed.at[self.piece(slot, p)],
            self.send.at[b, p], self.recv.at[slot, p], lax.rem(to + count, count),
        )

    def send_all(self):
        @pl.when(jnp.logical_not(self.inner))
        def _():
            for i in range(1, self.count):
                b = jnp.where(self.z == 0, self.count - i, i - 1)
                for p in range(self.pieces):
                    self.onward(b, p).start()

    def arrived(self, slot, p):
        at = self.piece(slot, p)
        push(
            self.landed.at[at], self.landed.at[at], self.send.at[0, p], self.recv.at[slot, p],
            lax.rem(self.z + 1, self.count),
        ).wait_recv()
        return self.landed[at, :].astype(F32)

    def relay(self, b, p):
        at = self.piece(b, p)
        self.parts[at, :] = (self.parts[at, :].astype(F32) + self.arrived(b, p)).astype(BF16)
        self.onward(b, p).start()

    def relay_in_turn(self, j):
        pieces = self.pieces

        @pl.when(self.inner & (j < pieces))
        def _():
            self.relay(self.count - 1 - self.z, j)

        @pl.when(self.inner & (j >= pieces))
        def _():
            self.relay(self.far_end, j - pieces)

        @pl.when(self.inner & (j > pieces))
        def _():
            self.relay(self.count - 1 - self.far_end, j - pieces - 1)

    def relay_last(self):
        @pl.when(self.inner)
        def _():
            self.relay(self.count - 1 - self.far_end, self.pieces - 1)

    def result(self, out):
        z, count = self.z, self.count
        for p in range(self.pieces):
            here = pl.ds(p * self.deep, self.deep)
            out[here, :] = self.parts[self.piece(z, p), :].astype(F32)

            @pl.when(z > 0)
            def _():
                out[here, :] += self.arrived(z, p)

            @pl.when(z < count - 1)
            def _():
                out[here, :] += self.arrived(count, p)

    def finish(self):
        def sent(i, _):
            b = near_order(self.z, self.count, i)
            for p in range(self.pieces):
                self.onward(b, p).wait_send()
            return 0

        lax.fori_loop(1, self.count, sent, 0)


class PairSum:
    def __init__(self, mine, paired, inbox, pair_send, pair_recv, send, recv):
        self.mine, self.paired, self.inbox = mine, paired, inbox
        self.pair_send, self.pair_recv, self.send, self.recv = pair_send, pair_recv, send, recv
        self.s, self.pairs = lax.axis_index("seq"), lax.axis_size("seq") // 2
        self.side, self.own = lax.rem(self.s, 2), self.s // 2
        self.deep, self.half = mine.shape[1], mine.shape[2] // 2
        self.levels = self.pairs.bit_length() - 1
        assert self.pairs == 1 << self.levels

    def block(self, k, other=False):
        i = 2 * k + (1 - self.side if other else self.side)
        return pl.ds(pl.multiple_of(i * self.deep, self.deep), self.deep)

    def to_partner(self, src, k):
        return push(
            src, self.paired.at[k], self.pair_send.at[k], self.pair_recv.at[k],
            self.s + 1 - 2 * self.side, "seq",
        )

    def bit(self, i, level):
        return lax.rem(i // (1 << level), 2)

    def move(self, side, slot, k, level):
        columns = pl.ds(side * self.half, self.half)
        to = self.s + (1 - 2 * self.bit(self.own, level)) * (2 << level)
        return push(
            self.mine.at[k, :, columns], self.inbox.at[slot, :, columns],
            self.send.at[side, slot], self.recv.at[side, slot], to, "seq",
        )

    def moves(self, side, step):
        order = list(range(self.levels))
        if side:
            order.reverse()
        level, free = order[step], sorted(order[step + 1 :])
        fixed = sum((self.bit(self.own, d) * (1 << d) for d in order[:step]), 0)
        offset = self.pairs - (1 << (self.levels - step))
        here = self.bit(self.own, level) * (1 << level)
        for c in range(1 << len(free)):
            rest = fixed + sum(((c >> j) & 1) << d for j, d in enumerate(free))
            yield offset + c, rest + here, rest + (1 << level) - here, level

    def pass_on(self, k):
        top = 1 << (self.levels - 1)
        pl.when(self.bit(k, 0) != self.bit(self.own, 0))(self.move(0, k // 2, k, 0).start)
        pl.when(k // top != self.own // top)(
            self.move(1, lax.rem(k, top), k, self.levels - 1).start
        )

    def advance(self, step):
        for side in range(2):
            columns = slice(side * self.half, (side + 1) * self.half)
            for slot, keep, gone, level in self.moves(side, step):
                self.move(side, slot, gone, level).wait_recv()
                self.mine[keep, :, columns] = (
                    self.mine[keep, :, columns].astype(F32)
                    + self.inbox[slot, :, columns].astype(F32)
                ).astype(BF16)
            if step + 1 < self.levels:
                for slot, keep, gone, level in self.moves(side, step + 1):
                    self.move(side, slot, gone, level).start()

    def finish(self, src):
        for k in range(self.pairs):
            self.to_partner(src(k), k).wait_send()
        for side in range(2):
            for step in range(self.levels):
                for slot, keep, gone, level in self.moves(side, step):
                    self.move(side, slot, gone, level).wait_send()


def gather_norm_kernel(own, gain, shard, normed, rows_of_all, rows_all, here_sem, send, recv,
                       w_sem, w_send, w_recv, w_pair, w_pair_recv):
    z, count, rows = lax.axis_index("head"), lax.axis_size("head"), own.shape[0]
    greet(("seq", "head"))
    line = Line(own, rows_all, send, recv)
    line.start()
    here = pltpu.make_async_copy(own, line.at(z), here_sem)
    here.start()

    s, deep, half = lax.axis_index("seq"), shard.shape[0], shard.shape[1] // 2
    side, pairs, own_pair = lax.rem(s, 2), lax.axis_size("seq") // 2, s // 2
    levels = pairs.bit_length() - 1
    assert pairs == 1 << levels
    orders = list(range(levels)), list(reversed(range(levels)))

    def bit(level):
        return lax.rem(own_pair // (1 << level), 2) * (1 << level)

    def block(k, of_side):
        return pl.ds(pl.multiple_of((2 * k + of_side) * deep, deep), deep)

    def across(part, step):
        level = orders[part][step]
        return own_pair + (1 << level) - 2 * bit(level)

    def known(part, step, start):
        done = orders[part][:step]
        base = start - sum((bit(d) for d in done), 0)
        for c in range(1 << step):
            yield base + sum(((c >> n) & 1) << d for n, d in enumerate(done))

    def hop(part, step, k):
        at = rows_of_all.at[block(k, side), pl.ds(part * half, half)]
        to = 2 * across(part, step) + side
        return push(at, at, w_send.at[part, step, k], w_recv.at[part, k], to, "seq")

    def begin(step):
        for part in range(2):
            for k in known(part, step, own_pair):
                hop(part, step, k).start()

    def advance(step):
        for part in range(2):
            for k in known(part, step, across(part, step)):
                hop(part, step, k).wait_recv()
        if step + 1 < levels:
            begin(step + 1)

    def to_partner(k, of_side):
        at = rows_of_all.at[block(k, of_side)]
        return push(at, at, w_pair.at[k], w_pair_recv.at[k], s + 1 - 2 * side, "seq")

    mine = pltpu.make_async_copy(shard, rows_of_all.at[block(own_pair, side)], w_sem)
    mine.start()
    mine.wait()
    begin(0)
    to_partner(own_pair, side).start()
    here.wait()
    band = 16

    def step(i, _):
        b = near_order(z, count, i)
        pl.when(i > 0)(lambda: line.receive(i, b))
        pl.when(i == 1)(lambda: advance(0))

        def norm(r, _):
            at = pl.ds(pl.multiple_of(b * rows + r * band, band), band)
            x = rows_all[at, :].astype(F32)
            inv = lax.rsqrt(jnp.mean(x * x, axis=-1, keepdims=True) + 1e-6)
            normed[at, :] = (x * inv * gain[...]).astype(BF16)
            return 0

        lax.fori_loop(0, rows // band, norm, 0)
        return 0

    lax.fori_loop(0, count, step, 0)
    for later in range(1, levels):
        advance(later)
    for k in range(pairs):
        pl.when(own_pair != k)(to_partner(k, side).start)
    for k in range(pairs):
        to_partner(k, 1 - side).wait_recv()
    for k in range(pairs):
        to_partner(k, side).wait_send()
    for part in range(2):
        for late in range(levels):
            for k in known(part, late, own_pair):
                hop(part, late, k).wait_send()
    line.finish()


def gather_norm(x, gain, shard):
    rows, width = x.shape
    seq = lax.axis_size("seq")
    anywhere = pl.BlockSpec(memory_space=pl.ANY)
    count = lax.axis_size("head")
    vmem = pl.BlockSpec(memory_space=pltpu.VMEM)
    dma = pltpu.SemaphoreType.DMA
    return pl.pallas_call(
        gather_norm_kernel,
        out_shape=(
            jax.ShapeDtypeStruct((count * rows, width), BF16),
            jax.ShapeDtypeStruct((seq * shard.shape[0], shard.shape[1]), BF16),
        ),
        in_specs=[vmem, vmem, anywhere],
        out_specs=(vmem, anywhere),
        scratch_shapes=[
            pltpu.VMEM((count * rows, width), BF16), dma(()), dma((count + 1, 1)), dma((count, 1)),
            dma(()), dma((2, (seq // 2).bit_length() - 1, seq // 2)), dma((2, seq // 2)),
            dma((seq // 2,)), dma((seq // 2,)),
        ],
        compiler_params=pltpu.CompilerParams(
            collective_id=1, has_side_effects=True, vmem_limit_bytes=32 << 20
        ),
        cost_estimate=cost(50),
        name="gather_norm",
    )(x, gain, shard)


def swap_slices(own, got, send, recv):
    side = lax.rem(lax.axis_index("seq"), 2)
    me, count = lax.axis_index("seq") // 2, lax.axis_size("seq") // 2

    def copy(hop, index):
        to = lax.rem(me + hop, count)
        return push(own.at[to], got.at[index], send.at[hop], recv.at[index], 2 * to + side, "seq")

    def start(hop, _):
        copy(hop, me).start()
        return 0

    def wait_recv(hop, _):
        copy(hop, lax.rem(me + hop, count)).wait_recv()
        return 0

    def wait_send(hop, _):
        copy(hop, me).wait_send()
        return 0

    def begin():
        lax.fori_loop(1, count, start, 0)
        got[me] = own[me]

    def end():
        lax.fori_loop(1, count, wait_recv, 0)

    def drain():
        lax.fori_loop(1, count, wait_send, 0)

    return begin, end, drain


def to_mate(src, dst, send, recv):
    s = lax.axis_index("seq")
    return push(src, dst, send, recv, s + 1 - 2 * lax.rem(s, 2), "seq")


def sided(own, mate):
    first = lax.rem(lax.axis_index("seq"), 2) == 0
    return jnp.where(first, own, mate), jnp.where(first, mate, own)


def scan_states(reverse, own, through, out):
    count, part = out.shape[0], out.shape[2]

    def step(k, state):
        j = count - 1 - k if reverse else k
        out[j] = state.astype(BF16)
        decay = through[j, :, 0:1, :].astype(F32) + through[j, :, 1:2, :].astype(F32)
        return decay * state + own[j, :, :part, :].astype(F32)

    lax.fori_loop(0, count, step, jnp.zeros(out.shape[1:], F32))


def front_kernel(keep, qkv, decay, og, gain, rows_own,
                 o_out, gated, through, pair_through, kept_out, rows_all,
                 kept, runs, state, sending, got, scanned, before, leaving, mate_out, mate_in,
                 back_out, back_in, first_state,
                 here_sem, go, come, s_send, s_recv, b_send, b_recv, z_send, z_recv, k_sem, m_sem):
    h, head = lax.axis_index("head"), lax.axis_size("head")
    count, micro, rows, dk = decay.shape
    dv = og.shape[-1]
    slices, part = scanned.shape[0], scanned.shape[2]
    scale = dk ** (-0.5)
    greet(("seq", "head"))
    line = Line(rows_own, rows_all, go, come)
    line.start()
    here = pltpu.make_async_copy(rows_own, line.at(h), here_sem)
    here.start()

    state[...] = jnp.zeros_like(state)

    def gather(b, carry):
        passed, alive = carry
        later_passed, later_alive = [], []
        for m in range(micro):
            run = running(decay[b, m])
            runs[b, m] = run
            last = run[rows - 1 : rows, :]
            carried = qkv[b, m, :, dk : 2 * dk].astype(F32) * jnp.exp(last - run)
            fresh = mms((qkv[b, m, :, 2 * dk :],), split(carried), (0, 0))
            kept[b, m] = fresh
            state[m] = jnp.exp(last) * (state[m] * keep[b, m]) + fresh
            later_passed.append(passed[m] + last)
            later_alive.append(alive[m] * keep[b, m])
        return later_passed, later_alive

    passed, alive = lax.fori_loop(
        0, count, gather,
        ([jnp.zeros((1, dk), F32)] * micro, [jnp.ones((1, dk), F32)] * micro),
    )
    tail = sending.shape[2] - part
    at = lax.broadcasted_iota(jnp.int32, (tail, dk), 0)
    half = dv // 2
    side = lax.rem(lax.axis_index("seq"), 2)
    own_half = pl.ds(pl.multiple_of(side * half, half), half)
    mate_half = pl.ds(pl.multiple_of((1 - side) * half, half), half)

    def as_rows(value):
        high, low = split(value)
        return jnp.where(at == 0, high.astype(F32), jnp.where(at == 1, low.astype(F32), 0.0))

    own_rows = [as_rows(jnp.exp(passed[m]) * alive[m]) for m in range(micro)]
    for m in range(micro):
        mate_out[m, :half, :] = state[m, mate_half, :].astype(BF16)
        mate_out[m, half:, :] = own_rows[m].astype(BF16)
    swap = to_mate(mate_out, mate_in, m_sem.at[0], m_sem.at[1])
    swap.start()
    swap.wait_recv()
    first_through = []
    for m in range(micro):
        firsts, seconds = sided(own_rows[m], mate_in[m, half:, :].astype(F32))
        pair_through[0, m], pair_through[1, m] = firsts.astype(BF16), seconds.astype(BF16)
        first, second = firsts[0:1] + firsts[1:2], seconds[0:1] + seconds[1:2]
        first_through.append(first)
        start, after = sided(state[m, own_half, :], mate_in[m, :half, :].astype(F32))
        first_state[m] = start
        pair = second * start + after
        both = as_rows(first * second).astype(BF16)
        for i in range(slices):
            sending[i, m, :part, :] = pair[i * part : (i + 1) * part, :].astype(BF16)
            sending[i, m, part:, :] = both
    begin, end, drain = swap_slices(sending, got, s_send, s_recv)
    begin()
    causal = lower_ones(rows)

    def inside(b, _):
        for m in range(micro):
            run = runs[b, m]
            queried = split(qkv[b, m, :, :dk].astype(F32) * (jnp.exp(run) * scale))
            keyed = split(qkv[b, m, :, dk : 2 * dk].astype(F32) * jnp.exp(-run))
            scores = jnp.where(causal, mms(queried, keyed, (1, 1)), 0.0)
            o_out[b, m] = mms(split(scores), (qkv[b, m, :, 2 * dk :],), (1, 0))
        return 0

    lax.fori_loop(0, count, inside, 0)
    line.receive(1, near_order(h, head, 1))
    end()
    through[...] = got[:, :, part:, :]
    scan_states(False, got, through, scanned)
    begin_back, end_back, drain_back = swap_slices(scanned, before, b_send, b_recv)
    begin_back()
    line.receive(2, near_order(h, head, 2))
    end_back()
    for m in range(micro):
        entry = before[:, m].astype(F32).reshape(half, dk)
        own, mate = sided(entry, first_through[m] * entry + first_state[m])
        state[m, own_half, :] = own
        back_out[m] = mate.astype(BF16)
    swap_back = to_mate(back_out, back_in, m_sem.at[2], m_sem.at[3])
    swap_back.start()
    swap_back.wait_recv()
    for m in range(micro):
        state[m, mate_half, :] = back_in[m].astype(F32)

    def to_owner(b):
        columns = gated.at[:, pl.ds(pl.multiple_of(h * dv, dv), dv)]
        return push(leaving.at[b], columns, z_send.at[b], z_recv.at[h], b)

    def save(b):
        return pltpu.make_async_copy(kept.at[b], kept_out.at[b], k_sem.at[b])

    def across(b, _):
        for m in range(micro):
            run = runs[b, m]
            queried = split(qkv[b, m, :, :dk].astype(F32) * (jnp.exp(run) * scale))
            entry = state[m] * keep[b, m]
            state[m] = jnp.exp(run[rows - 1 : rows, :]) * entry + kept[b, m]
            kept[b, m] = entry
            o = o_out[b, m] + mms(queried, split(entry), (1, 1))
            o_out[b, m] = o
            inv = lax.rsqrt(jnp.mean(o * o, axis=-1, keepdims=True) + 1e-5)
            normed = (o * inv * gain[...]).astype(BF16).astype(F32)
            gate = og[b, m]
            leaving[b, m * rows : (m + 1) * rows, :] = (normed * gate * sigmoid(gate)).astype(BF16)
        save(b).start()
        pl.when(b != h)(to_owner(b).start)

        @pl.when(b == 1)
        def _():
            line.receive(3, near_order(h, head, 3))

        return 0

    lax.fori_loop(0, count, across, 0)
    gated[:, pl.ds(pl.multiple_of(h * dv, dv), dv)] = leaving[h]
    for hop in range(1, head):
        other = lax.rem(h + hop, head)
        columns = gated.at[:, pl.ds(pl.multiple_of(other * dv, dv), dv)]
        push(leaving.at[other], columns, z_send.at[other], z_recv.at[other], other).wait_recv()
        to_owner(other).wait_send()
    for b in range(count):
        save(b).wait()
    here.wait()
    line.finish()
    drain()
    drain_back()
    swap.wait_send()
    swap_back.wait_send()


def attention_forward(keep, qkv, decays, og, gain, rows_own):
    blocks, micro, rows, width = qkv.shape
    dk, dv = decays.shape[-1], og.shape[-1]
    head, seq = lax.axis_size("head"), lax.axis_size("seq")
    assert blocks == head and head == 4
    pairs, half, tail = seq // 2, dv // 2, 16
    part = half // pairs
    own_rows = micro * rows
    vmem, anywhere = pl.BlockSpec(memory_space=pltpu.VMEM), pl.BlockSpec(memory_space=pl.ANY)
    dma = pltpu.SemaphoreType.DMA
    states, wider = (pairs, micro, part, dk), (pairs, micro, part + tail, dk)
    return pl.pallas_call(
        front_kernel,
        out_shape=(
            jax.ShapeDtypeStruct((blocks, micro, rows, dv), F32),
            jax.ShapeDtypeStruct((own_rows, head * dv), BF16),
            jax.ShapeDtypeStruct((pairs, micro, tail, dk), BF16),
            jax.ShapeDtypeStruct((2, micro, tail, dk), BF16),
            jax.ShapeDtypeStruct((blocks, micro, dv, dk), F32),
            jax.ShapeDtypeStruct((head * rows_own.shape[0], rows_own.shape[1]), BF16),
        ),
        in_specs=[vmem] * 5 + [anywhere],
        out_specs=(vmem,) * 4 + (anywhere,) * 2,
        scratch_shapes=[
            pltpu.VMEM((blocks, micro, dv, dk), F32), pltpu.VMEM((blocks, micro, rows, dk), F32),
            pltpu.VMEM((micro, dv, dk), F32), pltpu.VMEM(wider, BF16), pltpu.VMEM(wider, BF16),
            pltpu.VMEM(states, BF16), pltpu.VMEM(states, BF16),
            pltpu.VMEM((blocks, own_rows, dv), BF16),
            pltpu.VMEM((micro, half + tail, dk), BF16), pltpu.VMEM((micro, half + tail, dk), BF16),
            pltpu.VMEM((micro, half, dk), BF16), pltpu.VMEM((micro, half, dk), BF16),
            pltpu.VMEM((micro, half, dk), F32),
            dma(()), dma((head + 1, 1)), dma((head, 1)), dma((pairs,)), dma((pairs,)), dma((pairs,)),
            dma((pairs,)), dma((head,)), dma((head,)), dma((blocks,)), dma((4,)),
        ],
        compiler_params=pltpu.CompilerParams(
            collective_id=2, has_side_effects=True, vmem_limit_bytes=40 << 20
        ),
        cost_estimate=cost(90),
        name="attention_forward",
    )(keep, qkv, decays, og, gain, rows_own)


def ffn_kernel(count, x_own, c_all, w, g_x, f_parts, grad,
               wv, xs, cs, act, lin, parts, landed, turned, turned_c, tiles,
               w_sem, own_sem, go_sem, x_sem, p_sem, q_sem, o_sem):
    z = lax.axis_index("head")
    rows, width = x_own.shape
    hidden = act.shape[1] // 3
    chunk = lambda b: pl.ds(pl.multiple_of(b * rows, rows), rows)

    weights = [
        pltpu.make_async_copy(
            w.at[:, pl.ds(k * hidden, hidden)], wv.at[:, pl.ds(k * hidden, hidden)], w_sem.at[k]
        )
        for k in range(3)
    ]
    own = [
        pltpu.make_async_copy(x_own, xs.at[chunk(z)], own_sem.at[0]),
        pltpu.make_async_copy(c_all, cs, own_sem.at[1]),
    ]
    for copy in own + weights:
        copy.start()
    greet(("head",))
    line = Line(x_own, xs, go_sem, x_sem)
    line.start()
    for copy in own + weights:
        copy.wait()

    total = LineSum(parts, landed, p_sem, q_sem, rows)

    halves = x_sem.shape[1]
    deep = rows // halves
    each = total.pieces // halves

    def step(t, _):
        i, half = t // halves, lax.rem(t, halves)
        b = near_order(z, count, i)
        pl.when(i > 0)(lambda: line.receive(i, b, half))
        start = b * rows + half * deep
        at = pl.ds(pl.multiple_of(start, deep), deep)
        x = xs[at, :]
        lin[0] = jnp.dot(x, wv[:, :hidden], preferred_element_type=F32)
        lin[1] = jnp.dot(x, wv[:, hidden : 2 * hidden], preferred_element_type=F32)
        lin[2] = jnp.dot(cs[at, :], wv[:, 2 * hidden :], preferred_element_type=F32)
        band = 16

        def act_rows(r, _):
            here = pl.ds(pl.multiple_of(r * band, band), band)
            there = pl.ds(pl.multiple_of(start + r * band, band), band)
            gate, up, g_product = lin[0, here, :], lin[1, here, :], lin[2, here, :]
            sig = sigmoid(gate)
            gated = gate * sig
            act[there, :hidden] = (g_product * up * sig * (1.0 + gate * (1.0 - sig))).astype(BF16)
            act[there, hidden : 2 * hidden] = (g_product * gated).astype(BF16)
            act[there, 2 * hidden :] = (gated * up).astype(BF16)
            return 0

        lax.fori_loop(0, deep // band, act_rows, 0)
        parts[at, :] = mm(act[at, : 2 * hidden], wv[:, : 2 * hidden], (1, 1), None).astype(BF16)

        @pl.when((i > 0) & jnp.logical_not(total.inner))
        def _():
            for p in range(each):
                total.onward(b, half * each + p).start()

        return 0

    lax.fori_loop(0, count * halves, step, 0)

    high = tiles.shape[1]
    steps = width // high
    first = grad.shape[1] - 3 * hidden

    def store(t, r, k):
        down = pl.ds(pl.multiple_of(r * high, high), high)
        into = grad.at[down, pl.ds(first + k * hidden, hidden)]
        return pltpu.make_async_copy(tiles.at[lax.rem(t, 2)], into, o_sem.at[lax.rem(t, 2)])

    turned[...] = xs[...].T
    turned_c[...] = cs[...].T

    def tile(r, k):
        t = 3 * r + k

        @pl.when(t >= 2)
        def _():
            store(t, r, k).wait()

        left_rows = (turned_c if k == 2 else turned)[
            pl.ds(pl.multiple_of(r * high, high), high), :
        ]
        tiles[lax.rem(t, 2)] = jnp.dot(
            left_rows, act[:, k * hidden : (k + 1) * hidden], preferred_element_type=F32
        ).astype(BF16)
        store(t, r, k).start()

    def slab(r, _):
        tile(r, 0)
        tile(r, 1)
        total.relay_in_turn(2 * r)
        tile(r, 2)
        at = chunk(r)
        f_parts[r] = mm(act[at, 2 * hidden :], wv[:, 2 * hidden :], (1, 1), None).astype(BF16)
        total.relay_in_turn(2 * r + 1)
        return 0

    lax.fori_loop(0, steps, slab, 0)
    total.relay_last()
    total.result(g_x)
    total.finish()
    line.finish()
    store(3 * steps - 2, 0, 0).wait()
    store(3 * steps - 1, 0, 0).wait()


def feed_forward(x_own, c_all, w, hidden, count):
    rows, width = x_own.shape
    group = rows * count
    assert count == 4 and width % 4 == 0 and rows % 64 == 0
    anywhere = pl.BlockSpec(memory_space=pl.ANY)
    vmem = pl.BlockSpec(memory_space=pltpu.VMEM)
    dma = pltpu.SemaphoreType.DMA
    return pl.pallas_call(
        functools.partial(ffn_kernel, count),
        out_shape=(
            jax.ShapeDtypeStruct((rows, width), F32),
            jax.ShapeDtypeStruct((count, rows, width), BF16),
            jax.ShapeDtypeStruct(w.shape, BF16),
        ),
        in_specs=[anywhere] * 3,
        out_specs=(vmem, vmem, anywhere),
        scratch_shapes=[
            pltpu.VMEM((width, 3 * hidden), BF16),
            pltpu.VMEM((group, width), BF16),
            pltpu.VMEM((group, width), BF16),
            pltpu.VMEM((group, 3 * hidden), BF16),
            pltpu.VMEM((3, rows, hidden), F32),
            pltpu.VMEM((group, width), BF16),
            pltpu.VMEM((group + rows, width), BF16),
            pltpu.VMEM((width, group), BF16),
            pltpu.VMEM((width, group), BF16),
            pltpu.VMEM((2, width // 4, hidden), BF16),
            dma((3,)), dma((2,)), dma((count + 1, 1)), dma((count, 1)),
            dma((count, 4)), dma((count + 1, 4)), dma((2,)),
        ],
        compiler_params=pltpu.CompilerParams(
            collective_id=0, has_side_effects=True, vmem_limit_bytes=60 << 20
        ),
        cost_estimate=cost(100),
        name="feed_forward",
    )(x_own, c_all, w)


def back_kernel(keep, gated_own, og, o_in, qkv, decay, logits, through, pair_through, gain,
                kept_in, parts_in,
                g_proj, g_logits, g_gain, f_out,
                gated_all, go, runs, g_queried, g_keyed, g_values, pulls, weights, kept,
                parts, landed, state, sending, got, scanned, after, mate_out, mate_in,
                back_out, back_in, second_state, m_sem, in_sem, z_send, z_recv, s_send, s_recv, b_send, b_recv, p_sem, q_sem):
    h, head = lax.axis_index("head"), lax.axis_size("head")
    count, micro, rows, dk = decay.shape
    dv = og.shape[-1]
    width = qkv.shape[-1]
    slices, part = sending.shape[0], sending.shape[2]
    scale = dk ** (-0.5)
    loads = [
        pltpu.make_async_copy(parts_in, parts, in_sem.at[0]),
        pltpu.make_async_copy(kept_in, kept, in_sem.at[1]),
    ]
    for load in loads:
        load.start()
    greet(("seq", "head"))

    def to_head(hop, slot):
        to = lax.rem(h + hop, head)
        columns = gated_own.at[:, pl.ds(pl.multiple_of(to * dv, dv), dv)]
        return push(columns, gated_all.at[slot], z_send.at[hop], z_recv.at[slot], to)

    for hop in range(1, head):
        to_head(hop, h).start()
    gated_all[h] = gated_own[:, pl.ds(pl.multiple_of(h * dv, dv), dv)]

    causal = lower_ones(rows)

    def reach(b, carry):
        before, alive = carry
        later_before, later_alive = [], []
        for m in range(micro):
            run = running(decay[b, m])
            runs[b, m] = run
            later_alive.append(alive[m] * keep[b, m])
            weights[b, m] = jnp.exp(before[m]) * later_alive[m]
            later_before.append(before[m] + run[rows - 1 : rows, :])
        return later_before, later_alive

    lax.fori_loop(
        0, count, reach, ([jnp.zeros((1, dk), F32)] * micro, [jnp.ones((1, dk), F32)] * micro)
    )
    g_gain[...] = jnp.zeros_like(g_gain)
    state[...] = jnp.zeros_like(state)

    def gates(i, _):
        b = near_order(h, head, i)
        pl.when(i > 0)(lambda: to_head(lax.rem(b - h + head, head), b).wait_recv())
        for m in range(micro):
            gate, o = og[b, m], o_in[b, m]
            grad = gated_all[b, m * rows : (m + 1) * rows, :].astype(F32)
            sig = sigmoid(gate)
            inv = lax.rsqrt(jnp.mean(o * o, axis=-1, keepdims=True) + 1e-5)
            plain = o * inv
            normed = (plain * gain[...]).astype(BF16).astype(F32)
            g_on = (grad * gate * sig).astype(BF16).astype(F32)
            g_proj[b, m, :, width:] = (
                grad * normed * sig * (1.0 + gate * (1.0 - sig))
            ).astype(BF16)
            scaled = g_on * gain[...]
            g_o = inv * (scaled - plain * jnp.mean(scaled * plain, axis=-1, keepdims=True))
            go[b, m] = g_o
            g_gain[0:1, :] += jnp.sum(g_on * plain, axis=0, keepdims=True)
            queried = qkv[b, m, :, :dk].astype(F32) * (jnp.exp(runs[b, m]) * scale)
            pull = mms(split(g_o), split(queried), (0, 0))
            pulls[b, m] = pull
            state[m] += pull * weights[b, m]
        return 0

    lax.fori_loop(0, head, gates, 0)
    loads[0].wait()
    total = LineSum(parts, landed, p_sem, q_sem, f_out.shape[0])
    total.send_all()
    half = dv // 2
    side = lax.rem(lax.axis_index("seq"), 2)
    own_half = pl.ds(pl.multiple_of(side * half, half), half)
    mate_half = pl.ds(pl.multiple_of((1 - side) * half, half), half)
    mate_out[...] = state[:, mate_half, :].astype(BF16)
    swap = to_mate(mate_out, mate_in, m_sem.at[0], m_sem.at[1])
    swap.start()
    swap.wait_recv()
    passes = pair_through[:, :, 0:1, :].astype(F32) + pair_through[:, :, 1:2, :].astype(F32)
    for m in range(micro):
        start, later_state = sided(state[m, own_half, :], mate_in[m].astype(F32))
        second_state[m] = later_state
        pair = passes[0, m] * later_state + start
        for i in range(slices):
            sending[i, m] = pair[i * part : (i + 1) * part, :].astype(BF16)
    begin, end, drain = swap_slices(sending, got, s_send, s_recv)
    begin()
    loads[1].wait()

    def inside(b, _):
        for m in range(micro):
            q = qkv[b, m, :, :dk].astype(F32)
            k = qkv[b, m, :, dk : 2 * dk].astype(F32)
            v = (qkv[b, m, :, 2 * dk :],)
            run = runs[b, m]
            queried, keyed = split(q * (jnp.exp(run) * scale)), split(k * jnp.exp(-run))
            g_o, entry = split(go[b, m]), split(kept[b, m])
            scores = split(jnp.where(causal, mms(queried, keyed, (1, 1)), 0.0))
            g_scores = split(jnp.where(causal, mms(g_o, v, (1, 1)), 0.0))
            g_queried[b, m] = mms(g_scores, keyed, (1, 0)) + mms(g_o, entry, (1, 0))
            g_keyed[b, m] = mms(g_scores, queried, (0, 0))
            g_values[b, m] = mms(scores, g_o, (0, 0))
        pl.when(total.inner)(lambda: total.relay(total.far_end, b))
        return 0

    lax.fori_loop(0, count, inside, 0)
    end()
    scan_states(True, got, through, scanned)
    begin_back, end_back, drain_back = swap_slices(scanned, after, b_send, b_recv)
    begin_back()

    @pl.when(total.inner)
    def _():
        for p in range(total.pieces):
            total.relay(head - 1 - total.far_end, p)
        for p in range(total.pieces):
            total.relay(head - 1 - h, p)

    end_back()
    for m in range(micro):
        leave = after[:, m].astype(F32).reshape(half, dk)
        firsts = passes[1, m] * leave + second_state[m]
        own, _ = sided(firsts, leave)
        mate, _ = sided(leave, firsts)
        state[m, own_half, :] = own
        back_out[m] = mate.astype(BF16)
    swap_back = to_mate(back_out, back_in, m_sem.at[2], m_sem.at[3])
    swap_back.start()
    swap_back.wait_recv()
    for m in range(micro):
        state[m, mate_half, :] = back_in[m].astype(F32)

    def across(step, _):
        b = count - 1 - step
        for m in range(micro):
            q = qkv[b, m, :, :dk].astype(F32)
            k = qkv[b, m, :, dk : 2 * dk].astype(F32)
            v = (qkv[b, m, :, 2 * dk :],)
            run = runs[b, m]
            last = run[rows - 1 : rows, :]
            up, down, rest = jnp.exp(run) * scale, jnp.exp(-run), jnp.exp(last - run)
            decayed = jnp.exp(last)
            gs = state[m]
            gs_parts = split(gs)
            carried = k * rest
            g_v = g_values[b, m] + mms(split(carried), gs_parts, (1, 1))
            g_carried = mms(v, gs_parts, (1, 0))
            from_carried = g_carried * carried
            g_total = jnp.sum(decayed * kept[b, m] * gs, axis=0, keepdims=True) + jnp.sum(
                from_carried, axis=0, keepdims=True
            )
            state[m] = (decayed * gs + pulls[b, m]) * keep[b, m]
            gq, gk = g_queried[b, m], g_keyed[b, m]
            g_run = gq * (q * up) - gk * (k * down) - from_carried
            later = mms((causal.astype(F32).astype(BF16),), split(g_run), (0, 0)) + g_total
            g_proj[b, m, :, :dk] = (gq * up).astype(BF16)
            g_proj[b, m, :, dk : 2 * dk] = (gk * down + g_carried * rest).astype(BF16)
            g_proj[b, m, :, 2 * dk : width] = g_v.astype(BF16)
            g_logits[b, m] = (
                later.astype(BF16).astype(F32) * sigmoid(-logits[b, m]) * (1.0 / GATE_NORM)
            )
        return 0

    lax.fori_loop(0, count, across, 0)
    total.result(f_out)
    total.finish()
    drain()
    drain_back()
    swap.wait_send()
    swap_back.wait_send()
    for hop in range(1, head):
        to_head(hop, h).wait_send()


def attention_back(
    keep, gated_own, og, o, qkv, decays, logits, through, pair_through, gain, kept, parts
):
    blocks, micro, rows, width = qkv.shape
    dk, dv = decays.shape[-1], og.shape[-1]
    head, seq = lax.axis_size("head"), lax.axis_size("seq")
    own_rows = parts.shape[0] // head
    vmem, anywhere = pl.BlockSpec(memory_space=pltpu.VMEM), pl.BlockSpec(memory_space=pl.ANY)
    dma = pltpu.SemaphoreType.DMA
    blocked = lambda w, kind: pltpu.VMEM((blocks, micro, rows, w), kind)
    pairs, half = seq // 2, dv // 2
    states = (pairs, micro, half // pairs, dk)
    halves = (micro, half, dk)
    return pl.pallas_call(
        back_kernel,
        out_shape=(
            jax.ShapeDtypeStruct((blocks, micro, rows, width + dv), BF16),
            jax.ShapeDtypeStruct((blocks, micro, rows, dk), F32),
            jax.ShapeDtypeStruct((8, dv), F32),
            jax.ShapeDtypeStruct((own_rows, parts.shape[1]), F32),
        ),
        in_specs=[vmem] * 10 + [anywhere] * 2,
        out_specs=(vmem,) * 4,
        scratch_shapes=[
            pltpu.VMEM((blocks, micro * rows, dv), BF16), blocked(dv, F32), blocked(dk, F32),
            blocked(dk, F32), blocked(dk, F32), blocked(dv, F32),
            pltpu.VMEM((blocks, micro, dv, dk), F32), pltpu.VMEM((blocks, micro, 1, dk), F32),
            pltpu.VMEM((blocks, micro, dv, dk), F32),
            pltpu.VMEM(parts.shape, BF16),
            pltpu.VMEM((parts.shape[0] + own_rows, parts.shape[1]), BF16),
            pltpu.VMEM((micro, dv, dk), F32),
            pltpu.VMEM(states, BF16), pltpu.VMEM(states, BF16), pltpu.VMEM(states, BF16),
            pltpu.VMEM(states, BF16), pltpu.VMEM(halves, BF16), pltpu.VMEM(halves, BF16),
            pltpu.VMEM(halves, BF16), pltpu.VMEM(halves, BF16), pltpu.VMEM(halves, F32), dma((4,)),
            dma((2,)), dma((head,)), dma((head,)), dma((pairs,)), dma((pairs,)), dma((pairs,)),
            dma((pairs,)), dma((head, 4)), dma((head + 1, 4)),
        ],
        compiler_params=pltpu.CompilerParams(
            collective_id=3, has_side_effects=True, vmem_limit_bytes=60 << 20
        ),
        cost_estimate=cost(80),
        name="attention_back",
    )(keep, gated_own, og, o, qkv, decays, logits, through, pair_through, gain, kept,
      parts)


def finish_kernel(xn_in, proj_in, w_in, g_logits, ranked, up_own, rank_down, source,
                  gain, g_ffn, g_head,
                  g_x, grad, norm_sum, ffn_sum, head_sum, bias_sum, up_sum, down_sum,
                  turned, proj, w, outgoing, mine, paired, inbox, heads_in, parts, landed,
                  slim_high, slim_low, small, small_in, small_part,
                  small_heads, small_all, rows_sum, in_sem, pair_send, pair_recv, send, recv, x_send, x_recv,
                  p_sem, q_sem, a_send, a_recv, b_send, b_recv, c_send, c_recv):
    h, head = lax.axis_index("head"), lax.axis_size("head")
    rows, width = g_x.shape
    deep = grad.shape[0] * head
    pairs = lax.axis_size("seq") // 2

    loads = [
        pltpu.make_async_copy(proj_in, proj, in_sem.at[0]),
        pltpu.make_async_copy(w_in, w, in_sem.at[1]),
        pltpu.make_async_copy(xn_in, landed.at[pl.ds(0, xn_in.shape[0])], in_sem.at[2]),
    ]
    for load in loads:
        load.start()
    sums = PairSum(mine, paired, inbox, pair_send, pair_recv, send, recv)
    for load in loads:
        load.wait()
    turned[...] = landed[: xn_in.shape[0], :].T
    greet(("seq", "head"))
    total = LineSum(parts, landed, p_sem, q_sem, rows)
    logit_parts = split(g_logits[...])
    g_ranked = mms(logit_parts, split(up_own[...]), (1, 1))
    slim = split(g_ranked)
    slim_high[...], slim_low[...] = slim

    def chunk(i, _):
        b = near_order(h, head, head - 1 - i)
        at = pl.ds(pl.multiple_of(b * rows, rows), rows)
        rank_part = mms((slim_high[at, :], slim_low[at, :]), (rank_down[...],), (1, 1))
        parts[at, :] = (mm(proj[at, :], w[...], (1, 1), None) + rank_part).astype(BF16)

        @pl.when((b != h) & jnp.logical_not(total.inner))
        def _():
            for p in range(total.pieces):
                total.onward(b, p).start()

        return 0

    lax.fori_loop(0, head, chunk, 0)

    def gone(k, _):
        outgoing[k] = jnp.dot(
            turned[sums.block(k, True), :], proj[...], preferred_element_type=F32
        ).astype(BF16)
        sums.to_partner(outgoing.at[k], k).start()
        return 0

    lax.fori_loop(0, pairs, gone, 0)

    def kept(k, _):
        here = jnp.dot(turned[sums.block(k), :], proj[...], preferred_element_type=F32)
        sums.to_partner(outgoing.at[k], k).wait_recv()
        mine[k] = (here + paired[k].astype(F32)).astype(BF16)
        sums.pass_on(k)

        @pl.when(total.inner & (k < total.pieces))
        def _():
            total.relay(total.far_end, k)

        @pl.when(total.inner & (k > 0) & (k <= total.pieces))
        def _():
            total.relay(head - 1 - total.far_end, k - 1)

        return 0

    lax.fori_loop(0, pairs, kept, 0)

    @pl.when(total.inner)
    def _():
        for p in range(pairs, total.pieces + 1):
            if p < total.pieces:
                total.relay(total.far_end, p)
            total.relay(head - 1 - total.far_end, p - 1)
        for p in range(total.pieces):
            total.relay(head - 1 - h, p)

    thin = grad.shape[0]

    def to_head(hop, slot):
        to = lax.rem(h + hop, head)
        at = pl.ds(pl.multiple_of(to * thin, thin), thin)
        return push(mine.at[sums.own, at, :], heads_in.at[slot], x_send.at[hop], x_recv.at[slot], to)

    sums.advance(0)

    total.result(g_x)
    rows_sum[...] = jnp.zeros_like(rows_sum)
    band = rows_sum.shape[0]

    def norm_rows(r, _):
        at = pl.ds(pl.multiple_of(r * band, band), band)
        x = source[at, :].astype(F32)
        inv = lax.rsqrt(jnp.mean(x * x, axis=-1, keepdims=True) + 1e-6)
        plain, g = x * inv, g_x[at, :]
        scaled = g * gain[...]
        inner = jnp.mean(scaled * plain, axis=-1, keepdims=True)
        rows_sum[...] += g * plain
        g_x[at, :] = inv * (scaled - plain * inner)
        return 0

    lax.fori_loop(0, rows // band, norm_rows, 0)
    rank, dk = up_own.shape
    low, keys = rank // 2, up_sum.shape[1]
    g_down = mms(slim, (turned[...],), (0, 1))
    g_up = mms(split(ranked[...]), logit_parts, (0, 0))
    small[...] = jnp.zeros_like(small)
    small[:low, :width] = g_down[:low]
    small[:low, width:] = g_down[low:]
    own_keys = pl.multiple_of(h * dk, dk)
    small[low:, pl.ds(own_keys, dk)] = g_up[:low]
    small[low:, pl.ds(keys + own_keys, dk)] = g_up[low:]
    small[low : low + 1, width:] = jnp.sum(rows_sum[...], axis=0, keepdims=True)
    small[low + 1 : low + 2, width:] = g_ffn[...]
    small[low + 2 : low + 3, width : width + g_head.shape[1]] = g_head[0:1, :]
    small[low + 3 : low + 4, pl.ds(width + own_keys, dk)] = jnp.sum(
        g_logits[...], axis=0, keepdims=True
    )
    s, seq = lax.axis_index("seq"), lax.axis_size("seq")
    wide = small.shape[1] // seq

    def piece(ref, i):
        return ref.at[:, pl.ds(pl.multiple_of(i * wide, wide), wide)]

    def begin_small(axis, me, count, copy):
        for hop in range(1, count):
            copy(hop, me, lax.rem(me + hop, count)).start()

    def end_small(axis, me, count, copy):
        for hop in range(1, count):
            other = lax.rem(me + hop, count)
            copy(hop, other, other).wait_recv()

    def scatter(hop, slot, to):
        return push(
            piece(small, to), small_in.at[slot], a_send.at[hop], a_recv.at[slot], to, "seq"
        )

    def between(hop, slot, to):
        return push(small_part, small_heads.at[slot], b_send.at[hop], b_recv.at[slot], to)

    def spread(hop, slot, to):
        return push(
            small_part, piece(small_all, slot), c_send.at[hop], c_recv.at[slot], to, "seq"
        )

    begin_small("seq", s, seq, scatter)
    small_in[s] = small[:, pl.ds(pl.multiple_of(s * wide, wide), wide)]
    for step in range(1, sums.levels):
        sums.advance(step)
    for hop in range(1, head):
        to_head(hop, h).start()
    own_rows = pl.ds(pl.multiple_of(h * thin, thin), thin)
    heads_in[h] = mine[sums.own, own_rows, :]
    end_small("seq", s, seq, scatter)
    small_part[...] = jnp.sum(small_in[...], axis=0)
    begin_small("head", h, head, between)
    small_heads[h] = small_part[...]
    end_small("head", h, head, between)
    for hop in range(1, head):
        between(hop, h, lax.rem(h + hop, head)).wait_send()
    small_part[...] = jnp.sum(small_heads[...], axis=0)
    begin_small("seq", s, seq, spread)
    small_all[:, pl.ds(pl.multiple_of(s * wide, wide), wide)] = small_part[...]
    for hop in range(1, head):
        to_head(hop, lax.rem(h + hop, head)).wait_recv()
    dv = mine.shape[2] // 2 - dk
    for j in range(head):
        at, start = 0, 0
        for size in (dk, dk, dv, dv):
            grad[:, start + j * size : start + (j + 1) * size] = heads_in[j, :, at : at + size]
            at, start = at + size, start + head * size
    end_small("seq", s, seq, spread)
    down_sum[:low, :] = small_all[:low, :width]
    down_sum[low:, :] = small_all[:low, width:]
    up_sum[:low, :] = small_all[low:, :keys]
    up_sum[low:, :] = small_all[low:, keys : 2 * keys]
    norm_sum[...] = small_all[low : low + 1, width:]
    ffn_sum[...] = small_all[low + 1 : low + 2, width:]
    head_sum[...] = small_all[low + 2 : low + 3, width : width + head_sum.shape[1]]
    bias_sum[...] = small_all[low + 3 : low + 4, width : width + keys]
    for hop in range(1, seq):
        scatter(hop, s, lax.rem(s + hop, seq)).wait_send()
        spread(hop, s, lax.rem(s + hop, seq)).wait_send()
    sums.finish(lambda k: outgoing.at[k])
    for hop in range(1, head):
        to_head(hop, h).wait_send()
    total.finish()


def finish(
    xn, g_proj, w_in, g_logits, ranked, up_own, rank_down, source, gain, g_ffn, g_head
):
    seq, head = lax.axis_size("seq"), lax.axis_size("head")
    group, width = xn.shape
    columns, rank = w_in.shape[1], ranked.shape[1]
    deep, rows, pairs = width // seq, group // head, seq // 2
    dk = up_own.shape[1]
    vmem, anywhere = pl.BlockSpec(memory_space=pltpu.VMEM), pl.BlockSpec(memory_space=pl.ANY)
    dma = pltpu.SemaphoreType.DMA
    blocks = lambda count, w: pltpu.VMEM((count, deep, w), BF16)
    ends = lambda w: pltpu.VMEM((head, deep // head, w), BF16)
    moves = dma((2, pairs - 1))
    return pl.pallas_call(
        finish_kernel,
        out_shape=(
            jax.ShapeDtypeStruct((rows, width), F32),
            jax.ShapeDtypeStruct((deep // head, columns * head), BF16),
            jax.ShapeDtypeStruct((1, width), F32),
            jax.ShapeDtypeStruct((1, width), F32),
            jax.ShapeDtypeStruct((1, g_head.shape[1]), F32),
            jax.ShapeDtypeStruct((1, dk * head), F32),
            jax.ShapeDtypeStruct((rank, dk * head), F32),
            jax.ShapeDtypeStruct((rank, width), F32),
        ),
        in_specs=[anywhere] * 3 + [vmem] * 8,
        out_specs=(vmem,) * 8,
        scratch_shapes=[
            pltpu.VMEM((width, group), BF16), pltpu.VMEM(g_proj.shape, BF16),
            pltpu.VMEM(w_in.shape, BF16), blocks(pairs, columns), blocks(pairs, columns),
            blocks(pairs, columns), blocks(pairs - 1, columns), ends(columns),
            pltpu.VMEM((group, width), BF16), pltpu.VMEM((group + rows, width), BF16),
            pltpu.VMEM(ranked.shape, BF16), pltpu.VMEM(ranked.shape, BF16),
            pltpu.VMEM((rank, 2 * width), F32), pltpu.VMEM((seq, rank, 2 * width // seq), F32),
            pltpu.VMEM((rank, 2 * width // seq), F32),
            pltpu.VMEM((head, rank, 2 * width // seq), F32),
            pltpu.VMEM((rank, 2 * width), F32), pltpu.VMEM((16, width), F32),
            dma((3,)), dma((pairs,)), dma((pairs,)), moves, moves, dma((head,)), dma((head,)),
            dma((head, 4)), dma((head + 1, 4)),
            dma((seq,)), dma((seq,)), dma((head,)), dma((head,)), dma((seq,)), dma((seq,)),
        ],
        compiler_params=pltpu.CompilerParams(
            collective_id=5, has_side_effects=True, vmem_limit_bytes=60 << 20
        ),
        cost_estimate=cost(95),
        name="finish",
    )(xn, g_proj, w_in, g_logits, ranked, up_own, rank_down, source, gain, g_ffn, g_head)


def weight_grad_kernel(left, right, *rest):
    out, turned = rest[-2:]

    @pl.when(pl.program_id(1) == 0)
    def _():
        turned[...] = left[...].T

    out[...] = jnp.dot(turned[...], right[...], preferred_element_type=F32).astype(BF16)


def weight_grad(left, right, into, columns, start, tile):
    depth, rows = left.shape
    high = min(rows, 512)
    first = start // tile
    given = () if into is None else (into,)
    return pl.pallas_call(
        weight_grad_kernel,
        out_shape=jax.ShapeDtypeStruct((rows, columns), BF16),
        grid=(rows // high, right.shape[1] // tile),
        in_specs=[
            pl.BlockSpec((depth, high), lambda i, j: (0, i)),
            pl.BlockSpec((depth, tile), lambda i, j: (0, j)),
        ]
        + [pl.BlockSpec(memory_space=pl.ANY) for _ in given],
        out_specs=pl.BlockSpec((high, tile), lambda i, j: (i, first + j)),
        scratch_shapes=[pltpu.VMEM((high, depth), BF16)],
        input_output_aliases={2: 0} if given else {},
        compiler_params=pltpu.CompilerParams(
            dimension_semantics=("arbitrary", "arbitrary"), vmem_limit_bytes=48 << 20
        ),
        cost_estimate=pl.CostEstimate(
            flops=2 * depth * rows * right.shape[1],
            bytes_accessed=2 * (depth * rows + (depth + rows) * right.shape[1]),
            transcendentals=0,
        ),
        name="weight_grad",
    )(left, right, *given)


def gather_weight(w):
    return lax.all_gather(w, "seq", axis=0, tiled=True)


def scatter_grad(g):
    return lax.psum_scatter(g.astype(BF16), "seq", scatter_dimension=0, tiled=True)


def dot(a, b, contract, precision=None):
    return lax.dot_general(
        a, b, (((contract[0],), (contract[1],)), ((), ())),
        precision=precision, preferred_element_type=F32,
    )


def rms(x, epsilon):
    return lax.rsqrt(jnp.mean(x * x, axis=-1, keepdims=True) + epsilon)


def norm_back(grad, gain, normed, inv):
    scaled = grad * gain
    inner = jnp.mean(scaled * normed, axis=-1, keepdims=True)
    return inv * (scaled - normed * inner), jnp.sum(grad * normed, axis=0)


def on_device(
    tokens, starts, cotangent, mix_in, mix_out, gate_up, down_proj,
    norm_gain, ffn_gain, head_gain, rank_down, rank_up, gate_bias,
):
    micro, rows, width = tokens.shape
    heads, seq = lax.axis_size("head"), lax.axis_size("seq")
    head = lax.axis_index("head")
    keys, dv = rank_up.shape[1], head_gain.shape[0]
    dk, vals = keys // heads, dv * heads
    hidden_units = down_proj.shape[1]
    group = heads * micro * rows
    proj_width = 2 * dk + 2 * dv

    def own_columns(w, start, size):
        return lax.dynamic_slice_in_dim(w, start + head * size, size, 1)

    w_in_own = jnp.concatenate(
        [
            own_columns(mix_in, 0, dk),
            own_columns(mix_in, keys, dk),
            own_columns(mix_in, 2 * keys, dv),
            own_columns(mix_in, 2 * keys + vals, dv),
        ],
        axis=1,
    )
    later = gather_weight(
        jnp.concatenate(
            [gate_up.reshape(gate_up.shape[0], 2 * hidden_units), down_proj, mix_out], axis=1
        )
    )
    w_out = later[:, 3 * hidden_units :]
    up_own = own_columns(rank_up, 0, dk)
    bias_own = lax.dynamic_slice_in_dim(gate_bias, head * dk, dk, 0)

    xn, w_in = gather_norm(
        tokens.reshape(micro * rows, width), norm_gain.reshape(1, width), w_in_own
    )
    qkv = dot(xn, w_in[:, : 2 * dk + dv], (1, 0)).astype(BF16)
    og = dot(xn, w_in[:, 2 * dk + dv :], (1, 0))
    ranked = dot(xn, rank_down, (1, 0))
    logits = dot(ranked, up_own, (1, 0), HIGHEST) + bias_own
    decays = (jax.nn.log_sigmoid(logits) / GATE_NORM).astype(BF16)

    def blocks(x):
        return x.reshape(heads, micro, rows, x.shape[-1])

    qkv_b, og_b, decays_b = blocks(qkv), blocks(og), blocks(decays)
    gain_row = head_gain.reshape(1, dv)
    keep = 1.0 - jnp.broadcast_to(starts.T[:, :, None, None], (heads, micro, 1, dk)).astype(F32)
    o_b, gated, through, pair_through, kept, all_cot = attention_forward(
        keep, qkv_b, decays_b, og_b, gain_row, cotangent.reshape(micro * rows, width)
    )

    source = tokens.astype(F32).reshape(micro * rows, width)
    hidden = source + dot(gated, w_out, (1, 1))
    inv_ffn = rms(hidden, 1e-6)
    plain_ffn = hidden * inv_ffn
    h2 = (plain_ffn * ffn_gain).astype(BF16)

    g_h2, ffn_part, grads = feed_forward(h2, all_cot, later, hidden_units, heads)

    back_ffn, g_ffn_gain = norm_back(g_h2, ffn_gain, plain_ffn, inv_ffn)
    g_hidden = cotangent.astype(F32).reshape(micro * rows, width) + back_ffn
    g_mixed = g_hidden.astype(BF16)
    grads = scatter_grad(weight_grad(g_mixed, gated, grads, later.shape[1], 0, vals))
    g_gated = dot(g_mixed, w_out, (1, 0)).astype(BF16)
    g_proj_b, g_logits_b, g_head_gain, ffn_out = attention_back(
        keep, g_gated, og_b, o_b, qkv_b, decays_b, blocks(logits), through, pair_through, gain_row, kept, ffn_part.reshape(group, width),
    )
    output = (hidden + ffn_out).astype(BF16)
    g_proj, g_logits = g_proj_b.reshape(group, proj_width), g_logits_b.reshape(group, dk)
    back_in, grad_in, *small, g_rank_down = finish(
        xn, g_proj, w_in, g_logits, ranked, up_own, rank_down, tokens.reshape(micro * rows, width),
        norm_gain.reshape(1, width), g_ffn_gain.reshape(1, width), g_head_gain,
    )
    g_norm_gain, g_ffn_gain, g_head_gain, g_bias, g_rank_up = small
    input_grad = g_hidden + back_in
    slab = width // (seq * heads)
    grad_in, grads = lax.optimization_barrier((grad_in, grads))
    grad_ffn = grads[:, vals:]
    grad_out = lax.all_to_all(
        grads[:, :vals].reshape(heads, slab, vals), "head", split_axis=0, concat_axis=0, tiled=True
    )
    grad_out = grad_out.astype(F32).sum(0)
    return (
        output.reshape(tokens.shape),
        input_grad.reshape(tokens.shape),
        grad_in.astype(F32),
        grad_out,
        grad_ffn[:, : 2 * hidden_units].astype(F32).reshape(-1, 2, hidden_units),
        grad_ffn[:, 2 * hidden_units :].astype(F32),
        g_norm_gain.reshape(norm_gain.shape),
        g_ffn_gain.reshape(ffn_gain.shape),
        g_head_gain.reshape(head_gain.shape),
        g_rank_down.T,
        g_rank_up,
        g_bias.reshape(gate_bias.shape),
    )


def solution(mesh):
    rows = P(None, ("seq", "head"), None)
    return jax.shard_map(
        on_device,
        mesh=mesh,
        in_specs=(
            rows, P(None, "seq"), rows, P("seq", None), P("seq", None),
            P("seq", None, "head"), P("seq", "head"), P(), P(), P(), P(), P(), P(),
        ),
        out_specs=(
            rows, rows, P(("seq", "head"), None), P(("seq", "head"), None),
            P("seq", None, "head"), P("seq", "head"), P(), P(), P(), P(), P(), P(),
        ),
        check_vma=False,
    )
```

```python
import functools

import jax
import jax.numpy as jnp
from jax import lax
from jax.experimental import pallas as pl
from jax.experimental.pallas import tpu as pltpu
from jax.sharding import PartitionSpec as P

HIGHEST = lax.Precision.HIGHEST
GATE_NORM = 16.0
BF16 = jnp.bfloat16
F32 = jnp.float32


def mm(a, b, contract, precision=HIGHEST):
    return lax.dot_general(
        a, b, ((contract[:1], contract[1:]), ((), ())),
        precision=precision, preferred_element_type=F32,
    )


def split(x):
    high = x.astype(BF16)
    return high, (x - high.astype(F32)).astype(BF16)


def mms(left, right, contract):
    total = mm(left[0], right[0], contract, None)
    if len(right) > 1:
        total += mm(left[0], right[1], contract, None)
    if len(left) > 1:
        total += mm(left[1], right[0], contract, None)
    return total


def lower_ones(size):
    rows = lax.broadcasted_iota(jnp.int32, (size, size), 0)
    cols = lax.broadcasted_iota(jnp.int32, (size, size), 1)
    return rows >= cols


def running(decay_low):
    ones = lower_ones(decay_low.shape[0]).astype(F32).astype(BF16)
    return mm(ones, decay_low, (1, 0), None)


def sigmoid(x):
    return 1.0 / (1.0 + jnp.exp(-x))


def cost(micros):
    return pl.CostEstimate(flops=0, bytes_accessed=int(micros * 3.0e6), transcendentals=0)


def greet(axes):
    barrier = pltpu.get_barrier_semaphore()
    met = 0
    for axis in axes:
        me, count = lax.axis_index(axis), lax.axis_size(axis)
        for hop in range(1, count):
            pl.semaphore_signal(
                barrier, inc=1, device_id={axis: lax.rem(me + hop, count)},
                device_id_type=pl.DeviceIdType.MESH,
            )
        met += count - 1
    pl.semaphore_wait(barrier, met)


def push(src, dst, send, recv, to, axis="head"):
    return pltpu.make_async_remote_copy(
        src_ref=src, dst_ref=dst, send_sem=send, recv_sem=recv,
        device_id={axis: to}, device_id_type=pl.DeviceIdType.MESH,
    )


def near_order(z, count, i):
    both = jnp.minimum(z, count - 1 - z)
    left = z > count - 1 - z
    paired = jnp.where(i % 2 == 1, z - (i + 1) // 2, z + i // 2)
    single = jnp.where(left, z - (i - both), z + (i - both))
    return jnp.where(i <= 2 * both, paired, single)


class Line:
    def __init__(self, own, all_rows, send, recv):
        self.own, self.all, self.send, self.recv = own, all_rows, send, recv
        self.z, self.count = lax.axis_index("head"), lax.axis_size("head")
        self.rows, self.parts = own.shape[0], recv.shape[1]
        self.deep = self.rows // self.parts

    def at(self, b):
        return self.all.at[pl.ds(pl.multiple_of(b * self.rows, self.rows), self.rows)]

    def part(self, b, p):
        start = b * self.rows + p * self.deep
        return self.all.at[pl.ds(pl.multiple_of(start, self.deep), self.deep)]

    def first(self, way, p):
        to = lax.rem(self.z + (1 if way == 0 else self.count - 1), self.count)
        src = self.own.at[pl.ds(p * self.deep, self.deep)]
        return push(
            src, self.part(self.z, p), self.send.at[way, p], self.recv.at[self.z, p], to
        )

    def each_first(self, act):
        for p in range(self.parts):
            pl.when(self.z < self.count - 1)(lambda p=p: act(self.first(0, p)))
            pl.when(self.z > 0)(lambda p=p: act(self.first(1, p)))

    def start(self):
        self.each_first(lambda copy: copy.start())

    def passing(self, i, b, p):
        z, count = self.z, self.count
        to = jnp.where(b < z, z + 1, z - 1)
        going = ((b < z) & (z < count - 1)) | ((b > z) & (z > 0))
        copy = push(
            self.part(b, p), self.part(b, p), self.send.at[i + 1, p], self.recv.at[b, p],
            lax.rem(to + count, count),
        )
        return copy, going

    def receive(self, i, b, p=0):
        copy, going = self.passing(i, b, p)
        copy.wait_recv()
        pl.when(going)(copy.start)

    def finish(self):
        def sent(i, _):
            for p in range(self.parts):
                copy, going = self.passing(i, near_order(self.z, self.count, i), p)
                pl.when(going)(copy.wait_send)
            return 0

        lax.fori_loop(1, self.count, sent, 0)
        self.each_first(lambda copy: copy.wait_send())


class LineSum:
    def __init__(self, parts, landed, send, recv, rows):
        self.parts, self.landed, self.send, self.recv = parts, landed, send, recv
        self.z, self.count = lax.axis_index("head"), lax.axis_size("head")
        self.rows, self.pieces = rows, send.shape[1]
        self.deep = rows // self.pieces
        self.inner = (self.z > 0) & (self.z < self.count - 1)
        self.far_end = jnp.where(self.z < self.count - 1 - self.z, self.count - 1, 0)

    def piece(self, b, p):
        return pl.ds(pl.multiple_of(b * self.rows + p * self.deep, self.deep), self.deep)

    def onward(self, b, p):
        z, count = self.z, self.count
        to = jnp.where(b > z, z + 1, z - 1)
        slot = jnp.where((to == b) & (z > b), count, b)
        return push(
            self.parts.at[self.piece(b, p)], self.landed.at[self.piece(slot, p)],
            self.send.at[b, p], self.recv.at[slot, p], lax.rem(to + count, count),
        )

    def send_all(self):
        @pl.when(jnp.logical_not(self.inner))
        def _():
            for i in range(1, self.count):
                b = jnp.where(self.z == 0, self.count - i, i - 1)
                for p in range(self.pieces):
                    self.onward(b, p).start()

    def arrived(self, slot, p):
        at = self.piece(slot, p)
        push(
            self.landed.at[at], self.landed.at[at], self.send.at[0, p], self.recv.at[slot, p],
            lax.rem(self.z + 1, self.count),
        ).wait_recv()
        return self.landed[at, :].astype(F32)

    def relay(self, b, p):
        at = self.piece(b, p)
        self.parts[at, :] = (self.parts[at, :].astype(F32) + self.arrived(b, p)).astype(BF16)
        self.onward(b, p).start()

    def relay_in_turn(self, j):
        pieces = self.pieces

        @pl.when(self.inner & (j < pieces))
        def _():
            self.relay(self.count - 1 - self.z, j)

        @pl.when(self.inner & (j >= pieces))
        def _():
            self.relay(self.far_end, j - pieces)

        @pl.when(self.inner & (j > pieces))
        def _():
            self.relay(self.count - 1 - self.far_end, j - pieces - 1)

    def relay_last(self):
        @pl.when(self.inner)
        def _():
            self.relay(self.count - 1 - self.far_end, self.pieces - 1)

    def result(self, out):
        z, count = self.z, self.count
        for p in range(self.pieces):
            here = pl.ds(p * self.deep, self.deep)
            out[here, :] = self.parts[self.piece(z, p), :].astype(F32)

            @pl.when(z > 0)
            def _():
                out[here, :] += self.arrived(z, p)

            @pl.when(z < count - 1)
            def _():
                out[here, :] += self.arrived(count, p)

    def finish(self):
        def sent(i, _):
            b = near_order(self.z, self.count, i)
            for p in range(self.pieces):
                self.onward(b, p).wait_send()
            return 0

        lax.fori_loop(1, self.count, sent, 0)


class PairSum:
    def __init__(self, mine, paired, inbox, pair_send, pair_recv, send, recv):
        self.mine, self.paired, self.inbox = mine, paired, inbox
        self.pair_send, self.pair_recv, self.send, self.recv = pair_send, pair_recv, send, recv
        self.s, self.pairs = lax.axis_index("seq"), lax.axis_size("seq") // 2
        self.side, self.own = lax.rem(self.s, 2), self.s // 2
        self.deep, self.half = mine.shape[1], mine.shape[2] // 2
        self.levels = self.pairs.bit_length() - 1
        assert self.pairs == 1 << self.levels

    def block(self, k, other=False):
        i = 2 * k + (1 - self.side if other else self.side)
        return pl.ds(pl.multiple_of(i * self.deep, self.deep), self.deep)

    def to_partner(self, src, k):
        return push(
            src, self.paired.at[k], self.pair_send.at[k], self.pair_recv.at[k],
            self.s + 1 - 2 * self.side, "seq",
        )

    def bit(self, i, level):
        return lax.rem(i // (1 << level), 2)

    def move(self, side, slot, k, level):
        columns = pl.ds(side * self.half, self.half)
        to = self.s + (1 - 2 * self.bit(self.own, level)) * (2 << level)
        return push(
            self.mine.at[k, :, columns], self.inbox.at[slot, :, columns],
            self.send.at[side, slot], self.recv.at[side, slot], to, "seq",
        )

    def moves(self, side, step):
        order = list(range(self.levels))
        if side:
            order.reverse()
        level, free = order[step], sorted(order[step + 1 :])
        fixed = sum((self.bit(self.own, d) * (1 << d) for d in order[:step]), 0)
        offset = self.pairs - (1 << (self.levels - step))
        here = self.bit(self.own, level) * (1 << level)
        for c in range(1 << len(free)):
            rest = fixed + sum(((c >> j) & 1) << d for j, d in enumerate(free))
            yield offset + c, rest + here, rest + (1 << level) - here, level

    def pass_on(self, k):
        top = 1 << (self.levels - 1)
        pl.when(self.bit(k, 0) != self.bit(self.own, 0))(self.move(0, k // 2, k, 0).start)
        pl.when(k // top != self.own // top)(
            self.move(1, lax.rem(k, top), k, self.levels - 1).start
        )

    def advance(self, step):
        for side in range(2):
            columns = slice(side * self.half, (side + 1) * self.half)
            for slot, keep, gone, level in self.moves(side, step):
                self.move(side, slot, gone, level).wait_recv()
                self.mine[keep, :, columns] = (
                    self.mine[keep, :, columns].astype(F32)
                    + self.inbox[slot, :, columns].astype(F32)
                ).astype(BF16)
            if step + 1 < self.levels:
                for slot, keep, gone, level in self.moves(side, step + 1):
                    self.move(side, slot, gone, level).start()

    def finish(self, src):
        for k in range(self.pairs):
            self.to_partner(src(k), k).wait_send()
        for side in range(2):
            for step in range(self.levels):
                for slot, keep, gone, level in self.moves(side, step):
                    self.move(side, slot, gone, level).wait_send()


def gather_norm_kernel(own, gain, shard, normed, rows_of_all, rows_all, here_sem, send, recv,
                       w_sem, w_send, w_recv, w_pair, w_pair_recv):
    z, count, rows = lax.axis_index("head"), lax.axis_size("head"), own.shape[0]
    greet(("seq", "head"))
    line = Line(own, rows_all, send, recv)
    line.start()
    here = pltpu.make_async_copy(own, line.at(z), here_sem)
    here.start()

    s, deep, half = lax.axis_index("seq"), shard.shape[0], shard.shape[1] // 2
    side, pairs, own_pair = lax.rem(s, 2), lax.axis_size("seq") // 2, s // 2
    levels = pairs.bit_length() - 1
    assert pairs == 1 << levels
    orders = list(range(levels)), list(reversed(range(levels)))

    def bit(level):
        return lax.rem(own_pair // (1 << level), 2) * (1 << level)

    def block(k, of_side):
        return pl.ds(pl.multiple_of((2 * k + of_side) * deep, deep), deep)

    def across(part, step):
        level = orders[part][step]
        return own_pair + (1 << level) - 2 * bit(level)

    def known(part, step, start):
        done = orders[part][:step]
        base = start - sum((bit(d) for d in done), 0)
        for c in range(1 << step):
            yield base + sum(((c >> n) & 1) << d for n, d in enumerate(done))

    def hop(part, step, k):
        at = rows_of_all.at[block(k, side), pl.ds(part * half, half)]
        to = 2 * across(part, step) + side
        return push(at, at, w_send.at[part, step, k], w_recv.at[part, k], to, "seq")

    def begin(step):
        for part in range(2):
            for k in known(part, step, own_pair):
                hop(part, step, k).start()

    def advance(step):
        for part in range(2):
            for k in known(part, step, across(part, step)):
                hop(part, step, k).wait_recv()
        if step + 1 < levels:
            begin(step + 1)

    def to_partner(k, of_side):
        at = rows_of_all.at[block(k, of_side)]
        return push(at, at, w_pair.at[k], w_pair_recv.at[k], s + 1 - 2 * side, "seq")

    mine = pltpu.make_async_copy(shard, rows_of_all.at[block(own_pair, side)], w_sem)
    mine.start()
    mine.wait()
    begin(0)
    to_partner(own_pair, side).start()
    here.wait()
    band = 16

    def step(i, _):
        b = near_order(z, count, i)
        pl.when(i > 0)(lambda: line.receive(i, b))
        pl.when(i == 1)(lambda: advance(0))

        def norm(r, _):
            at = pl.ds(pl.multiple_of(b * rows + r * band, band), band)
            x = rows_all[at, :].astype(F32)
            inv = lax.rsqrt(jnp.mean(x * x, axis=-1, keepdims=True) + 1e-6)
            normed[at, :] = (x * inv * gain[...]).astype(BF16)
            return 0

        lax.fori_loop(0, rows // band, norm, 0)
        return 0

    lax.fori_loop(0, count, step, 0)
    for later in range(1, levels):
        advance(later)
    for k in range(pairs):
        pl.when(own_pair != k)(to_partner(k, side).start)
    for k in range(pairs):
        to_partner(k, 1 - side).wait_recv()
    for k in range(pairs):
        to_partner(k, side).wait_send()
    for part in range(2):
        for late in range(levels):
            for k in known(part, late, own_pair):
                hop(part, late, k).wait_send()
    line.finish()


def gather_norm(x, gain, shard):
    rows, width = x.shape
    seq = lax.axis_size("seq")
    anywhere = pl.BlockSpec(memory_space=pl.ANY)
    count = lax.axis_size("head")
    vmem = pl.BlockSpec(memory_space=pltpu.VMEM)
    dma = pltpu.SemaphoreType.DMA
    return pl.pallas_call(
        gather_norm_kernel,
        out_shape=(
            jax.ShapeDtypeStruct((count * rows, width), BF16),
            jax.ShapeDtypeStruct((seq * shard.shape[0], shard.shape[1]), BF16),
        ),
        in_specs=[vmem, vmem, anywhere],
        out_specs=(vmem, anywhere),
        scratch_shapes=[
            pltpu.VMEM((count * rows, width), BF16), dma(()), dma((count + 1, 1)), dma((count, 1)),
            dma(()), dma((2, (seq // 2).bit_length() - 1, seq // 2)), dma((2, seq // 2)),
            dma((seq // 2,)), dma((seq // 2,)),
        ],
        compiler_params=pltpu.CompilerParams(
            collective_id=1, has_side_effects=True, vmem_limit_bytes=32 << 20
        ),
        cost_estimate=cost(50),
        name="gather_norm",
    )(x, gain, shard)


def swap_slices(own, got, send, recv):
    side = lax.rem(lax.axis_index("seq"), 2)
    me, count = lax.axis_index("seq") // 2, lax.axis_size("seq") // 2

    def copy(hop, index):
        to = lax.rem(me + hop, count)
        return push(own.at[to], got.at[index], send.at[hop], recv.at[index], 2 * to + side, "seq")

    def start(hop, _):
        copy(hop, me).start()
        return 0

    def wait_recv(hop, _):
        copy(hop, lax.rem(me + hop, count)).wait_recv()
        return 0

    def wait_send(hop, _):
        copy(hop, me).wait_send()
        return 0

    def begin():
        lax.fori_loop(1, count, start, 0)
        got[me] = own[me]

    def end():
        lax.fori_loop(1, count, wait_recv, 0)

    def drain():
        lax.fori_loop(1, count, wait_send, 0)

    return begin, end, drain


def to_mate(src, dst, send, recv):
    s = lax.axis_index("seq")
    return push(src, dst, send, recv, s + 1 - 2 * lax.rem(s, 2), "seq")


def sided(own, mate):
    first = lax.rem(lax.axis_index("seq"), 2) == 0
    return jnp.where(first, own, mate), jnp.where(first, mate, own)


def scan_states(reverse, own, through, out):
    count, part = out.shape[0], out.shape[2]

    def step(k, state):
        j = count - 1 - k if reverse else k
        out[j] = state.astype(BF16)
        decay = through[j, :, 0:1, :].astype(F32) + through[j, :, 1:2, :].astype(F32)
        return decay * state + own[j, :, :part, :].astype(F32)

    lax.fori_loop(0, count, step, jnp.zeros(out.shape[1:], F32))


def front_kernel(keep, qkv, decay, og, gain, rows_own,
                 o_out, gated, through, pair_through, kept_out, rows_all,
                 kept, runs, state, sending, got, scanned, before, leaving, mate_out, mate_in,
                 back_out, back_in, first_state,
                 here_sem, go, come, s_send, s_recv, b_send, b_recv, z_send, z_recv, k_sem, m_sem):
    h, head = lax.axis_index("head"), lax.axis_size("head")
    count, micro, rows, dk = decay.shape
    dv = og.shape[-1]
    slices, part = scanned.shape[0], scanned.shape[2]
    scale = dk ** (-0.5)
    greet(("seq", "head"))
    line = Line(rows_own, rows_all, go, come)
    line.start()
    here = pltpu.make_async_copy(rows_own, line.at(h), here_sem)
    here.start()

    state[...] = jnp.zeros_like(state)

    def gather(b, carry):
        passed, alive = carry
        later_passed, later_alive = [], []
        for m in range(micro):
            run = running(decay[b, m])
            runs[b, m] = run
            last = run[rows - 1 : rows, :]
            carried = qkv[b, m, :, dk : 2 * dk].astype(F32) * jnp.exp(last - run)
            fresh = mms((qkv[b, m, :, 2 * dk :],), split(carried), (0, 0))
            kept[b, m] = fresh
            state[m] = jnp.exp(last) * (state[m] * keep[b, m]) + fresh
            later_passed.append(passed[m] + last)
            later_alive.append(alive[m] * keep[b, m])
        return later_passed, later_alive

    passed, alive = lax.fori_loop(
        0, count, gather,
        ([jnp.zeros((1, dk), F32)] * micro, [jnp.ones((1, dk), F32)] * micro),
    )
    tail = sending.shape[2] - part
    at = lax.broadcasted_iota(jnp.int32, (tail, dk), 0)
    half = dv // 2
    side = lax.rem(lax.axis_index("seq"), 2)
    own_half = pl.ds(pl.multiple_of(side * half, half), half)
    mate_half = pl.ds(pl.multiple_of((1 - side) * half, half), half)

    def as_rows(value):
        high, low = split(value)
        return jnp.where(at == 0, high.astype(F32), jnp.where(at == 1, low.astype(F32), 0.0))

    own_rows = [as_rows(jnp.exp(passed[m]) * alive[m]) for m in range(micro)]
    for m in range(micro):
        mate_out[m, :half, :] = state[m, mate_half, :].astype(BF16)
        mate_out[m, half:, :] = own_rows[m].astype(BF16)
    swap = to_mate(mate_out, mate_in, m_sem.at[0], m_sem.at[1])
    swap.start()
    swap.wait_recv()
    first_through = []
    for m in range(micro):
        firsts, seconds = sided(own_rows[m], mate_in[m, half:, :].astype(F32))
        pair_through[0, m], pair_through[1, m] = firsts.astype(BF16), seconds.astype(BF16)
        first, second = firsts[0:1] + firsts[1:2], seconds[0:1] + seconds[1:2]
        first_through.append(first)
        start, after = sided(state[m, own_half, :], mate_in[m, :half, :].astype(F32))
        first_state[m] = start
        pair = second * start + after
        both = as_rows(first * second).astype(BF16)
        for i in range(slices):
            sending[i, m, :part, :] = pair[i * part : (i + 1) * part, :].astype(BF16)
            sending[i, m, part:, :] = both
    begin, end, drain = swap_slices(sending, got, s_send, s_recv)
    begin()
    causal = lower_ones(rows)

    def inside(b, _):
        for m in range(micro):
            run = runs[b, m]
            queried = split(qkv[b, m, :, :dk].astype(F32) * (jnp.exp(run) * scale))
            keyed = split(qkv[b, m, :, dk : 2 * dk].astype(F32) * jnp.exp(-run))
            scores = jnp.where(causal, mms(queried, keyed, (1, 1)), 0.0)
            o_out[b, m] = mms(split(scores), (qkv[b, m, :, 2 * dk :],), (1, 0))
        return 0

    lax.fori_loop(0, count, inside, 0)
    line.receive(1, near_order(h, head, 1))
    end()
    through[...] = got[:, :, part:, :]
    scan_states(False, got, through, scanned)
    begin_back, end_back, drain_back = swap_slices(scanned, before, b_send, b_recv)
    begin_back()
    line.receive(2, near_order(h, head, 2))
    end_back()
    for m in range(micro):
        entry = before[:, m].astype(F32).reshape(half, dk)
        own, mate = sided(entry, first_through[m] * entry + first_state[m])
        state[m, own_half, :] = own
        back_out[m] = mate.astype(BF16)
    swap_back = to_mate(back_out, back_in, m_sem.at[2], m_sem.at[3])
    swap_back.start()
    swap_back.wait_recv()
    for m in range(micro):
        state[m, mate_half, :] = back_in[m].astype(F32)

    def to_owner(b):
        columns = gated.at[:, pl.ds(pl.multiple_of(h * dv, dv), dv)]
        return push(leaving.at[b], columns, z_send.at[b], z_recv.at[h], b)

    def save(b):
        return pltpu.make_async_copy(kept.at[b], kept_out.at[b], k_sem.at[b])

    def across(b, _):
        for m in range(micro):
            run = runs[b, m]
            queried = split(qkv[b, m, :, :dk].astype(F32) * (jnp.exp(run) * scale))
            entry = state[m] * keep[b, m]
            state[m] = jnp.exp(run[rows - 1 : rows, :]) * entry + kept[b, m]
            kept[b, m] = entry
            o = o_out[b, m] + mms(queried, split(entry), (1, 1))
            o_out[b, m] = o
            inv = lax.rsqrt(jnp.mean(o * o, axis=-1, keepdims=True) + 1e-5)
            normed = (o * inv * gain[...]).astype(BF16).astype(F32)
            gate = og[b, m]
            leaving[b, m * rows : (m + 1) * rows, :] = (normed * gate * sigmoid(gate)).astype(BF16)
        save(b).start()
        pl.when(b != h)(to_owner(b).start)

        @pl.when(b == 1)
        def _():
            line.receive(3, near_order(h, head, 3))

        return 0

    lax.fori_loop(0, count, across, 0)
    gated[:, pl.ds(pl.multiple_of(h * dv, dv), dv)] = leaving[h]
    for hop in range(1, head):
        other = lax.rem(h + hop, head)
        columns = gated.at[:, pl.ds(pl.multiple_of(other * dv, dv), dv)]
        push(leaving.at[other], columns, z_send.at[other], z_recv.at[other], other).wait_recv()
        to_owner(other).wait_send()
    for b in range(count):
        save(b).wait()
    here.wait()
    line.finish()
    drain()
    drain_back()
    swap.wait_send()
    swap_back.wait_send()


def attention_forward(keep, qkv, decays, og, gain, rows_own):
    blocks, micro, rows, width = qkv.shape
    dk, dv = decays.shape[-1], og.shape[-1]
    head, seq = lax.axis_size("head"), lax.axis_size("seq")
    assert blocks == head and head == 4
    pairs, half, tail = seq // 2, dv // 2, 16
    part = half // pairs
    own_rows = micro * rows
    vmem, anywhere = pl.BlockSpec(memory_space=pltpu.VMEM), pl.BlockSpec(memory_space=pl.ANY)
    dma = pltpu.SemaphoreType.DMA
    states, wider = (pairs, micro, part, dk), (pairs, micro, part + tail, dk)
    return pl.pallas_call(
        front_kernel,
        out_shape=(
            jax.ShapeDtypeStruct((blocks, micro, rows, dv), F32),
            jax.ShapeDtypeStruct((own_rows, head * dv), BF16),
            jax.ShapeDtypeStruct((pairs, micro, tail, dk), BF16),
            jax.ShapeDtypeStruct((2, micro, tail, dk), BF16),
            jax.ShapeDtypeStruct((blocks, micro, dv, dk), F32),
            jax.ShapeDtypeStruct((head * rows_own.shape[0], rows_own.shape[1]), BF16),
        ),
        in_specs=[vmem] * 5 + [anywhere],
        out_specs=(vmem,) * 4 + (anywhere,) * 2,
        scratch_shapes=[
            pltpu.VMEM((blocks, micro, dv, dk), F32), pltpu.VMEM((blocks, micro, rows, dk), F32),
            pltpu.VMEM((micro, dv, dk), F32), pltpu.VMEM(wider, BF16), pltpu.VMEM(wider, BF16),
            pltpu.VMEM(states, BF16), pltpu.VMEM(states, BF16),
            pltpu.VMEM((blocks, own_rows, dv), BF16),
            pltpu.VMEM((micro, half + tail, dk), BF16), pltpu.VMEM((micro, half + tail, dk), BF16),
            pltpu.VMEM((micro, half, dk), BF16), pltpu.VMEM((micro, half, dk), BF16),
            pltpu.VMEM((micro, half, dk), F32),
            dma(()), dma((head + 1, 1)), dma((head, 1)), dma((pairs,)), dma((pairs,)), dma((pairs,)),
            dma((pairs,)), dma((head,)), dma((head,)), dma((blocks,)), dma((4,)),
        ],
        compiler_params=pltpu.CompilerParams(
            collective_id=2, has_side_effects=True, vmem_limit_bytes=40 << 20
        ),
        cost_estimate=cost(90),
        name="attention_forward",
    )(keep, qkv, decays, og, gain, rows_own)


def ffn_kernel(count, x_own, c_all, w, g_x, f_parts, grad,
               wv, xs, cs, act, lin, parts, landed, turned, turned_c, tiles,
               w_sem, own_sem, go_sem, x_sem, p_sem, q_sem, o_sem):
    z = lax.axis_index("head")
    rows, width = x_own.shape
    hidden = act.shape[1] // 3
    chunk = lambda b: pl.ds(pl.multiple_of(b * rows, rows), rows)

    weights = [
        pltpu.make_async_copy(
            w.at[:, pl.ds(w.shape[1] + (k - 3) * hidden, hidden)],
            wv.at[:, pl.ds(k * hidden, hidden)],
            w_sem.at[k],
        )
        for k in range(3)
    ]
    own = [
        pltpu.make_async_copy(x_own, xs.at[chunk(z)], own_sem.at[0]),
        pltpu.make_async_copy(c_all, cs, own_sem.at[1]),
    ]
    for copy in own + weights:
        copy.start()
    greet(("head",))
    line = Line(x_own, xs, go_sem, x_sem)
    line.start()
    for copy in own + weights:
        copy.wait()

    total = LineSum(parts, landed, p_sem, q_sem, rows)

    halves = x_sem.shape[1]
    deep = rows // halves
    each = total.pieces // halves

    def step(t, _):
        i, half = t // halves, lax.rem(t, halves)
        b = near_order(z, count, i)
        pl.when(i > 0)(lambda: line.receive(i, b, half))
        start = b * rows + half * deep
        at = pl.ds(pl.multiple_of(start, deep), deep)
        x = xs[at, :]
        lin[0] = jnp.dot(x, wv[:, :hidden], preferred_element_type=F32)
        lin[1] = jnp.dot(x, wv[:, hidden : 2 * hidden], preferred_element_type=F32)
        lin[2] = jnp.dot(cs[at, :], wv[:, 2 * hidden :], preferred_element_type=F32)
        band = 16

        def act_rows(r, _):
            here = pl.ds(pl.multiple_of(r * band, band), band)
            there = pl.ds(pl.multiple_of(start + r * band, band), band)
            gate, up, g_product = lin[0, here, :], lin[1, here, :], lin[2, here, :]
            sig = sigmoid(gate)
            gated = gate * sig
            act[there, :hidden] = (g_product * up * sig * (1.0 + gate * (1.0 - sig))).astype(BF16)
            act[there, hidden : 2 * hidden] = (g_product * gated).astype(BF16)
            act[there, 2 * hidden :] = (gated * up).astype(BF16)
            return 0

        lax.fori_loop(0, deep // band, act_rows, 0)
        parts[at, :] = mm(act[at, : 2 * hidden], wv[:, : 2 * hidden], (1, 1), None).astype(BF16)

        @pl.when((i > 0) & jnp.logical_not(total.inner))
        def _():
            for p in range(each):
                total.onward(b, half * each + p).start()

        return 0

    lax.fori_loop(0, count * halves, step, 0)

    high = tiles.shape[1]
    steps = width // high
    first = grad.shape[1] - 3 * hidden

    def store(t, r, k):
        down = pl.ds(pl.multiple_of(r * high, high), high)
        into = grad.at[down, pl.ds(first + k * hidden, hidden)]
        return pltpu.make_async_copy(tiles.at[lax.rem(t, 2)], into, o_sem.at[lax.rem(t, 2)])

    turned[...] = xs[...].T
    turned_c[...] = cs[...].T

    def tile(r, k):
        t = 3 * r + k

        @pl.when(t >= 2)
        def _():
            store(t, r, k).wait()

        left_rows = (turned_c if k == 2 else turned)[
            pl.ds(pl.multiple_of(r * high, high), high), :
        ]
        tiles[lax.rem(t, 2)] = jnp.dot(
            left_rows, act[:, k * hidden : (k + 1) * hidden], preferred_element_type=F32
        ).astype(BF16)
        store(t, r, k).start()

    def slab(r, _):
        tile(r, 0)
        tile(r, 1)
        total.relay_in_turn(2 * r)
        tile(r, 2)
        at = chunk(r)
        f_parts[r] = mm(act[at, 2 * hidden :], wv[:, 2 * hidden :], (1, 1), None).astype(BF16)
        total.relay_in_turn(2 * r + 1)
        return 0

    lax.fori_loop(0, steps, slab, 0)
    total.relay_last()
    total.result(g_x)
    total.finish()
    line.finish()
    store(3 * steps - 2, 0, 0).wait()
    store(3 * steps - 1, 0, 0).wait()


def feed_forward(x_own, c_all, w, hidden, count):
    rows, width = x_own.shape
    group = rows * count
    assert count == 4 and width % 4 == 0 and rows % 64 == 0
    anywhere = pl.BlockSpec(memory_space=pl.ANY)
    vmem = pl.BlockSpec(memory_space=pltpu.VMEM)
    dma = pltpu.SemaphoreType.DMA
    return pl.pallas_call(
        functools.partial(ffn_kernel, count),
        out_shape=(
            jax.ShapeDtypeStruct((rows, width), F32),
            jax.ShapeDtypeStruct((count, rows, width), BF16),
            jax.ShapeDtypeStruct(w.shape, BF16),
        ),
        in_specs=[anywhere] * 3,
        out_specs=(vmem, vmem, anywhere),
        scratch_shapes=[
            pltpu.VMEM((width, 3 * hidden), BF16),
            pltpu.VMEM((group, width), BF16),
            pltpu.VMEM((group, width), BF16),
            pltpu.VMEM((group, 3 * hidden), BF16),
            pltpu.VMEM((3, rows, hidden), F32),
            pltpu.VMEM((group, width), BF16),
            pltpu.VMEM((group + rows, width), BF16),
            pltpu.VMEM((width, group), BF16),
            pltpu.VMEM((width, group), BF16),
            pltpu.VMEM((2, width // 4, hidden), BF16),
            dma((3,)), dma((2,)), dma((count + 1, 1)), dma((count, 1)),
            dma((count, 4)), dma((count + 1, 4)), dma((2,)),
        ],
        compiler_params=pltpu.CompilerParams(
            collective_id=0, has_side_effects=True, vmem_limit_bytes=60 << 20
        ),
        cost_estimate=cost(100),
        name="feed_forward",
    )(x_own, c_all, w)


def back_kernel(keep, gated_own, og, o_in, qkv, decay, logits, through, pair_through, gain,
                kept_in, parts_in,
                g_proj, g_logits, g_gain, f_out,
                gated_all, go, runs, g_queried, g_keyed, g_values, pulls, weights, kept,
                parts, landed, state, sending, got, scanned, after, mate_out, mate_in,
                back_out, back_in, second_state, m_sem, in_sem, z_send, z_recv, s_send, s_recv, b_send, b_recv, p_sem, q_sem):
    h, head = lax.axis_index("head"), lax.axis_size("head")
    count, micro, rows, dk = decay.shape
    dv = og.shape[-1]
    width = qkv.shape[-1]
    slices, part = sending.shape[0], sending.shape[2]
    scale = dk ** (-0.5)
    loads = [
        pltpu.make_async_copy(parts_in, parts, in_sem.at[0]),
        pltpu.make_async_copy(kept_in, kept, in_sem.at[1]),
    ]
    for load in loads:
        load.start()
    greet(("seq", "head"))

    def to_head(hop, slot):
        to = lax.rem(h + hop, head)
        columns = gated_own.at[:, pl.ds(pl.multiple_of(to * dv, dv), dv)]
        return push(columns, gated_all.at[slot], z_send.at[hop], z_recv.at[slot], to)

    for hop in range(1, head):
        to_head(hop, h).start()
    gated_all[h] = gated_own[:, pl.ds(pl.multiple_of(h * dv, dv), dv)]

    causal = lower_ones(rows)

    def reach(b, carry):
        before, alive = carry
        later_before, later_alive = [], []
        for m in range(micro):
            run = running(decay[b, m])
            runs[b, m] = run
            later_alive.append(alive[m] * keep[b, m])
            weights[b, m] = jnp.exp(before[m]) * later_alive[m]
            later_before.append(before[m] + run[rows - 1 : rows, :])
        return later_before, later_alive

    lax.fori_loop(
        0, count, reach, ([jnp.zeros((1, dk), F32)] * micro, [jnp.ones((1, dk), F32)] * micro)
    )
    g_gain[...] = jnp.zeros_like(g_gain)
    state[...] = jnp.zeros_like(state)

    def gates(i, _):
        b = near_order(h, head, i)
        pl.when(i > 0)(lambda: to_head(lax.rem(b - h + head, head), b).wait_recv())
        for m in range(micro):
            gate, o = og[b, m], o_in[b, m]
            grad = gated_all[b, m * rows : (m + 1) * rows, :].astype(F32)
            sig = sigmoid(gate)
            inv = lax.rsqrt(jnp.mean(o * o, axis=-1, keepdims=True) + 1e-5)
            plain = o * inv
            normed = (plain * gain[...]).astype(BF16).astype(F32)
            g_on = (grad * gate * sig).astype(BF16).astype(F32)
            g_proj[b, m, :, width:] = (
                grad * normed * sig * (1.0 + gate * (1.0 - sig))
            ).astype(BF16)
            scaled = g_on * gain[...]
            g_o = inv * (scaled - plain * jnp.mean(scaled * plain, axis=-1, keepdims=True))
            go[b, m] = g_o
            g_gain[0:1, :] += jnp.sum(g_on * plain, axis=0, keepdims=True)
            queried = qkv[b, m, :, :dk].astype(F32) * (jnp.exp(runs[b, m]) * scale)
            pull = mms(split(g_o), split(queried), (0, 0))
            pulls[b, m] = pull
            state[m] += pull * weights[b, m]
        return 0

    lax.fori_loop(0, head, gates, 0)
    loads[0].wait()
    total = LineSum(parts, landed, p_sem, q_sem, f_out.shape[0])
    total.send_all()
    half = dv // 2
    side = lax.rem(lax.axis_index("seq"), 2)
    own_half = pl.ds(pl.multiple_of(side * half, half), half)
    mate_half = pl.ds(pl.multiple_of((1 - side) * half, half), half)
    mate_out[...] = state[:, mate_half, :].astype(BF16)
    swap = to_mate(mate_out, mate_in, m_sem.at[0], m_sem.at[1])
    swap.start()
    swap.wait_recv()
    passes = pair_through[:, :, 0:1, :].astype(F32) + pair_through[:, :, 1:2, :].astype(F32)
    for m in range(micro):
        start, later_state = sided(state[m, own_half, :], mate_in[m].astype(F32))
        second_state[m] = later_state
        pair = passes[0, m] * later_state + start
        for i in range(slices):
            sending[i, m] = pair[i * part : (i + 1) * part, :].astype(BF16)
    begin, end, drain = swap_slices(sending, got, s_send, s_recv)
    begin()
    loads[1].wait()

    def inside(b, _):
        for m in range(micro):
            q = qkv[b, m, :, :dk].astype(F32)
            k = qkv[b, m, :, dk : 2 * dk].astype(F32)
            v = (qkv[b, m, :, 2 * dk :],)
            run = runs[b, m]
            queried, keyed = split(q * (jnp.exp(run) * scale)), split(k * jnp.exp(-run))
            g_o, entry = split(go[b, m]), split(kept[b, m])
            scores = split(jnp.where(causal, mms(queried, keyed, (1, 1)), 0.0))
            g_scores = split(jnp.where(causal, mms(g_o, v, (1, 1)), 0.0))
            g_queried[b, m] = mms(g_scores, keyed, (1, 0)) + mms(g_o, entry, (1, 0))
            g_keyed[b, m] = mms(g_scores, queried, (0, 0))
            g_values[b, m] = mms(scores, g_o, (0, 0))
        pl.when(total.inner)(lambda: total.relay(total.far_end, b))
        return 0

    lax.fori_loop(0, count, inside, 0)
    end()
    scan_states(True, got, through, scanned)
    begin_back, end_back, drain_back = swap_slices(scanned, after, b_send, b_recv)
    begin_back()

    @pl.when(total.inner)
    def _():
        for p in range(total.pieces):
            total.relay(head - 1 - total.far_end, p)
        for p in range(total.pieces):
            total.relay(head - 1 - h, p)

    end_back()
    for m in range(micro):
        leave = after[:, m].astype(F32).reshape(half, dk)
        firsts = passes[1, m] * leave + second_state[m]
        own, _ = sided(firsts, leave)
        mate, _ = sided(leave, firsts)
        state[m, own_half, :] = own
        back_out[m] = mate.astype(BF16)
    swap_back = to_mate(back_out, back_in, m_sem.at[2], m_sem.at[3])
    swap_back.start()
    swap_back.wait_recv()
    for m in range(micro):
        state[m, mate_half, :] = back_in[m].astype(F32)

    def across(step, _):
        b = count - 1 - step
        for m in range(micro):
            q = qkv[b, m, :, :dk].astype(F32)
            k = qkv[b, m, :, dk : 2 * dk].astype(F32)
            v = (qkv[b, m, :, 2 * dk :],)
            run = runs[b, m]
            last = run[rows - 1 : rows, :]
            up, down, rest = jnp.exp(run) * scale, jnp.exp(-run), jnp.exp(last - run)
            decayed = jnp.exp(last)
            gs = state[m]
            gs_parts = split(gs)
            carried = k * rest
            g_v = g_values[b, m] + mms(split(carried), gs_parts, (1, 1))
            g_carried = mms(v, gs_parts, (1, 0))
            from_carried = g_carried * carried
            g_total = jnp.sum(decayed * kept[b, m] * gs, axis=0, keepdims=True) + jnp.sum(
                from_carried, axis=0, keepdims=True
            )
            state[m] = (decayed * gs + pulls[b, m]) * keep[b, m]
            gq, gk = g_queried[b, m], g_keyed[b, m]
            g_run = gq * (q * up) - gk * (k * down) - from_carried
            later = mms((causal.astype(F32).astype(BF16),), split(g_run), (0, 0)) + g_total
            g_proj[b, m, :, :dk] = (gq * up).astype(BF16)
            g_proj[b, m, :, dk : 2 * dk] = (gk * down + g_carried * rest).astype(BF16)
            g_proj[b, m, :, 2 * dk : width] = g_v.astype(BF16)
            g_logits[b, m] = (
                later.astype(BF16).astype(F32) * sigmoid(-logits[b, m]) * (1.0 / GATE_NORM)
            )
        return 0

    lax.fori_loop(0, count, across, 0)
    total.result(f_out)
    total.finish()
    drain()
    drain_back()
    swap.wait_send()
    swap_back.wait_send()
    for hop in range(1, head):
        to_head(hop, h).wait_send()


def attention_back(
    keep, gated_own, og, o, qkv, decays, logits, through, pair_through, gain, kept, parts
):
    blocks, micro, rows, width = qkv.shape
    dk, dv = decays.shape[-1], og.shape[-1]
    head, seq = lax.axis_size("head"), lax.axis_size("seq")
    own_rows = parts.shape[0] // head
    vmem, anywhere = pl.BlockSpec(memory_space=pltpu.VMEM), pl.BlockSpec(memory_space=pl.ANY)
    dma = pltpu.SemaphoreType.DMA
    blocked = lambda w, kind: pltpu.VMEM((blocks, micro, rows, w), kind)
    pairs, half = seq // 2, dv // 2
    states = (pairs, micro, half // pairs, dk)
    halves = (micro, half, dk)
    return pl.pallas_call(
        back_kernel,
        out_shape=(
            jax.ShapeDtypeStruct((blocks, micro, rows, width + dv), BF16),
            jax.ShapeDtypeStruct((blocks, micro, rows, dk), F32),
            jax.ShapeDtypeStruct((8, dv), F32),
            jax.ShapeDtypeStruct((own_rows, parts.shape[1]), F32),
        ),
        in_specs=[vmem] * 10 + [anywhere] * 2,
        out_specs=(vmem,) * 4,
        scratch_shapes=[
            pltpu.VMEM((blocks, micro * rows, dv), BF16), blocked(dv, F32), blocked(dk, F32),
            blocked(dk, F32), blocked(dk, F32), blocked(dv, F32),
            pltpu.VMEM((blocks, micro, dv, dk), F32), pltpu.VMEM((blocks, micro, 1, dk), F32),
            pltpu.VMEM((blocks, micro, dv, dk), F32),
            pltpu.VMEM(parts.shape, BF16),
            pltpu.VMEM((parts.shape[0] + own_rows, parts.shape[1]), BF16),
            pltpu.VMEM((micro, dv, dk), F32),
            pltpu.VMEM(states, BF16), pltpu.VMEM(states, BF16), pltpu.VMEM(states, BF16),
            pltpu.VMEM(states, BF16), pltpu.VMEM(halves, BF16), pltpu.VMEM(halves, BF16),
            pltpu.VMEM(halves, BF16), pltpu.VMEM(halves, BF16), pltpu.VMEM(halves, F32), dma((4,)),
            dma((2,)), dma((head,)), dma((head,)), dma((pairs,)), dma((pairs,)), dma((pairs,)),
            dma((pairs,)), dma((head, 4)), dma((head + 1, 4)),
        ],
        compiler_params=pltpu.CompilerParams(
            collective_id=3, has_side_effects=True, vmem_limit_bytes=60 << 20
        ),
        cost_estimate=cost(80),
        name="attention_back",
    )(keep, gated_own, og, o, qkv, decays, logits, through, pair_through, gain, kept,
      parts)


def finish_kernel(xn_in, proj_in, w_in, g_logits, ranked, up_own, rank_down, source,
                  gain, g_ffn, g_head,
                  g_x, grad, norm_sum, ffn_sum, head_sum, bias_sum, up_sum, down_sum,
                  turned, proj, w, outgoing, mine, paired, inbox, heads_in, parts, landed,
                  slim_high, slim_low, small, small_in, small_part,
                  small_heads, small_all, rows_sum, in_sem, pair_send, pair_recv, send, recv, x_send, x_recv,
                  p_sem, q_sem, a_send, a_recv, b_send, b_recv, c_send, c_recv):
    h, head = lax.axis_index("head"), lax.axis_size("head")
    rows, width = g_x.shape
    deep = grad.shape[0] * head
    pairs = lax.axis_size("seq") // 2

    loads = [
        pltpu.make_async_copy(proj_in, proj, in_sem.at[0]),
        pltpu.make_async_copy(w_in, w, in_sem.at[1]),
        pltpu.make_async_copy(xn_in, landed.at[pl.ds(0, xn_in.shape[0])], in_sem.at[2]),
    ]
    for load in loads:
        load.start()
    sums = PairSum(mine, paired, inbox, pair_send, pair_recv, send, recv)
    for load in loads:
        load.wait()
    turned[...] = landed[: xn_in.shape[0], :].T
    greet(("seq", "head"))
    total = LineSum(parts, landed, p_sem, q_sem, rows)
    logit_parts = split(g_logits[...])
    g_ranked = mms(logit_parts, split(up_own[...]), (1, 1))
    slim = split(g_ranked)
    slim_high[...], slim_low[...] = slim

    def chunk(i, _):
        b = near_order(h, head, head - 1 - i)
        at = pl.ds(pl.multiple_of(b * rows, rows), rows)
        rank_part = mms((slim_high[at, :], slim_low[at, :]), (rank_down[...],), (1, 1))
        parts[at, :] = (mm(proj[at, :], w[...], (1, 1), None) + rank_part).astype(BF16)

        @pl.when((b != h) & jnp.logical_not(total.inner))
        def _():
            for p in range(total.pieces):
                total.onward(b, p).start()

        return 0

    lax.fori_loop(0, head, chunk, 0)

    def gone(k, _):
        outgoing[k] = jnp.dot(
            turned[sums.block(k, True), :], proj[...], preferred_element_type=F32
        ).astype(BF16)
        sums.to_partner(outgoing.at[k], k).start()
        return 0

    lax.fori_loop(0, pairs, gone, 0)

    def kept(k, _):
        here = jnp.dot(turned[sums.block(k), :], proj[...], preferred_element_type=F32)
        sums.to_partner(outgoing.at[k], k).wait_recv()
        mine[k] = (here + paired[k].astype(F32)).astype(BF16)
        sums.pass_on(k)

        @pl.when(total.inner & (k < total.pieces))
        def _():
            total.relay(total.far_end, k)

        @pl.when(total.inner & (k > 0) & (k <= total.pieces))
        def _():
            total.relay(head - 1 - total.far_end, k - 1)

        return 0

    lax.fori_loop(0, pairs, kept, 0)

    @pl.when(total.inner)
    def _():
        for p in range(pairs, total.pieces + 1):
            if p < total.pieces:
                total.relay(total.far_end, p)
            total.relay(head - 1 - total.far_end, p - 1)
        for p in range(total.pieces):
            total.relay(head - 1 - h, p)

    thin = grad.shape[0]

    def to_head(hop, slot):
        to = lax.rem(h + hop, head)
        at = pl.ds(pl.multiple_of(to * thin, thin), thin)
        return push(mine.at[sums.own, at, :], heads_in.at[slot], x_send.at[hop], x_recv.at[slot], to)

    sums.advance(0)

    total.result(g_x)
    rows_sum[...] = jnp.zeros_like(rows_sum)
    band = rows_sum.shape[0]

    def norm_rows(r, _):
        at = pl.ds(pl.multiple_of(r * band, band), band)
        x = source[at, :].astype(F32)
        inv = lax.rsqrt(jnp.mean(x * x, axis=-1, keepdims=True) + 1e-6)
        plain, g = x * inv, g_x[at, :]
        scaled = g * gain[...]
        inner = jnp.mean(scaled * plain, axis=-1, keepdims=True)
        rows_sum[...] += g * plain
        g_x[at, :] = inv * (scaled - plain * inner)
        return 0

    lax.fori_loop(0, rows // band, norm_rows, 0)
    rank, dk = up_own.shape
    low, keys = rank // 2, up_sum.shape[1]
    g_down = mms(slim, (turned[...],), (0, 1))
    g_up = mms(split(ranked[...]), logit_parts, (0, 0))
    small[...] = jnp.zeros_like(small)
    small[:low, :width] = g_down[:low]
    small[:low, width:] = g_down[low:]
    own_keys = pl.multiple_of(h * dk, dk)
    small[low:, pl.ds(own_keys, dk)] = g_up[:low]
    small[low:, pl.ds(keys + own_keys, dk)] = g_up[low:]
    small[low : low + 1, width:] = jnp.sum(rows_sum[...], axis=0, keepdims=True)
    small[low + 1 : low + 2, width:] = g_ffn[...]
    small[low + 2 : low + 3, width : width + g_head.shape[1]] = g_head[0:1, :]
    small[low + 3 : low + 4, pl.ds(width + own_keys, dk)] = jnp.sum(
        g_logits[...], axis=0, keepdims=True
    )
    s, seq = lax.axis_index("seq"), lax.axis_size("seq")
    wide = small.shape[1] // seq

    def piece(ref, i):
        return ref.at[:, pl.ds(pl.multiple_of(i * wide, wide), wide)]

    def begin_small(axis, me, count, copy):
        for hop in range(1, count):
            copy(hop, me, lax.rem(me + hop, count)).start()

    def end_small(axis, me, count, copy):
        for hop in range(1, count):
            other = lax.rem(me + hop, count)
            copy(hop, other, other).wait_recv()

    def scatter(hop, slot, to):
        return push(
            piece(small, to), small_in.at[slot], a_send.at[hop], a_recv.at[slot], to, "seq"
        )

    def between(hop, slot, to):
        return push(small_part, small_heads.at[slot], b_send.at[hop], b_recv.at[slot], to)

    def spread(hop, slot, to):
        return push(
            small_part, piece(small_all, slot), c_send.at[hop], c_recv.at[slot], to, "seq"
        )

    begin_small("seq", s, seq, scatter)
    small_in[s] = small[:, pl.ds(pl.multiple_of(s * wide, wide), wide)]
    for step in range(1, sums.levels):
        sums.advance(step)
    for hop in range(1, head):
        to_head(hop, h).start()
    own_rows = pl.ds(pl.multiple_of(h * thin, thin), thin)
    heads_in[h] = mine[sums.own, own_rows, :]
    end_small("seq", s, seq, scatter)
    small_part[...] = jnp.sum(small_in[...], axis=0)
    begin_small("head", h, head, between)
    small_heads[h] = small_part[...]
    end_small("head", h, head, between)
    for hop in range(1, head):
        between(hop, h, lax.rem(h + hop, head)).wait_send()
    small_part[...] = jnp.sum(small_heads[...], axis=0)
    begin_small("seq", s, seq, spread)
    small_all[:, pl.ds(pl.multiple_of(s * wide, wide), wide)] = small_part[...]
    for hop in range(1, head):
        to_head(hop, lax.rem(h + hop, head)).wait_recv()
    dv = mine.shape[2] // 2 - dk
    for j in range(head):
        at, start = 0, 0
        for size in (dk, dk, dv, dv):
            grad[:, start + j * size : start + (j + 1) * size] = heads_in[j, :, at : at + size]
            at, start = at + size, start + head * size
    end_small("seq", s, seq, spread)
    down_sum[:low, :] = small_all[:low, :width]
    down_sum[low:, :] = small_all[:low, width:]
    up_sum[:low, :] = small_all[low:, :keys]
    up_sum[low:, :] = small_all[low:, keys : 2 * keys]
    norm_sum[...] = small_all[low : low + 1, width:]
    ffn_sum[...] = small_all[low + 1 : low + 2, width:]
    head_sum[...] = small_all[low + 2 : low + 3, width : width + head_sum.shape[1]]
    bias_sum[...] = small_all[low + 3 : low + 4, width : width + keys]
    for hop in range(1, seq):
        scatter(hop, s, lax.rem(s + hop, seq)).wait_send()
        spread(hop, s, lax.rem(s + hop, seq)).wait_send()
    sums.finish(lambda k: outgoing.at[k])
    for hop in range(1, head):
        to_head(hop, h).wait_send()
    total.finish()


def finish(
    xn, g_proj, w_in, g_logits, ranked, up_own, rank_down, source, gain, g_ffn, g_head
):
    seq, head = lax.axis_size("seq"), lax.axis_size("head")
    group, width = xn.shape
    columns, rank = w_in.shape[1], ranked.shape[1]
    deep, rows, pairs = width // seq, group // head, seq // 2
    dk = up_own.shape[1]
    vmem, anywhere = pl.BlockSpec(memory_space=pltpu.VMEM), pl.BlockSpec(memory_space=pl.ANY)
    dma = pltpu.SemaphoreType.DMA
    blocks = lambda count, w: pltpu.VMEM((count, deep, w), BF16)
    ends = lambda w: pltpu.VMEM((head, deep // head, w), BF16)
    moves = dma((2, pairs - 1))
    return pl.pallas_call(
        finish_kernel,
        out_shape=(
            jax.ShapeDtypeStruct((rows, width), F32),
            jax.ShapeDtypeStruct((deep // head, columns * head), BF16),
            jax.ShapeDtypeStruct((1, width), F32),
            jax.ShapeDtypeStruct((1, width), F32),
            jax.ShapeDtypeStruct((1, g_head.shape[1]), F32),
            jax.ShapeDtypeStruct((1, dk * head), F32),
            jax.ShapeDtypeStruct((rank, dk * head), F32),
            jax.ShapeDtypeStruct((rank, width), F32),
        ),
        in_specs=[anywhere] * 3 + [vmem] * 8,
        out_specs=(vmem,) * 8,
        scratch_shapes=[
            pltpu.VMEM((width, group), BF16), pltpu.VMEM(g_proj.shape, BF16),
            pltpu.VMEM(w_in.shape, BF16), blocks(pairs, columns), blocks(pairs, columns),
            blocks(pairs, columns), blocks(pairs - 1, columns), ends(columns),
            pltpu.VMEM((group, width), BF16), pltpu.VMEM((group + rows, width), BF16),
            pltpu.VMEM(ranked.shape, BF16), pltpu.VMEM(ranked.shape, BF16),
            pltpu.VMEM((rank, 2 * width), F32), pltpu.VMEM((seq, rank, 2 * width // seq), F32),
            pltpu.VMEM((rank, 2 * width // seq), F32),
            pltpu.VMEM((head, rank, 2 * width // seq), F32),
            pltpu.VMEM((rank, 2 * width), F32), pltpu.VMEM((16, width), F32),
            dma((3,)), dma((pairs,)), dma((pairs,)), moves, moves, dma((head,)), dma((head,)),
            dma((head, 4)), dma((head + 1, 4)),
            dma((seq,)), dma((seq,)), dma((head,)), dma((head,)), dma((seq,)), dma((seq,)),
        ],
        compiler_params=pltpu.CompilerParams(
            collective_id=5, has_side_effects=True, vmem_limit_bytes=60 << 20
        ),
        cost_estimate=cost(95),
        name="finish",
    )(xn, g_proj, w_in, g_logits, ranked, up_own, rank_down, source, gain, g_ffn, g_head)


def weight_grad_kernel(left, right, *rest):
    out, turned = rest[-2:]

    @pl.when(pl.program_id(1) == 0)
    def _():
        turned[...] = left[...].T

    out[...] = jnp.dot(turned[...], right[...], preferred_element_type=F32).astype(BF16)


def weight_grad(left, right, into, columns, start, tile):
    depth, rows = left.shape
    high = min(rows, 512)
    first = start // tile
    given = () if into is None else (into,)
    return pl.pallas_call(
        weight_grad_kernel,
        out_shape=jax.ShapeDtypeStruct((rows, columns), BF16),
        grid=(rows // high, right.shape[1] // tile),
        in_specs=[
            pl.BlockSpec((depth, high), lambda i, j: (0, i)),
            pl.BlockSpec((depth, tile), lambda i, j: (0, j)),
        ]
        + [pl.BlockSpec(memory_space=pl.ANY) for _ in given],
        out_specs=pl.BlockSpec((high, tile), lambda i, j: (i, first + j)),
        scratch_shapes=[pltpu.VMEM((high, depth), BF16)],
        input_output_aliases={2: 0} if given else {},
        compiler_params=pltpu.CompilerParams(
            dimension_semantics=("arbitrary", "arbitrary"), vmem_limit_bytes=48 << 20
        ),
        cost_estimate=pl.CostEstimate(
            flops=2 * depth * rows * right.shape[1],
            bytes_accessed=2 * (depth * rows + (depth + rows) * right.shape[1]),
            transcendentals=0,
        ),
        name="weight_grad",
    )(left, right, *given)


def product_kernel(left, right, out, total):
    part = jnp.dot(left[...], right[...], preferred_element_type=F32)
    step, last = pl.program_id(0), pl.num_programs(0) - 1

    @pl.when(step == 0)
    def _():
        total[...] = part

    @pl.when((step > 0) & (step < last))
    def _():
        total[...] += part

    @pl.when(step == last)
    def _():
        out[...] = (total[...] + part).astype(BF16)


def rows_by_columns(left, right, columns):
    rows, depth = left.shape
    tile = depth // 4
    return pl.pallas_call(
        product_kernel,
        out_shape=jax.ShapeDtypeStruct((rows, columns), BF16),
        grid=(depth // tile,),
        in_specs=[
            pl.BlockSpec((rows, tile), lambda j: (0, j)),
            pl.BlockSpec((tile, columns), lambda j: (j, 0)),
        ],
        out_specs=pl.BlockSpec((rows, columns), lambda j: (0, 0)),
        scratch_shapes=[pltpu.VMEM((rows, columns), F32)],
        compiler_params=pltpu.CompilerParams(
            dimension_semantics=("arbitrary",), vmem_limit_bytes=32 << 20
        ),
        cost_estimate=cost(5),
        name="product",
    )(left, right)


def gather_weight(w):
    return lax.all_gather(w, "seq", axis=0, tiled=True)


def scatter_grad(g):
    return lax.psum_scatter(g.astype(BF16), "seq", scatter_dimension=0, tiled=True)


def dot(a, b, contract, precision=None):
    return lax.dot_general(
        a, b, (((contract[0],), (contract[1],)), ((), ())),
        precision=precision, preferred_element_type=F32,
    )


def rms(x, epsilon):
    return lax.rsqrt(jnp.mean(x * x, axis=-1, keepdims=True) + epsilon)


def norm_back(grad, gain, normed, inv):
    scaled = grad * gain
    inner = jnp.mean(scaled * normed, axis=-1, keepdims=True)
    return inv * (scaled - normed * inner), jnp.sum(grad * normed, axis=0)


def on_device(
    tokens, starts, cotangent, mix_in, mix_out, gate_up, down_proj,
    norm_gain, ffn_gain, head_gain, rank_down, rank_up, gate_bias,
):
    micro, rows, width = tokens.shape
    heads, seq = lax.axis_size("head"), lax.axis_size("seq")
    head = lax.axis_index("head")
    keys, dv = rank_up.shape[1], head_gain.shape[0]
    dk, vals = keys // heads, dv * heads
    hidden_units = down_proj.shape[1]
    group = heads * micro * rows
    proj_width = 2 * dk + 2 * dv

    def own_columns(w, start, size):
        return lax.dynamic_slice_in_dim(w, start + head * size, size, 1)

    w_in_own = jnp.concatenate(
        [
            own_columns(mix_in, 0, dk),
            own_columns(mix_in, keys, dk),
            own_columns(mix_in, 2 * keys, dv),
            own_columns(mix_in, 2 * keys + vals, dv),
        ],
        axis=1,
    )
    later = gather_weight(
        jnp.concatenate(
            [mix_out, gate_up.reshape(gate_up.shape[0], 2 * hidden_units), down_proj], axis=1
        )
    )
    w_out = later[:, :vals]
    up_own = own_columns(rank_up, 0, dk)
    bias_own = lax.dynamic_slice_in_dim(gate_bias, head * dk, dk, 0)

    xn, w_in = gather_norm(
        tokens.reshape(micro * rows, width), norm_gain.reshape(1, width), w_in_own
    )
    qkv = dot(xn, w_in[:, : 2 * dk + dv], (1, 0)).astype(BF16)
    og = dot(xn, w_in[:, 2 * dk + dv :], (1, 0))
    ranked = dot(xn, rank_down, (1, 0))
    logits = dot(ranked, up_own, (1, 0), HIGHEST) + bias_own
    decays = (jax.nn.log_sigmoid(logits) / GATE_NORM).astype(BF16)

    def blocks(x):
        return x.reshape(heads, micro, rows, x.shape[-1])

    qkv_b, og_b, decays_b = blocks(qkv), blocks(og), blocks(decays)
    gain_row = head_gain.reshape(1, dv)
    keep = 1.0 - jnp.broadcast_to(starts.T[:, :, None, None], (heads, micro, 1, dk)).astype(F32)
    o_b, gated, through, pair_through, kept, all_cot = attention_forward(
        keep, qkv_b, decays_b, og_b, gain_row, cotangent.reshape(micro * rows, width)
    )

    source = tokens.astype(F32).reshape(micro * rows, width)
    hidden = source + dot(gated, w_out, (1, 1))
    inv_ffn = rms(hidden, 1e-6)
    plain_ffn = hidden * inv_ffn
    h2 = (plain_ffn * ffn_gain).astype(BF16)

    g_h2, ffn_part, grads = feed_forward(h2, all_cot, later, hidden_units, heads)

    back_ffn, g_ffn_gain = norm_back(g_h2, ffn_gain, plain_ffn, inv_ffn)
    g_hidden = cotangent.astype(F32).reshape(micro * rows, width) + back_ffn
    g_mixed = g_hidden.astype(BF16)
    grads = scatter_grad(weight_grad(g_mixed, gated, grads, later.shape[1], 0, vals))
    g_gated = rows_by_columns(g_mixed, later, vals)
    g_proj_b, g_logits_b, g_head_gain, ffn_out = attention_back(
        keep, g_gated, og_b, o_b, qkv_b, decays_b, blocks(logits), through, pair_through, gain_row, kept, ffn_part.reshape(group, width),
    )
    output = (hidden + ffn_out).astype(BF16)
    g_proj, g_logits = g_proj_b.reshape(group, proj_width), g_logits_b.reshape(group, dk)
    back_in, grad_in, *small, g_rank_down = finish(
        xn, g_proj, w_in, g_logits, ranked, up_own, rank_down, tokens.reshape(micro * rows, width),
        norm_gain.reshape(1, width), g_ffn_gain.reshape(1, width), g_head_gain,
    )
    g_norm_gain, g_ffn_gain, g_head_gain, g_bias, g_rank_up = small
    input_grad = g_hidden + back_in
    slab = width // (seq * heads)
    grad_in, grads = lax.optimization_barrier((grad_in, grads))
    grad_ffn = grads[:, vals:]
    grad_out = lax.all_to_all(
        grads[:, :vals].reshape(heads, slab, vals), "head", split_axis=0, concat_axis=0, tiled=True
    )
    grad_out = grad_out.astype(F32).sum(0)
    return (
        output.reshape(tokens.shape),
        input_grad.reshape(tokens.shape),
        grad_in.astype(F32),
        grad_out,
        grad_ffn[:, : 2 * hidden_units].astype(F32).reshape(-1, 2, hidden_units),
        grad_ffn[:, 2 * hidden_units :].astype(F32),
        g_norm_gain.reshape(norm_gain.shape),
        g_ffn_gain.reshape(ffn_gain.shape),
        g_head_gain.reshape(head_gain.shape),
        g_rank_down.T,
        g_rank_up,
        g_bias.reshape(gate_bias.shape),
    )


def solution(mesh):
    rows = P(None, ("seq", "head"), None)
    return jax.shard_map(
        on_device,
        mesh=mesh,
        in_specs=(
            rows, P(None, "seq"), rows, P("seq", None), P("seq", None),
            P("seq", None, "head"), P("seq", "head"), P(), P(), P(), P(), P(), P(),
        ),
        out_specs=(
            rows, rows, P(("seq", "head"), None), P(("seq", "head"), None),
            P("seq", None, "head"), P("seq", "head"), P(), P(), P(), P(), P(), P(),
        ),
        check_vma=False,
    )
```
